32 devices in a mesh: dp: 8 (over z, y), mp: 4 (over x, core).
Axes of the slice: x: 2, y: 2, z: 4, core: 2. Of those that a mesh axis runs over, the one named last changes fastest.
Arguments:
- tokens: bfloat16 [64, 64, 1024], P(('dp', 'mp')), may hold values from -6 to 6
- lengths: int32 [64], P('dp'), may hold values from 32 to 64, as said below
- grid_order: int32 [64, 256], P(('dp', 'mp')), may hold values from 0 to 255, as said below
- grid_keep: int32 [64, 256], P(('dp', 'mp')), may hold values from 0 to 1, as said below
- ground_dist: float32 [64], P(('dp', 'mp')), may hold values from 0.5 to 4
- enc_norm: float32 [1024], replicated, may hold values from 0.5 to 1.5
- enc_query: bfloat16 [1024, 1024], P(None, 'mp'), may hold values from -0.1875 to 0.1875
- enc_key: bfloat16 [1024, 1024], P(None, 'mp'), may hold values from -0.1875 to 0.1875
- enc_value: bfloat16 [1024, 1024], P(None, 'mp'), may hold values from -0.1875 to 0.1875
- enc_proj: bfloat16 [1024, 1024], P('mp'), may hold values from -0.75 to 0.75
- enc_norm2: float32 [1024], replicated, may hold values from 0.5 to 1.5
- enc_up: bfloat16 [1024, 4096], P(None, 'mp'), may hold values from -0.1875 to 0.1875
- enc_down: bfloat16 [4096, 1024], P('mp'), may hold values from -0.09375 to 0.09375
- embed_proj: bfloat16 [1024, 512], P(None, 'mp'), may hold values from -0.1875 to 0.1875
- mask_token: float32 [512], replicated, may hold values from -4 to 4
- dec_norm: float32 [512], replicated, may hold values from 0.5 to 1.5
- dec_query: bfloat16 [512, 512], replicated, may hold values from -0.25 to 0.25
- dec_key: bfloat16 [512, 512], replicated, may hold values from -0.25 to 0.25
- dec_value: bfloat16 [512, 512], replicated, may hold values from -0.25 to 0.25
- dec_proj: bfloat16 [512, 512], replicated, may hold values from -2 to 2
- dec_norm2: float32 [512], replicated, may hold values from 0.5 to 1.5
- dec_up: bfloat16 [512, 2048], replicated, may hold values from -0.25 to 0.25
- dec_down: bfloat16 [2048, 512], replicated, may hold values from -0.125 to 0.125
- pred_proj: bfloat16 [512, 768], replicated, may hold values from -0.25 to 0.25
- cotangent: bfloat16 [64, 256, 768], P(('dp', 'mp')), may hold values from -6 to 6
Outputs:
- decoded: float32 [64, 256, 768], P(('dp', 'mp'))
- grad_tokens: float32 [64, 64, 1024], P(('dp', 'mp'))
- grad_enc_norm: float32 [1024], replicated
- grad_enc_query: float32 [1024, 1024], P('dp', 'mp')
- grad_enc_key: float32 [1024, 1024], P('dp', 'mp')
- grad_enc_value: float32 [1024, 1024], P('dp', 'mp')
- grad_enc_proj: float32 [1024, 1024], P('mp', 'dp')
- grad_enc_norm2: float32 [1024], replicated
- grad_enc_up: float32 [1024, 4096], P('dp', 'mp')
- grad_enc_down: float32 [4096, 1024], P('mp', 'dp')
- grad_embed_proj: float32 [1024, 512], P('dp', 'mp')
- grad_mask_token: float32 [512], replicated
- grad_dec_norm: float32 [512], replicated
- grad_dec_query: float32 [512, 512], P('dp', 'mp')
- grad_dec_key: float32 [512, 512], P('dp', 'mp')
- grad_dec_value: float32 [512, 512], P('dp', 'mp')
- grad_dec_proj: float32 [512, 512], P('dp', 'mp')
- grad_dec_norm2: float32 [512], replicated
- grad_dec_up: float32 [512, 2048], P('dp', 'mp')
- grad_dec_down: float32 [2048, 512], P('dp', 'mp')
- grad_pred_proj: float32 [512, 768], P('dp', 'mp')
The draws below stay inside these ranges and needn't reach their ends.
Inputs may be any that keep to these rules, and one draw needn't show every extreme that they name: Rows 0 to lengths[i] - 1 of tokens are image i's visible patches; some image has exactly 64. `grid_order`: each row, images in grid order, is a permutation of the 256 positions; its first lengths entries of the same image are the positions of that image's visible rows, in row order. `grid_keep`: 1 exactly at the positions that grid_order lists among the image's first lengths entries.
All inputs are finite; a program needn't handle non-finite values.
Results may differ from the reference program's by a relative error of at most 0.03.
Values may be sent and summed in bfloat16 or wider, within the bound.
A program may use at most 192 MiB of HBM per device.

```python
import math
import jax
import jax.numpy as jnp
from jax import lax

D = 1024
HE = 16
FE = 4096
DD = 512
HD = 16
FD = 2048
PIX = 768
SIDE = 16
VMAX = 64
IPD = 1
GRID = 256
IMG_DEV = 8
IMAGES = 64


def masking_plan(key):
    base_key = jax.random.fold_in(key, 11)
    order_keys = jax.random.split(jax.random.fold_in(base_key, 1), IMAGES)
    orders = jax.vmap(lambda one_key: jax.random.permutation(one_key, GRID))(order_keys).astype(jnp.int32)
    counts = jax.random.randint(jax.random.fold_in(base_key, 2), (IMAGES,), VMAX // 2, VMAX + 1).astype(jnp.int32)
    counts = counts.at[0].set(VMAX).at[1].set(VMAX // 2)
    rank_rows = jnp.argsort(orders, axis=-1).astype(jnp.int32)
    keep_flags = (rank_rows < counts[:, None]).astype(jnp.int32)
    return (orders, counts, keep_flags)


def to_grid_order_drawn(values):
    shaped = values.reshape((IMAGES // IMG_DEV, IMG_DEV // IPD, IPD) + values.shape[1:])
    return jnp.swapaxes(shaped, 0, 1).reshape(values.shape)


def draw_lengths(key, part):
    return masking_plan(key)[1]


def draw_grid_order(key, part):
    return to_grid_order_drawn(masking_plan(key)[0])


def draw_grid_keep(key, part):
    return to_grid_order_drawn(masking_plan(key)[2])


def block_scale(stream_key, dims, cuts, low, largest):
    def one(position, blocks):
        steps = jax.random.uniform(jax.random.fold_in(jax.random.fold_in(stream_key, 6), position), (blocks,), jnp.float32, low / len(cuts), largest / len(cuts))
        return jnp.repeat(jnp.exp(steps), dims[position] // blocks).reshape((-1,) + (1,) * (len(dims) - position - 1))

    factor_of = one(*cuts[0])
    for cut in cuts[1:]:
        factor_of = factor_of * one(*cut)
    return factor_of


def bell_draw(stream_key, extent, width, bound, cuts=(), held_as=jnp.bfloat16):
    values = jax.random.normal(stream_key, extent, jnp.float32) * width
    if len(cuts) > 0:
        values = block_scale(stream_key, extent, cuts, -0.22, 0.18) * values
    return jnp.clip(values, min=-bound, max=bound).astype(held_as)


def setup_inputs(seed: int = 0) -> dict:
    seeds = jax.random.split(jax.random.key(seed), 26)
    tokens = bell_draw(seeds[0], (IMAGES, VMAX, D), 1.0, 6.0, ((0, 32),))
    lengths = draw_lengths(jax.random.fold_in(seeds[25], 71), 0)
    grid_order = draw_grid_order(jax.random.fold_in(seeds[25], 71), 0)
    grid_keep = draw_grid_keep(jax.random.fold_in(seeds[25], 71), 0)
    ground_dist = jnp.clip(jnp.exp(math.log(4.0) - 2.0794415 * jax.random.uniform(seeds[4], (IMAGES,), jnp.float32) ** block_scale(seeds[4], (IMAGES,), ((0, 32),), -0.2, 0.2)), 0.5, 4.0)
    enc_norm = jnp.clip(1.0 + 0.1 * jax.random.normal(seeds[5], (D,), jnp.float32), 0.5, 1.5)
    enc_query = bell_draw(seeds[6], (D, D), D ** -0.5, 0.1875, ((1, 4),))
    enc_key = bell_draw(seeds[7], (D, D), D ** -0.5, 0.1875, ((1, 4),))
    enc_value = bell_draw(seeds[8], (D, D), D ** -0.5, 0.1875, ((1, 4),))
    enc_proj = bell_draw(seeds[9], (D, D), (D // 16) ** -0.5, 0.75, ((0, 4),))
    enc_norm2 = jnp.clip(1.0 + 0.1 * jax.random.normal(seeds[10], (D,), jnp.float32), 0.5, 1.5)
    enc_up = bell_draw(seeds[11], (D, FE), D ** -0.5, 0.1875, ((1, 4),))
    enc_down = bell_draw(seeds[12], (FE, D), FE ** -0.5, 0.09375, ((0, 4),))
    embed_proj = bell_draw(seeds[13], (D, DD), D ** -0.5, 0.1875, ((1, 4),))
    mask_token = bell_draw(seeds[14], (DD,), 1.0, 4.0, (), jnp.float32)
    dec_norm = jnp.clip(1.0 + 0.1 * jax.random.normal(seeds[15], (DD,), jnp.float32), 0.5, 1.5)
    dec_query = bell_draw(seeds[16], (DD, DD), DD ** -0.5, 0.25)
    dec_key = bell_draw(seeds[17], (DD, DD), DD ** -0.5, 0.25)
    dec_value = bell_draw(seeds[18], (DD, DD), DD ** -0.5, 0.25)
    dec_proj = bell_draw(seeds[19], (DD, DD), (max(DD // 64, 1)) ** -0.5, 2.0)
    dec_norm2 = jnp.clip(1.0 + 0.1 * jax.random.normal(seeds[20], (DD,), jnp.float32), 0.5, 1.5)
    dec_up = bell_draw(seeds[21], (DD, FD), DD ** -0.5, 0.25)
    dec_down = bell_draw(seeds[22], (FD, DD), FD ** -0.5, 0.125)
    pred_proj = bell_draw(seeds[23], (DD, PIX), DD ** -0.5, 0.25)
    cotangent = bell_draw(seeds[24], (IMAGES, GRID, PIX), 1.0, 6.0, ((0, 32),))
    return {"tokens": tokens, "lengths": lengths, "grid_order": grid_order, "grid_keep": grid_keep, "ground_dist": ground_dist, "enc_norm": enc_norm, "enc_query": enc_query, "enc_key": enc_key, "enc_value": enc_value, "enc_proj": enc_proj, "enc_norm2": enc_norm2, "enc_up": enc_up, "enc_down": enc_down, "embed_proj": embed_proj, "mask_token": mask_token, "dec_norm": dec_norm, "dec_query": dec_query, "dec_key": dec_key, "dec_value": dec_value, "dec_proj": dec_proj, "dec_norm2": dec_norm2, "dec_up": dec_up, "dec_down": dec_down, "pred_proj": pred_proj, "cotangent": cotangent}


eps_norm = 1e-06
masked_score = -1e+30
top_precision = lax.Precision.HIGHEST

@jax.custom_vjp
def low(v):
    return lax.optimization_barrier(v.astype(jnp.bfloat16)).astype(jnp.float32)

@jax.custom_vjp
def low_back(v):
    return v

def low_keep(v):
    return (low(v), None)

def low_pass(kept, grad):
    return (grad,)

def back_keep(v):
    return (v, None)

def back_low(kept, grad):
    return (low(grad),)
low.defvjp(low_keep, low_pass)
low_back.defvjp(back_keep, back_low)

def layer_norm(values, scale_gain):
    center = values - lax.optimization_barrier(jnp.mean(values, axis=-1, keepdims=True))
    spread = lax.optimization_barrier(jnp.mean(center * center, axis=-1, keepdims=True))
    return center * lax.rsqrt(spread + eps_norm) * scale_gain

def matmul(left_side, right_side):
    flat_rows = left_side.reshape(-1, left_side.shape[-1])
    product = jnp.dot(flat_rows, right_side, precision=top_precision, preferred_element_type=jnp.float32)
    return product.reshape(left_side.shape[:-1] + (right_side.shape[1],))

def ref_block(inputs, key_valid, weights, head_count):
    gain_attn, w_query, w_key, w_value, w_out, gain_mlp, w_up, w_down = weights
    images, length, width_in = inputs.shape
    normed = low(layer_norm(inputs, gain_attn))
    queries = low(low_back(matmul(normed, w_query)))
    keys_all = low(low_back(matmul(normed, w_key)))
    values_all = low(low_back(matmul(normed, w_value)))
    head_size = queries.shape[-1] // head_count
    shaped_q = queries.reshape(images, length, head_count, head_size)
    shaped_k = keys_all.reshape(images, length, head_count, head_size)
    shaped_v = values_all.reshape(images, length, head_count, head_size)
    scaling = float(head_size) ** (-0.5)
    scores = low_back(jnp.einsum('nqhd,nkhd->nhqk', shaped_q, shaped_k, precision=top_precision)) * scaling
    if key_valid is not None:
        scores = jnp.where(key_valid[:, None, None, :], scores, masked_score)
    prob_rows = low(jax.nn.softmax(scores, axis=-1))
    mixed_rows = jnp.einsum('nhqk,nkhd->nqhd', prob_rows, shaped_v, precision=top_precision)
    mixed_rows = low(low_back(mixed_rows)).reshape(images, length, head_count * head_size)
    middle = inputs + low_back(matmul(mixed_rows, w_out))
    second = low(layer_norm(middle, gain_mlp))
    pre_act = low_back(matmul(second, w_up))
    active = low(jax.nn.gelu(pre_act, approximate=False))
    return middle + low_back(matmul(active, w_down))

def grid_codes(distance, side_count, columns):
    quarter = columns // 4
    frequency = 10000.0 ** (-jnp.arange(quarter, dtype=jnp.float32) / quarter)
    places = jnp.arange(side_count * side_count)
    row_pos = (places // side_count).astype(jnp.float32)
    col_pos = (places % side_count).astype(jnp.float32)
    row_angle = distance[:, None, None] * row_pos[None, :, None] * frequency[None, None, :]
    col_angle = distance[:, None, None] * col_pos[None, :, None] * frequency[None, None, :]
    return jnp.concatenate([jnp.sin(row_angle), jnp.cos(row_angle), jnp.sin(col_angle), jnp.cos(col_angle)], axis=-1)

def placement_table(visible_order, keep_flags, visible):
    positions = jnp.arange(visible_order.shape[1])
    matches = (visible_order[:, None, :visible] == positions[None, :, None]) & (keep_flags[:, :, None] == 1)
    return matches.astype(jnp.float32)

def to_grid_order(values):
    shaped = values.reshape((values.shape[0] // IMG_DEV, IMG_DEV // IPD, IPD) + values.shape[1:])
    return jnp.swapaxes(shaped, 0, 1).reshape(values.shape)

def forward(params, lengths, grid_order, grid_keep, ground_dist):
    tokens = params[0]
    enc_weights = params[1:9]
    embed_proj = params[9]
    mask_token = params[10]
    dec_weights = params[11:19]
    pred_proj = params[19]
    image_total = tokens.shape[0]
    group_count = image_total // IMG_DEV
    key_valid = jnp.arange(VMAX)[None, :] < lengths[:, None]

    def encode(pieces):
        block_tokens, block_valid = pieces
        hidden = ref_block(block_tokens, block_valid, enc_weights, HE)
        return low(low_back(matmul(low(hidden), embed_proj)))
    embedded = lax.map(jax.checkpoint(encode), (tokens.reshape(group_count, IMG_DEV, VMAX, D), key_valid.reshape(group_count, IMG_DEV, VMAX)))
    embedded = to_grid_order(embedded.reshape(image_total, VMAX, DD))
    grid_code = grid_codes(ground_dist, SIDE, DD)
    masked = (1 - grid_keep).astype(jnp.float32)[..., None]

    def decode(pieces):
        block_emb, block_order, block_keep, block_masked, block_codes = pieces
        pick_table = placement_table(block_order, block_keep, VMAX)
        dec_start = jnp.einsum('npt,ntc->npc', pick_table, block_emb, precision=top_precision)
        dec_start = dec_start + block_masked * mask_token + block_codes
        hidden = ref_block(dec_start, None, dec_weights, HD)
        return matmul(low(hidden), pred_proj)
    decoded = lax.map(jax.checkpoint(decode), (embedded.reshape(group_count, IMG_DEV, VMAX, DD), grid_order.reshape(group_count, IMG_DEV, GRID), grid_keep.reshape(group_count, IMG_DEV, GRID), masked.reshape(group_count, IMG_DEV, GRID, 1), grid_code.reshape(group_count, IMG_DEV, GRID, DD)))
    return decoded.reshape(image_total, GRID, PIX)

def reference(tokens, lengths, grid_order, grid_keep, ground_dist, enc_norm, enc_query, enc_key, enc_value, enc_proj, enc_norm2, enc_up, enc_down, embed_proj, mask_token, dec_norm, dec_query, dec_key, dec_value, dec_proj, dec_norm2, dec_up, dec_down, pred_proj, cotangent):
    weights = (enc_norm, enc_query, enc_key, enc_value, enc_proj, enc_norm2, enc_up, enc_down, embed_proj, mask_token, dec_norm, dec_query, dec_key, dec_value, dec_proj, dec_norm2, dec_up, dec_down, pred_proj)
    primal = (tokens.astype(jnp.float32),) + tuple((weight.astype(jnp.float32) for weight in weights))

    def run_forward(*params):
        return forward(params, lengths, grid_order, grid_keep, ground_dist)
    decoded, pullback = jax.vjp(run_forward, *primal)
    gradients = pullback(cotangent.astype(jnp.float32))
    return (decoded, gradients[0], gradients[1], gradients[2], gradients[3], gradients[4], gradients[5], gradients[6], gradients[7], gradients[8], gradients[9], gradients[10], gradients[11], gradients[12], gradients[13], gradients[14], gradients[15], gradients[16], gradients[17], gradients[18], gradients[19])
```

```python
import jax
import jax.numpy as jnp
from jax import lax
from jax.experimental import pallas as pl
from jax.experimental.pallas import tpu as pltpu
from jax.sharding import PartitionSpec as P

HE = 16
HD = 16
SIDE = 16
IPD = 1


eps_norm = 1e-06
masked_score = -1e30
low_type = jnp.bfloat16
full_type = jnp.float32


def layer_norm(values, scale_gain):
    center = values - jnp.mean(values, axis=-1, keepdims=True)
    spread = jnp.mean(center * center, axis=-1, keepdims=True)
    return center * lax.rsqrt(spread + eps_norm) * scale_gain


def exact_gelu(values):
    return jax.nn.gelu(values, approximate=False)


def matmul(left_side, right_side):
    flat_rows = left_side.reshape(-1, left_side.shape[-1])
    product = jnp.dot(flat_rows, right_side, preferred_element_type=full_type)
    return product.reshape(left_side.shape[:-1] + (right_side.shape[1],))


def matmul_t(left_side, right_side):
    flat_rows = left_side.reshape(-1, left_side.shape[-1])
    product = lax.dot_general(
        flat_rows, right_side, (((1,), (1,)), ((), ())), preferred_element_type=full_type
    )
    return product.reshape(left_side.shape[:-1] + (right_side.shape[0],))


def outer_sum(left_side, right_side):
    return lax.dot_general(
        left_side.reshape(-1, left_side.shape[-1]),
        right_side.reshape(-1, right_side.shape[-1]),
        (((0,), (0,)), ((), ())),
        preferred_element_type=full_type,
    )


def spread_rows(values, tensor_split):
    if tensor_split:
        return lax.all_gather(values, "mp", axis=0, tiled=True)
    return values


def collect_rows(values, tensor_split):
    if tensor_split:
        return lax.psum_scatter(
            values.astype(jnp.bfloat16), "mp", scatter_dimension=0, tiled=True
        ).astype(jnp.float32)
    return values


def images_per_block(images, length):
    grouped = 1
    while grouped * length < 512 and grouped < images:
        grouped = grouped * 2
    return grouped


def in_blocks(blocked_array, grouped):
    return blocked_array.reshape(
        (blocked_array.shape[0] // grouped, grouped) + blocked_array.shape[1:]
    )


def with_heads(blocked_array, head_count):
    return blocked_array.reshape(
        blocked_array.shape[:2] + (head_count, blocked_array.shape[2] // head_count)
    )


def attend_forward(queries, keys_all, values_all, key_valid, head_count):
    images, length, columns = queries.shape
    grouped = images_per_block(images, length)
    scaling = float(columns // head_count) ** (-0.5)

    def one_block(pieces):
        query_b, key_b, value_b, valid_b = pieces
        scores = (
            jnp.einsum("nqhd,nkhd->nhqk", query_b, key_b, preferred_element_type=full_type)
            * scaling
        )
        scores = jnp.where(valid_b[:, None, None, :], scores, masked_score)
        row_max = jnp.max(scores, axis=-1, keepdims=True)
        weights = jnp.exp(scores - row_max)
        totals = jnp.sum(weights, axis=-1, keepdims=True)
        prob_rows = (weights / totals).astype(low_type)
        mixed_b = jnp.einsum(
            "nhqk,nkhd->nqhd", prob_rows, value_b, preferred_element_type=full_type
        )
        return (mixed_b.astype(low_type), (row_max + jnp.log(totals))[..., 0])

    pieces_in = (
        in_blocks(with_heads(queries, head_count), grouped),
        in_blocks(with_heads(keys_all, head_count), grouped),
        in_blocks(with_heads(values_all, head_count), grouped),
        in_blocks(key_valid, grouped),
    )
    mixed_rows, log_total = lax.map(one_block, pieces_in)
    return (
        mixed_rows.reshape(images, length, columns),
        log_total.reshape(images, head_count, length),
    )


def attend_backward(queries, keys_all, values_all, key_valid, log_total, grad_mixed, head_count):
    images, length, columns = queries.shape
    grouped = images_per_block(images, length)
    scaling = float(columns // head_count) ** (-0.5)

    def one_block(pieces):
        query_b, key_b, value_b, valid_b, total_b, grad_b = pieces
        scores = (
            jnp.einsum("nqhd,nkhd->nhqk", query_b, key_b, preferred_element_type=full_type)
            * scaling
        )
        scores = jnp.where(valid_b[:, None, None, :], scores, masked_score)
        prob_rows = jnp.exp(scores - total_b[..., None])
        grad_value_b = jnp.einsum(
            "nhqk,nqhd->nkhd", prob_rows.astype(low_type), grad_b, preferred_element_type=full_type
        )
        grad_probs = jnp.einsum(
            "nqhd,nkhd->nhqk", grad_b, value_b, preferred_element_type=full_type
        )
        grad_scores = prob_rows * (
            grad_probs - jnp.sum(grad_probs * prob_rows, axis=-1, keepdims=True)
        )
        grad_scores = (grad_scores * scaling).astype(low_type)
        grad_query_b = jnp.einsum(
            "nhqk,nkhd->nqhd", grad_scores, key_b, preferred_element_type=full_type
        )
        grad_key_b = jnp.einsum(
            "nhqk,nqhd->nkhd", grad_scores, query_b, preferred_element_type=full_type
        )
        return (
            grad_query_b.astype(low_type),
            grad_key_b.astype(low_type),
            grad_value_b.astype(low_type),
        )

    pieces_in = (
        in_blocks(with_heads(queries, head_count), grouped),
        in_blocks(with_heads(keys_all, head_count), grouped),
        in_blocks(with_heads(values_all, head_count), grouped),
        in_blocks(key_valid, grouped),
        in_blocks(log_total, grouped),
        in_blocks(with_heads(grad_mixed, head_count), grouped),
    )
    grad_query, grad_key, grad_value = lax.map(one_block, pieces_in)
    return (
        grad_query.reshape(images, length, columns),
        grad_key.reshape(images, length, columns),
        grad_value.reshape(images, length, columns),
    )


def block_forward(inputs, key_valid, weights, head_count, tensor_split):
    gain_attn, w_query, w_key, w_value, w_out, gain_mlp, w_up, w_down = weights
    normed = spread_rows(layer_norm(inputs, gain_attn).astype(low_type), tensor_split)
    queries = matmul(normed, w_query).astype(low_type)
    keys_all = matmul(normed, w_key).astype(low_type)
    values_all = matmul(normed, w_value).astype(low_type)
    mixed_rows, log_total = attend_forward(queries, keys_all, values_all, key_valid, head_count)
    middle = inputs + collect_rows(matmul(mixed_rows, w_out), tensor_split)
    second = spread_rows(layer_norm(middle, gain_mlp).astype(low_type), tensor_split)
    pre_act = matmul(second, w_up)
    active = exact_gelu(pre_act).astype(low_type)
    outputs = middle + collect_rows(matmul(active, w_down), tensor_split)
    kept_state = (
        inputs,
        normed,
        queries,
        keys_all,
        values_all,
        mixed_rows,
        log_total,
        middle,
        second,
        pre_act,
        active,
    )
    return (outputs, kept_state)


def block_backward(grad_out, kept_state, key_valid, weights, head_count, tensor_split):
    gain_attn, w_query, w_key, w_value, w_out, gain_mlp, w_up, w_down = weights
    (
        inputs,
        normed,
        queries,
        keys_all,
        values_all,
        mixed_rows,
        log_total,
        middle,
        second,
        pre_act,
        active,
    ) = kept_state
    grad_branch = spread_rows(grad_out.astype(low_type), tensor_split)
    grad_down = outer_sum(grad_branch, active) if tensor_split else outer_sum(active, grad_branch)
    grad_active = matmul_t(grad_branch, w_down)
    grad_pre = jax.vjp(exact_gelu, pre_act)[1](grad_active)[0].astype(low_type)
    grad_up = outer_sum(second, grad_pre)
    grad_second = collect_rows(matmul_t(grad_pre, w_up), tensor_split)
    norm_grad, grad_gain_mlp = jax.vjp(layer_norm, middle, gain_mlp)[1](grad_second)
    grad_middle = grad_out + norm_grad
    grad_attn = spread_rows(grad_middle.astype(low_type), tensor_split)
    grad_w_out = outer_sum(grad_attn, mixed_rows) if tensor_split else outer_sum(mixed_rows, grad_attn)
    grad_mixed = matmul_t(grad_attn, w_out).astype(low_type)
    grad_query, grad_key, grad_value = attend_backward(
        queries, keys_all, values_all, key_valid, log_total, grad_mixed, head_count
    )
    grad_w_query = outer_sum(normed, grad_query)
    grad_w_key = outer_sum(normed, grad_key)
    grad_w_value = outer_sum(normed, grad_value)
    grad_normed = (
        matmul_t(grad_query, w_query) + matmul_t(grad_key, w_key) + matmul_t(grad_value, w_value)
    )
    grad_normed = collect_rows(grad_normed, tensor_split)
    input_grad, grad_gain_attn = jax.vjp(layer_norm, inputs, gain_attn)[1](grad_normed)
    return (
        grad_middle + input_grad,
        (
            grad_gain_attn,
            grad_w_query,
            grad_w_key,
            grad_w_value,
            grad_w_out,
            grad_gain_mlp,
            grad_up,
            grad_down,
        ),
    )


def grid_codes(distance, side_count, columns):
    quarter = columns // 4
    frequency = 10000.0 ** (-jnp.arange(quarter, dtype=full_type) / quarter)
    places = jnp.arange(side_count * side_count)
    row_pos = (places // side_count).astype(full_type)
    col_pos = (places % side_count).astype(full_type)
    row_angle = distance[:, None, None] * row_pos[None, :, None] * frequency[None, None, :]
    col_angle = distance[:, None, None] * col_pos[None, :, None] * frequency[None, None, :]
    return jnp.concatenate(
        [jnp.sin(row_angle), jnp.cos(row_angle), jnp.sin(col_angle), jnp.cos(col_angle)], axis=-1
    )


def placement_table(visible_order, keep_flags, visible):
    positions = jnp.arange(visible_order.shape[1])
    matches = (visible_order[:, None, :visible] == positions[None, :, None]) & (
        keep_flags[:, :, None] == 1
    )
    return matches.astype(low_type)


MESH = pl.DeviceIdType.MESH
LANES = 128


def log2_of(count):
    bits = count.bit_length() - 1
    assert 1 << bits == count
    return bits


def bit_reverse(index, bits):
    out = 0
    for position in range(bits):
        out = out * 2 + ((index >> position) & 1)
    return out


def partner(axis, bit):
    dp, mp = lax.axis_index("dp"), lax.axis_index("mp")
    step = 1 << bit
    if axis == "dp":
        return (dp ^ step, mp), (dp >> bit) & 1
    return (dp, mp ^ step), (mp >> bit) & 1


def enter_barrier(partners):
    barrier = pltpu.get_barrier_semaphore()
    for peer in partners:
        pl.semaphore_signal(barrier, inc=1, device_id=peer, device_id_type=MESH)
    pl.semaphore_wait(barrier, len(partners))


class HalvingSum:
    def __init__(self, stages, buffers, window, send_sems, recv_sems):
        self.stages, self.buffers, self.window = stages, buffers, window
        self.send_sems, self.recv_sems = send_sems, recv_sems
        self.copies = [None] * len(stages)

    def view(self, index, start, size):
        return self.buffers[index].at[(pl.ds(start, size),) + self.window]

    def start(self, index):
        peer, mine = partner(*self.stages[index])
        half = self.buffers[index].shape[0] // 2
        copy = pltpu.make_async_remote_copy(
            src_ref=self.view(index, (1 - mine) * half, half),
            dst_ref=self.view(index + 1, 0, half),
            send_sem=self.send_sems.at[index],
            recv_sem=self.recv_sems.at[index],
            device_id=peer,
            device_id_type=MESH,
        )
        copy.start()
        self.copies[index] = copy

    def finish(self, index):
        self.copies[index].wait()
        peer, mine = partner(*self.stages[index])
        half = self.buffers[index].shape[0] // 2

        def one(position, carry):
            there = self.buffers[index + 1].at[(position,) + self.window]
            here = self.buffers[index].at[(mine * half + position,) + self.window]
            there[...] = there[...] + here[...]
            return carry

        lax.fori_loop(0, half, one, 0)


def dec_pieces(data_count, model_count, shapes):
    offset, pieces = 0, []
    for rows, columns in shapes:
        height, width = rows // data_count, columns // model_count
        tiles = -(-width // LANES)
        pieces.append((offset, height, width, tiles))
        offset += height * tiles
    return pieces, offset


def pack_dec(matrices, data_count, model_count):
    pieces, total = dec_pieces(data_count, model_count, [m.shape for m in matrices])
    blocks = []
    for matrix, (offset, height, width, tiles) in zip(matrices, pieces):
        block = matrix.astype(low_type).reshape(data_count, height, model_count, width)
        block = jnp.pad(block, ((0, 0), (0, 0), (0, 0), (0, tiles * LANES - width)))
        block = block.reshape(data_count, height, model_count, tiles, LANES)
        block = jnp.transpose(block, (2, 0, 3, 1, 4))
        blocks.append(block.reshape(model_count, data_count, tiles * height, LANES))
    packed = jnp.concatenate(blocks, axis=2)
    packed = reversed_order(reversed_order(packed, 0), 1)
    return packed.reshape((model_count * data_count,) + packed.shape[2:])


def reversed_order(values, axis):
    count = values.shape[axis]
    bits = log2_of(count)
    shape = values.shape
    split = values.reshape(shape[:axis] + (2,) * bits + shape[axis + 1 :])
    order = list(range(split.ndim))
    order[axis : axis + bits] = order[axis : axis + bits][::-1]
    return jnp.transpose(split, order).reshape(shape)


def reduce_kernel(data_count, model_count, enc_cuts, dec_cuts, pieces, enc_widths, *refs):
    data_bits, model_bits = log2_of(data_count), log2_of(model_count)
    enc_stages = [("dp", bit) for bit in range(data_bits)]
    dec_stages = [("mp", bit) for bit in range(model_bits)] + enc_stages
    refs = list(refs)
    enc_in, dec_in, norm_in = refs[:3]
    enc_outs = refs[3 : 3 + len(enc_widths)]
    dec_outs = refs[3 + len(enc_widths) : 3 + len(enc_widths) + len(pieces)]
    rest = refs[3 + len(enc_widths) + len(pieces) :]
    norm_out, rest = rest[0], rest[1:]
    enc_bufs, rest = [enc_in] + rest[: len(enc_stages)], rest[len(enc_stages) :]
    dec_bufs, rest = [dec_in] + rest[: len(dec_stages)], rest[len(dec_stages) :]
    norm_acc, norm_got, enc_send, enc_recv, dec_send, dec_recv, norm_send, norm_recv = rest
    enter_barrier([partner(*stage)[0] for stage in dec_stages])

    columns = enc_in.shape[2] // enc_cuts
    enc = [
        HalvingSum(
            enc_stages,
            enc_bufs,
            (slice(None), pl.ds(cut * columns, columns)),
            enc_send.at[cut],
            enc_recv.at[cut],
        )
        for cut in range(enc_cuts)
    ]
    height = dec_in.shape[1] // dec_cuts
    dec = [
        HalvingSum(
            dec_stages,
            dec_bufs,
            (pl.ds(cut * height, height), slice(None)),
            dec_send.at[cut],
            dec_recv.at[cut],
        )
        for cut in range(dec_cuts)
    ]
    for one in dec + enc:
        one.start(0)
    norm_acc[0] = norm_in[...]
    for index, stage in enumerate(dec_stages):
        peer, mine = partner(*stage)
        copy = pltpu.make_async_remote_copy(
            src_ref=norm_acc.at[index],
            dst_ref=norm_got.at[index],
            send_sem=norm_send.at[index],
            recv_sem=norm_recv.at[index],
            device_id=peer,
            device_id_type=MESH,
        )
        copy.start()
        for one in dec + (enc if index < len(enc_stages) else []):
            one.finish(index)
            if index + 1 < len(one.stages):
                one.start(index + 1)
        copy.wait()
        norm_acc[index + 1] = norm_acc[index] + norm_got[index]
    norm_out[...] = norm_acc[len(dec_stages)]
    offset = 0
    for out, (width, flipped) in zip(enc_outs, enc_widths):
        block = enc_bufs[-1][0, :, offset : offset + width].astype(full_type)
        out[...] = block.T if flipped else block
        offset += width
    for out, (offset, rows, width, tiles) in zip(dec_outs, pieces):
        for tile in range(tiles):
            lanes = min(LANES, width - tile * LANES)
            block = dec_bufs[-1][0, offset + tile * rows : offset + (tile + 1) * rows, :lanes]
            out[:, tile * LANES : tile * LANES + lanes] = block.astype(full_type)


def reduce_all(enc_grads, dec_grads, norm_grads):
    data_count, model_count = lax.axis_size("dp"), lax.axis_size("mp")
    data_bits, model_bits = log2_of(data_count), log2_of(model_count)
    enc_widths = [(grad.shape[1], flipped) for grad, flipped in enc_grads]
    enc_packed = jnp.concatenate([grad.astype(low_type) for grad, flipped in enc_grads], axis=1)
    rows = enc_packed.shape[0] // data_count
    enc_cuts = 5
    dec_cuts = 2
    slack = -enc_packed.shape[1] % (enc_cuts * LANES)
    if slack:
        enc_packed = jnp.pad(enc_packed, ((0, 0), (0, slack)))
    enc_packed = reversed_order(enc_packed.reshape(data_count, rows, -1), 0)
    pieces, height = dec_pieces(data_count, model_count, [grad.shape for grad in dec_grads])
    dec_packed = pack_dec(dec_grads, data_count, model_count)
    flat = jnp.concatenate([grad.reshape(-1) for grad in norm_grads]).reshape(-1, LANES)
    stages = data_bits + model_bits
    scratch = []
    for bit in range(data_bits):
        scratch.append(pltpu.VMEM((data_count >> (bit + 1),) + enc_packed.shape[1:], low_type))
    for bit in range(stages):
        scratch.append(
            pltpu.VMEM(((data_count * model_count) >> (bit + 1), height, LANES), low_type)
        )
    scratch += [
        pltpu.VMEM((stages + 1,) + flat.shape, full_type),
        pltpu.VMEM((stages,) + flat.shape, full_type),
        pltpu.SemaphoreType.DMA((enc_cuts, data_bits)),
        pltpu.SemaphoreType.DMA((enc_cuts, data_bits)),
        pltpu.SemaphoreType.DMA((dec_cuts, stages)),
        pltpu.SemaphoreType.DMA((dec_cuts, stages)),
        pltpu.SemaphoreType.DMA((stages,)),
        pltpu.SemaphoreType.DMA((stages,)),
    ]
    out_shape = [
        jax.ShapeDtypeStruct((width, rows) if flipped else (rows, width), full_type)
        for width, flipped in enc_widths
    ]
    out_shape += [
        jax.ShapeDtypeStruct((high, width), full_type) for offset, high, width, tiles in pieces
    ]
    out_shape.append(jax.ShapeDtypeStruct(flat.shape, full_type))

    def kernel(*refs):
        reduce_kernel(data_count, model_count, enc_cuts, dec_cuts, pieces, enc_widths, *refs)

    outs = pl.pallas_call(
        kernel,
        out_shape=out_shape,
        in_specs=[pl.BlockSpec(memory_space=pltpu.VMEM)] * 3,
        out_specs=[pl.BlockSpec(memory_space=pltpu.VMEM)] * len(out_shape),
        scratch_shapes=scratch,
        compiler_params=pltpu.CompilerParams(
            collective_id=0, has_side_effects=True, vmem_limit_bytes=56 * 2**20
        ),
    )(enc_packed, dec_packed, flat)
    sums, position = [], 0
    flat_sum = outs[-1].reshape(-1)
    for grad in norm_grads:
        sums.append(flat_sum[position : position + grad.shape[0]])
        position += grad.shape[0]
    return outs[: len(enc_grads)], outs[len(enc_grads) : -1], sums


def per_device(
    tokens,
    lengths,
    grid_order,
    grid_keep,
    ground_dist,
    enc_norm,
    enc_query,
    enc_key,
    enc_value,
    enc_proj,
    enc_norm2,
    enc_up,
    enc_down,
    embed_proj,
    mask_token,
    dec_norm,
    dec_query,
    dec_key,
    dec_value,
    dec_proj,
    dec_norm2,
    dec_up,
    dec_down,
    pred_proj,
    cotangent,
):
    data_count = lax.axis_size("dp")
    model_count = lax.axis_size("mp")
    enc_weights = (enc_norm, enc_query, enc_key, enc_value, enc_proj, enc_norm2, enc_up, enc_down)
    dec_weights = (dec_norm, dec_query, dec_key, dec_value, dec_proj, dec_norm2, dec_up, dec_down)
    enc_heads = HE // model_count
    key_valid = jnp.arange(tokens.shape[1])[None, :] < lengths[:, None]
    enc_out, enc_saved = block_forward(
        tokens.astype(full_type), key_valid, enc_weights, enc_heads, True
    )
    enc_low = enc_out.astype(low_type)
    enc_all = spread_rows(enc_low, True)
    embedded = matmul(enc_all, embed_proj).astype(low_type)
    sectioned = embedded.reshape((data_count, -1) + embedded.shape[1:])
    arrived = lax.all_to_all(
        lax.all_to_all(sectioned, "dp", split_axis=0, concat_axis=0, tiled=True),
        "mp",
        split_axis=0,
        concat_axis=3,
        tiled=True,
    )
    arrived = arrived.reshape((-1,) + arrived.shape[2:])
    pick_table = placement_table(grid_order, grid_keep, arrived.shape[1])
    masked = (1 - grid_keep).astype(full_type)[..., None]
    dec_start = jnp.einsum("npt,ntc->npc", pick_table, arrived, preferred_element_type=full_type)
    dec_start = dec_start + masked * mask_token + grid_codes(ground_dist, SIDE, mask_token.shape[0])
    all_valid = jnp.ones(dec_start.shape[:2], jnp.bool_)
    dec_out, dec_saved = block_forward(dec_start, all_valid, dec_weights, HD, False)
    dec_low = dec_out.astype(low_type)
    decoded = matmul(dec_low, pred_proj)
    grad_pred = outer_sum(dec_low, cotangent)
    grad_dec_out = matmul_t(cotangent, pred_proj)
    grad_start, dec_grads = block_backward(
        grad_dec_out, dec_saved, all_valid, dec_weights, HD, False
    )
    grad_mask = jnp.sum(masked * grad_start, axis=(0, 1))
    grad_arrived = jnp.einsum("npt,npc->ntc", pick_table.astype(full_type), grad_start).astype(
        low_type
    )
    sent_back = grad_arrived.reshape((-1, IPD) + grad_arrived.shape[1:])
    returned = lax.all_to_all(
        lax.all_to_all(sent_back, "mp", split_axis=3, concat_axis=0, tiled=True),
        "dp",
        split_axis=0,
        concat_axis=0,
        tiled=True,
    )
    returned = returned.reshape((-1,) + returned.shape[2:])
    grad_embed = outer_sum(enc_all, returned)
    grad_enc_out = collect_rows(matmul_t(returned, embed_proj), True)
    grad_tokens, enc_grads = block_backward(
        grad_enc_out, enc_saved, key_valid, enc_weights, enc_heads, True
    )
    enc_out_grads, dec_final, norm_grads = reduce_all(
        [
            (enc_grads[1], False),
            (enc_grads[2], False),
            (enc_grads[3], False),
            (enc_grads[6], False),
            (grad_embed, False),
            (enc_grads[4], True),
            (enc_grads[7], True),
        ],
        [
            dec_grads[1],
            dec_grads[2],
            dec_grads[3],
            dec_grads[4],
            dec_grads[6],
            dec_grads[7],
            grad_pred,
        ],
        [enc_grads[0], enc_grads[5], dec_grads[0], dec_grads[5], grad_mask],
    )
    row_sums = enc_out_grads[:5]
    col_sums = enc_out_grads[5:]
    embed_final = row_sums[4]
    return (
        decoded,
        grad_tokens,
        norm_grads[0],
        row_sums[0],
        row_sums[1],
        row_sums[2],
        col_sums[0],
        norm_grads[1],
        row_sums[3],
        col_sums[1],
        embed_final,
        norm_grads[4],
        norm_grads[2],
        dec_final[0],
        dec_final[1],
        dec_final[2],
        dec_final[3],
        norm_grads[3],
        dec_final[4],
        dec_final[5],
        dec_final[6],
    )


def solution(mesh):
    return jax.shard_map(
        per_device,
        mesh=mesh,
        in_specs=(
            P(("dp", "mp"), None, None),
            P("dp"),
            P(("dp", "mp"), None),
            P(("dp", "mp"), None),
            P(("dp", "mp")),
            P(),
            P(None, "mp"),
            P(None, "mp"),
            P(None, "mp"),
            P("mp", None),
            P(),
            P(None, "mp"),
            P("mp", None),
            P(None, "mp"),
            P(),
            P(),
            P(),
            P(),
            P(),
            P(),
            P(),
            P(),
            P(),
            P(),
            P(("dp", "mp"), None, None),
        ),
        out_specs=(
            P(("dp", "mp"), None, None),
            P(("dp", "mp"), None, None),
            P(),
            P("dp", "mp"),
            P("dp", "mp"),
            P("dp", "mp"),
            P("mp", "dp"),
            P(),
            P("dp", "mp"),
            P("mp", "dp"),
            P("dp", "mp"),
            P(),
            P(),
            P("dp", "mp"),
            P("dp", "mp"),
            P("dp", "mp"),
            P("dp", "mp"),
            P(),
            P("dp", "mp"),
            P("dp", "mp"),
            P("dp", "mp"),
        ),
        check_vma=False,
    )
```

```python
import math

import jax
import jax.numpy as jnp
from jax import lax
from jax.experimental import pallas as pl
from jax.experimental.pallas import tpu as pltpu
from jax.sharding import PartitionSpec as P

HE = 16
HD = 16
SIDE = 16
IPD = 1


eps_norm = 1e-06
masked_score = -1e30
low_type = jnp.bfloat16
full_type = jnp.float32


MESH = pl.DeviceIdType.MESH
LANES = 128


def log2_of(count):
    bits = count.bit_length() - 1
    assert 1 << bits == count
    return bits


def bit_reverse(index, bits):
    out = 0
    for position in range(bits):
        out = out * 2 + ((index >> position) & 1)
    return out


def partner(axis, bit):
    dp, mp = lax.axis_index("dp"), lax.axis_index("mp")
    step = 1 << bit
    if axis == "dp":
        return (dp ^ step, mp), (dp >> bit) & 1
    return (dp, mp ^ step), (mp >> bit) & 1


def enter_barrier(partners):
    barrier = pltpu.get_barrier_semaphore()
    for peer in partners:
        pl.semaphore_signal(barrier, inc=1, device_id=peer, device_id_type=MESH)
    pl.semaphore_wait(barrier, len(partners))


class HalvingSum:
    def __init__(self, stages, buffers, window, send_sems, recv_sems):
        self.stages, self.buffers, self.window = stages, buffers, window
        self.send_sems, self.recv_sems = send_sems, recv_sems
        self.copies = [None] * len(stages)

    def view(self, index, start, size):
        return self.buffers[index].at[(pl.ds(start, size),) + self.window]

    def start(self, index):
        peer, mine = partner(*self.stages[index])
        half = self.buffers[index].shape[0] // 2
        copy = pltpu.make_async_remote_copy(
            src_ref=self.view(index, (1 - mine) * half, half),
            dst_ref=self.view(index + 1, 0, half),
            send_sem=self.send_sems.at[index],
            recv_sem=self.recv_sems.at[index],
            device_id=peer,
            device_id_type=MESH,
        )
        copy.start()
        self.copies[index] = copy

    def finish(self, index):
        self.copies[index].wait()
        peer, mine = partner(*self.stages[index])
        half = self.buffers[index].shape[0] // 2

        def one(position, carry):
            there = self.buffers[index + 1].at[(position,) + self.window]
            here = self.buffers[index].at[(mine * half + position,) + self.window]
            there[...] = there[...] + here[...]
            return carry

        lax.fori_loop(0, half, one, 0)


def dec_pieces(data_count, model_count, shapes):
    offset, pieces = 0, []
    for rows, columns in shapes:
        height, width = rows // data_count, columns // model_count
        tiles = -(-width // LANES)
        pieces.append((offset, height, width, tiles))
        offset += height * tiles
    return pieces, offset


LOG2E = 1.4426950408889634


def dot_as(left, right, left_dim, right_dim):
    return lax.dot_general(
        left, right, (((left_dim,), (right_dim,)), ((), ())), preferred_element_type=full_type
    )


def norm_parts(values):
    center = values - jnp.mean(values, axis=-1, keepdims=True)
    scale = lax.rsqrt(jnp.mean(center * center, axis=-1, keepdims=True) + eps_norm)
    return center * scale, scale


def norm_back(normed, scale, grad_scaled):
    first = jnp.mean(grad_scaled, axis=-1, keepdims=True)
    second = jnp.mean(grad_scaled * normed, axis=-1, keepdims=True)
    return (grad_scaled - first - normed * second) * scale


def gelu_pair(values):
    below = 0.5 + 0.5 * lax.erf(values * (0.5**0.5))
    density = jnp.exp2(values * values * (-0.5 * LOG2E)) * ((2.0 * math.pi) ** -0.5)
    return values * below, below + values * density


def decoder_kernel(images, heads, side, pieces, data_count, model_count, *refs):
    (
        arrived,
        order_ref,
        keep_ref,
        dist_ref,
        gain_attn,
        w_query,
        w_key,
        w_value,
        w_out,
        gain_mlp,
        w_up,
        w_down,
        w_pred,
        mask_token,
        cotangent,
        decoded,
        packed,
        grad_arrived,
        small,
        xs,
        qkv_weights,
        a_s,
        qkv_s,
        e_s,
        inv_s,
        o_s,
        mid_s,
        c_s,
        g_s,
        du_s,
        low_s,
        dy_s,
        dm_s,
        db_s,
        do_s,
    ) = refs
    length = side * side
    visible = arrived.shape[1]
    width = w_query.shape[0]
    hidden = w_up.shape[1]
    size = width // heads
    scaling = float(size) ** -0.5
    chunk = 512
    place = lax.broadcasted_iota(jnp.int32, (length, visible), 0)
    turn = lax.broadcasted_iota(jnp.int32, (length, visible), 1)

    def picks(image):
        order = order_ref[image, :, :visible]
        count = jnp.sum(keep_ref[image], axis=1, keepdims=True)
        return jnp.where((order == place) & (turn < count), 1.0, 0.0)

    def rows_of(image):
        return pl.ds(pl.multiple_of(image * length, length), length)

    for position, weight in enumerate((w_query, w_key, w_value)):
        qkv_weights[position * width : (position + 1) * width, :] = weight[...].T
    small[...] = jnp.zeros_like(small)

    def first_part(image, carry):
        rows = rows_of(image)
        pick = picks(image)
        hidden_rows = 1.0 - jnp.sum(pick, axis=1, keepdims=True)
        quarter = width // 4
        lane = lax.broadcasted_iota(jnp.int32, (side, quarter), 1).astype(full_type)
        line = lax.broadcasted_iota(jnp.int32, (side, quarter), 0).astype(full_type)
        angle = dist_ref[image] * line * jnp.exp(lane * (-math.log(10000.0) / quarter))
        table = jnp.concatenate([jnp.sin(angle), jnp.cos(angle)], axis=1)
        by_row = jnp.broadcast_to(table[:, None, :], (side, side, 2 * quarter))
        by_col = jnp.broadcast_to(table[None, :, :], (side, side, 2 * quarter))
        codes = jnp.concatenate(
            [by_row.reshape(length, 2 * quarter), by_col.reshape(length, 2 * quarter)], axis=1
        )
        start = jnp.dot(pick.astype(low_type), arrived[image], preferred_element_type=full_type)
        start = start + hidden_rows * mask_token[...] + codes
        xs[...] = start
        normed, scale = norm_parts(start)
        a_s[rows, :] = (normed * gain_attn[...]).astype(low_type)
        for position in range(3):
            part = dot_as(
                qkv_weights[position * width : (position + 1) * width, :], a_s[rows, :], 1, 1
            )
            if position == 0:
                part = part * (scaling * LOG2E)
            qkv_s[position * width : (position + 1) * width, rows] = part.astype(low_type)

        def one_head(head, inner):
            span = pl.multiple_of(head * size, size)
            query = qkv_s[pl.ds(span, size), rows]
            key = qkv_s[pl.ds(width + span, size), rows]
            value = qkv_s[pl.ds(2 * width + span, size), rows]
            scores = dot_as(key, query, 0, 0)
            weights = jnp.exp2(scores - jnp.max(scores, axis=0, keepdims=True))
            inverse = 1.0 / jnp.sum(weights, axis=0, keepdims=True)
            weights = weights.astype(low_type)
            e_s[head] = weights
            inv_s[head] = inverse
            mixed = jnp.dot(value, weights, preferred_element_type=full_type)
            o_s[pl.ds(span, size), rows] = (mixed * inverse).astype(low_type)
            return inner

        lax.fori_loop(0, heads, one_head, 0, unroll=4)

        middle = start + dot_as(o_s[:, rows], w_out[...], 0, 0)
        mid_s[...] = middle
        normed, scale = norm_parts(middle)
        c_s[rows, :] = (normed * gain_mlp[...]).astype(low_type)
        for position in range(hidden // chunk):
            cols = slice(position * chunk, (position + 1) * chunk)
            pre = jnp.dot(c_s[rows, :], w_up[:, cols], preferred_element_type=full_type)
            active, slope = gelu_pair(pre)
            g_s[rows, cols] = active.astype(low_type)
            du_s[rows, cols] = slope.astype(low_type)
        outputs = middle + jnp.dot(g_s[rows, :], w_down[...], preferred_element_type=full_type)
        low_s[rows, :] = outputs.astype(low_type)
        decoded[image] = jnp.dot(low_s[rows, :], w_pred[...], preferred_element_type=full_type)

        grad_out = dot_as(cotangent[image], w_pred[...], 1, 1)
        dm_s[rows, :] = grad_out.astype(low_type)
        for position in range(hidden // chunk):
            cols = slice(position * chunk, (position + 1) * chunk)
            grad_active = dot_as(dm_s[rows, :], w_down[cols, :], 1, 1)
            du_s[rows, cols] = (grad_active * du_s[rows, cols].astype(full_type)).astype(low_type)
        grad_second = dot_as(du_s[rows, :], w_up[...], 1, 1)
        normed, scale = norm_parts(mid_s[...])
        small[1:2, :] += jnp.sum(grad_second * normed, axis=0, keepdims=True)
        grad_middle = grad_out + norm_back(normed, scale, grad_second * gain_mlp[...])
        dy_s[...] = grad_middle
        db_s[rows, :] = grad_middle.astype(low_type)
        do_s[...] = dot_as(w_out[...], db_s[rows, :], 1, 1)

        def back_head(head, inner):
            span = pl.multiple_of(head * size, size)
            query = qkv_s[pl.ds(span, size), rows]
            key = qkv_s[pl.ds(width + span, size), rows]
            value = qkv_s[pl.ds(2 * width + span, size), rows]
            weights = e_s[head]
            grad_full = do_s[pl.ds(span, size), :] * (inv_s[head] * scaling)
            mixed = o_s[pl.ds(span, size), rows].astype(full_type)
            shift = jnp.sum(grad_full * mixed, axis=0, keepdims=True)
            grad_low = grad_full.astype(low_type)
            grad_probs = dot_as(value, grad_low, 0, 0)
            grad_scores = (weights.astype(full_type) * (grad_probs - shift)).astype(low_type)
            grad_value = dot_as(grad_low, weights, 1, 1) * (1.0 / scaling)
            grad_query = jnp.dot(key, grad_scores, preferred_element_type=full_type)
            grad_key = dot_as(query, grad_scores, 1, 1) * (1.0 / (scaling * LOG2E))
            qkv_s[pl.ds(span, size), rows] = grad_query.astype(low_type)
            qkv_s[pl.ds(width + span, size), rows] = grad_key.astype(low_type)
            qkv_s[pl.ds(2 * width + span, size), rows] = grad_value.astype(low_type)
            return inner

        lax.fori_loop(0, heads, back_head, 0, unroll=4)

        grad_normed = dot_as(qkv_s[:, rows], qkv_weights[...], 0, 0)
        normed, scale = norm_parts(xs[...])
        small[0:1, :] += jnp.sum(grad_normed * normed, axis=0, keepdims=True)
        grad_start = dy_s[...] + norm_back(normed, scale, grad_normed * gain_attn[...])
        small[2:3, :] += jnp.sum(hidden_rows * grad_start, axis=0, keepdims=True)
        grad_arrived[image] = dot_as(
            pick.astype(low_type), grad_start.astype(low_type), 0, 0
        ).astype(low_type)
        return carry

    lax.fori_loop(0, images, first_part, 0)

    data_bits, model_bits = log2_of(data_count), log2_of(model_count)

    def store(piece, product):
        offset, height, span, tiles = piece
        for column in range(model_count):
            for tile in range(tiles):
                lanes = min(LANES, span - tile * LANES)
                first = column * span + tile * LANES
                block = product[:, first : first + lanes].astype(low_type)
                for row in range(data_count):
                    spot = bit_reverse(column, model_bits) * data_count
                    spot = spot + bit_reverse(row, data_bits)
                    packed[
                        spot, offset + tile * height : offset + (tile + 1) * height, :lanes
                    ] = block[row * height : (row + 1) * height, :]

    for position in range(3):
        grads = qkv_s[position * width : (position + 1) * width, :]
        store(pieces[position], dot_as(a_s[...], grads, 0, 1))
    store(pieces[3], jnp.dot(o_s[...], db_s[...], preferred_element_type=full_type))
    store(pieces[4], dot_as(c_s[...], du_s[...], 0, 0))
    store(pieces[5], dot_as(g_s[...], dm_s[...], 0, 0))
    store(pieces[6], dot_as(low_s[...], cotangent[...].reshape(-1, cotangent.shape[2]), 0, 0))


def decode(
    arrived, grid_order, grid_keep, ground_dist, weights, mask_token, pred_proj, cotangent
):
    gain_attn, w_query, w_key, w_value, w_out, gain_mlp, w_up, w_down = weights
    data_count, model_count = lax.axis_size("dp"), lax.axis_size("mp")
    images, length, pixels = cotangent.shape
    width, hidden = w_up.shape
    rows = images * length
    matrices = [w_query, w_key, w_value, w_out, w_up, w_down, pred_proj]
    pieces, height = dec_pieces(data_count, model_count, [m.shape for m in matrices])

    def kernel(*refs):
        decoder_kernel(images, HD, SIDE, pieces, data_count, model_count, *refs)

    vmem = pl.BlockSpec(memory_space=pltpu.VMEM)
    return pl.pallas_call(
        kernel,
        out_shape=[
            jax.ShapeDtypeStruct((images, length, pixels), full_type),
            jax.ShapeDtypeStruct((data_count * model_count, height, LANES), low_type),
            jax.ShapeDtypeStruct(arrived.shape, low_type),
            jax.ShapeDtypeStruct((3, width), full_type),
        ],
        in_specs=[vmem] * 3 + [pl.BlockSpec(memory_space=pltpu.SMEM)] + [vmem] * 11,
        out_specs=[vmem] * 4,
        scratch_shapes=[
            pltpu.VMEM((length, width), full_type),
            pltpu.VMEM((3 * width, width), low_type),
            pltpu.VMEM((rows, width), low_type),
            pltpu.VMEM((3 * width, rows), low_type),
            pltpu.VMEM((HD, length, length), low_type),
            pltpu.VMEM((HD, 1, length), full_type),
            pltpu.VMEM((width, rows), low_type),
            pltpu.VMEM((length, width), full_type),
            pltpu.VMEM((rows, width), low_type),
            pltpu.VMEM((rows, hidden), low_type),
            pltpu.VMEM((rows, hidden), low_type),
            pltpu.VMEM((rows, width), low_type),
            pltpu.VMEM((length, width), full_type),
            pltpu.VMEM((rows, width), low_type),
            pltpu.VMEM((rows, width), low_type),
            pltpu.VMEM((width, length), full_type),
        ],
        compiler_params=pltpu.CompilerParams(vmem_limit_bytes=60 * 2**20),
    )(
        arrived,
        grid_order[:, None, :],
        grid_keep[:, None, :],
        ground_dist,
        gain_attn.reshape(1, -1),
        w_query,
        w_key,
        w_value,
        w_out,
        gain_mlp.reshape(1, -1),
        w_up,
        w_down,
        pred_proj,
        mask_token.reshape(1, -1),
        cotangent,
    )


def low_bit(mask):
    return (mask & -mask).bit_length() - 1


def visit_order(count):
    return sorted(range(count), key=lambda mask: (mask.bit_length(), -mask))


def visit_mask(step, count):
    mask = jnp.int32(0)
    for position, value in enumerate(visit_order(count)):
        mask = jnp.where(step == position, value, mask)
    return mask


class Gather:
    def __init__(self, own, slot_view, send_sems, recv_sems):
        self.own, self.slot_view = own, slot_view
        self.send_sems, self.recv_sems = send_sems, recv_sems
        self.count = lax.axis_size("mp")
        self.index = lax.axis_index("mp")

    def copy(self, mask):
        bit = low_bit(mask)
        carried = mask ^ (1 << bit)
        place = self.slot_view(self.index ^ carried)
        return pltpu.make_async_remote_copy(
            src_ref=self.own if carried == 0 else place,
            dst_ref=place,
            send_sem=self.send_sems.at[mask],
            recv_sem=self.recv_sems.at[mask],
            device_id=partner("mp", bit)[0],
            device_id_type=MESH,
        )

    def start(self):
        for bit in reversed(range(log2_of(self.count))):
            self.copy(1 << bit).start()

    def arrive(self, mask):
        self.copy(mask).wait_recv()
        for bit in reversed(range(low_bit(mask))):
            self.copy(mask | (1 << bit)).start()

    def arrive_group(self, length):
        group = [mask for mask in range(1, self.count) if mask.bit_length() == length]
        for mask in sorted(group, key=lambda one: -low_bit(one)):
            self.arrive(mask)

    def arrive_all(self):
        for length in range(1, log2_of(self.count) + 1):
            self.arrive_group(length)

    def arrive_at(self, step):
        for length in range(1, log2_of(self.count) + 1):
            @pl.when(step == 1 << (length - 1))
            def _():
                self.arrive_group(length)

    def drain(self):
        for mask in range(1, self.count):
            self.copy(mask).wait_send()


class Scatter:
    def __init__(self, parts, total, landing, send_sems, recv_sems):
        self.parts, self.total, self.landing = parts, total, landing
        self.send_sems, self.recv_sems = send_sems, recv_sems
        self.count = lax.axis_size("mp")
        self.index = lax.axis_index("mp")

    def copy(self, mask):
        return pltpu.make_async_remote_copy(
            src_ref=self.parts.at[self.index ^ mask],
            dst_ref=self.landing.at[mask],
            send_sem=self.send_sems.at[mask],
            recv_sem=self.recv_sems.at[mask],
            device_id=partner("mp", low_bit(mask))[0],
            device_id_type=MESH,
        )

    def put(self, mask, product):
        @pl.when(mask == 0)
        def _():
            self.total[...] = self.total[...] + product

        @pl.when(mask != 0)
        def _():
            self.parts[self.index ^ mask] = product.astype(low_type)

        for odd in range(1, self.count, 2):
            @pl.when(mask == odd)
            def _():
                self.copy(odd).start()

    def finish_bit(self, bit):
        step = 1 << bit
        masks = [mask for mask in range(1, self.count) if low_bit(mask) == bit]
        for mask in reversed(masks):
            self.copy(mask).wait_recv()
            rest = mask ^ step
            if rest:
                place = self.index ^ rest
                self.parts[place] = self.parts[place] + self.landing[mask]
                if low_bit(rest) == bit + 1:
                    self.copy(rest).start()
            else:
                self.total[...] = self.total[...] + self.landing[mask].astype(full_type)

    def drain(self):
        for mask in range(1, self.count):
            self.copy(mask).wait_send()


def exchange_partners(images):
    data_count, model_count = lax.axis_size("dp"), lax.axis_size("mp")
    data, model = lax.axis_index("dp"), lax.axis_index("mp")
    out = []
    for image in range(images):
        spot = (model * images + image) * data_count + data
        device = spot // images
        out.append((device // model_count, device % model_count, spot % images))
    return out


def is_here(peer):
    return (peer[0] == lax.axis_index("dp")) & (peer[1] == lax.axis_index("mp"))


class Exchange:
    def __init__(self, images, source, target, send_sems, recv_sems):
        self.partners = exchange_partners(images)
        self.source, self.target = source, target
        self.send_sems, self.recv_sems = send_sems, recv_sems

    def copy(self, image):
        data, model, slot = self.partners[image]
        return pltpu.make_async_remote_copy(
            src_ref=self.source.at[image],
            dst_ref=self.target.at[slot],
            send_sem=self.send_sems.at[image],
            recv_sem=self.recv_sems.at[slot],
            device_id=(data, model),
            device_id_type=MESH,
        )

    def start(self):
        for image, (data, model, slot) in enumerate(self.partners):
            here = is_here((data, model))

            @pl.when(here)
            def _():
                self.target[slot] = self.source[image]

            @pl.when(jnp.logical_not(here))
            def _():
                self.copy(image).start()

    def finish(self):
        for image, (data, model, slot) in enumerate(self.partners):
            @pl.when(jnp.logical_not(is_here((data, model))))
            def _():
                pltpu.make_async_remote_copy(
                    src_ref=self.source.at[image],
                    dst_ref=self.target.at[image],
                    send_sem=self.send_sems.at[image],
                    recv_sem=self.recv_sems.at[image],
                    device_id=(data, model),
                    device_id_type=MESH,
                ).wait()


def encoder_barrier(images, axes):
    barrier = pltpu.get_barrier_semaphore()
    count = images
    for axis in axes:
        for bit in range(log2_of(lax.axis_size(axis))):
            count += 1
            pl.semaphore_signal(
                barrier, inc=1, device_id=partner(axis, bit)[0], device_id_type=MESH
            )
    for data, model, slot in exchange_partners(images):
        pl.semaphore_signal(barrier, inc=1, device_id=(data, model), device_id_type=MESH)
    pl.semaphore_wait(barrier, count)


def encoder_kernel(images, visible, heads, *refs):
    (
        lengths,
        tokens,
        gain_attn,
        w_query,
        w_key,
        w_value,
        w_out,
        gain_mlp,
        w_up,
        w_down,
        w_embed,
        arrived,
        a_s,
        qkv_s,
        e_s,
        inv_s,
        o_own,
        c_s,
        g_s,
        slope_s,
        mid_s,
        low_s,
        embed_full,
        qkv_weights,
        token_slots,
        out_full,
        o_full,
        embed_slots,
        parts,
        landing,
        total,
        embedded,
        sems,
        swap_sems,
    ) = refs
    count = lax.axis_size("mp")
    index = lax.axis_index("mp")
    block_rows = images * visible
    columns = w_query.shape[1]
    size = columns // heads
    scaling = float(size) ** -0.5
    hidden = w_up.shape[1]
    chunk = 512

    encoder_barrier(images, ["mp"])
    token_gather = Gather(
        tokens, lambda slot: token_slots.at[slot], sems.at[0], sems.at[1]
    )
    out_gather = Gather(
        w_out,
        lambda slot: out_full.at[pl.ds(pl.multiple_of(slot * columns, columns), columns)],
        sems.at[2],
        sems.at[3],
    )
    o_gather = Gather(
        o_own,
        lambda slot: o_full.at[pl.ds(pl.multiple_of(slot * columns, columns), columns)],
        sems.at[4],
        sems.at[5],
    )
    embed_gather = Gather(w_embed, lambda slot: embed_slots.at[slot], sems.at[6], sems.at[7])
    scatter = Scatter(parts, total, landing, sems.at[8], sems.at[9])
    swap = Exchange(images, embedded, arrived, swap_sems.at[0], swap_sems.at[1])

    token_gather.start()
    token_slots[index] = tokens[...]
    out_full[pl.ds(pl.multiple_of(index * columns, columns), columns), :] = w_out[...]
    embed_slots[index] = w_embed[...]
    for position, weight in enumerate((w_query, w_key, w_value)):
        qkv_weights[position * columns : (position + 1) * columns, :] = weight[...].T

    def rows_of(slot):
        return pl.ds(pl.multiple_of(slot * block_rows, block_rows), block_rows)

    def attend(step, carry):
        token_gather.arrive_at(step)

        @pl.when(step == count // 2)
        def _():
            out_gather.start()

        slot = index ^ visit_mask(step, count)
        rows = rows_of(slot)
        normed, scale = norm_parts(token_slots[slot].astype(full_type))
        a_s[rows, :] = (normed * gain_attn[...]).astype(low_type)
        for position in range(3):
            span = slice(position * columns, (position + 1) * columns)
            part = dot_as(qkv_weights[span, :], a_s[rows, :], 1, 1)
            if position == 0:
                part = part * (scaling * LOG2E)
            qkv_s[span, rows] = part.astype(low_type)
        key_row = lax.broadcasted_iota(jnp.int32, (block_rows, block_rows), 0)
        query_row = lax.broadcasted_iota(jnp.int32, (block_rows, block_rows), 1)
        valid = jnp.zeros((block_rows, block_rows), jnp.bool_)
        for image in range(images):
            first = image * visible
            keys = (key_row >= first) & (key_row < first + lengths[slot * images + image])
            valid = valid | (keys & (query_row >= first) & (query_row < first + visible))
        for head in range(heads):
            span = slice(head * size, (head + 1) * size)
            query = qkv_s[span, rows]
            key = qkv_s[columns + head * size : columns + (head + 1) * size, rows]
            value = qkv_s[2 * columns + head * size : 2 * columns + (head + 1) * size, rows]
            scores = jnp.where(valid, dot_as(key, query, 0, 0), masked_score)
            weights = jnp.exp2(scores - jnp.max(scores, axis=0, keepdims=True))
            inverse = 1.0 / jnp.sum(weights, axis=0, keepdims=True)
            weights = weights.astype(low_type)
            e_s[slot * heads + head] = weights
            inv_s[slot * heads + head] = inverse
            mixed = jnp.dot(value, weights, preferred_element_type=full_type)
            o_own[span, rows] = (mixed * inverse).astype(low_type)
        return carry

    lax.fori_loop(0, count, attend, 0)
    o_gather.start()
    o_full[pl.ds(pl.multiple_of(index * columns, columns), columns), :] = o_own[...]
    out_gather.arrive_all()
    o_gather.arrive_all()
    embed_gather.start()
    total[...] = jnp.zeros_like(total)

    def expand(step, carry):
        mask = count - 1 - step
        slot = index ^ mask
        rows = rows_of(slot)
        middle = token_slots[slot].astype(full_type) + dot_as(o_full[:, rows], out_full[...], 0, 0)

        @pl.when(mask == 0)
        def _():
            mid_s[...] = middle

        normed, scale = norm_parts(middle)
        c_s[rows, :] = (normed * gain_mlp[...]).astype(low_type)
        for first in range(0, hidden, chunk):
            cols = slice(first, first + chunk)
            pre = jnp.dot(c_s[rows, :], w_up[:, cols], preferred_element_type=full_type)
            active, slope = gelu_pair(pre)
            g_s[rows, cols] = active.astype(low_type)
            slope_s[rows, cols] = slope.astype(low_type)
        scatter.put(
            mask, jnp.dot(g_s[rows, :], w_down[...], preferred_element_type=full_type)
        )
        return carry

    lax.fori_loop(0, count, expand, 0)
    bits = log2_of(count)
    for bit in range(bits):
        if bit == bits - 1:
            embed_gather.arrive_all()
            width = w_embed.shape[1]
            for slot in range(count):
                embed_full[:, slot * width : (slot + 1) * width] = embed_slots[slot]
        scatter.finish_bit(bit)
    low_s[...] = (mid_s[...] + total[...]).astype(low_type)
    out = jnp.dot(low_s[...], embed_full[...], preferred_element_type=full_type)
    embedded[...] = out.astype(low_type).reshape(embedded.shape)
    swap.start()
    for one in (token_gather, out_gather, o_gather, embed_gather, scatter):
        one.drain()
    swap.finish()


def encode(tokens, lengths, weights, embed_proj):
    gain_attn, w_query, w_key, w_value, w_out, gain_mlp, w_up, w_down = weights
    model_count = lax.axis_size("mp")
    images, visible, width = tokens.shape
    rows = images * visible
    heads = HE // model_count
    columns, hidden = w_query.shape[1], w_up.shape[1]
    out_width = embed_proj.shape[1] * model_count
    every = rows * model_count

    def kernel(*refs):
        encoder_kernel(images, visible, heads, *refs)

    vmem = pl.BlockSpec(memory_space=pltpu.VMEM)
    shapes = [
        ((images, visible, out_width), low_type),
        ((every, width), low_type),
        ((3 * columns, every), low_type),
        ((model_count * heads, rows, rows), low_type),
        ((model_count * heads, 1, rows), full_type),
        ((columns, every), low_type),
        ((every, width), low_type),
        ((every, hidden), low_type),
        ((every, hidden), low_type),
        ((rows, width), full_type),
        ((rows, width), low_type),
        ((width, out_width), low_type),
        ((3 * columns, width), low_type),
    ]
    return pl.pallas_call(
        kernel,
        out_shape=[jax.ShapeDtypeStruct(shape, kind) for shape, kind in shapes],
        in_specs=[pl.BlockSpec(memory_space=pltpu.SMEM)] + [vmem] * 10,
        out_specs=[vmem] * len(shapes),
        scratch_shapes=[
            pltpu.VMEM((model_count, rows, width), low_type),
            pltpu.VMEM((width, width), low_type),
            pltpu.VMEM((width, every), low_type),
            pltpu.VMEM((model_count,) + embed_proj.shape, low_type),
            pltpu.VMEM((model_count, rows, width), low_type),
            pltpu.VMEM((model_count, rows, width), low_type),
            pltpu.VMEM((rows, width), full_type),
            pltpu.VMEM((images, visible, out_width), low_type),
            pltpu.SemaphoreType.DMA((10, model_count)),
            pltpu.SemaphoreType.DMA((2, images)),
        ],
        compiler_params=pltpu.CompilerParams(
            collective_id=1, has_side_effects=True, vmem_limit_bytes=60 * 2**20
        ),
    )(
        lengths,
        tokens.reshape(rows, width),
        gain_attn.reshape(1, -1),
        w_query,
        w_key,
        w_value,
        w_out,
        gain_mlp.reshape(1, -1),
        w_up,
        w_down,
        embed_proj,
    )


class Bulk:
    def __init__(self, one):
        self.one, self.stage = one, None

    def start(self):
        self.one.start(0)
        self.stage = 0

    def done(self):
        return self.stage == len(self.one.stages)

    def advance(self):
        if self.done():
            return
        self.one.finish(self.stage)
        self.stage += 1
        if not self.done():
            self.one.start(self.stage)


def encoder_back_kernel(plan, *refs):
    images, visible, heads, dec_pieces_list, embed_piece = plan
    refs = list(refs)

    def take(number):
        head = refs[:number]
        del refs[:number]
        return head

    (
        grad_arrived,
        tokens,
        gain_attn,
        w_out,
        gain_mlp,
        w_up,
        w_down,
        a_s,
        qkv_s,
        e_s,
        inv_s,
        o_own,
        c_s,
        g_s,
        slope_s,
        mid_s,
        low_s,
        embed_full,
        qkv_weights,
        dec_packed,
        dec_small,
    ) = take(21)
    data_count, model_count = lax.axis_size("dp"), lax.axis_size("mp")
    data_bits, model_bits = log2_of(data_count), log2_of(model_count)
    (grad_tokens, g_query, g_key, g_value, g_up, g_out, g_down, g_embed, norm_wide, norm_thin) = (
        take(10)
    )
    dec_outs = take(len(dec_pieces_list))
    (
        demb_own,
        demb_slots,
        dm_s,
        du_s,
        db_own,
        db_s,
        dqkv_s,
        total,
        parts_mlp,
        landing_mlp,
        parts_attn,
        landing_attn,
        dy_s,
        do_s,
        sems,
        swap_sems,
        row_packed,
        col_packed,
        embed_packed,
    ) = take(19)
    row_bufs = [row_packed] + take(data_bits)
    col_bufs = [col_packed] + take(data_bits)
    dec_bufs = [dec_packed] + take(data_bits + model_bits)
    embed_bufs = [embed_packed] + take(data_bits + model_bits)
    wide_acc, wide_got, thin_acc, thin_got = take(4)
    row_sems, col_sems, dec_sems, embed_sems, norm_sems = take(5)
    assert not refs

    index = lax.axis_index("mp")
    count = model_count
    block_rows = images * visible
    columns = w_out.shape[0]
    size = columns // heads
    scaling = float(size) ** -0.5
    hidden, width = w_down.shape
    chunk = 512
    enc_stages = [("dp", bit) for bit in range(data_bits)]
    all_stages = [("mp", bit) for bit in range(model_bits)] + enc_stages

    encoder_barrier(images, ["mp", "dp"])
    swap = Exchange(images, grad_arrived, demb_own, swap_sems.at[0], swap_sems.at[1])
    swap.start()

    def bulk(stages, bufs, axis, first, extent, pair, cut):
        window = [slice(None), slice(None)]
        window[axis - 1] = pl.ds(first, extent)
        return Bulk(
            HalvingSum(stages, bufs, tuple(window), pair.at[0, cut], pair.at[1, cut])
        )

    cuts = dec_sems.shape[1]
    height = dec_packed.shape[1] // cuts
    dec_sums = [
        bulk(all_stages, dec_bufs, 1, cut * height, height, dec_sems, cut) for cut in range(cuts)
    ]
    embed_sum = bulk(all_stages, embed_bufs, 1, 0, embed_packed.shape[1], embed_sems, 0)
    up_sums = [
        bulk(enc_stages, row_bufs, 2, cut * (hidden // 2), hidden // 2, row_sems, cut)
        for cut in range(2)
    ]
    qkv_sum = bulk(enc_stages, row_bufs, 2, hidden, 3 * columns, row_sems, 2)
    down_sums = [
        bulk(enc_stages, col_bufs, 1, cut * (hidden // 2), hidden // 2, col_sems, cut)
        for cut in range(2)
    ]
    out_sum = bulk(enc_stages, col_bufs, 1, hidden, columns, col_sems, 2)

    for one in dec_sums:
        one.start()
    swap.finish()
    demb_gather = Gather(demb_own, lambda slot: demb_slots.at[slot], sems.at[0], sems.at[1])
    demb_gather.start()
    demb_slots[index] = demb_own[...]

    def rows_of(slot):
        return pl.ds(pl.multiple_of(slot * block_rows, block_rows), block_rows)

    def first_back(step, carry):
        demb_gather.arrive_at(step)
        mask = visit_mask(step, count)
        slot = index ^ mask
        rows = rows_of(slot)
        grad_rows = demb_slots[slot].reshape(block_rows, -1)
        grad_out = dot_as(grad_rows, embed_full[...], 1, 1)

        @pl.when(mask == 0)
        def _():
            dy_s[...] = grad_out

        dm_s[rows, :] = grad_out.astype(low_type)
        for first in range(0, hidden, chunk):
            cols = slice(first, first + chunk)
            grad_active = dot_as(dm_s[rows, :], w_down[cols, :], 1, 1)
            du_s[rows, cols] = (grad_active * slope_s[rows, cols].astype(full_type)).astype(
                low_type
            )
        return carry

    lax.fori_loop(0, count, first_back, 0)
    scatter = Scatter(parts_mlp, total, landing_mlp, sems.at[2], sems.at[3])
    total[...] = jnp.zeros_like(total)

    def second_back(step, carry):
        mask = count - 1 - step
        rows = rows_of(index ^ mask)
        scatter.put(mask, dot_as(du_s[rows, :], w_up[...], 1, 1))
        return carry

    lax.fori_loop(0, count, second_back, 0)
    for bit in range(model_bits - 1):
        scatter.finish_bit(bit)

    def store_rows(product, first):
        high = width // data_count
        for row in range(data_count):
            row_packed[bit_reverse(row, data_bits), :, first : first + product.shape[1]] = (
                product[row * high : (row + 1) * high, :].astype(low_type)
            )

    def store_cols(product, first):
        wide = width // data_count
        for col in range(data_count):
            col_packed[
                bit_reverse(col, data_bits), first : first + product.shape[0], :wide
            ] = product[:, col * wide : (col + 1) * wide].astype(low_type)

    for cut in range(2):
        cols = slice(cut * (hidden // 2), (cut + 1) * (hidden // 2))
        store_cols(dot_as(g_s[:, cols], dm_s[...], 0, 0), cut * (hidden // 2))
        down_sums[cut].start()
    for one in dec_sums[: cuts // 2]:
        one.advance()
    scatter.finish_bit(model_bits - 1)

    normed, scale = norm_parts(mid_s[...])
    grad_second = total[...]
    wide_acc[0, 1:2, :] = jnp.sum(grad_second * normed, axis=0, keepdims=True)
    grad_middle = dy_s[...] + norm_back(normed, scale, grad_second * gain_mlp[...])
    dy_s[...] = grad_middle
    db_own[...] = grad_middle.astype(low_type)
    db_gather = Gather(db_own, lambda slot: db_s.at[rows_of(slot)], sems.at[4], sems.at[5])
    db_gather.start()
    db_s[rows_of(index), :] = db_own[...]
    for cut in range(2):
        cols = slice(cut * (hidden // 2), (cut + 1) * (hidden // 2))
        store_rows(dot_as(c_s[...], du_s[:, cols], 0, 0), cut * (hidden // 2))
        up_sums[cut].start()
    for one in dec_sums[cuts // 2 :]:
        one.advance()
    offset, high, span, tiles = embed_piece
    product = dot_as(low_s[...], demb_own[...].reshape(block_rows, -1), 0, 0)
    for column in range(model_count):
        for row in range(data_count):
            spot = bit_reverse(column, model_bits) * data_count + bit_reverse(row, data_bits)
            for tile in range(tiles):
                lanes = min(LANES, span - tile * LANES)
                first = column * span + tile * LANES
                embed_packed[spot, tile * high : (tile + 1) * high, :lanes] = product[
                    row * high : (row + 1) * high, first : first + lanes
                ].astype(low_type)
    embed_sum.start()

    second_scatter = Scatter(parts_attn, total, landing_attn, sems.at[6], sems.at[7])
    total[...] = jnp.zeros_like(total)

    def third_back(step, carry):
        db_gather.arrive_at(step)
        mask = visit_mask(step, count)
        slot = index ^ mask
        rows = rows_of(slot)
        do_s[...] = dot_as(w_out[...], db_s[rows, :], 1, 1)
        for head in range(heads):
            span = slice(head * size, (head + 1) * size)
            key_span = slice(columns + head * size, columns + (head + 1) * size)
            value_span = slice(2 * columns + head * size, 2 * columns + (head + 1) * size)
            query, key, value = qkv_s[span, rows], qkv_s[key_span, rows], qkv_s[value_span, rows]
            weights = e_s[slot * heads + head]
            grad_full = do_s[span, :] * (inv_s[slot * heads + head] * scaling)
            shift = jnp.sum(
                grad_full * o_own[span, rows].astype(full_type), axis=0, keepdims=True
            )
            grad_low = grad_full.astype(low_type)
            grad_probs = dot_as(value, grad_low, 0, 0)
            grad_scores = (weights.astype(full_type) * (grad_probs - shift)).astype(low_type)
            grad_value = dot_as(grad_low, weights, 1, 1) * (1.0 / scaling)
            grad_query = jnp.dot(key, grad_scores, preferred_element_type=full_type)
            grad_key = dot_as(query, grad_scores, 1, 1) * (1.0 / (scaling * LOG2E))
            dqkv_s[span, rows] = grad_query.astype(low_type)
            dqkv_s[key_span, rows] = grad_key.astype(low_type)
            dqkv_s[value_span, rows] = grad_value.astype(low_type)
        second_scatter.put(mask, dot_as(dqkv_s[:, rows], qkv_weights[...], 0, 0))
        return carry

    lax.fori_loop(0, count, third_back, 0)
    for bit in range(model_bits - 1):
        second_scatter.finish_bit(bit)
    store_cols(jnp.dot(o_own[...], db_s[...], preferred_element_type=full_type), hidden)
    out_sum.start()
    store_rows(dot_as(a_s[...], dqkv_s[...], 0, 1), hidden)
    qkv_sum.start()
    second_scatter.finish_bit(model_bits - 1)
    normed, scale = norm_parts(tokens[...].astype(full_type))
    grad_normed = total[...]
    wide_acc[0, 0:1, :] = jnp.sum(grad_normed * normed, axis=0, keepdims=True)
    grad_tokens[...] = dy_s[...] + norm_back(normed, scale, grad_normed * gain_attn[...])
    thin_acc[0] = dec_small[...]

    def norm_copies(stage):
        peer = partner(*all_stages[stage])[0]
        return [
            pltpu.make_async_remote_copy(
                src_ref=acc.at[stage],
                dst_ref=got.at[stage],
                send_sem=norm_sems.at[0, kind, stage],
                recv_sem=norm_sems.at[1, kind, stage],
                device_id=peer,
                device_id_type=MESH,
            )
            for kind, (acc, got) in enumerate(((wide_acc, wide_got), (thin_acc, thin_got)))
        ]

    everything = down_sums + up_sums + [out_sum, qkv_sum] + dec_sums + [embed_sum]
    for stage in range(len(all_stages)):
        copies = norm_copies(stage)
        for copy in copies:
            copy.start()
        for one in everything:
            one.advance()
        for copy in copies:
            copy.wait()
        wide_acc[stage + 1] = wide_acc[stage] + wide_got[stage]
        thin_acc[stage + 1] = thin_acc[stage] + thin_got[stage]
    for one in everything:
        while not one.done():
            one.advance()
    norm_wide[...] = wide_acc[len(all_stages)]
    norm_thin[...] = thin_acc[len(all_stages)]
    for one in (demb_gather, scatter, db_gather, second_scatter):
        one.drain()

    rows_out, cols_out = row_bufs[-1], col_bufs[-1]
    g_up[...] = rows_out[0, :, :hidden].astype(full_type)
    for position, out in enumerate((g_query, g_key, g_value)):
        first = hidden + position * columns
        out[...] = rows_out[0, :, first : first + columns].astype(full_type)
    wide = width // data_count
    g_down[...] = cols_out[0, :hidden, :wide].astype(full_type)
    g_out[...] = cols_out[0, hidden : hidden + columns, :wide].astype(full_type)
    unpack([g_embed], [embed_piece], embed_bufs[-1])
    unpack(dec_outs, dec_pieces_list, dec_bufs[-1])


def unpack(outs, pieces, source):
    for out, (offset, rows, width, tiles) in zip(outs, pieces):
        for tile in range(tiles):
            lanes = min(LANES, width - tile * LANES)
            block = source[0, offset + tile * rows : offset + (tile + 1) * rows, :lanes]
            out[:, tile * LANES : tile * LANES + lanes] = block.astype(full_type)


def encode_back(grad_arrived, tokens, weights, saved, embed_proj, dec_packed, dec_small, dec_shapes):
    gain_attn, w_query, w_key, w_value, w_out, gain_mlp, w_up, w_down = weights
    data_count, model_count = lax.axis_size("dp"), lax.axis_size("mp")
    data_bits, model_bits = log2_of(data_count), log2_of(model_count)
    images, visible, width = tokens.shape
    rows = images * visible
    every = rows * model_count
    heads = HE // model_count
    columns, hidden = w_query.shape[1], w_up.shape[1]
    out_width = embed_proj.shape[1] * model_count
    pieces, height = dec_pieces(data_count, model_count, dec_shapes)
    embed_pieces, embed_height = dec_pieces(data_count, model_count, [(width, out_width)])
    high, wide = width // data_count, width // data_count
    wide_pad = -(-wide // LANES) * LANES
    devices = data_count * model_count
    stages = data_bits + model_bits
    dec_cuts = 4
    plan = (images, visible, heads, pieces, embed_pieces[0])

    def kernel(*refs):
        encoder_back_kernel(plan, *refs)

    vmem = pl.BlockSpec(memory_space=pltpu.VMEM)
    outs = [
        (rows, width),
        (high, columns),
        (high, columns),
        (high, columns),
        (high, hidden),
        (columns, wide),
        (hidden, wide),
        (embed_pieces[0][1], embed_pieces[0][2]),
        (2, width),
        dec_small.shape,
    ] + [(piece[1], piece[2]) for piece in pieces]
    row_shape = (high, hidden + 3 * columns)
    col_shape = (hidden + columns, wide_pad)
    scratch = [
        pltpu.VMEM((images, visible, out_width), low_type),
        pltpu.VMEM((model_count, images, visible, out_width), low_type),
        pltpu.VMEM((every, width), low_type),
        pltpu.VMEM((every, hidden), low_type),
        pltpu.VMEM((rows, width), low_type),
        pltpu.VMEM((every, width), low_type),
        pltpu.VMEM((3 * columns, every), low_type),
        pltpu.VMEM((rows, width), full_type),
        pltpu.VMEM((model_count, rows, width), low_type),
        pltpu.VMEM((model_count, rows, width), low_type),
        pltpu.VMEM((model_count, rows, width), low_type),
        pltpu.VMEM((model_count, rows, width), low_type),
        pltpu.VMEM((rows, width), full_type),
        pltpu.VMEM((columns, rows), full_type),
        pltpu.SemaphoreType.DMA((8, model_count)),
        pltpu.SemaphoreType.DMA((2, images)),
        pltpu.VMEM((data_count,) + row_shape, low_type),
        pltpu.VMEM((data_count,) + col_shape, low_type),
        pltpu.VMEM((devices, embed_height, LANES), low_type),
    ]
    scratch += [pltpu.VMEM((data_count >> (bit + 1),) + row_shape, low_type) for bit in range(data_bits)]
    scratch += [pltpu.VMEM((data_count >> (bit + 1),) + col_shape, low_type) for bit in range(data_bits)]
    scratch += [pltpu.VMEM((devices >> (bit + 1), height, LANES), low_type) for bit in range(stages)]
    scratch += [
        pltpu.VMEM((devices >> (bit + 1), embed_height, LANES), low_type) for bit in range(stages)
    ]
    for shape in ((2, width), dec_small.shape):
        scratch += [
            pltpu.VMEM((stages + 1,) + shape, full_type),
            pltpu.VMEM((stages,) + shape, full_type),
        ]
    scratch += [
        pltpu.SemaphoreType.DMA((2, 3, data_bits)),
        pltpu.SemaphoreType.DMA((2, 3, data_bits)),
        pltpu.SemaphoreType.DMA((2, dec_cuts, stages)),
        pltpu.SemaphoreType.DMA((2, 1, stages)),
        pltpu.SemaphoreType.DMA((2, 2, stages)),
    ]
    return pl.pallas_call(
        kernel,
        out_shape=[jax.ShapeDtypeStruct(shape, full_type) for shape in outs],
        in_specs=[vmem] * 21,
        out_specs=[vmem] * len(outs),
        scratch_shapes=scratch,
        compiler_params=pltpu.CompilerParams(
            collective_id=2, has_side_effects=True, vmem_limit_bytes=62 * 2**20
        ),
    )(
        grad_arrived,
        tokens.reshape(rows, width),
        gain_attn.reshape(1, -1),
        w_out,
        gain_mlp.reshape(1, -1),
        w_up,
        w_down,
        *saved,
        dec_packed,
        dec_small,
    )


def layer_norm(values, scale_gain):
    center = values - jnp.mean(values, axis=-1, keepdims=True)
    spread = jnp.mean(center * center, axis=-1, keepdims=True)
    return center * lax.rsqrt(spread + eps_norm) * scale_gain


def exact_gelu(values):
    return jax.nn.gelu(values, approximate=False)


def matmul(left_side, right_side):
    flat_rows = left_side.reshape(-1, left_side.shape[-1])
    product = jnp.dot(flat_rows, right_side, preferred_element_type=full_type)
    return product.reshape(left_side.shape[:-1] + (right_side.shape[1],))


def matmul_t(left_side, right_side):
    flat_rows = left_side.reshape(-1, left_side.shape[-1])
    product = lax.dot_general(
        flat_rows, right_side, (((1,), (1,)), ((), ())), preferred_element_type=full_type
    )
    return product.reshape(left_side.shape[:-1] + (right_side.shape[0],))


def outer_sum(left_side, right_side):
    return lax.dot_general(
        left_side.reshape(-1, left_side.shape[-1]),
        right_side.reshape(-1, right_side.shape[-1]),
        (((0,), (0,)), ((), ())),
        preferred_element_type=full_type,
    )


def spread_rows(values, tensor_split):
    if tensor_split:
        return lax.all_gather(values, "mp", axis=0, tiled=True)
    return values


def collect_rows(values, tensor_split):
    if tensor_split:
        return lax.psum_scatter(
            values.astype(jnp.bfloat16), "mp", scatter_dimension=0, tiled=True
        ).astype(jnp.float32)
    return values


def images_per_block(images, length):
    grouped = 1
    while grouped * length < 512 and grouped < images:
        grouped = grouped * 2
    return grouped


def in_blocks(blocked_array, grouped):
    return blocked_array.reshape(
        (blocked_array.shape[0] // grouped, grouped) + blocked_array.shape[1:]
    )


def with_heads(blocked_array, head_count):
    return blocked_array.reshape(
        blocked_array.shape[:2] + (head_count, blocked_array.shape[2] // head_count)
    )


def attend_forward(queries, keys_all, values_all, key_valid, head_count):
    images, length, columns = queries.shape
    grouped = images_per_block(images, length)
    scaling = float(columns // head_count) ** (-0.5)

    def one_block(pieces):
        query_b, key_b, value_b, valid_b = pieces
        scores = (
            jnp.einsum("nqhd,nkhd->nhqk", query_b, key_b, preferred_element_type=full_type)
            * scaling
        )
        scores = jnp.where(valid_b[:, None, None, :], scores, masked_score)
        row_max = jnp.max(scores, axis=-1, keepdims=True)
        weights = jnp.exp(scores - row_max)
        totals = jnp.sum(weights, axis=-1, keepdims=True)
        prob_rows = (weights / totals).astype(low_type)
        mixed_b = jnp.einsum(
            "nhqk,nkhd->nqhd", prob_rows, value_b, preferred_element_type=full_type
        )
        return (mixed_b.astype(low_type), (row_max + jnp.log(totals))[..., 0])

    pieces_in = (
        in_blocks(with_heads(queries, head_count), grouped),
        in_blocks(with_heads(keys_all, head_count), grouped),
        in_blocks(with_heads(values_all, head_count), grouped),
        in_blocks(key_valid, grouped),
    )
    mixed_rows, log_total = lax.map(one_block, pieces_in)
    return (
        mixed_rows.reshape(images, length, columns),
        log_total.reshape(images, head_count, length),
    )


def attend_backward(queries, keys_all, values_all, key_valid, log_total, grad_mixed, head_count):
    images, length, columns = queries.shape
    grouped = images_per_block(images, length)
    scaling = float(columns // head_count) ** (-0.5)

    def one_block(pieces):
        query_b, key_b, value_b, valid_b, total_b, grad_b = pieces
        scores = (
            jnp.einsum("nqhd,nkhd->nhqk", query_b, key_b, preferred_element_type=full_type)
            * scaling
        )
        scores = jnp.where(valid_b[:, None, None, :], scores, masked_score)
        prob_rows = jnp.exp(scores - total_b[..., None])
        grad_value_b = jnp.einsum(
            "nhqk,nqhd->nkhd", prob_rows.astype(low_type), grad_b, preferred_element_type=full_type
        )
        grad_probs = jnp.einsum(
            "nqhd,nkhd->nhqk", grad_b, value_b, preferred_element_type=full_type
        )
        grad_scores = prob_rows * (
            grad_probs - jnp.sum(grad_probs * prob_rows, axis=-1, keepdims=True)
        )
        grad_scores = (grad_scores * scaling).astype(low_type)
        grad_query_b = jnp.einsum(
            "nhqk,nkhd->nqhd", grad_scores, key_b, preferred_element_type=full_type
        )
        grad_key_b = jnp.einsum(
            "nhqk,nqhd->nkhd", grad_scores, query_b, preferred_element_type=full_type
        )
        return (
            grad_query_b.astype(low_type),
            grad_key_b.astype(low_type),
            grad_value_b.astype(low_type),
        )

    pieces_in = (
        in_blocks(with_heads(queries, head_count), grouped),
        in_blocks(with_heads(keys_all, head_count), grouped),
        in_blocks(with_heads(values_all, head_count), grouped),
        in_blocks(key_valid, grouped),
        in_blocks(log_total, grouped),
        in_blocks(with_heads(grad_mixed, head_count), grouped),
    )
    grad_query, grad_key, grad_value = lax.map(one_block, pieces_in)
    return (
        grad_query.reshape(images, length, columns),
        grad_key.reshape(images, length, columns),
        grad_value.reshape(images, length, columns),
    )


def block_forward(inputs, key_valid, weights, head_count, tensor_split):
    gain_attn, w_query, w_key, w_value, w_out, gain_mlp, w_up, w_down = weights
    normed = spread_rows(layer_norm(inputs, gain_attn).astype(low_type), tensor_split)
    queries = matmul(normed, w_query).astype(low_type)
    keys_all = matmul(normed, w_key).astype(low_type)
    values_all = matmul(normed, w_value).astype(low_type)
    mixed_rows, log_total = attend_forward(queries, keys_all, values_all, key_valid, head_count)
    middle = inputs + collect_rows(matmul(mixed_rows, w_out), tensor_split)
    second = spread_rows(layer_norm(middle, gain_mlp).astype(low_type), tensor_split)
    pre_act = matmul(second, w_up)
    active = exact_gelu(pre_act).astype(low_type)
    outputs = middle + collect_rows(matmul(active, w_down), tensor_split)
    kept_state = (
        inputs,
        normed,
        queries,
        keys_all,
        values_all,
        mixed_rows,
        log_total,
        middle,
        second,
        pre_act,
        active,
    )
    return (outputs, kept_state)


def block_backward(grad_out, kept_state, key_valid, weights, head_count, tensor_split):
    gain_attn, w_query, w_key, w_value, w_out, gain_mlp, w_up, w_down = weights
    (
        inputs,
        normed,
        queries,
        keys_all,
        values_all,
        mixed_rows,
        log_total,
        middle,
        second,
        pre_act,
        active,
    ) = kept_state
    grad_branch = spread_rows(grad_out.astype(low_type), tensor_split)
    grad_down = outer_sum(active, grad_branch)
    grad_active = matmul_t(grad_branch, w_down)
    grad_pre = jax.vjp(exact_gelu, pre_act)[1](grad_active)[0].astype(low_type)
    grad_up = outer_sum(second, grad_pre)
    grad_second = collect_rows(matmul_t(grad_pre, w_up), tensor_split)
    norm_grad, grad_gain_mlp = jax.vjp(layer_norm, middle, gain_mlp)[1](grad_second)
    grad_middle = grad_out + norm_grad
    grad_attn = spread_rows(grad_middle.astype(low_type), tensor_split)
    grad_w_out = outer_sum(mixed_rows, grad_attn)
    grad_mixed = matmul_t(grad_attn, w_out).astype(low_type)
    grad_query, grad_key, grad_value = attend_backward(
        queries, keys_all, values_all, key_valid, log_total, grad_mixed, head_count
    )
    grad_w_query = outer_sum(normed, grad_query)
    grad_w_key = outer_sum(normed, grad_key)
    grad_w_value = outer_sum(normed, grad_value)
    grad_normed = (
        matmul_t(grad_query, w_query) + matmul_t(grad_key, w_key) + matmul_t(grad_value, w_value)
    )
    grad_normed = collect_rows(grad_normed, tensor_split)
    input_grad, grad_gain_attn = jax.vjp(layer_norm, inputs, gain_attn)[1](grad_normed)
    return (
        grad_middle + input_grad,
        (
            grad_gain_attn,
            grad_w_query,
            grad_w_key,
            grad_w_value,
            grad_w_out,
            grad_gain_mlp,
            grad_up,
            grad_down,
        ),
    )


def grid_codes(distance, side_count, columns):
    quarter = columns // 4
    frequency = 10000.0 ** (-jnp.arange(quarter, dtype=full_type) / quarter)
    places = jnp.arange(side_count * side_count)
    row_pos = (places // side_count).astype(full_type)
    col_pos = (places % side_count).astype(full_type)
    row_angle = distance[:, None, None] * row_pos[None, :, None] * frequency[None, None, :]
    col_angle = distance[:, None, None] * col_pos[None, :, None] * frequency[None, None, :]
    return jnp.concatenate(
        [jnp.sin(row_angle), jnp.cos(row_angle), jnp.sin(col_angle), jnp.cos(col_angle)], axis=-1
    )


def placement_table(visible_order, keep_flags, visible):
    positions = jnp.arange(visible_order.shape[1])
    matches = (visible_order[:, None, :visible] == positions[None, :, None]) & (
        keep_flags[:, :, None] == 1
    )
    return matches.astype(low_type)


def owner_blocks(full_grad, data_count, model_count):
    row_count, col_count = full_grad.shape
    reshaped = full_grad.reshape(
        data_count, row_count // data_count, model_count, col_count // model_count
    )
    return jnp.transpose(reshaped, (0, 2, 1, 3)).reshape(
        data_count * model_count, row_count // data_count, col_count // model_count
    )


def per_device_plain(
    tokens,
    lengths,
    grid_order,
    grid_keep,
    ground_dist,
    enc_norm,
    enc_query,
    enc_key,
    enc_value,
    enc_proj,
    enc_norm2,
    enc_up,
    enc_down,
    embed_proj,
    mask_token,
    dec_norm,
    dec_query,
    dec_key,
    dec_value,
    dec_proj,
    dec_norm2,
    dec_up,
    dec_down,
    pred_proj,
    cotangent,
):
    data_count = lax.axis_size("dp")
    model_count = lax.axis_size("mp")
    enc_weights = (enc_norm, enc_query, enc_key, enc_value, enc_proj, enc_norm2, enc_up, enc_down)
    dec_weights = (dec_norm, dec_query, dec_key, dec_value, dec_proj, dec_norm2, dec_up, dec_down)
    enc_heads = HE // model_count
    key_valid = jnp.arange(tokens.shape[1])[None, :] < lengths[:, None]
    enc_out, enc_saved = block_forward(
        tokens.astype(full_type), key_valid, enc_weights, enc_heads, True
    )
    enc_low = enc_out.astype(low_type)
    enc_all = spread_rows(enc_low, True)
    embedded = matmul(enc_all, embed_proj).astype(low_type)
    sectioned = embedded.reshape((data_count, -1) + embedded.shape[1:])
    arrived = lax.all_to_all(
        lax.all_to_all(sectioned, "dp", split_axis=0, concat_axis=0, tiled=True),
        "mp",
        split_axis=0,
        concat_axis=3,
        tiled=True,
    )
    arrived = arrived.reshape((-1,) + arrived.shape[2:])
    pick_table = placement_table(grid_order, grid_keep, arrived.shape[1])
    masked = (1 - grid_keep).astype(full_type)[..., None]
    dec_start = jnp.einsum("npt,ntc->npc", pick_table, arrived, preferred_element_type=full_type)
    dec_start = dec_start + masked * mask_token + grid_codes(ground_dist, SIDE, mask_token.shape[0])
    all_valid = jnp.ones(dec_start.shape[:2], jnp.bool_)
    dec_out, dec_saved = block_forward(dec_start, all_valid, dec_weights, HD, False)
    dec_low = dec_out.astype(low_type)
    decoded = matmul(dec_low, pred_proj)
    grad_pred = outer_sum(dec_low, cotangent)
    grad_dec_out = matmul_t(cotangent, pred_proj)
    grad_start, dec_grads = block_backward(
        grad_dec_out, dec_saved, all_valid, dec_weights, HD, False
    )
    grad_mask = jnp.sum(masked * grad_start, axis=(0, 1))
    grad_arrived = jnp.einsum("npt,npc->ntc", pick_table.astype(full_type), grad_start).astype(
        low_type
    )
    sent_back = grad_arrived.reshape((-1, IPD) + grad_arrived.shape[1:])
    returned = lax.all_to_all(
        lax.all_to_all(sent_back, "mp", split_axis=3, concat_axis=0, tiled=True),
        "dp",
        split_axis=0,
        concat_axis=0,
        tiled=True,
    )
    returned = returned.reshape((-1,) + returned.shape[2:])
    grad_embed = outer_sum(enc_all, returned)
    grad_enc_out = collect_rows(matmul_t(returned, embed_proj), True)
    grad_tokens, enc_grads = block_backward(
        grad_enc_out, enc_saved, key_valid, enc_weights, enc_heads, True
    )
    col_sums = (
        lax.psum_scatter(
            enc_grads[4].astype(jnp.bfloat16), "dp", scatter_dimension=1, tiled=True
        ).astype(jnp.float32),
        lax.psum_scatter(
            enc_grads[7].astype(jnp.bfloat16), "dp", scatter_dimension=1, tiled=True
        ).astype(jnp.float32),
    )
    norm_grads = lax.psum(
        (enc_grads[0], enc_grads[5], dec_grads[0], dec_grads[5], grad_mask), ("dp", "mp")
    )
    dec_list = (
        dec_grads[1],
        dec_grads[2],
        dec_grads[3],
        dec_grads[4],
        dec_grads[6],
        dec_grads[7],
        grad_pred,
    )
    row_sums = (
        lax.psum_scatter(
            enc_grads[1].astype(jnp.bfloat16), "dp", scatter_dimension=0, tiled=True
        ).astype(jnp.float32),
        lax.psum_scatter(
            enc_grads[2].astype(jnp.bfloat16), "dp", scatter_dimension=0, tiled=True
        ).astype(jnp.float32),
        lax.psum_scatter(
            enc_grads[3].astype(jnp.bfloat16), "dp", scatter_dimension=0, tiled=True
        ).astype(jnp.float32),
        lax.psum_scatter(
            enc_grads[6].astype(jnp.bfloat16), "dp", scatter_dimension=0, tiled=True
        ).astype(jnp.float32),
        lax.psum_scatter(
            grad_embed.astype(jnp.bfloat16), "dp", scatter_dimension=0, tiled=True
        ).astype(jnp.float32),
    )
    summed = (
        lax.psum_scatter(
            owner_blocks(dec_list[0], data_count, model_count),
            ("dp", "mp"),
            scatter_dimension=0,
            tiled=True,
        ),
        lax.psum_scatter(
            owner_blocks(dec_list[1], data_count, model_count),
            ("dp", "mp"),
            scatter_dimension=0,
            tiled=True,
        ),
        lax.psum_scatter(
            owner_blocks(dec_list[2], data_count, model_count),
            ("dp", "mp"),
            scatter_dimension=0,
            tiled=True,
        ),
        lax.psum_scatter(
            owner_blocks(dec_list[3], data_count, model_count),
            ("dp", "mp"),
            scatter_dimension=0,
            tiled=True,
        ),
        lax.psum_scatter(
            owner_blocks(dec_list[4], data_count, model_count),
            ("dp", "mp"),
            scatter_dimension=0,
            tiled=True,
        ),
        lax.psum_scatter(
            owner_blocks(dec_list[5], data_count, model_count),
            ("dp", "mp"),
            scatter_dimension=0,
            tiled=True,
        ),
        lax.psum_scatter(
            owner_blocks(dec_list[6], data_count, model_count),
            ("dp", "mp"),
            scatter_dimension=0,
            tiled=True,
        ),
    )
    embed_final = row_sums[4]
    dec_final = tuple((summed[index_num][0] for index_num in range(7)))
    return (
        decoded,
        grad_tokens,
        norm_grads[0],
        row_sums[0],
        row_sums[1],
        row_sums[2],
        col_sums[0],
        norm_grads[1],
        row_sums[3],
        col_sums[1],
        embed_final,
        norm_grads[4],
        norm_grads[2],
        dec_final[0],
        dec_final[1],
        dec_final[2],
        dec_final[3],
        norm_grads[3],
        dec_final[4],
        dec_final[5],
        dec_final[6],
    )


VMEM_BUDGET = 56 * 2**20


def kernel_bytes(tokens, enc_up, enc_query, dec_up, pred_proj):
    data_count, model_count = lax.axis_size("dp"), lax.axis_size("mp")
    images, visible, width = tokens.shape
    every = images * visible * model_count
    hidden, columns = enc_up.shape[1], enc_query.shape[1]
    out_width, wide = dec_up.shape[0], max(width // data_count, LANES)
    shapes = [(out_width, out_width)] * 4
    shapes += [dec_up.shape, dec_up.shape[::-1], pred_proj.shape, (width, out_width)]
    height = dec_pieces(data_count, model_count, shapes)[1]
    rows = 8 * every * width + 3 * every * hidden
    sums = width * (hidden + 3 * columns) + data_count * (hidden + columns) * wide
    sums = 2 * (sums + data_count * model_count * height * LANES)
    return 2 * (rows + sums + 2 * width * hidden + 4 * width * columns)


def per_device(
    tokens,
    lengths,
    grid_order,
    grid_keep,
    ground_dist,
    enc_norm,
    enc_query,
    enc_key,
    enc_value,
    enc_proj,
    enc_norm2,
    enc_up,
    enc_down,
    embed_proj,
    mask_token,
    dec_norm,
    dec_query,
    dec_key,
    dec_value,
    dec_proj,
    dec_norm2,
    dec_up,
    dec_down,
    pred_proj,
    cotangent,
):
    if kernel_bytes(tokens, enc_up, enc_query, dec_up, pred_proj) > VMEM_BUDGET:
        return per_device_plain(
            tokens,
            lengths,
            grid_order,
            grid_keep,
            ground_dist,
            enc_norm,
            enc_query,
            enc_key,
            enc_value,
            enc_proj,
            enc_norm2,
            enc_up,
            enc_down,
            embed_proj,
            mask_token,
            dec_norm,
            dec_query,
            dec_key,
            dec_value,
            dec_proj,
            dec_norm2,
            dec_up,
            dec_down,
            pred_proj,
            cotangent,
        )
    enc_weights = (enc_norm, enc_query, enc_key, enc_value, enc_proj, enc_norm2, enc_up, enc_down)
    dec_weights = (dec_norm, dec_query, dec_key, dec_value, dec_proj, dec_norm2, dec_up, dec_down)
    arrived, *saved = encode(tokens, lengths, enc_weights, embed_proj)
    decoded, dec_packed, grad_arrived, dec_small = decode(
        arrived, grid_order, grid_keep, ground_dist, dec_weights, mask_token, pred_proj, cotangent
    )
    matrices = [dec_query, dec_key, dec_value, dec_proj, dec_up, dec_down, pred_proj]
    (
        grad_tokens,
        g_query,
        g_key,
        g_value,
        g_up,
        g_out,
        g_down,
        g_embed,
        norm_wide,
        norm_thin,
        *dec_grads,
    ) = encode_back(
        grad_arrived,
        tokens,
        enc_weights,
        saved,
        embed_proj,
        dec_packed,
        dec_small,
        [matrix.shape for matrix in matrices],
    )
    return (
        decoded,
        grad_tokens.reshape(tokens.shape),
        norm_wide[0],
        g_query,
        g_key,
        g_value,
        g_out,
        norm_wide[1],
        g_up,
        g_down,
        g_embed,
        norm_thin[2],
        norm_thin[0],
        dec_grads[0],
        dec_grads[1],
        dec_grads[2],
        dec_grads[3],
        norm_thin[1],
        dec_grads[4],
        dec_grads[5],
        dec_grads[6],
    )


def solution(mesh):
    return jax.shard_map(
        per_device,
        mesh=mesh,
        in_specs=(
            P(("dp", "mp"), None, None),
            P("dp"),
            P(("dp", "mp"), None),
            P(("dp", "mp"), None),
            P(("dp", "mp")),
            P(),
            P(None, "mp"),
            P(None, "mp"),
            P(None, "mp"),
            P("mp", None),
            P(),
            P(None, "mp"),
            P("mp", None),
            P(None, "mp"),
            P(),
            P(),
            P(),
            P(),
            P(),
            P(),
            P(),
            P(),
            P(),
            P(),
            P(("dp", "mp"), None, None),
        ),
        out_specs=(
            P(("dp", "mp"), None, None),
            P(("dp", "mp"), None, None),
            P(),
            P("dp", "mp"),
            P("dp", "mp"),
            P("dp", "mp"),
            P("mp", "dp"),
            P(),
            P("dp", "mp"),
            P("mp", "dp"),
            P("dp", "mp"),
            P(),
            P(),
            P("dp", "mp"),
            P("dp", "mp"),
            P("dp", "mp"),
            P("dp", "mp"),
            P(),
            P("dp", "mp"),
            P("dp", "mp"),
            P("dp", "mp"),
        ),
        check_vma=False,
    )
```

```python
import math

import jax
import jax.numpy as jnp
from jax import lax
from jax.experimental import pallas as pl
from jax.experimental.pallas import tpu as pltpu
from jax.sharding import PartitionSpec as P

HE = 16
HD = 16
SIDE = 16
IPD = 1


eps_norm = 1e-06
masked_score = -1e30
low_type = jnp.bfloat16
full_type = jnp.float32


MESH = pl.DeviceIdType.MESH
LANES = 128


def log2_of(count):
    bits = count.bit_length() - 1
    assert 1 << bits == count
    return bits


def spot_of(data, model, stages):
    out = 0
    for axis, bit in stages:
        out = out * 2 + (((data if axis == "dp" else model) >> bit) & 1)
    return out


def partner(axis, bit):
    dp, mp = lax.axis_index("dp"), lax.axis_index("mp")
    step = 1 << bit
    if axis == "dp":
        return (dp ^ step, mp), (dp >> bit) & 1
    return (dp, mp ^ step), (mp >> bit) & 1


def enter_barrier(partners):
    barrier = pltpu.get_barrier_semaphore()
    for peer in partners:
        pl.semaphore_signal(barrier, inc=1, device_id=peer, device_id_type=MESH)
    pl.semaphore_wait(barrier, len(partners))


class HalvingSum:
    def __init__(self, stages, buffers, window, send_sems, recv_sems):
        self.stages, self.buffers, self.window = stages, buffers, window
        self.send_sems, self.recv_sems = send_sems, recv_sems

    def view(self, index, start, size):
        return self.buffers[index].at[(pl.ds(start, size),) + self.window]

    def copy(self, index):
        peer, mine = partner(*self.stages[index])
        half = self.buffers[index].shape[0] // 2
        return pltpu.make_async_remote_copy(
            src_ref=self.view(index, (1 - mine) * half, half),
            dst_ref=self.view(index + 1, 0, half),
            send_sem=self.send_sems.at[index],
            recv_sem=self.recv_sems.at[index],
            device_id=peer,
            device_id_type=MESH,
        )

    def start(self, index):
        self.copy(index).start()

    def finish(self, index):
        self.copy(index).wait()
        peer, mine = partner(*self.stages[index])
        half = self.buffers[index].shape[0] // 2

        def one(position, carry):
            there = self.buffers[index + 1].at[(position,) + self.window]
            here = self.buffers[index].at[(mine * half + position,) + self.window]
            there[...] = there[...] + here[...]
            return carry

        lax.fori_loop(0, half, one, 0)


def dec_pieces(data_count, model_count, shapes):
    offset, pieces = 0, []
    for rows, columns in shapes:
        height, width = rows // data_count, columns // model_count
        tiles = -(-width // LANES)
        pieces.append((offset, height, width, tiles))
        offset += height * tiles
    return pieces, offset


LOG2E = 1.4426950408889634


def dot_as(left, right, left_dim, right_dim):
    return lax.dot_general(
        left, right, (((left_dim,), (right_dim,)), ((), ())), preferred_element_type=full_type
    )


def norm_parts(values):
    center = values - jnp.mean(values, axis=-1, keepdims=True)
    scale = lax.rsqrt(jnp.mean(center * center, axis=-1, keepdims=True) + eps_norm)
    return center * scale, scale


def norm_back(normed, scale, grad_scaled):
    first = jnp.mean(grad_scaled, axis=-1, keepdims=True)
    second = jnp.mean(grad_scaled * normed, axis=-1, keepdims=True)
    return (grad_scaled - first - normed * second) * scale


def gelu_pair(values):
    below = 0.5 + 0.5 * lax.erf(values * (0.5**0.5))
    density = jnp.exp2(values * values * (-0.5 * LOG2E)) * ((2.0 * math.pi) ** -0.5)
    return values * below, below + values * density


def low_bit(mask):
    return (mask & -mask).bit_length() - 1


def visit_order(count):
    return sorted(range(count), key=lambda mask: (mask.bit_length(), -mask))


def visit_mask(step, count):
    mask = jnp.int32(0)
    for position, value in enumerate(visit_order(count)):
        mask = jnp.where(step == position, value, mask)
    return mask


class Gather:
    def __init__(self, own, slot_view, send_sems, recv_sems):
        self.own, self.slot_view = own, slot_view
        self.send_sems, self.recv_sems = send_sems, recv_sems
        self.count = lax.axis_size("mp")
        self.index = lax.axis_index("mp")

    def copy(self, mask):
        bit = low_bit(mask)
        carried = mask ^ (1 << bit)
        place = self.slot_view(self.index ^ carried)
        return pltpu.make_async_remote_copy(
            src_ref=self.own if carried == 0 and self.own is not None else place,
            dst_ref=place,
            send_sem=self.send_sems.at[mask],
            recv_sem=self.recv_sems.at[mask],
            device_id=partner("mp", bit)[0],
            device_id_type=MESH,
        )

    def start(self):
        for bit in reversed(range(log2_of(self.count))):
            self.copy(1 << bit).start()

    def arrive(self, mask):
        self.copy(mask).wait_recv()
        for bit in reversed(range(low_bit(mask))):
            self.copy(mask | (1 << bit)).start()

    def arrive_group(self, length):
        group = [mask for mask in range(1, self.count) if mask.bit_length() == length]
        for mask in sorted(group, key=lambda one: -low_bit(one)):
            self.arrive(mask)

    def arrive_all(self):
        for length in range(1, log2_of(self.count) + 1):
            self.arrive_group(length)

    def arrive_at(self, step):
        for length in range(1, log2_of(self.count) + 1):
            @pl.when(step == 1 << (length - 1))
            def _():
                self.arrive_group(length)

    def drain(self):
        for mask in range(1, self.count):
            self.copy(mask).wait_send()


class Scatter:
    def __init__(self, parts, total, landing, send_sems, recv_sems):
        self.parts, self.total, self.landing = parts, total, landing
        self.send_sems, self.recv_sems = send_sems, recv_sems
        self.count = lax.axis_size("mp")
        self.index = lax.axis_index("mp")

    def copy(self, mask):
        return pltpu.make_async_remote_copy(
            src_ref=self.parts.at[mask - 1],
            dst_ref=self.landing.at[mask - 1],
            send_sem=self.send_sems.at[mask],
            recv_sem=self.recv_sems.at[mask],
            device_id=partner("mp", low_bit(mask))[0],
            device_id_type=MESH,
        )

    def put(self, mask, product):
        @pl.when(mask == 0)
        def _():
            self.total[...] = self.total[...] + product

        @pl.when(mask != 0)
        def _():
            self.parts[mask - 1] = product.astype(low_type)

        for odd in range(1, self.count, 2):
            @pl.when(mask == odd)
            def _():
                self.copy(odd).start()

    def finish_bit(self, bit):
        step = 1 << bit
        masks = [mask for mask in range(1, self.count) if low_bit(mask) == bit]
        for mask in reversed(masks):
            self.copy(mask).wait_recv()
            rest = mask ^ step
            if rest:
                self.parts[rest - 1] = self.parts[rest - 1] + self.landing[mask - 1]
                if low_bit(rest) == bit + 1:
                    self.copy(rest).start()
            else:
                self.total[...] = self.total[...] + self.landing[mask - 1].astype(full_type)

    def drain(self):
        for mask in range(1, self.count):
            self.copy(mask).wait_send()


def exchange_partners(images):
    data_count, model_count = lax.axis_size("dp"), lax.axis_size("mp")
    data, model = lax.axis_index("dp"), lax.axis_index("mp")
    out = []
    for image in range(images):
        spot = (model * images + image) * data_count + data
        device = spot // images
        out.append((device // model_count, device % model_count, spot % images))
    return out


def is_here(peer):
    return (peer[0] == lax.axis_index("dp")) & (peer[1] == lax.axis_index("mp"))


class Exchange:
    def __init__(self, images, source, target, send_sems, recv_sems):
        self.partners = exchange_partners(images)
        self.source, self.target = source, target
        self.send_sems, self.recv_sems = send_sems, recv_sems

    def copy(self, image):
        data, model, slot = self.partners[image]
        return pltpu.make_async_remote_copy(
            src_ref=self.source.at[image],
            dst_ref=self.target.at[slot],
            send_sem=self.send_sems.at[image],
            recv_sem=self.recv_sems.at[slot],
            device_id=(data, model),
            device_id_type=MESH,
        )

    def start(self):
        for image, (data, model, slot) in enumerate(self.partners):
            here = is_here((data, model))

            @pl.when(here)
            def _():
                self.target[slot] = self.source[image]

            @pl.when(jnp.logical_not(here))
            def _():
                self.copy(image).start()

    def finish(self):
        for image, (data, model, slot) in enumerate(self.partners):
            @pl.when(jnp.logical_not(is_here((data, model))))
            def _():
                pltpu.make_async_remote_copy(
                    src_ref=self.source.at[image],
                    dst_ref=self.target.at[image],
                    send_sem=self.send_sems.at[image],
                    recv_sem=self.recv_sems.at[image],
                    device_id=(data, model),
                    device_id_type=MESH,
                ).wait()


class Move:
    def __init__(self, source, target, sem):
        self.copy = pltpu.make_async_copy(source, target, sem)
        self.copy.start()

    def wait(self):
        if self.copy is not None:
            self.copy.wait()
            self.copy = None


def encoder_barrier(images, axes):
    barrier = pltpu.get_barrier_semaphore()
    count = images
    for axis in axes:
        for bit in range(log2_of(lax.axis_size(axis))):
            count += 1
            pl.semaphore_signal(
                barrier, inc=1, device_id=partner(axis, bit)[0], device_id_type=MESH
            )
    for data, model, slot in exchange_partners(images):
        pl.semaphore_signal(barrier, inc=1, device_id=(data, model), device_id_type=MESH)
    pl.semaphore_wait(barrier, count)


def encoder_kernel(images, visible, heads, *refs):
    (
        lengths,
        tokens,
        gain_attn,
        w_query_hbm,
        w_key_hbm,
        w_value_hbm,
        w_out,
        gain_mlp,
        w_up_hbm,
        w_down_hbm,
        w_embed,
        arrived,
        *saved_hbm,
    ) = refs[:24]
    (
        w_query,
        w_key,
        w_value,
        w_up,
        w_down,
        a_s,
        qkv_s,
        e_s,
        inv_s,
        o_own,
        c_s,
        g_s,
        slope_s,
        mid_s,
        low_s,
        embed_full,
        qkv_weights,
        move_sems,
        token_slots,
        out_full,
        o_full,
        embed_slots,
        parts,
        landing,
        total,
        embedded,
        sems,
        swap_sems,
    ) = refs[24:]
    count = lax.axis_size("mp")
    index = lax.axis_index("mp")
    block_rows = images * visible
    columns = w_query.shape[1]
    size = columns // heads
    scaling = float(size) ** -0.5
    hidden = w_up.shape[1]
    chunk = 512

    loads = [
        Move(source, target, move_sems.at[position])
        for position, (source, target) in enumerate(
            (
                (w_query_hbm, w_query),
                (w_key_hbm, w_key),
                (w_value_hbm, w_value),
                (w_up_hbm, w_up),
                (w_down_hbm, w_down),
            )
        )
    ]
    saved = [a_s, qkv_s, e_s, inv_s, o_own, c_s, g_s, slope_s, mid_s, low_s, embed_full, qkv_weights]
    stores = []

    def save(*arrays):
        for array in arrays:
            position = [array is one for one in saved].index(True)
            stores.append(Move(array, saved_hbm[position], move_sems.at[len(loads) + position]))

    encoder_barrier(images, ["mp"])
    token_gather = Gather(
        tokens, lambda slot: token_slots.at[slot], sems.at[0], sems.at[1]
    )
    out_gather = Gather(
        w_out,
        lambda slot: out_full.at[pl.ds(pl.multiple_of(slot * columns, columns), columns)],
        sems.at[2],
        sems.at[3],
    )
    o_gather = Gather(
        o_own,
        lambda slot: o_full.at[pl.ds(pl.multiple_of(slot * columns, columns), columns)],
        sems.at[4],
        sems.at[5],
    )
    embed_gather = Gather(w_embed, lambda slot: embed_slots.at[slot], sems.at[6], sems.at[7])
    scatter = Scatter(parts, total, landing, sems.at[8], sems.at[9])
    swap = Exchange(images, embedded, arrived, swap_sems.at[0], swap_sems.at[1])

    token_gather.start()
    token_slots[index] = tokens[...]
    out_full[pl.ds(pl.multiple_of(index * columns, columns), columns), :] = w_out[...]
    embed_slots[index] = w_embed[...]
    for position, weight in enumerate((w_query, w_key, w_value)):
        loads[position].wait()
        qkv_weights[position * columns : (position + 1) * columns, :] = weight[...].T
    save(qkv_weights)

    def rows_of(slot):
        return pl.ds(pl.multiple_of(slot * block_rows, block_rows), block_rows)

    def attend(step, carry):
        token_gather.arrive_at(step)

        @pl.when(step == count // 2)
        def _():
            out_gather.start()

        slot = index ^ visit_mask(step, count)
        rows = rows_of(slot)
        normed, scale = norm_parts(token_slots[slot].astype(full_type))
        a_s[rows, :] = (normed * gain_attn[...]).astype(low_type)
        for position in range(3):
            span = slice(position * columns, (position + 1) * columns)
            part = dot_as(qkv_weights[span, :], a_s[rows, :], 1, 1)
            if position == 0:
                part = part * (scaling * LOG2E)
            qkv_s[span, rows] = part.astype(low_type)
        key_row = lax.broadcasted_iota(jnp.int32, (block_rows, block_rows), 0)
        query_row = lax.broadcasted_iota(jnp.int32, (block_rows, block_rows), 1)
        valid = jnp.zeros((block_rows, block_rows), jnp.bool_)
        for image in range(images):
            first = image * visible
            keys = (key_row >= first) & (key_row < first + lengths[slot * images + image])
            valid = valid | (keys & (query_row >= first) & (query_row < first + visible))
        for head in range(heads):
            span = slice(head * size, (head + 1) * size)
            query = qkv_s[span, rows]
            key = qkv_s[columns + head * size : columns + (head + 1) * size, rows]
            value = qkv_s[2 * columns + head * size : 2 * columns + (head + 1) * size, rows]
            scores = jnp.where(valid, dot_as(key, query, 0, 0), masked_score)
            weights = jnp.exp2(scores - jnp.max(scores, axis=0, keepdims=True))
            inverse = 1.0 / jnp.sum(weights, axis=0, keepdims=True)
            weights = weights.astype(low_type)
            e_s[slot * heads + head] = weights
            inv_s[slot * heads + head] = inverse
            mixed = jnp.dot(value, weights, preferred_element_type=full_type)
            o_own[span, rows] = (mixed * inverse).astype(low_type)
        return carry

    lax.fori_loop(0, count, attend, 0)
    o_gather.start()
    save(a_s, qkv_s, e_s, inv_s, o_own)
    for move in loads:
        move.wait()
    o_full[pl.ds(pl.multiple_of(index * columns, columns), columns), :] = o_own[...]
    out_gather.arrive_all()
    o_gather.arrive_all()
    embed_gather.start()
    total[...] = jnp.zeros_like(total)

    def expand(step, carry):
        mask = count - 1 - step
        slot = index ^ mask
        rows = rows_of(slot)
        middle = token_slots[slot].astype(full_type) + dot_as(o_full[:, rows], out_full[...], 0, 0)

        @pl.when(mask == 0)
        def _():
            mid_s[...] = middle

        normed, scale = norm_parts(middle)
        c_s[rows, :] = (normed * gain_mlp[...]).astype(low_type)
        for first in range(0, hidden, chunk):
            cols = slice(first, first + chunk)
            pre = jnp.dot(c_s[rows, :], w_up[:, cols], preferred_element_type=full_type)
            active, slope = gelu_pair(pre)
            g_s[rows, cols] = active.astype(low_type)
            slope_s[rows, cols] = slope.astype(low_type)
        scatter.put(
            mask, jnp.dot(g_s[rows, :], w_down[...], preferred_element_type=full_type)
        )
        return carry

    lax.fori_loop(0, count, expand, 0)
    save(c_s, g_s, slope_s, mid_s)
    bits = log2_of(count)
    for bit in range(bits):
        if bit == bits - 1:
            embed_gather.arrive_all()
            width = w_embed.shape[1]
            for slot in range(count):
                embed_full[:, slot * width : (slot + 1) * width] = embed_slots[slot]
        scatter.finish_bit(bit)
    low_s[...] = (mid_s[...] + total[...]).astype(low_type)
    out = jnp.dot(low_s[...], embed_full[...], preferred_element_type=full_type)
    embedded[...] = out.astype(low_type).reshape(embedded.shape)
    swap.start()
    save(embed_full, low_s)
    for one in (token_gather, out_gather, o_gather, embed_gather, scatter):
        one.drain()
    for move in stores:
        move.wait()
    swap.finish()


def encode(tokens, lengths, weights, embed_proj):
    gain_attn, w_query, w_key, w_value, w_out, gain_mlp, w_up, w_down = weights
    model_count = lax.axis_size("mp")
    images, visible, width = tokens.shape
    rows = images * visible
    heads = HE // model_count
    columns, hidden = w_query.shape[1], w_up.shape[1]
    out_width = embed_proj.shape[1] * model_count
    every = rows * model_count

    def kernel(*refs):
        encoder_kernel(images, visible, heads, *refs)

    vmem = pl.BlockSpec(memory_space=pltpu.VMEM)
    hbm = pl.BlockSpec(memory_space=pl.ANY)
    shapes = [
        ((images, visible, out_width), low_type),
        ((every, width), low_type),
        ((3 * columns, every), low_type),
        ((model_count * heads, rows, rows), low_type),
        ((model_count * heads, 1, rows), full_type),
        ((columns, every), low_type),
        ((every, width), low_type),
        ((every, hidden), low_type),
        ((every, hidden), low_type),
        ((rows, width), full_type),
        ((rows, width), low_type),
        ((width, out_width), low_type),
        ((3 * columns, width), low_type),
    ]
    return pl.pallas_call(
        kernel,
        out_shape=[jax.ShapeDtypeStruct(shape, kind) for shape, kind in shapes],
        in_specs=[pl.BlockSpec(memory_space=pltpu.SMEM)]
        + [vmem] * 2
        + [hbm] * 3
        + [vmem] * 2
        + [hbm] * 2
        + [vmem],
        out_specs=[vmem] + [hbm] * (len(shapes) - 1),
        scratch_shapes=[
            pltpu.VMEM((width, columns), low_type),
            pltpu.VMEM((width, columns), low_type),
            pltpu.VMEM((width, columns), low_type),
            pltpu.VMEM((width, hidden), low_type),
            pltpu.VMEM((hidden, width), low_type),
        ]
        + [pltpu.VMEM(shape, kind) for shape, kind in shapes[1:]]
        + [
            pltpu.SemaphoreType.DMA((5 + len(shapes),)),
            pltpu.VMEM((model_count, rows, width), low_type),
            pltpu.VMEM((width, width), low_type),
            pltpu.VMEM((width, every), low_type),
            pltpu.VMEM((model_count,) + embed_proj.shape, low_type),
            pltpu.VMEM((model_count - 1, rows, width), low_type),
            pltpu.VMEM((model_count - 1, rows, width), low_type),
            pltpu.VMEM((rows, width), full_type),
            pltpu.VMEM((images, visible, out_width), low_type),
            pltpu.SemaphoreType.DMA((10, model_count)),
            pltpu.SemaphoreType.DMA((2, images)),
        ],
        compiler_params=pltpu.CompilerParams(
            collective_id=1, has_side_effects=True, vmem_limit_bytes=60 * 2**20
        ),
    )(
        lengths,
        tokens.reshape(rows, width),
        gain_attn.reshape(1, -1),
        w_query,
        w_key,
        w_value,
        w_out,
        gain_mlp.reshape(1, -1),
        w_up,
        w_down,
        embed_proj,
    )


CUTS = 4
LATE_UP = 0


def at_step(step, when, sums):
    @pl.when(step == when)
    def _():
        for one in sums:
            one.advance()


class Bulk:
    def __init__(self, one):
        self.one, self.stage = one, None

    def start(self):
        self.one.start(0)
        self.stage = 0

    def done(self):
        return self.stage == len(self.one.stages)

    def advance(self):
        if self.done():
            return
        self.one.finish(self.stage)
        self.stage += 1
        if not self.done():
            self.one.start(self.stage)


def back_kernel(plan, *refs):
    images, visible, enc_heads, heads, side, pieces, embed_piece, scopes = plan
    refs = list(refs)

    def take(number):
        head = refs[:number]
        del refs[:number]
        return head

    (
        dist_ref,
        arrived,
        order_ref,
        keep_ref,
        dec_gain_attn,
        dec_gain_mlp,
        mask_token,
        tokens,
        gain_attn,
        gain_mlp,
    ) = take(10)
    dec_hbm = take(8)
    enc_hbm = take(15)
    decoded, grad_tokens, norm_wide, norm_thin, rows_out, cols_out, dec_out, embed_out = take(8)
    move_sems, decoded_sems = take(2)
    grad_arrived, dec_packed, small = take(3)
    demb_own, demb_slots, db_s, total = take(4)
    parts_mlp, landing_mlp, parts_attn, landing_attn = take(4)
    sems, swap_sems = take(2)
    data_count, model_count = lax.axis_size("dp"), lax.axis_size("mp")
    data_bits, model_bits = log2_of(data_count), log2_of(model_count)
    row_packed, col_packed, embed_packed = take(3)
    row_bufs = [row_packed] + take(data_bits)
    col_bufs = [col_packed] + take(data_bits)
    dec_bufs = [dec_packed] + take(data_bits + model_bits)
    embed_bufs = [embed_packed] + take(data_bits + model_bits)
    wide_acc, wide_got, thin_acc, thin_got = take(4)
    row_sems, col_sems, dec_sems, embed_sems, norm_sems = take(5)
    assert not refs

    index = lax.axis_index("mp")
    count = model_count
    enc_stages = [("dp", bit) for bit in range(data_bits)]
    late_stages = enc_stages[1:] + enc_stages[:1]
    model_stages = [("mp", bit) for bit in range(model_bits)]
    all_stages = model_stages + enc_stages
    crossed_stages = model_stages + late_stages
    spread_stages = model_stages[:1] + enc_stages + model_stages[1:]
    chunk = 512

    def bulk(stages, bufs, axis, first, extent, pair, cut):
        window = [slice(None), slice(None)]
        window[axis - 1] = pl.ds(first, extent)
        return Bulk(HalvingSum(stages, bufs, tuple(window), pair.at[0, cut], pair.at[1, cut]))

    dec_orders = [spread_stages] * 5 + [crossed_stages] * 2
    dec_spans = [(pieces[0][0], pieces[4][0])]
    for piece in pieces[4:]:
        dec_spans.append((piece[0], piece[0] + piece[1] * piece[3]))
    dec_sums = [
        bulk(dec_orders[3 + cut], dec_bufs, 1, first, last - first, dec_sems, cut)
        for cut, (first, last) in enumerate(dec_spans)
    ]
    attn_sum, up_sum, down_sum, pred_sum = dec_sums

    def store_dec(which, product):
        offset, height, span, tiles = pieces[which]
        for column in range(model_count):
            for tile in range(tiles):
                lanes = min(LANES, span - tile * LANES)
                first = column * span + tile * LANES
                block = product[:, first : first + lanes].astype(low_type)
                for row in range(data_count):
                    dec_packed[
                        spot_of(row, column, dec_orders[which]),
                        offset + tile * height : offset + (tile + 1) * height,
                        :lanes,
                    ] = block[row * height : (row + 1) * height, :]

    swap = Exchange(images, grad_arrived, demb_own, swap_sems.at[0], swap_sems.at[1])

    def decoder(
        w_out,
        xs,
        qkv_weights,
        a_s,
        qkv_s,
        e_s,
        inv_s,
        o_s,
        dy_s,
        db_dec,
        do_s,
    ):
        length = side * side
        width = w_out.shape[0]
        size = width // heads
        scaling = float(size) ** -0.5
        place = lax.broadcasted_iota(jnp.int32, (length, visible), 0)
        turn = lax.broadcasted_iota(jnp.int32, (length, visible), 1)
        out_move = Move(dec_hbm[3], w_out, move_sems.at[3])

        def turned(*inputs):
            turned_moves = [
                Move(dec_hbm[position], one, move_sems.at[position])
                for position, one in enumerate(inputs)
            ]
            encoder_barrier(images, ["mp", "dp"])
            for position, one in enumerate(inputs):
                turned_moves[position].wait()
                qkv_weights[position * width : (position + 1) * width, :] = one[...].T

        pl.run_scoped(turned, *scopes[3])

        def picks(image):
            order = order_ref[image, :, :visible]
            kept = jnp.sum(keep_ref[image], axis=1, keepdims=True)
            return jnp.where((order == place) & (turn < kept), 1.0, 0.0)

        def rows_of(image):
            if isinstance(image, int):
                return slice(image * length, (image + 1) * length)
            return pl.ds(pl.multiple_of(image * length, length), length)

        def dense(w_up, w_down, w_pred, cotangent, mid_s, c_s, g_s, du_s, low_s, dm_s, staged):
            hidden = w_up.shape[1]
            second_moves = [
                Move(source, target, move_sems.at[4 + position])
                for position, (source, target) in enumerate(
                    zip(dec_hbm[4:], (w_up, w_down, w_pred, cotangent))
                )
            ]
            out_move.wait()
            for move in second_moves:
                move.wait()
            small[...] = jnp.zeros_like(small)

            def stage_copy(image):
                return pltpu.make_async_copy(staged, decoded.at[image], decoded_sems.at[image])

            def one_image(image, carry):
                rows = rows_of(image)
                pick = picks(image)
                hidden_rows = 1.0 - jnp.sum(pick, axis=1, keepdims=True)
                quarter = width // 4
                lane = lax.broadcasted_iota(jnp.int32, (side, quarter), 1).astype(full_type)
                line = lax.broadcasted_iota(jnp.int32, (side, quarter), 0).astype(full_type)
                angle = dist_ref[image] * line * jnp.exp(lane * (-math.log(10000.0) / quarter))
                table = jnp.concatenate([jnp.sin(angle), jnp.cos(angle)], axis=1)
                by_row = jnp.broadcast_to(table[:, None, :], (side, side, 2 * quarter))
                by_col = jnp.broadcast_to(table[None, :, :], (side, side, 2 * quarter))
                codes = jnp.concatenate(
                    [by_row.reshape(length, 2 * quarter), by_col.reshape(length, 2 * quarter)],
                    axis=1,
                )
                start = jnp.dot(
                    pick.astype(low_type), arrived[image], preferred_element_type=full_type
                )
                start = start + hidden_rows * mask_token[...] + codes
                xs[rows, :] = start
                normed, scale = norm_parts(start)
                a_s[rows, :] = (normed * dec_gain_attn[...]).astype(low_type)
                for position in range(3):
                    span = slice(position * width, (position + 1) * width)
                    part = dot_as(qkv_weights[span, :], a_s[rows, :], 1, 1)
                    if position == 0:
                        part = part * (scaling * LOG2E)
                    qkv_s[span, rows] = part.astype(low_type)

                def one_head(head, inner):
                    span = pl.multiple_of(head * size, size)
                    query = qkv_s[pl.ds(span, size), rows]
                    key = qkv_s[pl.ds(width + span, size), rows]
                    value = qkv_s[pl.ds(2 * width + span, size), rows]
                    scores = dot_as(key, query, 0, 0)
                    weights = jnp.exp2(scores - jnp.max(scores, axis=0, keepdims=True))
                    inverse = 1.0 / jnp.sum(weights, axis=0, keepdims=True)
                    weights = weights.astype(low_type)
                    e_s[image * heads + head] = weights
                    inv_s[image * heads + head] = inverse
                    mixed = jnp.dot(value, weights, preferred_element_type=full_type)
                    o_s[pl.ds(span, size), rows] = (mixed * inverse).astype(low_type)
                    return inner

                lax.fori_loop(0, heads, one_head, 0, unroll=4)

                middle = start + dot_as(o_s[:, rows], w_out[...], 0, 0)
                mid_s[...] = middle
                normed, scale = norm_parts(middle)
                c_s[rows, :] = (normed * dec_gain_mlp[...]).astype(low_type)
                for first in range(0, hidden, chunk):
                    cols = slice(first, first + chunk)
                    pre = jnp.dot(c_s[rows, :], w_up[:, cols], preferred_element_type=full_type)
                    active, slope = gelu_pair(pre)
                    g_s[rows, cols] = active.astype(low_type)
                    du_s[rows, cols] = slope.astype(low_type)
                outputs = middle + jnp.dot(
                    g_s[rows, :], w_down[...], preferred_element_type=full_type
                )
                low_s[rows, :] = outputs.astype(low_type)

                @pl.when(image > 0)
                def _():
                    stage_copy(image - 1).wait()

                staged[...] = jnp.dot(
                    low_s[rows, :], w_pred[...], preferred_element_type=full_type
                )
                stage_copy(image).start()

                grad_out = dot_as(cotangent[image], w_pred[...], 1, 1)
                dm_s[rows, :] = grad_out.astype(low_type)
                for first in range(0, hidden, chunk):
                    cols = slice(first, first + chunk)
                    grad_active = dot_as(dm_s[rows, :], w_down[cols, :], 1, 1)
                    du_s[rows, cols] = (grad_active * du_s[rows, cols].astype(full_type)).astype(
                        low_type
                    )
                grad_second = dot_as(du_s[rows, :], w_up[...], 1, 1)
                normed, scale = norm_parts(mid_s[...])
                small[1:2, :] += jnp.sum(grad_second * normed, axis=0, keepdims=True)
                grad_middle = grad_out + norm_back(
                    normed, scale, grad_second * dec_gain_mlp[...]
                )
                dy_s[rows, :] = grad_middle
                db_dec[rows, :] = grad_middle.astype(low_type)
                return carry

            lax.fori_loop(0, images, one_image, 0)
            all_pixels = cotangent[...].reshape(-1, cotangent.shape[2])
            store_dec(6, dot_as(low_s[...], all_pixels, 0, 0))
            pred_sum.start()
            store_dec(5, dot_as(g_s[...], dm_s[...], 0, 0))
            down_sum.start()
            pred_sum.advance()
            store_dec(4, dot_as(c_s[...], du_s[...], 0, 0))
            up_sum.start()
            down_sum.advance()
            stage_copy(images - 1).wait()

        pl.run_scoped(dense, *scopes[1])

        for image in range(images):
            rows = rows_of(image)
            do_s[...] = dot_as(w_out[...], db_dec[rows, :], 1, 1)

            def back_head(head, inner):
                span = pl.multiple_of(head * size, size)
                query = qkv_s[pl.ds(span, size), rows]
                key = qkv_s[pl.ds(width + span, size), rows]
                value = qkv_s[pl.ds(2 * width + span, size), rows]
                weights = e_s[image * heads + head]
                grad_full = do_s[pl.ds(span, size), :] * (inv_s[image * heads + head] * scaling)
                mixed = o_s[pl.ds(span, size), rows].astype(full_type)
                shift = jnp.sum(grad_full * mixed, axis=0, keepdims=True)
                grad_low = grad_full.astype(low_type)
                grad_probs = dot_as(value, grad_low, 0, 0)
                grad_scores = (weights.astype(full_type) * (grad_probs - shift)).astype(low_type)
                grad_value = dot_as(grad_low, weights, 1, 1) * (1.0 / scaling)
                grad_query = jnp.dot(key, grad_scores, preferred_element_type=full_type)
                grad_key = dot_as(query, grad_scores, 1, 1) * (1.0 / (scaling * LOG2E))
                qkv_s[pl.ds(span, size), rows] = grad_query.astype(low_type)
                qkv_s[pl.ds(width + span, size), rows] = grad_key.astype(low_type)
                qkv_s[pl.ds(2 * width + span, size), rows] = grad_value.astype(low_type)
                return inner

            lax.fori_loop(0, heads, back_head, 0, unroll=4)

            grad_normed = dot_as(qkv_s[:, rows], qkv_weights[...], 0, 0)
            normed, scale = norm_parts(xs[rows, :])
            small[0:1, :] += jnp.sum(grad_normed * normed, axis=0, keepdims=True)
            grad_start = dy_s[rows, :] + norm_back(
                normed, scale, grad_normed * dec_gain_attn[...]
            )
            pick = picks(image)
            hidden_rows = 1.0 - jnp.sum(pick, axis=1, keepdims=True)
            small[2:3, :] += jnp.sum(hidden_rows * grad_start, axis=0, keepdims=True)
            grad_arrived[image] = dot_as(
                pick.astype(low_type), grad_start.astype(low_type), 0, 0
            ).astype(low_type)
            if image == 0:
                up_sum.advance()
                pred_sum.advance()
        swap.start()
        for position in range(3):
            grads = qkv_s[position * width : (position + 1) * width, :]
            store_dec(position, dot_as(a_s[...], grads, 0, 1))
        store_dec(3, jnp.dot(o_s[...], db_dec[...], preferred_element_type=full_type))
        attn_sum.start()
        pred_sum.advance()
        down_sum.advance()

    pl.run_scoped(decoder, *scopes[0])
    thin_acc[0] = small[...]

    def encoder(*local):
        local = list(local)
        loaded = local[:15]
        (
            w_out,
            w_up,
            w_down,
            a_s,
            qkv_s,
            e_s,
            inv_s,
            o_own,
            c_s,
            g_s,
            slope_s,
            mid_s,
            low_s,
            embed_full,
            qkv_weights,
        ) = loaded
        dm_s, du_s, dqkv_s, dy_s, do_s = local[15:]
        block_rows = images * visible
        columns = w_out.shape[0]
        size = columns // enc_heads
        scaling = float(size) ** -0.5
        hidden, width = w_down.shape
        moves = {}
        for position in (13, 2, 10, 1, 9, 11, 8, 12, 0, 4, 5, 6, 7, 14, 3):
            moves[position] = Move(enc_hbm[position], loaded[position], move_sems.at[8 + position])

        def ready(*arrays):
            for array in arrays:
                moves[[array is one for one in loaded].index(True)].wait()

        embed_sum = bulk(spread_stages, embed_bufs, 1, 0, embed_packed.shape[1], embed_sems, 0)
        part = hidden // CUTS
        up_orders = [enc_stages] * (CUTS - LATE_UP) + [late_stages] * LATE_UP
        up_sums = [
            bulk(up_orders[cut], row_bufs, 2, cut * part, part, row_sems, cut)
            for cut in range(CUTS)
        ]
        qkv_orders = [enc_stages, enc_stages, enc_stages]
        qkv_sums = [
            bulk(order, row_bufs, 2, hidden + cut * columns, columns, row_sems, CUTS + cut)
            for cut, order in enumerate(qkv_orders)
        ]
        down_sums = [
            bulk(enc_stages, col_bufs, 1, cut * part, part, col_sems, cut) for cut in range(CUTS)
        ]
        out_sum = bulk(late_stages, col_bufs, 1, hidden, columns, col_sems, CUTS)

        swap.finish()
        demb_gather = Gather(demb_own, lambda slot: demb_slots.at[slot], sems.at[0], sems.at[1])
        demb_gather.start()
        demb_slots[index] = demb_own[...]
        ready(low_s)
        offset, high, span, tiles = embed_piece
        product = dot_as(low_s[...], demb_own[...].reshape(block_rows, -1), 0, 0)
        for column in range(model_count):
            for row in range(data_count):
                spot = spot_of(row, column, spread_stages)
                for tile in range(tiles):
                    lanes = min(LANES, span - tile * LANES)
                    first = column * span + tile * LANES
                    embed_packed[spot, tile * high : (tile + 1) * high, :lanes] = product[
                        row * high : (row + 1) * high, first : first + lanes
                    ].astype(low_type)
        embed_sum.start()
        attn_sum.advance()
        up_sum.advance()
        pred_sum.advance()
        ready(embed_full, w_down, slope_s)

        def rows_of(slot):
            return pl.ds(pl.multiple_of(slot * block_rows, block_rows), block_rows)

        def first_back(step, carry):
            demb_gather.arrive_at(step)
            at_step(step, 2, [embed_sum, down_sum])
            mask = visit_mask(step, count)
            slot = index ^ mask
            rows = rows_of(slot)
            grad_rows = demb_slots[slot].reshape(block_rows, -1)
            grad_out = dot_as(grad_rows, embed_full[...], 1, 1)

            @pl.when(mask == 0)
            def _():
                dy_s[...] = grad_out

            dm_s[rows, :] = grad_out.astype(low_type)
            for first in range(0, hidden, chunk):
                cols = slice(first, first + chunk)
                grad_active = dot_as(dm_s[rows, :], w_down[cols, :], 1, 1)
                du_s[rows, cols] = (grad_active * slope_s[rows, cols].astype(full_type)).astype(
                    low_type
                )
            return carry

        lax.fori_loop(0, count, first_back, 0)
        ready(w_up)
        scatter = Scatter(parts_mlp, total, landing_mlp, sems.at[2], sems.at[3])
        total[...] = jnp.zeros_like(total)

        def second_back(step, carry):
            at_step(step, 1, [up_sum, attn_sum, down_sum])
            mask = count - 1 - step
            rows = rows_of(index ^ mask)
            scatter.put(mask, dot_as(du_s[rows, :], w_up[...], 1, 1))
            return carry

        lax.fori_loop(0, count, second_back, 0)
        for bit in range(model_bits - 1):
            scatter.finish_bit(bit)

        def store_rows(product, first, stages):
            high = width // data_count
            for row in range(data_count):
                row_packed[spot_of(row, 0, stages), :, first : first + product.shape[1]] = (
                    product[row * high : (row + 1) * high, :].astype(low_type)
                )

        def store_cols(product, first, stages):
            wide = width // data_count
            for col in range(data_count):
                col_packed[
                    spot_of(col, 0, stages), first : first + product.shape[0], :wide
                ] = product[:, col * wide : (col + 1) * wide].astype(low_type)

        ready(g_s)
        for cut in range(CUTS):
            cols = slice(cut * part, (cut + 1) * part)
            store_cols(dot_as(g_s[:, cols], dm_s[...], 0, 0), cut * part, enc_stages)
            down_sums[cut].start()
        ready(mid_s)
        for one in (embed_sum, up_sum, attn_sum, pred_sum):
            one.advance()
        scatter.finish_bit(model_bits - 1)

        normed, scale = norm_parts(mid_s[...])
        grad_second = total[...]
        wide_acc[0, 1:2, :] = jnp.sum(grad_second * normed, axis=0, keepdims=True)
        grad_middle = dy_s[...] + norm_back(normed, scale, grad_second * gain_mlp[...])
        dy_s[...] = grad_middle
        db_s[rows_of(index), :] = grad_middle.astype(low_type)
        db_gather = Gather(None, lambda slot: db_s.at[rows_of(slot)], sems.at[4], sems.at[5])
        db_gather.start()
        ready(c_s)
        for cut in range(CUTS):
            cols = slice(cut * part, (cut + 1) * part)
            store_rows(dot_as(c_s[...], du_s[:, cols], 0, 0), cut * part, up_orders[cut])
            up_sums[cut].start()
        for one in (embed_sum, attn_sum, down_sum, up_sum):
            one.advance()

        ready(w_out, qkv_s, e_s, inv_s, o_own, qkv_weights)
        second_scatter = Scatter(parts_attn, total, landing_attn, sems.at[6], sems.at[7])
        total[...] = jnp.zeros_like(total)

        def third_back(step, carry):
            db_gather.arrive_at(step)
            at_step(step, 1, [embed_sum, attn_sum] + down_sums[:2])
            at_step(step, count - 1, [embed_sum] + down_sums[2:])
            mask = visit_mask(step, count)
            slot = index ^ mask
            rows = rows_of(slot)
            do_s[...] = dot_as(w_out[...], db_s[rows, :], 1, 1)
            for head in range(enc_heads):
                span = slice(head * size, (head + 1) * size)
                key_span = slice(columns + head * size, columns + (head + 1) * size)
                value_span = slice(2 * columns + head * size, 2 * columns + (head + 1) * size)
                query, key, value = qkv_s[span, rows], qkv_s[key_span, rows], qkv_s[value_span, rows]
                weights = e_s[slot * enc_heads + head]
                grad_full = do_s[span, :] * (inv_s[slot * enc_heads + head] * scaling)
                shift = jnp.sum(
                    grad_full * o_own[span, rows].astype(full_type), axis=0, keepdims=True
                )
                grad_low = grad_full.astype(low_type)
                grad_probs = dot_as(value, grad_low, 0, 0)
                grad_scores = (weights.astype(full_type) * (grad_probs - shift)).astype(low_type)
                grad_value = dot_as(grad_low, weights, 1, 1) * (1.0 / scaling)
                grad_query = jnp.dot(key, grad_scores, preferred_element_type=full_type)
                grad_key = dot_as(query, grad_scores, 1, 1) * (1.0 / (scaling * LOG2E))
                dqkv_s[span, rows] = grad_query.astype(low_type)
                dqkv_s[key_span, rows] = grad_key.astype(low_type)
                dqkv_s[value_span, rows] = grad_value.astype(low_type)
            second_scatter.put(mask, dot_as(dqkv_s[:, rows], qkv_weights[...], 0, 0))
            return carry

        lax.fori_loop(0, count, third_back, 0)
        for bit in range(model_bits - 1):
            second_scatter.finish_bit(bit)
        store_cols(
            jnp.dot(o_own[...], db_s[...], preferred_element_type=full_type), hidden, late_stages
        )
        out_sum.start()
        ready(a_s)
        for cut, order in enumerate(qkv_orders):
            span = slice(cut * columns, (cut + 1) * columns)
            product = dot_as(a_s[...], dqkv_s[span, :], 0, 1)
            store_rows(product, hidden + cut * columns, order)
            qkv_sums[cut].start()
        for one in up_sums[:2] + down_sums:
            one.advance()
        second_scatter.finish_bit(model_bits - 1)
        normed, scale = norm_parts(tokens[...].astype(full_type))
        grad_normed = total[...]
        wide_acc[0, 0:1, :] = jnp.sum(grad_normed * normed, axis=0, keepdims=True)
        grad_tokens[...] = dy_s[...] + norm_back(normed, scale, grad_normed * gain_attn[...])

        def norm_copies(stage):
            peer = partner(*all_stages[stage])[0]
            return [
                pltpu.make_async_remote_copy(
                    src_ref=acc.at[stage],
                    dst_ref=got.at[stage],
                    send_sem=norm_sems.at[0, kind, stage],
                    recv_sem=norm_sems.at[1, kind, stage],
                    device_id=peer,
                    device_id_type=MESH,
                )
                for kind, (acc, got) in enumerate(((wide_acc, wide_got), (thin_acc, thin_got)))
            ]

        sums = dec_sums + [embed_sum] + down_sums + up_sums
        last = [out_sum] + qkv_sums
        rounds = [sums, sums]
        for turn in range(len(last) + data_bits - 1):
            rounds.append([last[turn - back] for back in range(data_bits) if 0 <= turn - back < len(last)])
        pending = []
        for turn, group in enumerate(rounds):
            if turn < len(all_stages):
                pending = norm_copies(turn)
                for copy in pending:
                    copy.start()
            for one in group:
                one.advance()
            if turn < len(all_stages):
                for copy in pending:
                    copy.wait()
                wide_acc[turn + 1] = wide_acc[turn] + wide_got[turn]
                thin_acc[turn + 1] = thin_acc[turn] + thin_got[turn]
        everything = sums + last
        for one in everything:
            while not one.done():
                one.advance()
        norm_wide[...] = wide_acc[len(all_stages)]
        norm_thin[...] = thin_acc[len(all_stages)]
        for one in (demb_gather, scatter, db_gather, second_scatter):
            one.drain()


    pl.run_scoped(encoder, *scopes[2])
    rows_out[...] = row_bufs[-1][0]
    cols_out[...] = col_bufs[-1][0]
    dec_out[...] = dec_bufs[-1][0]
    embed_out[...] = embed_bufs[-1][0]


def unpack_kernel(widths, dec_list, embed_list, *refs):
    hidden, columns, wide = widths
    grad_tokens, norm_wide, norm_thin, rows_in, cols_in, dec_in, embed_in = refs[:7]
    out_tokens, g_query, g_key, g_value, g_up, g_out, g_down, g_embed = refs[7:15]
    small = refs[15:20]
    dec_outs = refs[20:]
    out_tokens[...] = grad_tokens[...]
    g_up[...] = rows_in[:, :hidden].astype(full_type)
    for position, out in enumerate((g_query, g_key, g_value)):
        first = hidden + position * columns
        out[...] = rows_in[:, first : first + columns].astype(full_type)
    g_down[...] = cols_in[:hidden, :wide].astype(full_type)
    g_out[...] = cols_in[hidden : hidden + columns, :wide].astype(full_type)
    for position in range(2):
        small[position][...] = norm_wide[position : position + 1, :]
    for position in range(3):
        small[2 + position][...] = norm_thin[position : position + 1, :]
    for outs, pieces, source in (([g_embed], embed_list, embed_in), (dec_outs, dec_list, dec_in)):
        for out, (offset, rows, width, tiles) in zip(outs, pieces):
            for tile in range(tiles):
                lanes = min(LANES, width - tile * LANES)
                block = source[offset + tile * rows : offset + (tile + 1) * rows, :lanes]
                out[:, tile * LANES : tile * LANES + lanes] = block.astype(full_type)


def decode_and_back(
    arrived,
    grid_order,
    grid_keep,
    ground_dist,
    dec_weights,
    mask_token,
    pred_proj,
    cotangent,
    tokens,
    weights,
    saved,
    embed_proj,
):
    gain_attn, w_query, w_key, w_value, w_out, gain_mlp, w_up, w_down = weights
    (dec_gain_attn, dec_query, dec_key, dec_value, dec_proj, dec_gain_mlp, dec_up, dec_down) = (
        dec_weights
    )
    data_count, model_count = lax.axis_size("dp"), lax.axis_size("mp")
    data_bits, model_bits = log2_of(data_count), log2_of(model_count)
    images, visible, width = tokens.shape
    rows = images * visible
    every = rows * model_count
    enc_heads = HE // model_count
    columns, hidden = w_query.shape[1], w_up.shape[1]
    out_width = embed_proj.shape[1] * model_count
    length, pixels = cotangent.shape[1:]
    grid_rows = images * length
    dec_hidden = dec_up.shape[1]
    matrices = [dec_query, dec_key, dec_value, dec_proj, dec_up, dec_down, pred_proj]
    pieces, height = dec_pieces(data_count, model_count, [one.shape for one in matrices])
    embed_pieces, embed_height = dec_pieces(data_count, model_count, [(width, out_width)])
    high, wide = width // data_count, width // data_count
    wide_pad = -(-wide // LANES) * LANES
    devices = data_count * model_count
    stages = data_bits + model_bits
    row_shape = (high, hidden + 3 * columns)
    col_shape = (hidden + columns, wide_pad)
    vmem = pl.BlockSpec(memory_space=pltpu.VMEM)
    hbm = pl.BlockSpec(memory_space=pl.ANY)
    low = lambda *shape: pltpu.VMEM(shape, low_type)
    full = lambda *shape: pltpu.VMEM(shape, full_type)
    loaded = [w_out, w_up, w_down, *saved]
    turned_scope = [low(out_width, out_width)] * 3
    attn_scope = [
        low(out_width, out_width),
        full(grid_rows, out_width),
        low(3 * out_width, out_width),
        low(grid_rows, out_width),
        low(3 * out_width, grid_rows),
        low(images * HD, length, length),
        full(images * HD, 1, length),
        low(out_width, grid_rows),
        full(grid_rows, out_width),
        low(grid_rows, out_width),
        full(out_width, length),
    ]
    dense_scope = [
        low(out_width, dec_hidden),
        low(dec_hidden, out_width),
        low(out_width, pixels),
        low(images, length, pixels),
        full(length, out_width),
        low(grid_rows, out_width),
        low(grid_rows, dec_hidden),
        low(grid_rows, dec_hidden),
        low(grid_rows, out_width),
        low(grid_rows, out_width),
        full(length, pixels),
    ]
    enc_scope = [pltpu.VMEM(one.shape, one.dtype) for one in loaded] + [
        low(every, width),
        low(every, hidden),
        low(3 * columns, every),
        full(rows, width),
        full(columns, rows),
    ]
    plan = (
        images,
        visible,
        enc_heads,
        HD,
        SIDE,
        pieces,
        embed_pieces[0],
        (attn_scope, dense_scope, enc_scope, turned_scope),
    )

    def kernel(*refs):
        back_kernel(plan, *refs)

    outs = [
        (cotangent.shape, full_type),
        ((rows, width), full_type),
        ((2, width), full_type),
        ((3, out_width), full_type),
        (row_shape, low_type),
        (col_shape, low_type),
        ((height, LANES), low_type),
        ((embed_height, LANES), low_type),
    ]
    scratch = [
        pltpu.SemaphoreType.DMA((8 + len(loaded),)),
        pltpu.SemaphoreType.DMA((images,)),
        low(images, visible, out_width),
        low(devices, height, LANES),
        full(3, out_width),
        low(images, visible, out_width),
        low(model_count, images, visible, out_width),
        low(every, width),
        full(rows, width),
        low(model_count - 1, rows, width),
        low(model_count - 1, rows, width),
        low(model_count - 1, rows, width),
        low(model_count - 1, rows, width),
        pltpu.SemaphoreType.DMA((8, model_count)),
        pltpu.SemaphoreType.DMA((2, images)),
        low(data_count, *row_shape),
        low(data_count, *col_shape),
        low(devices, embed_height, LANES),
    ]
    scratch += [low(data_count >> (bit + 1), *row_shape) for bit in range(data_bits)]
    scratch += [low(data_count >> (bit + 1), *col_shape) for bit in range(data_bits)]
    scratch += [low(devices >> (bit + 1), height, LANES) for bit in range(stages)]
    scratch += [low(devices >> (bit + 1), embed_height, LANES) for bit in range(stages)]
    for shape in ((2, width), (3, out_width)):
        scratch += [full(stages + 1, *shape), full(stages, *shape)]
    scratch += [
        pltpu.SemaphoreType.DMA((2, CUTS + 3, data_bits)),
        pltpu.SemaphoreType.DMA((2, CUTS + 1, data_bits)),
        pltpu.SemaphoreType.DMA((2, 4, stages)),
        pltpu.SemaphoreType.DMA((2, 1, stages)),
        pltpu.SemaphoreType.DMA((2, 2, stages)),
    ]
    results = pl.pallas_call(
        kernel,
        out_shape=[jax.ShapeDtypeStruct(shape, kind) for shape, kind in outs],
        in_specs=[pl.BlockSpec(memory_space=pltpu.SMEM)] + [vmem] * 9 + [hbm] * (8 + len(loaded)),
        out_specs=[hbm] + [vmem] * (len(outs) - 1),
        scratch_shapes=scratch,
        compiler_params=pltpu.CompilerParams(
            collective_id=2, has_side_effects=True, vmem_limit_bytes=255 * 2**18
        ),
    )(
        ground_dist,
        arrived,
        grid_order[:, None, :],
        grid_keep[:, None, :],
        dec_gain_attn.reshape(1, -1),
        dec_gain_mlp.reshape(1, -1),
        mask_token.reshape(1, -1),
        tokens.reshape(rows, width),
        gain_attn.reshape(1, -1),
        gain_mlp.reshape(1, -1),
        dec_query,
        dec_key,
        dec_value,
        dec_proj,
        dec_up,
        dec_down,
        pred_proj,
        cotangent,
        *loaded,
    )
    final = [
        (rows, width),
        (high, columns),
        (high, columns),
        (high, columns),
        (high, hidden),
        (columns, wide),
        (hidden, wide),
        (embed_pieces[0][1], embed_pieces[0][2]),
    ]
    final += [(1, width)] * 2 + [(1, out_width)] * 3
    final += [(piece[1], piece[2]) for piece in pieces]

    def last_kernel(*refs):
        unpack_kernel((hidden, columns, wide), pieces, embed_pieces, *refs)

    return results[0], pl.pallas_call(
        last_kernel,
        out_shape=[jax.ShapeDtypeStruct(shape, full_type) for shape in final],
        in_specs=[vmem] * (len(outs) - 1),
        out_specs=[vmem] * len(final),
    )(*results[1:])


def layer_norm(values, scale_gain):
    center = values - jnp.mean(values, axis=-1, keepdims=True)
    spread = jnp.mean(center * center, axis=-1, keepdims=True)
    return center * lax.rsqrt(spread + eps_norm) * scale_gain


def exact_gelu(values):
    return jax.nn.gelu(values, approximate=False)


def matmul(left_side, right_side):
    flat_rows = left_side.reshape(-1, left_side.shape[-1])
    product = jnp.dot(flat_rows, right_side, preferred_element_type=full_type)
    return product.reshape(left_side.shape[:-1] + (right_side.shape[1],))


def matmul_t(left_side, right_side):
    flat_rows = left_side.reshape(-1, left_side.shape[-1])
    product = lax.dot_general(
        flat_rows, right_side, (((1,), (1,)), ((), ())), preferred_element_type=full_type
    )
    return product.reshape(left_side.shape[:-1] + (right_side.shape[0],))


def outer_sum(left_side, right_side):
    return lax.dot_general(
        left_side.reshape(-1, left_side.shape[-1]),
        right_side.reshape(-1, right_side.shape[-1]),
        (((0,), (0,)), ((), ())),
        preferred_element_type=full_type,
    )


def spread_rows(values, tensor_split):
    if tensor_split:
        return lax.all_gather(values, "mp", axis=0, tiled=True)
    return values


def collect_rows(values, tensor_split):
    if tensor_split:
        return lax.psum_scatter(
            values.astype(jnp.bfloat16), "mp", scatter_dimension=0, tiled=True
        ).astype(jnp.float32)
    return values


def images_per_block(images, length):
    grouped = 1
    while grouped * length < 512 and grouped < images:
        grouped = grouped * 2
    return grouped


def in_blocks(blocked_array, grouped):
    return blocked_array.reshape(
        (blocked_array.shape[0] // grouped, grouped) + blocked_array.shape[1:]
    )


def with_heads(blocked_array, head_count):
    return blocked_array.reshape(
        blocked_array.shape[:2] + (head_count, blocked_array.shape[2] // head_count)
    )


def attend_forward(queries, keys_all, values_all, key_valid, head_count):
    images, length, columns = queries.shape
    grouped = images_per_block(images, length)
    scaling = float(columns // head_count) ** (-0.5)

    def one_block(pieces):
        query_b, key_b, value_b, valid_b = pieces
        scores = (
            jnp.einsum("nqhd,nkhd->nhqk", query_b, key_b, preferred_element_type=full_type)
            * scaling
        )
        scores = jnp.where(valid_b[:, None, None, :], scores, masked_score)
        row_max = jnp.max(scores, axis=-1, keepdims=True)
        weights = jnp.exp(scores - row_max)
        totals = jnp.sum(weights, axis=-1, keepdims=True)
        prob_rows = (weights / totals).astype(low_type)
        mixed_b = jnp.einsum(
            "nhqk,nkhd->nqhd", prob_rows, value_b, preferred_element_type=full_type
        )
        return (mixed_b.astype(low_type), (row_max + jnp.log(totals))[..., 0])

    pieces_in = (
        in_blocks(with_heads(queries, head_count), grouped),
        in_blocks(with_heads(keys_all, head_count), grouped),
        in_blocks(with_heads(values_all, head_count), grouped),
        in_blocks(key_valid, grouped),
    )
    mixed_rows, log_total = lax.map(one_block, pieces_in)
    return (
        mixed_rows.reshape(images, length, columns),
        log_total.reshape(images, head_count, length),
    )


def attend_backward(queries, keys_all, values_all, key_valid, log_total, grad_mixed, head_count):
    images, length, columns = queries.shape
    grouped = images_per_block(images, length)
    scaling = float(columns // head_count) ** (-0.5)

    def one_block(pieces):
        query_b, key_b, value_b, valid_b, total_b, grad_b = pieces
        scores = (
            jnp.einsum("nqhd,nkhd->nhqk", query_b, key_b, preferred_element_type=full_type)
            * scaling
        )
        scores = jnp.where(valid_b[:, None, None, :], scores, masked_score)
        prob_rows = jnp.exp(scores - total_b[..., None])
        grad_value_b = jnp.einsum(
            "nhqk,nqhd->nkhd", prob_rows.astype(low_type), grad_b, preferred_element_type=full_type
        )
        grad_probs = jnp.einsum(
            "nqhd,nkhd->nhqk", grad_b, value_b, preferred_element_type=full_type
        )
        grad_scores = prob_rows * (
            grad_probs - jnp.sum(grad_probs * prob_rows, axis=-1, keepdims=True)
        )
        grad_scores = (grad_scores * scaling).astype(low_type)
        grad_query_b = jnp.einsum(
            "nhqk,nkhd->nqhd", grad_scores, key_b, preferred_element_type=full_type
        )
        grad_key_b = jnp.einsum(
            "nhqk,nqhd->nkhd", grad_scores, query_b, preferred_element_type=full_type
        )
        return (
            grad_query_b.astype(low_type),
            grad_key_b.astype(low_type),
            grad_value_b.astype(low_type),
        )

    pieces_in = (
        in_blocks(with_heads(queries, head_count), grouped),
        in_blocks(with_heads(keys_all, head_count), grouped),
        in_blocks(with_heads(values_all, head_count), grouped),
        in_blocks(key_valid, grouped),
        in_blocks(log_total, grouped),
        in_blocks(with_heads(grad_mixed, head_count), grouped),
    )
    grad_query, grad_key, grad_value = lax.map(one_block, pieces_in)
    return (
        grad_query.reshape(images, length, columns),
        grad_key.reshape(images, length, columns),
        grad_value.reshape(images, length, columns),
    )


def block_forward(inputs, key_valid, weights, head_count, tensor_split):
    gain_attn, w_query, w_key, w_value, w_out, gain_mlp, w_up, w_down = weights
    normed = spread_rows(layer_norm(inputs, gain_attn).astype(low_type), tensor_split)
    queries = matmul(normed, w_query).astype(low_type)
    keys_all = matmul(normed, w_key).astype(low_type)
    values_all = matmul(normed, w_value).astype(low_type)
    mixed_rows, log_total = attend_forward(queries, keys_all, values_all, key_valid, head_count)
    middle = inputs + collect_rows(matmul(mixed_rows, w_out), tensor_split)
    second = spread_rows(layer_norm(middle, gain_mlp).astype(low_type), tensor_split)
    pre_act = matmul(second, w_up)
    active = exact_gelu(pre_act).astype(low_type)
    outputs = middle + collect_rows(matmul(active, w_down), tensor_split)
    kept_state = (
        inputs,
        normed,
        queries,
        keys_all,
        values_all,
        mixed_rows,
        log_total,
        middle,
        second,
        pre_act,
        active,
    )
    return (outputs, kept_state)


def block_backward(grad_out, kept_state, key_valid, weights, head_count, tensor_split):
    gain_attn, w_query, w_key, w_value, w_out, gain_mlp, w_up, w_down = weights
    (
        inputs,
        normed,
        queries,
        keys_all,
        values_all,
        mixed_rows,
        log_total,
        middle,
        second,
        pre_act,
        active,
    ) = kept_state
    grad_branch = spread_rows(grad_out.astype(low_type), tensor_split)
    grad_down = outer_sum(active, grad_branch)
    grad_active = matmul_t(grad_branch, w_down)
    grad_pre = jax.vjp(exact_gelu, pre_act)[1](grad_active)[0].astype(low_type)
    grad_up = outer_sum(second, grad_pre)
    grad_second = collect_rows(matmul_t(grad_pre, w_up), tensor_split)
    norm_grad, grad_gain_mlp = jax.vjp(layer_norm, middle, gain_mlp)[1](grad_second)
    grad_middle = grad_out + norm_grad
    grad_attn = spread_rows(grad_middle.astype(low_type), tensor_split)
    grad_w_out = outer_sum(mixed_rows, grad_attn)
    grad_mixed = matmul_t(grad_attn, w_out).astype(low_type)
    grad_query, grad_key, grad_value = attend_backward(
        queries, keys_all, values_all, key_valid, log_total, grad_mixed, head_count
    )
    grad_w_query = outer_sum(normed, grad_query)
    grad_w_key = outer_sum(normed, grad_key)
    grad_w_value = outer_sum(normed, grad_value)
    grad_normed = (
        matmul_t(grad_query, w_query) + matmul_t(grad_key, w_key) + matmul_t(grad_value, w_value)
    )
    grad_normed = collect_rows(grad_normed, tensor_split)
    input_grad, grad_gain_attn = jax.vjp(layer_norm, inputs, gain_attn)[1](grad_normed)
    return (
        grad_middle + input_grad,
        (
            grad_gain_attn,
            grad_w_query,
            grad_w_key,
            grad_w_value,
            grad_w_out,
            grad_gain_mlp,
            grad_up,
            grad_down,
        ),
    )


def grid_codes(distance, side_count, columns):
    quarter = columns // 4
    frequency = 10000.0 ** (-jnp.arange(quarter, dtype=full_type) / quarter)
    places = jnp.arange(side_count * side_count)
    row_pos = (places // side_count).astype(full_type)
    col_pos = (places % side_count).astype(full_type)
    row_angle = distance[:, None, None] * row_pos[None, :, None] * frequency[None, None, :]
    col_angle = distance[:, None, None] * col_pos[None, :, None] * frequency[None, None, :]
    return jnp.concatenate(
        [jnp.sin(row_angle), jnp.cos(row_angle), jnp.sin(col_angle), jnp.cos(col_angle)], axis=-1
    )


def placement_table(visible_order, keep_flags, visible):
    positions = jnp.arange(visible_order.shape[1])
    matches = (visible_order[:, None, :visible] == positions[None, :, None]) & (
        keep_flags[:, :, None] == 1
    )
    return matches.astype(low_type)


def owner_blocks(full_grad, data_count, model_count):
    row_count, col_count = full_grad.shape
    reshaped = full_grad.reshape(
        data_count, row_count // data_count, model_count, col_count // model_count
    )
    return jnp.transpose(reshaped, (0, 2, 1, 3)).reshape(
        data_count * model_count, row_count // data_count, col_count // model_count
    )


def per_device_plain(
    tokens,
    lengths,
    grid_order,
    grid_keep,
    ground_dist,
    enc_norm,
    enc_query,
    enc_key,
    enc_value,
    enc_proj,
    enc_norm2,
    enc_up,
    enc_down,
    embed_proj,
    mask_token,
    dec_norm,
    dec_query,
    dec_key,
    dec_value,
    dec_proj,
    dec_norm2,
    dec_up,
    dec_down,
    pred_proj,
    cotangent,
):
    data_count = lax.axis_size("dp")
    model_count = lax.axis_size("mp")
    enc_weights = (enc_norm, enc_query, enc_key, enc_value, enc_proj, enc_norm2, enc_up, enc_down)
    dec_weights = (dec_norm, dec_query, dec_key, dec_value, dec_proj, dec_norm2, dec_up, dec_down)
    enc_heads = HE // model_count
    key_valid = jnp.arange(tokens.shape[1])[None, :] < lengths[:, None]
    enc_out, enc_saved = block_forward(
        tokens.astype(full_type), key_valid, enc_weights, enc_heads, True
    )
    enc_low = enc_out.astype(low_type)
    enc_all = spread_rows(enc_low, True)
    embedded = matmul(enc_all, embed_proj).astype(low_type)
    sectioned = embedded.reshape((data_count, -1) + embedded.shape[1:])
    arrived = lax.all_to_all(
        lax.all_to_all(sectioned, "dp", split_axis=0, concat_axis=0, tiled=True),
        "mp",
        split_axis=0,
        concat_axis=3,
        tiled=True,
    )
    arrived = arrived.reshape((-1,) + arrived.shape[2:])
    pick_table = placement_table(grid_order, grid_keep, arrived.shape[1])
    masked = (1 - grid_keep).astype(full_type)[..., None]
    dec_start = jnp.einsum("npt,ntc->npc", pick_table, arrived, preferred_element_type=full_type)
    dec_start = dec_start + masked * mask_token + grid_codes(ground_dist, SIDE, mask_token.shape[0])
    all_valid = jnp.ones(dec_start.shape[:2], jnp.bool_)
    dec_out, dec_saved = block_forward(dec_start, all_valid, dec_weights, HD, False)
    dec_low = dec_out.astype(low_type)
    decoded = matmul(dec_low, pred_proj)
    grad_pred = outer_sum(dec_low, cotangent)
    grad_dec_out = matmul_t(cotangent, pred_proj)
    grad_start, dec_grads = block_backward(
        grad_dec_out, dec_saved, all_valid, dec_weights, HD, False
    )
    grad_mask = jnp.sum(masked * grad_start, axis=(0, 1))
    grad_arrived = jnp.einsum("npt,npc->ntc", pick_table.astype(full_type), grad_start).astype(
        low_type
    )
    sent_back = grad_arrived.reshape((-1, IPD) + grad_arrived.shape[1:])
    returned = lax.all_to_all(
        lax.all_to_all(sent_back, "mp", split_axis=3, concat_axis=0, tiled=True),
        "dp",
        split_axis=0,
        concat_axis=0,
        tiled=True,
    )
    returned = returned.reshape((-1,) + returned.shape[2:])
    grad_embed = outer_sum(enc_all, returned)
    grad_enc_out = collect_rows(matmul_t(returned, embed_proj), True)
    grad_tokens, enc_grads = block_backward(
        grad_enc_out, enc_saved, key_valid, enc_weights, enc_heads, True
    )
    col_sums = (
        lax.psum_scatter(
            enc_grads[4].astype(jnp.bfloat16), "dp", scatter_dimension=1, tiled=True
        ).astype(jnp.float32),
        lax.psum_scatter(
            enc_grads[7].astype(jnp.bfloat16), "dp", scatter_dimension=1, tiled=True
        ).astype(jnp.float32),
    )
    norm_grads = lax.psum(
        (enc_grads[0], enc_grads[5], dec_grads[0], dec_grads[5], grad_mask), ("dp", "mp")
    )
    dec_list = (
        dec_grads[1],
        dec_grads[2],
        dec_grads[3],
        dec_grads[4],
        dec_grads[6],
        dec_grads[7],
        grad_pred,
    )
    row_sums = (
        lax.psum_scatter(
            enc_grads[1].astype(jnp.bfloat16), "dp", scatter_dimension=0, tiled=True
        ).astype(jnp.float32),
        lax.psum_scatter(
            enc_grads[2].astype(jnp.bfloat16), "dp", scatter_dimension=0, tiled=True
        ).astype(jnp.float32),
        lax.psum_scatter(
            enc_grads[3].astype(jnp.bfloat16), "dp", scatter_dimension=0, tiled=True
        ).astype(jnp.float32),
        lax.psum_scatter(
            enc_grads[6].astype(jnp.bfloat16), "dp", scatter_dimension=0, tiled=True
        ).astype(jnp.float32),
        lax.psum_scatter(
            grad_embed.astype(jnp.bfloat16), "dp", scatter_dimension=0, tiled=True
        ).astype(jnp.float32),
    )
    summed = (
        lax.psum_scatter(
            owner_blocks(dec_list[0], data_count, model_count),
            ("dp", "mp"),
            scatter_dimension=0,
            tiled=True,
        ),
        lax.psum_scatter(
            owner_blocks(dec_list[1], data_count, model_count),
            ("dp", "mp"),
            scatter_dimension=0,
            tiled=True,
        ),
        lax.psum_scatter(
            owner_blocks(dec_list[2], data_count, model_count),
            ("dp", "mp"),
            scatter_dimension=0,
            tiled=True,
        ),
        lax.psum_scatter(
            owner_blocks(dec_list[3], data_count, model_count),
            ("dp", "mp"),
            scatter_dimension=0,
            tiled=True,
        ),
        lax.psum_scatter(
            owner_blocks(dec_list[4], data_count, model_count),
            ("dp", "mp"),
            scatter_dimension=0,
            tiled=True,
        ),
        lax.psum_scatter(
            owner_blocks(dec_list[5], data_count, model_count),
            ("dp", "mp"),
            scatter_dimension=0,
            tiled=True,
        ),
        lax.psum_scatter(
            owner_blocks(dec_list[6], data_count, model_count),
            ("dp", "mp"),
            scatter_dimension=0,
            tiled=True,
        ),
    )
    embed_final = row_sums[4]
    dec_final = tuple((summed[index_num][0] for index_num in range(7)))
    return (
        decoded,
        grad_tokens,
        norm_grads[0],
        row_sums[0],
        row_sums[1],
        row_sums[2],
        col_sums[0],
        norm_grads[1],
        row_sums[3],
        col_sums[1],
        embed_final,
        norm_grads[4],
        norm_grads[2],
        dec_final[0],
        dec_final[1],
        dec_final[2],
        dec_final[3],
        norm_grads[3],
        dec_final[4],
        dec_final[5],
        dec_final[6],
    )


VMEM_BUDGET = 56 * 2**20


def kernel_bytes(tokens, enc_up, enc_query, dec_up, pred_proj):
    data_count, model_count = lax.axis_size("dp"), lax.axis_size("mp")
    images, visible, width = tokens.shape
    every = images * visible * model_count
    hidden, columns = enc_up.shape[1], enc_query.shape[1]
    out_width, wide = dec_up.shape[0], max(width // data_count, LANES)
    shapes = [(out_width, out_width)] * 4
    shapes += [dec_up.shape, dec_up.shape[::-1], pred_proj.shape, (width, out_width)]
    height = dec_pieces(data_count, model_count, shapes)[1]
    rows = 8 * every * width + 3 * every * hidden
    sums = width * (hidden + 3 * columns) + data_count * (hidden + columns) * wide
    sums = 2 * (sums + data_count * model_count * height * LANES)
    return 2 * (rows + sums + 2 * width * hidden + 4 * width * columns)


def per_device(
    tokens,
    lengths,
    grid_order,
    grid_keep,
    ground_dist,
    enc_norm,
    enc_query,
    enc_key,
    enc_value,
    enc_proj,
    enc_norm2,
    enc_up,
    enc_down,
    embed_proj,
    mask_token,
    dec_norm,
    dec_query,
    dec_key,
    dec_value,
    dec_proj,
    dec_norm2,
    dec_up,
    dec_down,
    pred_proj,
    cotangent,
):
    if kernel_bytes(tokens, enc_up, enc_query, dec_up, pred_proj) > VMEM_BUDGET:
        return per_device_plain(
            tokens,
            lengths,
            grid_order,
            grid_keep,
            ground_dist,
            enc_norm,
            enc_query,
            enc_key,
            enc_value,
            enc_proj,
            enc_norm2,
            enc_up,
            enc_down,
            embed_proj,
            mask_token,
            dec_norm,
            dec_query,
            dec_key,
            dec_value,
            dec_proj,
            dec_norm2,
            dec_up,
            dec_down,
            pred_proj,
            cotangent,
        )
    enc_weights = (enc_norm, enc_query, enc_key, enc_value, enc_proj, enc_norm2, enc_up, enc_down)
    dec_weights = (dec_norm, dec_query, dec_key, dec_value, dec_proj, dec_norm2, dec_up, dec_down)
    arrived, *saved = encode(tokens, lengths, enc_weights, embed_proj)
    decoded, grads = decode_and_back(
        arrived,
        grid_order,
        grid_keep,
        ground_dist,
        dec_weights,
        mask_token,
        pred_proj,
        cotangent,
        tokens,
        enc_weights,
        saved,
        embed_proj,
    )
    (
        grad_tokens,
        g_query,
        g_key,
        g_value,
        g_up,
        g_out,
        g_down,
        g_embed,
        n_enc_attn,
        n_enc_mlp,
        n_dec_attn,
        n_dec_mlp,
        n_mask,
        *dec_grads,
    ) = grads
    return (
        decoded,
        grad_tokens.reshape(tokens.shape),
        n_enc_attn[0],
        g_query,
        g_key,
        g_value,
        g_out,
        n_enc_mlp[0],
        g_up,
        g_down,
        g_embed,
        n_mask[0],
        n_dec_attn[0],
        dec_grads[0],
        dec_grads[1],
        dec_grads[2],
        dec_grads[3],
        n_dec_mlp[0],
        dec_grads[4],
        dec_grads[5],
        dec_grads[6],
    )


def solution(mesh):
    return jax.shard_map(
        per_device,
        mesh=mesh,
        in_specs=(
            P(("dp", "mp"), None, None),
            P("dp"),
            P(("dp", "mp"), None),
            P(("dp", "mp"), None),
            P(("dp", "mp")),
            P(),
            P(None, "mp"),
            P(None, "mp"),
            P(None, "mp"),
            P("mp", None),
            P(),
            P(None, "mp"),
            P("mp", None),
            P(None, "mp"),
            P(),
            P(),
            P(),
            P(),
            P(),
            P(),
            P(),
            P(),
            P(),
            P(),
            P(("dp", "mp"), None, None),
        ),
        out_specs=(
            P(("dp", "mp"), None, None),
            P(("dp", "mp"), None, None),
            P(),
            P("dp", "mp"),
            P("dp", "mp"),
            P("dp", "mp"),
            P("mp", "dp"),
            P(),
            P("dp", "mp"),
            P("mp", "dp"),
            P("dp", "mp"),
            P(),
            P(),
            P("dp", "mp"),
            P("dp", "mp"),
            P("dp", "mp"),
            P("dp", "mp"),
            P(),
            P("dp", "mp"),
            P("dp", "mp"),
            P("dp", "mp"),
        ),
        check_vma=False,
    )
```

```python
import math

import jax
import jax.numpy as jnp
from jax import lax
from jax.experimental import pallas as pl
from jax.experimental.pallas import tpu as pltpu
from jax.sharding import PartitionSpec as P

HE = 16
HD = 16
SIDE = 16
IPD = 1


eps_norm = 1e-06
masked_score = -1e30
low_type = jnp.bfloat16
full_type = jnp.float32


MESH = pl.DeviceIdType.MESH
LANES = 128


def log2_of(count):
    bits = count.bit_length() - 1
    assert 1 << bits == count
    return bits


def spot_of(data, model, stages):
    out = 0
    for axis, bit in stages:
        out = out * 2 + (((data if axis == "dp" else model) >> bit) & 1)
    return out


def partner(axis, bit):
    dp, mp = lax.axis_index("dp"), lax.axis_index("mp")
    step = 1 << bit
    if axis == "dp":
        return (dp ^ step, mp), (dp >> bit) & 1
    return (dp, mp ^ step), (mp >> bit) & 1


def enter_barrier(partners):
    barrier = pltpu.get_barrier_semaphore()
    for peer in partners:
        pl.semaphore_signal(barrier, inc=1, device_id=peer, device_id_type=MESH)
    pl.semaphore_wait(barrier, len(partners))


class HalvingSum:
    def __init__(self, stages, buffers, window, send_sems, recv_sems):
        self.stages, self.buffers, self.window = stages, buffers, window
        self.send_sems, self.recv_sems = send_sems, recv_sems

    def view(self, index, start, size):
        return self.buffers[index].at[(pl.ds(start, size),) + self.window]

    def copy(self, index):
        peer, mine = partner(*self.stages[index])
        half = self.buffers[index].shape[0] // 2
        return pltpu.make_async_remote_copy(
            src_ref=self.view(index, (1 - mine) * half, half),
            dst_ref=self.view(index + 1, 0, half),
            send_sem=self.send_sems.at[index],
            recv_sem=self.recv_sems.at[index],
            device_id=peer,
            device_id_type=MESH,
        )

    def start(self, index):
        self.copy(index).start()

    def finish(self, index):
        self.copy(index).wait()
        peer, mine = partner(*self.stages[index])
        half = self.buffers[index].shape[0] // 2

        def one(position, carry):
            there = self.buffers[index + 1].at[(position,) + self.window]
            here = self.buffers[index].at[(mine * half + position,) + self.window]
            there[...] = there[...] + here[...]
            return carry

        lax.fori_loop(0, half, one, 0)


def dec_pieces(data_count, model_count, shapes):
    offset, pieces = 0, []
    for rows, columns in shapes:
        height, width = rows // data_count, columns // model_count
        tiles = -(-width // LANES)
        pieces.append((offset, height, width, tiles))
        offset += height * tiles
    return pieces, offset


LOG2E = 1.4426950408889634


def dot_as(left, right, left_dim, right_dim):
    return lax.dot_general(
        left, right, (((left_dim,), (right_dim,)), ((), ())), preferred_element_type=full_type
    )


def norm_parts(values):
    center = values - jnp.mean(values, axis=-1, keepdims=True)
    scale = lax.rsqrt(jnp.mean(center * center, axis=-1, keepdims=True) + eps_norm)
    return center * scale, scale


def norm_back(normed, scale, grad_scaled):
    first = jnp.mean(grad_scaled, axis=-1, keepdims=True)
    second = jnp.mean(grad_scaled * normed, axis=-1, keepdims=True)
    return (grad_scaled - first - normed * second) * scale


def gelu_pair(values):
    below = 0.5 + 0.5 * lax.erf(values * (0.5**0.5))
    density = jnp.exp2(values * values * (-0.5 * LOG2E)) * ((2.0 * math.pi) ** -0.5)
    return values * below, below + values * density


def low_bit(mask):
    return (mask & -mask).bit_length() - 1


def visit_order(count):
    return sorted(range(count), key=lambda mask: (mask.bit_length(), -mask))


def visit_mask(step, count):
    mask = jnp.int32(0)
    for position, value in enumerate(visit_order(count)):
        mask = jnp.where(step == position, value, mask)
    return mask


class Gather:
    def __init__(self, own, slot_view, send_sems, recv_sems):
        self.own, self.slot_view = own, slot_view
        self.send_sems, self.recv_sems = send_sems, recv_sems
        self.count = lax.axis_size("mp")
        self.index = lax.axis_index("mp")

    def copy(self, mask):
        bit = low_bit(mask)
        carried = mask ^ (1 << bit)
        place = self.slot_view(self.index ^ carried)
        return pltpu.make_async_remote_copy(
            src_ref=self.own if carried == 0 and self.own is not None else place,
            dst_ref=place,
            send_sem=self.send_sems.at[mask],
            recv_sem=self.recv_sems.at[mask],
            device_id=partner("mp", bit)[0],
            device_id_type=MESH,
        )

    def start(self):
        for bit in reversed(range(log2_of(self.count))):
            self.copy(1 << bit).start()

    def arrive(self, mask):
        self.copy(mask).wait_recv()
        for bit in reversed(range(low_bit(mask))):
            self.copy(mask | (1 << bit)).start()

    def arrive_group(self, length):
        group = [mask for mask in range(1, self.count) if mask.bit_length() == length]
        for mask in sorted(group, key=lambda one: -low_bit(one)):
            self.arrive(mask)

    def arrive_all(self):
        for length in range(1, log2_of(self.count) + 1):
            self.arrive_group(length)

    def arrive_at(self, step):
        for length in range(1, log2_of(self.count) + 1):
            @pl.when(step == 1 << (length - 1))
            def _():
                self.arrive_group(length)

    def drain(self):
        for mask in range(1, self.count):
            self.copy(mask).wait_send()


class Scatter:
    def __init__(self, parts, total, landing, send_sems, recv_sems):
        self.parts, self.total, self.landing = parts, total, landing
        self.send_sems, self.recv_sems = send_sems, recv_sems
        self.count = lax.axis_size("mp")
        self.index = lax.axis_index("mp")

    def copy(self, mask):
        return pltpu.make_async_remote_copy(
            src_ref=self.parts.at[mask - 1],
            dst_ref=self.landing.at[mask - 1],
            send_sem=self.send_sems.at[mask],
            recv_sem=self.recv_sems.at[mask],
            device_id=partner("mp", low_bit(mask))[0],
            device_id_type=MESH,
        )

    def put(self, mask, product):
        @pl.when(mask == 0)
        def _():
            self.total[...] = self.total[...] + product

        @pl.when(mask != 0)
        def _():
            self.parts[mask - 1] = product.astype(low_type)

        for odd in range(1, self.count, 2):
            @pl.when(mask == odd)
            def _():
                self.copy(odd).start()

    def finish_bit(self, bit):
        step = 1 << bit
        masks = [mask for mask in range(1, self.count) if low_bit(mask) == bit]
        for mask in reversed(masks):
            self.copy(mask).wait_recv()
            rest = mask ^ step
            if rest:
                self.parts[rest - 1] = self.parts[rest - 1] + self.landing[mask - 1]
                if low_bit(rest) == bit + 1:
                    self.copy(rest).start()
            else:
                self.total[...] = self.total[...] + self.landing[mask - 1].astype(full_type)

    def drain(self):
        for mask in range(1, self.count):
            self.copy(mask).wait_send()


def exchange_partners(images):
    data_count, model_count = lax.axis_size("dp"), lax.axis_size("mp")
    data, model = lax.axis_index("dp"), lax.axis_index("mp")
    out = []
    for image in range(images):
        spot = (model * images + image) * data_count + data
        device = spot // images
        out.append((device // model_count, device % model_count, spot % images))
    return out


def is_here(peer):
    return (peer[0] == lax.axis_index("dp")) & (peer[1] == lax.axis_index("mp"))


class Exchange:
    def __init__(self, images, source, target, send_sems, recv_sems):
        self.partners = exchange_partners(images)
        self.source, self.target = source, target
        self.send_sems, self.recv_sems = send_sems, recv_sems

    def copy(self, image):
        data, model, slot = self.partners[image]
        return pltpu.make_async_remote_copy(
            src_ref=self.source.at[image],
            dst_ref=self.target.at[slot],
            send_sem=self.send_sems.at[image],
            recv_sem=self.recv_sems.at[slot],
            device_id=(data, model),
            device_id_type=MESH,
        )

    def start(self):
        for image, (data, model, slot) in enumerate(self.partners):
            here = is_here((data, model))

            @pl.when(here)
            def _():
                self.target[slot] = self.source[image]

            @pl.when(jnp.logical_not(here))
            def _():
                self.copy(image).start()

    def finish(self):
        for image, (data, model, slot) in enumerate(self.partners):
            @pl.when(jnp.logical_not(is_here((data, model))))
            def _():
                pltpu.make_async_remote_copy(
                    src_ref=self.source.at[image],
                    dst_ref=self.target.at[image],
                    send_sem=self.send_sems.at[image],
                    recv_sem=self.recv_sems.at[image],
                    device_id=(data, model),
                    device_id_type=MESH,
                ).wait()


class Move:
    def __init__(self, source, target, sem):
        self.copy = pltpu.make_async_copy(source, target, sem)
        self.copy.start()

    def wait(self):
        if self.copy is not None:
            self.copy.wait()
            self.copy = None


def encoder_barrier(images, axes):
    barrier = pltpu.get_barrier_semaphore()
    count = images
    for axis in axes:
        for bit in range(log2_of(lax.axis_size(axis))):
            count += 1
            pl.semaphore_signal(
                barrier, inc=1, device_id=partner(axis, bit)[0], device_id_type=MESH
            )
    for data, model, slot in exchange_partners(images):
        pl.semaphore_signal(barrier, inc=1, device_id=(data, model), device_id_type=MESH)
    pl.semaphore_wait(barrier, count)


def encoder_kernel(images, visible, heads, *refs):
    (
        lengths,
        tokens,
        gain_attn,
        w_query_hbm,
        w_key_hbm,
        w_value_hbm,
        w_out,
        gain_mlp,
        w_up_hbm,
        w_down_hbm,
        w_embed,
        arrived,
        *saved_hbm,
    ) = refs[:24]
    (
        w_query,
        w_key,
        w_value,
        w_up,
        w_down,
        a_s,
        qkv_s,
        e_s,
        inv_s,
        o_own,
        c_s,
        g_s,
        slope_s,
        mid_s,
        low_s,
        embed_full,
        qkv_weights,
        move_sems,
        token_slots,
        out_full,
        o_full,
        embed_slots,
        parts,
        landing,
        total,
        embedded,
        sems,
        swap_sems,
    ) = refs[24:]
    count = lax.axis_size("mp")
    index = lax.axis_index("mp")
    block_rows = images * visible
    columns = w_query.shape[1]
    size = columns // heads
    scaling = float(size) ** -0.5
    hidden = w_up.shape[1]
    chunk = 512

    loads = [
        Move(source, target, move_sems.at[position])
        for position, (source, target) in enumerate(
            (
                (w_query_hbm, w_query),
                (w_key_hbm, w_key),
                (w_value_hbm, w_value),
                (w_up_hbm, w_up),
                (w_down_hbm, w_down),
            )
        )
    ]
    saved = [a_s, qkv_s, e_s, inv_s, o_own, c_s, g_s, slope_s, mid_s, low_s, embed_full, qkv_weights]
    stores = []

    def save(*arrays):
        for array in arrays:
            position = [array is one for one in saved].index(True)
            stores.append(Move(array, saved_hbm[position], move_sems.at[len(loads) + position]))

    encoder_barrier(images, ["mp"])
    token_gather = Gather(
        tokens, lambda slot: token_slots.at[slot], sems.at[0], sems.at[1]
    )
    out_gather = Gather(
        w_out,
        lambda slot: out_full.at[pl.ds(pl.multiple_of(slot * columns, columns), columns)],
        sems.at[2],
        sems.at[3],
    )
    o_gather = Gather(
        o_own,
        lambda slot: o_full.at[pl.ds(pl.multiple_of(slot * columns, columns), columns)],
        sems.at[4],
        sems.at[5],
    )
    embed_gather = Gather(w_embed, lambda slot: embed_slots.at[slot], sems.at[6], sems.at[7])
    scatter = Scatter(parts, total, landing, sems.at[8], sems.at[9])
    swap = Exchange(images, embedded, arrived, swap_sems.at[0], swap_sems.at[1])

    token_gather.start()
    out_gather.start()
    token_slots[index] = tokens[...]
    out_full[pl.ds(pl.multiple_of(index * columns, columns), columns), :] = w_out[...]
    embed_slots[index] = w_embed[...]
    for position, weight in enumerate((w_query, w_key, w_value)):
        loads[position].wait()
        qkv_weights[position * columns : (position + 1) * columns, :] = weight[...].T
    save(qkv_weights)

    def rows_of(slot):
        return pl.ds(pl.multiple_of(slot * block_rows, block_rows), block_rows)

    def attend(step, carry):
        token_gather.arrive_at(step)

        slot = index ^ visit_mask(step, count)
        rows = rows_of(slot)
        normed, scale = norm_parts(token_slots[slot].astype(full_type))
        a_s[rows, :] = (normed * gain_attn[...]).astype(low_type)
        for position in range(3):
            span = slice(position * columns, (position + 1) * columns)
            part = dot_as(qkv_weights[span, :], a_s[rows, :], 1, 1)
            if position == 0:
                part = part * (scaling * LOG2E)
            qkv_s[span, rows] = part.astype(low_type)
        key_row = lax.broadcasted_iota(jnp.int32, (block_rows, block_rows), 0)
        query_row = lax.broadcasted_iota(jnp.int32, (block_rows, block_rows), 1)
        valid = jnp.zeros((block_rows, block_rows), jnp.bool_)
        for image in range(images):
            first = image * visible
            keys = (key_row >= first) & (key_row < first + lengths[slot * images + image])
            valid = valid | (keys & (query_row >= first) & (query_row < first + visible))
        for head in range(heads):
            span = slice(head * size, (head + 1) * size)
            query = qkv_s[span, rows]
            key = qkv_s[columns + head * size : columns + (head + 1) * size, rows]
            value = qkv_s[2 * columns + head * size : 2 * columns + (head + 1) * size, rows]
            scores = jnp.where(valid, dot_as(key, query, 0, 0), masked_score)
            weights = jnp.exp2(scores - jnp.max(scores, axis=0, keepdims=True))
            inverse = 1.0 / jnp.sum(weights, axis=0, keepdims=True)
            weights = weights.astype(low_type)
            e_s[slot * heads + head] = weights
            inv_s[slot * heads + head] = inverse
            mixed = jnp.dot(value, weights, preferred_element_type=full_type)
            o_own[span, rows] = (mixed * inverse).astype(low_type)
        return carry

    lax.fori_loop(0, count, attend, 0)
    o_gather.start()
    embed_gather.start()
    save(a_s, qkv_s, e_s, inv_s, o_own)
    for move in loads:
        move.wait()
    o_full[pl.ds(pl.multiple_of(index * columns, columns), columns), :] = o_own[...]
    out_gather.arrive_all()
    o_gather.arrive_all()
    total[...] = jnp.zeros_like(total)

    def expand(step, carry):
        mask = count - 1 - step
        slot = index ^ mask
        rows = rows_of(slot)
        middle = token_slots[slot].astype(full_type) + dot_as(o_full[:, rows], out_full[...], 0, 0)

        @pl.when(mask == 0)
        def _():
            mid_s[...] = middle

        normed, scale = norm_parts(middle)
        c_s[rows, :] = (normed * gain_mlp[...]).astype(low_type)
        for first in range(0, hidden, chunk):
            cols = slice(first, first + chunk)
            pre = jnp.dot(c_s[rows, :], w_up[:, cols], preferred_element_type=full_type)
            active, slope = gelu_pair(pre)
            g_s[rows, cols] = active.astype(low_type)
            slope_s[rows, cols] = slope.astype(low_type)
        scatter.put(
            mask, jnp.dot(g_s[rows, :], w_down[...], preferred_element_type=full_type)
        )
        return carry

    lax.fori_loop(0, count, expand, 0)
    save(c_s, g_s, slope_s, mid_s)
    bits = log2_of(count)
    for bit in range(bits):
        if bit == bits - 1:
            embed_gather.arrive_all()
            width = w_embed.shape[1]
            for slot in range(count):
                embed_full[:, slot * width : (slot + 1) * width] = embed_slots[slot]
        scatter.finish_bit(bit)
    low_s[...] = (mid_s[...] + total[...]).astype(low_type)
    out = jnp.dot(low_s[...], embed_full[...], preferred_element_type=full_type)
    embedded[...] = out.astype(low_type).reshape(embedded.shape)
    swap.start()
    save(embed_full, low_s)
    for one in (token_gather, out_gather, o_gather, embed_gather, scatter):
        one.drain()
    for move in stores:
        move.wait()
    swap.finish()


def encode(tokens, lengths, weights, embed_proj):
    gain_attn, w_query, w_key, w_value, w_out, gain_mlp, w_up, w_down = weights
    model_count = lax.axis_size("mp")
    images, visible, width = tokens.shape
    rows = images * visible
    heads = HE // model_count
    columns, hidden = w_query.shape[1], w_up.shape[1]
    out_width = embed_proj.shape[1] * model_count
    every = rows * model_count

    def kernel(*refs):
        encoder_kernel(images, visible, heads, *refs)

    vmem = pl.BlockSpec(memory_space=pltpu.VMEM)
    hbm = pl.BlockSpec(memory_space=pl.ANY)
    shapes = [
        ((images, visible, out_width), low_type),
        ((every, width), low_type),
        ((3 * columns, every), low_type),
        ((model_count * heads, rows, rows), low_type),
        ((model_count * heads, 1, rows), full_type),
        ((columns, every), low_type),
        ((every, width), low_type),
        ((every, hidden), low_type),
        ((every, hidden), low_type),
        ((rows, width), full_type),
        ((rows, width), low_type),
        ((width, out_width), low_type),
        ((3 * columns, width), low_type),
    ]
    return pl.pallas_call(
        kernel,
        out_shape=[jax.ShapeDtypeStruct(shape, kind) for shape, kind in shapes],
        in_specs=[pl.BlockSpec(memory_space=pltpu.SMEM)]
        + [vmem] * 2
        + [hbm] * 3
        + [vmem] * 2
        + [hbm] * 2
        + [vmem],
        out_specs=[vmem] + [hbm] * (len(shapes) - 1),
        scratch_shapes=[
            pltpu.VMEM((width, columns), low_type),
            pltpu.VMEM((width, columns), low_type),
            pltpu.VMEM((width, columns), low_type),
            pltpu.VMEM((width, hidden), low_type),
            pltpu.VMEM((hidden, width), low_type),
        ]
        + [pltpu.VMEM(shape, kind) for shape, kind in shapes[1:]]
        + [
            pltpu.SemaphoreType.DMA((5 + len(shapes),)),
            pltpu.VMEM((model_count, rows, width), low_type),
            pltpu.VMEM((width, width), low_type),
            pltpu.VMEM((width, every), low_type),
            pltpu.VMEM((model_count,) + embed_proj.shape, low_type),
            pltpu.VMEM((model_count - 1, rows, width), low_type),
            pltpu.VMEM((model_count - 1, rows, width), low_type),
            pltpu.VMEM((rows, width), full_type),
            pltpu.VMEM((images, visible, out_width), low_type),
            pltpu.SemaphoreType.DMA((10, model_count)),
            pltpu.SemaphoreType.DMA((2, images)),
        ],
        compiler_params=pltpu.CompilerParams(
            collective_id=1, has_side_effects=True, vmem_limit_bytes=60 * 2**20
        ),
    )(
        lengths,
        tokens.reshape(rows, width),
        gain_attn.reshape(1, -1),
        w_query,
        w_key,
        w_value,
        w_out,
        gain_mlp.reshape(1, -1),
        w_up,
        w_down,
        embed_proj,
    )


EARLY_DOWN, EARLY_UP, UP_FIRST = True, False, True
SUM_ORDERS = {
    "attn": ["crossed"],
    "dup": ["spread", "spreadz", "all", "spreadz"],
    "ddn": ["spread", "spread", "spread", "spread"],
    "pred": ["all"],
    "emb": ["spread", "spread"],
    "dn": ["Z", "Y", "Y", "Y"],
    "up": ["Y", "Y", "Y", "Y"],
    "oq": ["Y", "Y", "Y", "Y"],
}
PLAN = {
    "a3": [
        "pred0",
        "ddn0",
        "ddn1",
        "ddn2",
        "ddn3",
        "dup0",
        "dup1",
        "dup2",
        "dup3",
    ],
    "a4": [
        "ddn0",
        "dup1",
        "pred0",
        "ddn1",
    ],
    "a5": [
        "dup3",
        "dup2",
        "ddn2",
        "attn0",
        "ddn0",
        "ddn3",
    ],
    "f1": [
        "ddn1",
        "dup1",
        "emb0",
        "emb1",
        "dup0",
    ],
    "f2": [
        "pred0",
        "ddn2",
        "dup3",
    ],
    "f3": [
        "dup2",
        "ddn3",
    ],
    "b0": [
        "ddn0",
        "dup1",
        "ddn1",
        "dup0",
        "emb0",
        "pred0",
        "dup2",
        "ddn2",
        "emb1",
        "dup3",
        "ddn3",
    ],
    "s2": [
        "attn0",
        "ddn0",
        "dup1",
    ],
    "s3": [
        "ddn1",
        "ddn2",
        "dup3",
    ],
    "b2": [
        "ddn3",
        "dn0",
        "dn1",
    ],
    "b4": [
        "dup0",
        "emb0",
        "pred0",
    ],
    "b5": [
        "dup2",
        "emb1",
        "dn2",
        "dup0",
    ],
    "t2": [
        "attn0",
        "dn3",
        "dn1",
        "dn0",
        "up0",
    ],
    "b6": [
        "emb0",
        "emb1",
        "dn2",
    ],
    "b7": [
        "up1",
    ],
    "tail": [
        "dn3",
        "attn0",
        "up2",
        "dn1",
        "emb0",
        "up0",
        "emb1",
        "norm",
        "up3",
        "dn2",
        "up1",
        "norm",
        "dn0",
        "dn3",
        "up2",
        "o",
        "up0",
        "up3",
        "q",
        "up1",
        "up2",
        "o",
        "k",
        "up3",
        "q",
        "v",
        "o",
        "k",
        "attn0",
        "norm",
        "q",
        "v",
        "norm",
        "k",
        "v",
        "norm",
    ],
}


class Bulk:
    def __init__(self, one):
        self.one, self.stage = one, None

    def start(self):
        self.one.start(0)
        self.stage = 0

    def done(self):
        return self.stage == len(self.one.stages)

    def advance(self):
        if self.stage is None or self.done():
            return
        self.one.finish(self.stage)
        self.stage += 1
        if not self.done():
            self.one.start(self.stage)


def back_kernel(plan, *refs):
    images, visible, enc_heads, heads, side, pieces, embed_piece, scopes = plan
    refs = list(refs)

    def take(number):
        head = refs[:number]
        del refs[:number]
        return head

    (
        dist_ref,
        arrived,
        order_ref,
        keep_ref,
        dec_gain_attn,
        dec_gain_mlp,
        mask_token,
        tokens,
        gain_attn,
        gain_mlp,
    ) = take(10)
    dec_hbm = take(8)
    enc_hbm = take(15)
    decoded, grad_tokens, norm_wide, norm_thin, rows_out, cols_out, dec_out, embed_out = take(8)
    move_sems, decoded_sems = take(2)
    grad_arrived, dec_packed, small = take(3)
    demb_own, demb_slots, db_s, total = take(4)
    parts_mlp, landing_mlp, parts_attn, landing_attn = take(4)
    sems, swap_sems = take(2)
    data_count, model_count = lax.axis_size("dp"), lax.axis_size("mp")
    data_bits, model_bits = log2_of(data_count), log2_of(model_count)
    row_packed, col_packed, embed_packed = take(3)
    row_bufs = [row_packed] + take(data_bits)
    col_bufs = [col_packed] + take(data_bits)
    dec_bufs = [dec_packed] + take(data_bits + model_bits)
    embed_bufs = [embed_packed] + take(data_bits + model_bits)
    wide_acc, wide_got, thin_acc, thin_got = take(4)
    row_sems, col_sems, dec_sems, embed_sems, norm_sems = take(5)
    assert not refs

    index = lax.axis_index("mp")
    count = model_count
    enc_stages = [("dp", bit) for bit in range(data_bits)]
    late_stages = enc_stages[1:] + enc_stages[:1]
    model_stages = [("mp", bit) for bit in range(model_bits)]
    all_stages = model_stages + enc_stages
    near, far = model_stages[:1], model_stages[1:]
    orders = {
        "Y": enc_stages,
        "Z": late_stages,
        "all": all_stages,
        "crossed": model_stages + late_stages,
        "spread": near + enc_stages + far,
        "spreadz": near + late_stages + far,
    }
    sums = {}

    def pump(point):
        for name in PLAN.get(point, ()):
            if name in sums:
                sums[name].advance()

    def pump_at(step, point):
        for turn in range(count):
            if PLAN.get(point + str(turn)):
                @pl.when(step == turn)
                def _():
                    pump(point + str(turn))

    chunk = 512

    def bulk(stages, bufs, axis, first, extent, pair, cut):
        window = [slice(None), slice(None)]
        window[axis - 1] = pl.ds(first, extent)
        return Bulk(HalvingSum(stages, bufs, tuple(window), pair.at[0, cut], pair.at[1, cut]))

    limits = [pieces[0][0]] + [piece[0] for piece in pieces[4:]] + [dec_packed.shape[1]]
    dec_rows = []
    for kind, first, last in zip(("attn", "dup", "ddn", "pred"), limits, limits[1:]):
        names = SUM_ORDERS[kind]
        extent = (last - first) // len(names)
        for cut, order in enumerate(names):
            begin = first + cut * extent
            sums[kind + str(cut)] = bulk(
                orders[order], dec_bufs, 1, begin, extent, dec_sems, len(dec_rows)
            )
            dec_rows.append((begin, begin + extent, orders[order]))

    def start(kind):
        for cut in range(len(SUM_ORDERS[kind])):
            sums[kind + str(cut)].start()

    def store_dec(which, product):
        offset, height, span, tiles = pieces[which]
        for column in range(model_count):
            for tile in range(tiles):
                lanes = min(LANES, span - tile * LANES)
                first = column * span + tile * LANES
                block = product[:, first : first + lanes].astype(low_type)
                base = offset + tile * height
                for begin, end, order in dec_rows:
                    low_row, high_row = max(begin, base), min(end, base + height)
                    if low_row >= high_row:
                        continue
                    for row in range(data_count):
                        shift = row * height - base
                        dec_packed[spot_of(row, column, order), low_row:high_row, :lanes] = block[
                            low_row + shift : high_row + shift, :
                        ]

    swap = Exchange(images, grad_arrived, demb_own, swap_sems.at[0], swap_sems.at[1])

    def decoder(
        w_out,
        xs,
        qkv_weights,
        a_s,
        qkv_s,
        e_s,
        inv_s,
        o_s,
        dy_s,
        db_dec,
        do_s,
    ):
        length = side * side
        width = w_out.shape[0]
        size = width // heads
        scaling = float(size) ** -0.5
        place = lax.broadcasted_iota(jnp.int32, (length, visible), 0)
        turn = lax.broadcasted_iota(jnp.int32, (length, visible), 1)
        out_move = Move(dec_hbm[3], w_out, move_sems.at[3])

        def turned(*inputs):
            turned_moves = [
                Move(dec_hbm[position], one, move_sems.at[position])
                for position, one in enumerate(inputs)
            ]
            encoder_barrier(images, ["mp", "dp"])
            for position, one in enumerate(inputs):
                turned_moves[position].wait()
                qkv_weights[position * width : (position + 1) * width, :] = one[...].T

        pl.run_scoped(turned, *scopes[3])

        def picks(image):
            order = jnp.zeros((1, visible), jnp.int32)
            flags = jnp.zeros((1, length), jnp.int32)
            for one in range(images):
                order = jnp.where(image == one, order_ref[one : one + 1, :visible], order)
                flags = jnp.where(image == one, keep_ref[one : one + 1, :], flags)
            kept = jnp.sum(flags, axis=1, keepdims=True)
            return jnp.where((order == place) & (turn < kept), 1.0, 0.0)

        def rows_of(image):
            if isinstance(image, int):
                return slice(image * length, (image + 1) * length)
            return pl.ds(pl.multiple_of(image * length, length), length)

        def dense(w_up, w_down, w_pred, cotangent, mid_s, c_s, g_s, du_s, low_s, dm_s, staged):
            hidden = w_up.shape[1]
            second_moves = [
                Move(source, target, move_sems.at[4 + position])
                for position, (source, target) in enumerate(
                    zip(dec_hbm[4:], (w_up, w_down, w_pred, cotangent))
                )
            ]
            out_move.wait()
            for move in second_moves:
                move.wait()
            small[...] = jnp.zeros_like(small)

            def stage_copy(image):
                return pltpu.make_async_copy(staged, decoded.at[image], decoded_sems.at[image])

            def one_image(image, carry):
                rows = rows_of(image)
                pick = picks(image)
                hidden_rows = 1.0 - jnp.sum(pick, axis=1, keepdims=True)
                quarter = width // 4
                lane = lax.broadcasted_iota(jnp.int32, (side, quarter), 1).astype(full_type)
                line = lax.broadcasted_iota(jnp.int32, (side, quarter), 0).astype(full_type)
                angle = dist_ref[image] * line * jnp.exp(lane * (-math.log(10000.0) / quarter))
                table = jnp.concatenate([jnp.sin(angle), jnp.cos(angle)], axis=1)
                by_row = jnp.broadcast_to(table[:, None, :], (side, side, 2 * quarter))
                by_col = jnp.broadcast_to(table[None, :, :], (side, side, 2 * quarter))
                codes = jnp.concatenate(
                    [by_row.reshape(length, 2 * quarter), by_col.reshape(length, 2 * quarter)],
                    axis=1,
                )
                start = jnp.dot(
                    pick.astype(low_type), arrived[image], preferred_element_type=full_type
                )
                start = start + hidden_rows * mask_token[...] + codes
                xs[rows, :] = start
                normed, scale = norm_parts(start)
                a_s[rows, :] = (normed * dec_gain_attn[...]).astype(low_type)
                for position in range(3):
                    span = slice(position * width, (position + 1) * width)
                    part = dot_as(qkv_weights[span, :], a_s[rows, :], 1, 1)
                    if position == 0:
                        part = part * (scaling * LOG2E)
                    qkv_s[span, rows] = part.astype(low_type)

                def one_head(head, inner):
                    span = pl.multiple_of(head * size, size)
                    query = qkv_s[pl.ds(span, size), rows]
                    key = qkv_s[pl.ds(width + span, size), rows]
                    value = qkv_s[pl.ds(2 * width + span, size), rows]
                    scores = dot_as(key, query, 0, 0)
                    weights = jnp.exp2(scores - jnp.max(scores, axis=0, keepdims=True))
                    inverse = 1.0 / jnp.sum(weights, axis=0, keepdims=True)
                    weights = weights.astype(low_type)
                    e_s[image * heads + head] = weights
                    inv_s[image * heads + head] = inverse
                    mixed = jnp.dot(value, weights, preferred_element_type=full_type)
                    o_s[pl.ds(span, size), rows] = (mixed * inverse).astype(low_type)
                    return inner

                lax.fori_loop(0, heads, one_head, 0, unroll=heads)

                middle = start + dot_as(o_s[:, rows], w_out[...], 0, 0)
                mid_s[...] = middle
                normed, scale = norm_parts(middle)
                c_s[rows, :] = (normed * dec_gain_mlp[...]).astype(low_type)
                for first in range(0, hidden, chunk):
                    cols = slice(first, first + chunk)
                    pre = jnp.dot(c_s[rows, :], w_up[:, cols], preferred_element_type=full_type)
                    active, slope = gelu_pair(pre)
                    g_s[rows, cols] = active.astype(low_type)
                    du_s[rows, cols] = slope.astype(low_type)
                outputs = middle + jnp.dot(
                    g_s[rows, :], w_down[...], preferred_element_type=full_type
                )
                low_s[rows, :] = outputs.astype(low_type)

                @pl.when(image > 0)
                def _():
                    stage_copy(image - 1).wait()

                staged[...] = jnp.dot(
                    low_s[rows, :], w_pred[...], preferred_element_type=full_type
                )
                stage_copy(image).start()

                grad_out = dot_as(cotangent[image], w_pred[...], 1, 1)
                dm_s[rows, :] = grad_out.astype(low_type)
                for first in range(0, hidden, chunk):
                    cols = slice(first, first + chunk)
                    grad_active = dot_as(dm_s[rows, :], w_down[cols, :], 1, 1)
                    du_s[rows, cols] = (grad_active * du_s[rows, cols].astype(full_type)).astype(
                        low_type
                    )
                grad_second = dot_as(du_s[rows, :], w_up[...], 1, 1)
                normed, scale = norm_parts(mid_s[...])
                small[1:2, :] += jnp.sum(grad_second * normed, axis=0, keepdims=True)
                grad_middle = grad_out + norm_back(
                    normed, scale, grad_second * dec_gain_mlp[...]
                )
                dy_s[rows, :] = grad_middle
                db_dec[rows, :] = grad_middle.astype(low_type)
                return carry

            lax.fori_loop(0, images, one_image, 0)
            all_pixels = cotangent[...].reshape(-1, cotangent.shape[2])
            store_dec(6, dot_as(low_s[...], all_pixels, 0, 0))
            start("pred")
            store_dec(5, dot_as(g_s[...], dm_s[...], 0, 0))
            start("ddn")
            pump("a1")
            store_dec(4, dot_as(c_s[...], du_s[...], 0, 0))
            start("dup")
            pump("a2")
            stage_copy(images - 1).wait()

        pl.run_scoped(dense, *scopes[1])

        for image in range(images):
            rows = rows_of(image)
            do_s[...] = dot_as(w_out[...], db_dec[rows, :], 1, 1)

            def back_head(head, inner):
                span = pl.multiple_of(head * size, size)
                query = qkv_s[pl.ds(span, size), rows]
                key = qkv_s[pl.ds(width + span, size), rows]
                value = qkv_s[pl.ds(2 * width + span, size), rows]
                weights = e_s[image * heads + head]
                grad_full = do_s[pl.ds(span, size), :] * (inv_s[image * heads + head] * scaling)
                mixed = o_s[pl.ds(span, size), rows].astype(full_type)
                shift = jnp.sum(grad_full * mixed, axis=0, keepdims=True)
                grad_low = grad_full.astype(low_type)
                grad_probs = dot_as(value, grad_low, 0, 0)
                grad_scores = (weights.astype(full_type) * (grad_probs - shift)).astype(low_type)
                grad_value = dot_as(grad_low, weights, 1, 1) * (1.0 / scaling)
                grad_query = jnp.dot(key, grad_scores, preferred_element_type=full_type)
                grad_key = dot_as(query, grad_scores, 1, 1) * (1.0 / (scaling * LOG2E))
                qkv_s[pl.ds(span, size), rows] = grad_query.astype(low_type)
                qkv_s[pl.ds(width + span, size), rows] = grad_key.astype(low_type)
                qkv_s[pl.ds(2 * width + span, size), rows] = grad_value.astype(low_type)
                return inner

            lax.fori_loop(0, heads, back_head, 0, unroll=heads)

            grad_normed = dot_as(qkv_s[:, rows], qkv_weights[...], 0, 0)
            normed, scale = norm_parts(xs[rows, :])
            small[0:1, :] += jnp.sum(grad_normed * normed, axis=0, keepdims=True)
            grad_start = dy_s[rows, :] + norm_back(
                normed, scale, grad_normed * dec_gain_attn[...]
            )
            pick = picks(image)
            hidden_rows = 1.0 - jnp.sum(pick, axis=1, keepdims=True)
            small[2:3, :] += jnp.sum(hidden_rows * grad_start, axis=0, keepdims=True)
            grad_arrived[image] = dot_as(
                pick.astype(low_type), grad_start.astype(low_type), 0, 0
            ).astype(low_type)
            if image == 0:
                pump("a3")
        swap.start()
        for position in range(3):
            grads = qkv_s[position * width : (position + 1) * width, :]
            store_dec(position, dot_as(a_s[...], grads, 0, 1))
        store_dec(3, jnp.dot(o_s[...], db_dec[...], preferred_element_type=full_type))
        start("attn")
        pump("a4")

    pl.run_scoped(decoder, *scopes[0])
    thin_acc[0] = small[...]

    def encoder(*local):
        local = list(local)
        loaded = local[:15]
        (
            w_out,
            w_up,
            w_down,
            a_s,
            qkv_s,
            e_s,
            inv_s,
            o_own,
            c_s,
            g_s,
            slope_s,
            mid_s,
            low_s,
            embed_full,
            qkv_weights,
        ) = loaded
        dm_s, du_s, dqkv_s, dy_s, do_s = local[15:]
        block_rows = images * visible
        columns = w_out.shape[0]
        size = columns // enc_heads
        scaling = float(size) ** -0.5
        hidden, width = w_down.shape
        moves = {}
        for position in (13, 2, 10, 1, 9, 11, 8, 12, 0, 4, 5, 6, 7, 14, 3):
            moves[position] = Move(enc_hbm[position], loaded[position], move_sems.at[8 + position])

        def ready(*arrays):
            for array in arrays:
                moves[[array is one for one in loaded].index(True)].wait()

        def cut_sums(kind, bufs, axis, extent, pair, base=0):
            for cut, order in enumerate(SUM_ORDERS[kind]):
                sums[kind + str(cut)] = bulk(
                    orders[order], bufs, axis, cut * extent, extent, pair, base + cut
                )

        embed_cuts = len(SUM_ORDERS["emb"])
        embed_part = embed_packed.shape[1] // embed_cuts
        cut_sums("emb", embed_bufs, 1, embed_part, embed_sems)
        up_part = hidden // len(SUM_ORDERS["up"])
        down_part = hidden // len(SUM_ORDERS["dn"])
        cut_sums("up", row_bufs, 2, up_part, row_sems)
        cut_sums("dn", col_bufs, 1, down_part, col_sems)
        out_order, *qkv_orders = (orders[one] for one in SUM_ORDERS["oq"])
        for cut, name in enumerate("qkv"):
            sums[name] = bulk(
                qkv_orders[cut],
                row_bufs,
                2,
                hidden + cut * columns,
                columns,
                row_sems,
                len(SUM_ORDERS["up"]) + cut,
            )
        sums["o"] = bulk(
            out_order, col_bufs, 1, hidden, columns, col_sems, len(SUM_ORDERS["dn"])
        )

        swap.finish()
        demb_gather = Gather(demb_own, lambda slot: demb_slots.at[slot], sems.at[0], sems.at[1])
        demb_gather.start()
        demb_slots[index] = demb_own[...]
        ready(low_s)
        offset, high, span, tiles = embed_piece
        product = dot_as(low_s[...], demb_own[...].reshape(block_rows, -1), 0, 0)
        for column in range(model_count):
            for row in range(data_count):
                for cut, order in enumerate(SUM_ORDERS["emb"]):
                    spot = spot_of(row, column, orders[order])
                    for tile in range(tiles):
                        lanes = min(LANES, span - tile * LANES)
                        first = column * span + tile * LANES
                        base = tile * high
                        begin = max(base, cut * embed_part)
                        end = min(base + high, (cut + 1) * embed_part)
                        if begin < end:
                            shift = row * high - base
                            embed_packed[spot, begin:end, :lanes] = product[
                                begin + shift : end + shift, first : first + lanes
                            ].astype(low_type)
        start("emb")
        pump("a5")
        ready(embed_full, w_down, slope_s)

        def rows_of(slot):
            return pl.ds(pl.multiple_of(slot * block_rows, block_rows), block_rows)

        def first_back(step, carry):
            demb_gather.arrive_at(step)
            pump_at(step, "f")
            mask = visit_mask(step, count)
            slot = index ^ mask
            rows = rows_of(slot)
            grad_rows = demb_slots[slot].reshape(block_rows, -1)
            grad_out = dot_as(grad_rows, embed_full[...], 1, 1)

            @pl.when(mask == 0)
            def _():
                dy_s[...] = grad_out

            dm_s[rows, :] = grad_out.astype(low_type)
            for first in range(0, hidden, chunk):
                cols = slice(first, first + chunk)
                grad_active = dot_as(dm_s[rows, :], w_down[cols, :], 1, 1)
                du_s[rows, cols] = (grad_active * slope_s[rows, cols].astype(full_type)).astype(
                    low_type
                )
            return carry

        lax.fori_loop(0, count, first_back, 0)

        def store_rows(product, first, stages):
            high = width // data_count
            for row in range(data_count):
                row_packed[spot_of(row, 0, stages), :, first : first + product.shape[1]] = (
                    product[row * high : (row + 1) * high, :].astype(low_type)
                )

        def store_cols(product, first, stages):
            wide = width // data_count
            for col in range(data_count):
                col_packed[
                    spot_of(col, 0, stages), first : first + product.shape[0], :wide
                ] = product[:, col * wide : (col + 1) * wide].astype(low_type)

        def down_grads():
            ready(g_s)
            for cut, order in enumerate(SUM_ORDERS["dn"]):
                cols = slice(cut * down_part, (cut + 1) * down_part)
                product = dot_as(g_s[:, cols], dm_s[...], 0, 0)
                store_cols(product, cut * down_part, orders[order])
                sums["dn" + str(cut)].start()
            pump("b0" if EARLY_DOWN else "b3")

        def up_grads():
            ready(c_s)
            for cut, order in enumerate(SUM_ORDERS["up"]):
                cols = slice(cut * up_part, (cut + 1) * up_part)
                product = dot_as(c_s[...], du_s[:, cols], 0, 0)
                store_rows(product, cut * up_part, orders[order])
                sums["up" + str(cut)].start()
            pump("b1" if EARLY_UP else "b4")

        if EARLY_DOWN:
            down_grads()
        if EARLY_UP:
            up_grads()
        ready(w_up)
        scatter = Scatter(parts_mlp, total, landing_mlp, sems.at[2], sems.at[3])
        total[...] = jnp.zeros_like(total)

        def second_back(step, carry):
            pump_at(step, "s")
            mask = count - 1 - step
            rows = rows_of(index ^ mask)
            scatter.put(mask, dot_as(du_s[rows, :], w_up[...], 1, 1))
            return carry

        lax.fori_loop(0, count, second_back, 0)
        for bit in range(model_bits - 1):
            scatter.finish_bit(bit)

        pump("b2")
        if not EARLY_DOWN:
            down_grads()
        if not EARLY_UP and UP_FIRST:
            up_grads()
        ready(mid_s)
        scatter.finish_bit(model_bits - 1)

        normed, scale = norm_parts(mid_s[...])
        grad_second = total[...]
        wide_acc[0, 1:2, :] = jnp.sum(grad_second * normed, axis=0, keepdims=True)
        grad_middle = dy_s[...] + norm_back(normed, scale, grad_second * gain_mlp[...])
        dy_s[...] = grad_middle
        db_s[rows_of(index), :] = grad_middle.astype(low_type)
        db_gather = Gather(None, lambda slot: db_s.at[rows_of(slot)], sems.at[4], sems.at[5])
        db_gather.start()
        pump("b5")
        if not EARLY_UP and not UP_FIRST:
            up_grads()
        ready(w_out, qkv_s, e_s, inv_s, o_own, qkv_weights)
        second_scatter = Scatter(parts_attn, total, landing_attn, sems.at[6], sems.at[7])
        total[...] = jnp.zeros_like(total)

        def third_back(step, carry):
            db_gather.arrive_at(step)
            pump_at(step, "t")
            mask = visit_mask(step, count)
            slot = index ^ mask
            rows = rows_of(slot)
            do_s[...] = dot_as(w_out[...], db_s[rows, :], 1, 1)
            for head in range(enc_heads):
                span = slice(head * size, (head + 1) * size)
                key_span = slice(columns + head * size, columns + (head + 1) * size)
                value_span = slice(2 * columns + head * size, 2 * columns + (head + 1) * size)
                query, key, value = qkv_s[span, rows], qkv_s[key_span, rows], qkv_s[value_span, rows]
                weights = e_s[slot * enc_heads + head]
                grad_full = do_s[span, :] * (inv_s[slot * enc_heads + head] * scaling)
                shift = jnp.sum(
                    grad_full * o_own[span, rows].astype(full_type), axis=0, keepdims=True
                )
                grad_low = grad_full.astype(low_type)
                grad_probs = dot_as(value, grad_low, 0, 0)
                grad_scores = (weights.astype(full_type) * (grad_probs - shift)).astype(low_type)
                grad_value = dot_as(grad_low, weights, 1, 1) * (1.0 / scaling)
                grad_query = jnp.dot(key, grad_scores, preferred_element_type=full_type)
                grad_key = dot_as(query, grad_scores, 1, 1) * (1.0 / (scaling * LOG2E))
                dqkv_s[span, rows] = grad_query.astype(low_type)
                dqkv_s[key_span, rows] = grad_key.astype(low_type)
                dqkv_s[value_span, rows] = grad_value.astype(low_type)
            second_scatter.put(mask, dot_as(dqkv_s[:, rows], qkv_weights[...], 0, 0))
            return carry

        lax.fori_loop(0, count, third_back, 0)
        for bit in range(model_bits - 1):
            second_scatter.finish_bit(bit)
        pump("b6")
        store_cols(
            jnp.dot(o_own[...], db_s[...], preferred_element_type=full_type), hidden, out_order
        )
        sums["o"].start()
        ready(a_s)
        for cut, order in enumerate(qkv_orders):
            span = slice(cut * columns, (cut + 1) * columns)
            product = dot_as(a_s[...], dqkv_s[span, :], 0, 1)
            store_rows(product, hidden + cut * columns, order)
            sums["qkv"[cut]].start()
        pump("b7")
        second_scatter.finish_bit(model_bits - 1)
        normed, scale = norm_parts(tokens[...].astype(full_type))
        grad_normed = total[...]
        wide_acc[0, 0:1, :] = jnp.sum(grad_normed * normed, axis=0, keepdims=True)
        grad_tokens[...] = dy_s[...] + norm_back(normed, scale, grad_normed * gain_attn[...])

        def norm_copies(stage):
            peer = partner(*all_stages[stage])[0]
            return [
                pltpu.make_async_remote_copy(
                    src_ref=acc.at[stage],
                    dst_ref=got.at[stage],
                    send_sem=norm_sems.at[0, kind, stage],
                    recv_sem=norm_sems.at[1, kind, stage],
                    device_id=peer,
                    device_id_type=MESH,
                )
                for kind, (acc, got) in enumerate(((wide_acc, wide_got), (thin_acc, thin_got)))
            ]

        def norm_step(turn):
            for copy in norm_copies(turn):
                copy.wait()
            wide_acc[turn + 1] = wide_acc[turn] + wide_got[turn]
            thin_acc[turn + 1] = thin_acc[turn] + thin_got[turn]
            if turn + 1 < len(all_stages):
                for copy in norm_copies(turn + 1):
                    copy.start()

        for copy in norm_copies(0):
            copy.start()
        turn = 0
        for name in PLAN["tail"]:
            if name == "norm":
                if turn < len(all_stages):
                    norm_step(turn)
                    turn += 1
            elif name in sums:
                sums[name].advance()
        for later in range(turn, len(all_stages)):
            norm_step(later)
        for one in sums.values():
            while not one.done():
                one.advance()
        norm_wide[...] = wide_acc[len(all_stages)]
        norm_thin[...] = thin_acc[len(all_stages)]
        for one in (demb_gather, scatter, db_gather, second_scatter):
            one.drain()


    pl.run_scoped(encoder, *scopes[2])
    rows_out[...] = row_bufs[-1][0]
    cols_out[...] = col_bufs[-1][0]
    dec_out[...] = dec_bufs[-1][0]
    embed_out[...] = embed_bufs[-1][0]


def unpack_kernel(widths, dec_list, embed_list, *refs):
    hidden, columns, wide = widths
    grad_tokens, norm_wide, norm_thin, rows_in, cols_in, dec_in, embed_in = refs[:7]
    out_tokens, g_query, g_key, g_value, g_up, g_out, g_down, g_embed = refs[7:15]
    small = refs[15:20]
    dec_outs = refs[20:]
    out_tokens[...] = grad_tokens[...]
    g_up[...] = rows_in[:, :hidden].astype(full_type)
    for position, out in enumerate((g_query, g_key, g_value)):
        first = hidden + position * columns
        out[...] = rows_in[:, first : first + columns].astype(full_type)
    g_down[...] = cols_in[:hidden, :wide].astype(full_type)
    g_out[...] = cols_in[hidden : hidden + columns, :wide].astype(full_type)
    for position in range(2):
        small[position][...] = norm_wide[position : position + 1, :]
    for position in range(3):
        small[2 + position][...] = norm_thin[position : position + 1, :]
    for outs, pieces, source in (([g_embed], embed_list, embed_in), (dec_outs, dec_list, dec_in)):
        for out, (offset, rows, width, tiles) in zip(outs, pieces):
            for tile in range(tiles):
                lanes = min(LANES, width - tile * LANES)
                block = source[offset + tile * rows : offset + (tile + 1) * rows, :lanes]
                out[:, tile * LANES : tile * LANES + lanes] = block.astype(full_type)


def decode_and_back(
    arrived,
    grid_order,
    grid_keep,
    ground_dist,
    dec_weights,
    mask_token,
    pred_proj,
    cotangent,
    tokens,
    weights,
    saved,
    embed_proj,
):
    gain_attn, w_query, w_key, w_value, w_out, gain_mlp, w_up, w_down = weights
    (dec_gain_attn, dec_query, dec_key, dec_value, dec_proj, dec_gain_mlp, dec_up, dec_down) = (
        dec_weights
    )
    data_count, model_count = lax.axis_size("dp"), lax.axis_size("mp")
    data_bits, model_bits = log2_of(data_count), log2_of(model_count)
    images, visible, width = tokens.shape
    rows = images * visible
    every = rows * model_count
    enc_heads = HE // model_count
    columns, hidden = w_query.shape[1], w_up.shape[1]
    out_width = embed_proj.shape[1] * model_count
    length, pixels = cotangent.shape[1:]
    grid_rows = images * length
    dec_hidden = dec_up.shape[1]
    matrices = [dec_query, dec_key, dec_value, dec_proj, dec_up, dec_down, pred_proj]
    pieces, height = dec_pieces(data_count, model_count, [one.shape for one in matrices])
    embed_pieces, embed_height = dec_pieces(data_count, model_count, [(width, out_width)])
    high, wide = width // data_count, width // data_count
    wide_pad = -(-wide // LANES) * LANES
    devices = data_count * model_count
    stages = data_bits + model_bits
    dec_cuts = sum(len(SUM_ORDERS[kind]) for kind in ("attn", "dup", "ddn", "pred"))
    row_shape = (high, hidden + 3 * columns)
    col_shape = (hidden + columns, wide_pad)
    vmem = pl.BlockSpec(memory_space=pltpu.VMEM)
    hbm = pl.BlockSpec(memory_space=pl.ANY)
    low = lambda *shape: pltpu.VMEM(shape, low_type)
    full = lambda *shape: pltpu.VMEM(shape, full_type)
    loaded = [w_out, w_up, w_down, *saved]
    turned_scope = [low(out_width, out_width)] * 3
    attn_scope = [
        low(out_width, out_width),
        full(grid_rows, out_width),
        low(3 * out_width, out_width),
        low(grid_rows, out_width),
        low(3 * out_width, grid_rows),
        low(images * HD, length, length),
        full(images * HD, 1, length),
        low(out_width, grid_rows),
        full(grid_rows, out_width),
        low(grid_rows, out_width),
        full(out_width, length),
    ]
    dense_scope = [
        low(out_width, dec_hidden),
        low(dec_hidden, out_width),
        low(out_width, pixels),
        low(images, length, pixels),
        full(length, out_width),
        low(grid_rows, out_width),
        low(grid_rows, dec_hidden),
        low(grid_rows, dec_hidden),
        low(grid_rows, out_width),
        low(grid_rows, out_width),
        full(length, pixels),
    ]
    enc_scope = [pltpu.VMEM(one.shape, one.dtype) for one in loaded] + [
        low(every, width),
        low(every, hidden),
        low(3 * columns, every),
        full(rows, width),
        full(columns, rows),
    ]
    plan = (
        images,
        visible,
        enc_heads,
        HD,
        SIDE,
        pieces,
        embed_pieces[0],
        (attn_scope, dense_scope, enc_scope, turned_scope),
    )

    def kernel(*refs):
        back_kernel(plan, *refs)

    outs = [
        (cotangent.shape, full_type),
        ((rows, width), full_type),
        ((2, width), full_type),
        ((3, out_width), full_type),
        (row_shape, low_type),
        (col_shape, low_type),
        ((height, LANES), low_type),
        ((embed_height, LANES), low_type),
    ]
    scratch = [
        pltpu.SemaphoreType.DMA((8 + len(loaded),)),
        pltpu.SemaphoreType.DMA((images,)),
        low(images, visible, out_width),
        low(devices, height, LANES),
        full(3, out_width),
        low(images, visible, out_width),
        low(model_count, images, visible, out_width),
        low(every, width),
        full(rows, width),
        low(model_count - 1, rows, width),
        low(model_count - 1, rows, width),
        low(model_count - 1, rows, width),
        low(model_count - 1, rows, width),
        pltpu.SemaphoreType.DMA((8, model_count)),
        pltpu.SemaphoreType.DMA((2, images)),
        low(data_count, *row_shape),
        low(data_count, *col_shape),
        low(devices, embed_height, LANES),
    ]
    scratch += [low(data_count >> (bit + 1), *row_shape) for bit in range(data_bits)]
    scratch += [low(data_count >> (bit + 1), *col_shape) for bit in range(data_bits)]
    scratch += [low(devices >> (bit + 1), height, LANES) for bit in range(stages)]
    scratch += [low(devices >> (bit + 1), embed_height, LANES) for bit in range(stages)]
    for shape in ((2, width), (3, out_width)):
        scratch += [full(stages + 1, *shape), full(stages, *shape)]
    scratch += [
        pltpu.SemaphoreType.DMA((2, len(SUM_ORDERS["up"]) + 3, data_bits)),
        pltpu.SemaphoreType.DMA((2, len(SUM_ORDERS["dn"]) + 1, data_bits)),
        pltpu.SemaphoreType.DMA((2, dec_cuts, stages)),
        pltpu.SemaphoreType.DMA((2, len(SUM_ORDERS["emb"]), stages)),
        pltpu.SemaphoreType.DMA((2, 2, stages)),
    ]
    results = pl.pallas_call(
        kernel,
        out_shape=[jax.ShapeDtypeStruct(shape, kind) for shape, kind in outs],
        in_specs=[pl.BlockSpec(memory_space=pltpu.SMEM)] + [vmem] * 9 + [hbm] * (8 + len(loaded)),
        out_specs=[hbm] + [vmem] * (len(outs) - 1),
        scratch_shapes=scratch,
        compiler_params=pltpu.CompilerParams(
            collective_id=2, has_side_effects=True, vmem_limit_bytes=255 * 2**18
        ),
    )(
        ground_dist,
        arrived,
        grid_order,
        grid_keep,
        dec_gain_attn.reshape(1, -1),
        dec_gain_mlp.reshape(1, -1),
        mask_token.reshape(1, -1),
        tokens.reshape(rows, width),
        gain_attn.reshape(1, -1),
        gain_mlp.reshape(1, -1),
        dec_query,
        dec_key,
        dec_value,
        dec_proj,
        dec_up,
        dec_down,
        pred_proj,
        cotangent,
        *loaded,
    )
    final = [
        (rows, width),
        (high, columns),
        (high, columns),
        (high, columns),
        (high, hidden),
        (columns, wide),
        (hidden, wide),
        (embed_pieces[0][1], embed_pieces[0][2]),
    ]
    final += [(1, width)] * 2 + [(1, out_width)] * 3
    final += [(piece[1], piece[2]) for piece in pieces]

    def last_kernel(*refs):
        unpack_kernel((hidden, columns, wide), pieces, embed_pieces, *refs)

    return results[0], pl.pallas_call(
        last_kernel,
        out_shape=[jax.ShapeDtypeStruct(shape, full_type) for shape in final],
        in_specs=[vmem] * (len(outs) - 1),
        out_specs=[vmem] * len(final),
    )(*results[1:])


def layer_norm(values, scale_gain):
    center = values - jnp.mean(values, axis=-1, keepdims=True)
    spread = jnp.mean(center * center, axis=-1, keepdims=True)
    return center * lax.rsqrt(spread + eps_norm) * scale_gain


def exact_gelu(values):
    return jax.nn.gelu(values, approximate=False)


def matmul(left_side, right_side):
    flat_rows = left_side.reshape(-1, left_side.shape[-1])
    product = jnp.dot(flat_rows, right_side, preferred_element_type=full_type)
    return product.reshape(left_side.shape[:-1] + (right_side.shape[1],))


def matmul_t(left_side, right_side):
    flat_rows = left_side.reshape(-1, left_side.shape[-1])
    product = lax.dot_general(
        flat_rows, right_side, (((1,), (1,)), ((), ())), preferred_element_type=full_type
    )
    return product.reshape(left_side.shape[:-1] + (right_side.shape[0],))


def outer_sum(left_side, right_side):
    return lax.dot_general(
        left_side.reshape(-1, left_side.shape[-1]),
        right_side.reshape(-1, right_side.shape[-1]),
        (((0,), (0,)), ((), ())),
        preferred_element_type=full_type,
    )


def spread_rows(values, tensor_split):
    if tensor_split:
        return lax.all_gather(values, "mp", axis=0, tiled=True)
    return values


def collect_rows(values, tensor_split):
    if tensor_split:
        return lax.psum_scatter(
            values.astype(jnp.bfloat16), "mp", scatter_dimension=0, tiled=True
        ).astype(jnp.float32)
    return values


def images_per_block(images, length):
    grouped = 1
    while grouped * length < 512 and grouped < images:
        grouped = grouped * 2
    return grouped


def in_blocks(blocked_array, grouped):
    return blocked_array.reshape(
        (blocked_array.shape[0] // grouped, grouped) + blocked_array.shape[1:]
    )


def with_heads(blocked_array, head_count):
    return blocked_array.reshape(
        blocked_array.shape[:2] + (head_count, blocked_array.shape[2] // head_count)
    )


def attend_forward(queries, keys_all, values_all, key_valid, head_count):
    images, length, columns = queries.shape
    grouped = images_per_block(images, length)
    scaling = float(columns // head_count) ** (-0.5)

    def one_block(pieces):
        query_b, key_b, value_b, valid_b = pieces
        scores = (
            jnp.einsum("nqhd,nkhd->nhqk", query_b, key_b, preferred_element_type=full_type)
            * scaling
        )
        scores = jnp.where(valid_b[:, None, None, :], scores, masked_score)
        row_max = jnp.max(scores, axis=-1, keepdims=True)
        weights = jnp.exp(scores - row_max)
        totals = jnp.sum(weights, axis=-1, keepdims=True)
        prob_rows = (weights / totals).astype(low_type)
        mixed_b = jnp.einsum(
            "nhqk,nkhd->nqhd", prob_rows, value_b, preferred_element_type=full_type
        )
        return (mixed_b.astype(low_type), (row_max + jnp.log(totals))[..., 0])

    pieces_in = (
        in_blocks(with_heads(queries, head_count), grouped),
        in_blocks(with_heads(keys_all, head_count), grouped),
        in_blocks(with_heads(values_all, head_count), grouped),
        in_blocks(key_valid, grouped),
    )
    mixed_rows, log_total = lax.map(one_block, pieces_in)
    return (
        mixed_rows.reshape(images, length, columns),
        log_total.reshape(images, head_count, length),
    )


def attend_backward(queries, keys_all, values_all, key_valid, log_total, grad_mixed, head_count):
    images, length, columns = queries.shape
    grouped = images_per_block(images, length)
    scaling = float(columns // head_count) ** (-0.5)

    def one_block(pieces):
        query_b, key_b, value_b, valid_b, total_b, grad_b = pieces
        scores = (
            jnp.einsum("nqhd,nkhd->nhqk", query_b, key_b, preferred_element_type=full_type)
            * scaling
        )
        scores = jnp.where(valid_b[:, None, None, :], scores, masked_score)
        prob_rows = jnp.exp(scores - total_b[..., None])
        grad_value_b = jnp.einsum(
            "nhqk,nqhd->nkhd", prob_rows.astype(low_type), grad_b, preferred_element_type=full_type
        )
        grad_probs = jnp.einsum(
            "nqhd,nkhd->nhqk", grad_b, value_b, preferred_element_type=full_type
        )
        grad_scores = prob_rows * (
            grad_probs - jnp.sum(grad_probs * prob_rows, axis=-1, keepdims=True)
        )
        grad_scores = (grad_scores * scaling).astype(low_type)
        grad_query_b = jnp.einsum(
            "nhqk,nkhd->nqhd", grad_scores, key_b, preferred_element_type=full_type
        )
        grad_key_b = jnp.einsum(
            "nhqk,nqhd->nkhd", grad_scores, query_b, preferred_element_type=full_type
        )
        return (
            grad_query_b.astype(low_type),
            grad_key_b.astype(low_type),
            grad_value_b.astype(low_type),
        )

    pieces_in = (
        in_blocks(with_heads(queries, head_count), grouped),
        in_blocks(with_heads(keys_all, head_count), grouped),
        in_blocks(with_heads(values_all, head_count), grouped),
        in_blocks(key_valid, grouped),
        in_blocks(log_total, grouped),
        in_blocks(with_heads(grad_mixed, head_count), grouped),
    )
    grad_query, grad_key, grad_value = lax.map(one_block, pieces_in)
    return (
        grad_query.reshape(images, length, columns),
        grad_key.reshape(images, length, columns),
        grad_value.reshape(images, length, columns),
    )


def block_forward(inputs, key_valid, weights, head_count, tensor_split):
    gain_attn, w_query, w_key, w_value, w_out, gain_mlp, w_up, w_down = weights
    normed = spread_rows(layer_norm(inputs, gain_attn).astype(low_type), tensor_split)
    queries = matmul(normed, w_query).astype(low_type)
    keys_all = matmul(normed, w_key).astype(low_type)
    values_all = matmul(normed, w_value).astype(low_type)
    mixed_rows, log_total = attend_forward(queries, keys_all, values_all, key_valid, head_count)
    middle = inputs + collect_rows(matmul(mixed_rows, w_out), tensor_split)
    second = spread_rows(layer_norm(middle, gain_mlp).astype(low_type), tensor_split)
    pre_act = matmul(second, w_up)
    active = exact_gelu(pre_act).astype(low_type)
    outputs = middle + collect_rows(matmul(active, w_down), tensor_split)
    kept_state = (
        inputs,
        normed,
        queries,
        keys_all,
        values_all,
        mixed_rows,
        log_total,
        middle,
        second,
        pre_act,
        active,
    )
    return (outputs, kept_state)


def block_backward(grad_out, kept_state, key_valid, weights, head_count, tensor_split):
    gain_attn, w_query, w_key, w_value, w_out, gain_mlp, w_up, w_down = weights
    (
        inputs,
        normed,
        queries,
        keys_all,
        values_all,
        mixed_rows,
        log_total,
        middle,
        second,
        pre_act,
        active,
    ) = kept_state
    grad_branch = spread_rows(grad_out.astype(low_type), tensor_split)
    grad_down = outer_sum(active, grad_branch)
    grad_active = matmul_t(grad_branch, w_down)
    grad_pre = jax.vjp(exact_gelu, pre_act)[1](grad_active)[0].astype(low_type)
    grad_up = outer_sum(second, grad_pre)
    grad_second = collect_rows(matmul_t(grad_pre, w_up), tensor_split)
    norm_grad, grad_gain_mlp = jax.vjp(layer_norm, middle, gain_mlp)[1](grad_second)
    grad_middle = grad_out + norm_grad
    grad_attn = spread_rows(grad_middle.astype(low_type), tensor_split)
    grad_w_out = outer_sum(mixed_rows, grad_attn)
    grad_mixed = matmul_t(grad_attn, w_out).astype(low_type)
    grad_query, grad_key, grad_value = attend_backward(
        queries, keys_all, values_all, key_valid, log_total, grad_mixed, head_count
    )
    grad_w_query = outer_sum(normed, grad_query)
    grad_w_key = outer_sum(normed, grad_key)
    grad_w_value = outer_sum(normed, grad_value)
    grad_normed = (
        matmul_t(grad_query, w_query) + matmul_t(grad_key, w_key) + matmul_t(grad_value, w_value)
    )
    grad_normed = collect_rows(grad_normed, tensor_split)
    input_grad, grad_gain_attn = jax.vjp(layer_norm, inputs, gain_attn)[1](grad_normed)
    return (
        grad_middle + input_grad,
        (
            grad_gain_attn,
            grad_w_query,
            grad_w_key,
            grad_w_value,
            grad_w_out,
            grad_gain_mlp,
            grad_up,
            grad_down,
        ),
    )


def grid_codes(distance, side_count, columns):
    quarter = columns // 4
    frequency = 10000.0 ** (-jnp.arange(quarter, dtype=full_type) / quarter)
    places = jnp.arange(side_count * side_count)
    row_pos = (places // side_count).astype(full_type)
    col_pos = (places % side_count).astype(full_type)
    row_angle = distance[:, None, None] * row_pos[None, :, None] * frequency[None, None, :]
    col_angle = distance[:, None, None] * col_pos[None, :, None] * frequency[None, None, :]
    return jnp.concatenate(
        [jnp.sin(row_angle), jnp.cos(row_angle), jnp.sin(col_angle), jnp.cos(col_angle)], axis=-1
    )


def placement_table(visible_order, keep_flags, visible):
    positions = jnp.arange(visible_order.shape[1])
    matches = (visible_order[:, None, :visible] == positions[None, :, None]) & (
        keep_flags[:, :, None] == 1
    )
    return matches.astype(low_type)


def owner_blocks(full_grad, data_count, model_count):
    row_count, col_count = full_grad.shape
    reshaped = full_grad.reshape(
        data_count, row_count // data_count, model_count, col_count // model_count
    )
    return jnp.transpose(reshaped, (0, 2, 1, 3)).reshape(
        data_count * model_count, row_count // data_count, col_count // model_count
    )


def per_device_plain(
    tokens,
    lengths,
    grid_order,
    grid_keep,
    ground_dist,
    enc_norm,
    enc_query,
    enc_key,
    enc_value,
    enc_proj,
    enc_norm2,
    enc_up,
    enc_down,
    embed_proj,
    mask_token,
    dec_norm,
    dec_query,
    dec_key,
    dec_value,
    dec_proj,
    dec_norm2,
    dec_up,
    dec_down,
    pred_proj,
    cotangent,
):
    data_count = lax.axis_size("dp")
    model_count = lax.axis_size("mp")
    enc_weights = (enc_norm, enc_query, enc_key, enc_value, enc_proj, enc_norm2, enc_up, enc_down)
    dec_weights = (dec_norm, dec_query, dec_key, dec_value, dec_proj, dec_norm2, dec_up, dec_down)
    enc_heads = HE // model_count
    key_valid = jnp.arange(tokens.shape[1])[None, :] < lengths[:, None]
    enc_out, enc_saved = block_forward(
        tokens.astype(full_type), key_valid, enc_weights, enc_heads, True
    )
    enc_low = enc_out.astype(low_type)
    enc_all = spread_rows(enc_low, True)
    embedded = matmul(enc_all, embed_proj).astype(low_type)
    sectioned = embedded.reshape((data_count, -1) + embedded.shape[1:])
    arrived = lax.all_to_all(
        lax.all_to_all(sectioned, "dp", split_axis=0, concat_axis=0, tiled=True),
        "mp",
        split_axis=0,
        concat_axis=3,
        tiled=True,
    )
    arrived = arrived.reshape((-1,) + arrived.shape[2:])
    pick_table = placement_table(grid_order, grid_keep, arrived.shape[1])
    masked = (1 - grid_keep).astype(full_type)[..., None]
    dec_start = jnp.einsum("npt,ntc->npc", pick_table, arrived, preferred_element_type=full_type)
    dec_start = dec_start + masked * mask_token + grid_codes(ground_dist, SIDE, mask_token.shape[0])
    all_valid = jnp.ones(dec_start.shape[:2], jnp.bool_)
    dec_out, dec_saved = block_forward(dec_start, all_valid, dec_weights, HD, False)
    dec_low = dec_out.astype(low_type)
    decoded = matmul(dec_low, pred_proj)
    grad_pred = outer_sum(dec_low, cotangent)
    grad_dec_out = matmul_t(cotangent, pred_proj)
    grad_start, dec_grads = block_backward(
        grad_dec_out, dec_saved, all_valid, dec_weights, HD, False
    )
    grad_mask = jnp.sum(masked * grad_start, axis=(0, 1))
    grad_arrived = jnp.einsum("npt,npc->ntc", pick_table.astype(full_type), grad_start).astype(
        low_type
    )
    sent_back = grad_arrived.reshape((-1, IPD) + grad_arrived.shape[1:])
    returned = lax.all_to_all(
        lax.all_to_all(sent_back, "mp", split_axis=3, concat_axis=0, tiled=True),
        "dp",
        split_axis=0,
        concat_axis=0,
        tiled=True,
    )
    returned = returned.reshape((-1,) + returned.shape[2:])
    grad_embed = outer_sum(enc_all, returned)
    grad_enc_out = collect_rows(matmul_t(returned, embed_proj), True)
    grad_tokens, enc_grads = block_backward(
        grad_enc_out, enc_saved, key_valid, enc_weights, enc_heads, True
    )
    col_sums = (
        lax.psum_scatter(
            enc_grads[4].astype(jnp.bfloat16), "dp", scatter_dimension=1, tiled=True
        ).astype(jnp.float32),
        lax.psum_scatter(
            enc_grads[7].astype(jnp.bfloat16), "dp", scatter_dimension=1, tiled=True
        ).astype(jnp.float32),
    )
    norm_grads = lax.psum(
        (enc_grads[0], enc_grads[5], dec_grads[0], dec_grads[5], grad_mask), ("dp", "mp")
    )
    dec_list = (
        dec_grads[1],
        dec_grads[2],
        dec_grads[3],
        dec_grads[4],
        dec_grads[6],
        dec_grads[7],
        grad_pred,
    )
    row_sums = (
        lax.psum_scatter(
            enc_grads[1].astype(jnp.bfloat16), "dp", scatter_dimension=0, tiled=True
        ).astype(jnp.float32),
        lax.psum_scatter(
            enc_grads[2].astype(jnp.bfloat16), "dp", scatter_dimension=0, tiled=True
        ).astype(jnp.float32),
        lax.psum_scatter(
            enc_grads[3].astype(jnp.bfloat16), "dp", scatter_dimension=0, tiled=True
        ).astype(jnp.float32),
        lax.psum_scatter(
            enc_grads[6].astype(jnp.bfloat16), "dp", scatter_dimension=0, tiled=True
        ).astype(jnp.float32),
        lax.psum_scatter(
            grad_embed.astype(jnp.bfloat16), "dp", scatter_dimension=0, tiled=True
        ).astype(jnp.float32),
    )
    summed = (
        lax.psum_scatter(
            owner_blocks(dec_list[0], data_count, model_count),
            ("dp", "mp"),
            scatter_dimension=0,
            tiled=True,
        ),
        lax.psum_scatter(
            owner_blocks(dec_list[1], data_count, model_count),
            ("dp", "mp"),
            scatter_dimension=0,
            tiled=True,
        ),
        lax.psum_scatter(
            owner_blocks(dec_list[2], data_count, model_count),
            ("dp", "mp"),
            scatter_dimension=0,
            tiled=True,
        ),
        lax.psum_scatter(
            owner_blocks(dec_list[3], data_count, model_count),
            ("dp", "mp"),
            scatter_dimension=0,
            tiled=True,
        ),
        lax.psum_scatter(
            owner_blocks(dec_list[4], data_count, model_count),
            ("dp", "mp"),
            scatter_dimension=0,
            tiled=True,
        ),
        lax.psum_scatter(
            owner_blocks(dec_list[5], data_count, model_count),
            ("dp", "mp"),
            scatter_dimension=0,
            tiled=True,
        ),
        lax.psum_scatter(
            owner_blocks(dec_list[6], data_count, model_count),
            ("dp", "mp"),
            scatter_dimension=0,
            tiled=True,
        ),
    )
    embed_final = row_sums[4]
    dec_final = tuple((summed[index_num][0] for index_num in range(7)))
    return (
        decoded,
        grad_tokens,
        norm_grads[0],
        row_sums[0],
        row_sums[1],
        row_sums[2],
        col_sums[0],
        norm_grads[1],
        row_sums[3],
        col_sums[1],
        embed_final,
        norm_grads[4],
        norm_grads[2],
        dec_final[0],
        dec_final[1],
        dec_final[2],
        dec_final[3],
        norm_grads[3],
        dec_final[4],
        dec_final[5],
        dec_final[6],
    )


VMEM_BUDGET = 56 * 2**20


def kernel_bytes(tokens, enc_up, enc_query, dec_up, pred_proj):
    data_count, model_count = lax.axis_size("dp"), lax.axis_size("mp")
    images, visible, width = tokens.shape
    every = images * visible * model_count
    hidden, columns = enc_up.shape[1], enc_query.shape[1]
    out_width, wide = dec_up.shape[0], max(width // data_count, LANES)
    shapes = [(out_width, out_width)] * 4
    shapes += [dec_up.shape, dec_up.shape[::-1], pred_proj.shape, (width, out_width)]
    height = dec_pieces(data_count, model_count, shapes)[1]
    rows = 8 * every * width + 3 * every * hidden
    sums = width * (hidden + 3 * columns) + data_count * (hidden + columns) * wide
    sums = 2 * (sums + data_count * model_count * height * LANES)
    return 2 * (rows + sums + 2 * width * hidden + 4 * width * columns)


def per_device(
    tokens,
    lengths,
    grid_order,
    grid_keep,
    ground_dist,
    enc_norm,
    enc_query,
    enc_key,
    enc_value,
    enc_proj,
    enc_norm2,
    enc_up,
    enc_down,
    embed_proj,
    mask_token,
    dec_norm,
    dec_query,
    dec_key,
    dec_value,
    dec_proj,
    dec_norm2,
    dec_up,
    dec_down,
    pred_proj,
    cotangent,
):
    if kernel_bytes(tokens, enc_up, enc_query, dec_up, pred_proj) > VMEM_BUDGET:
        return per_device_plain(
            tokens,
            lengths,
            grid_order,
            grid_keep,
            ground_dist,
            enc_norm,
            enc_query,
            enc_key,
            enc_value,
            enc_proj,
            enc_norm2,
            enc_up,
            enc_down,
            embed_proj,
            mask_token,
            dec_norm,
            dec_query,
            dec_key,
            dec_value,
            dec_proj,
            dec_norm2,
            dec_up,
            dec_down,
            pred_proj,
            cotangent,
        )
    enc_weights = (enc_norm, enc_query, enc_key, enc_value, enc_proj, enc_norm2, enc_up, enc_down)
    dec_weights = (dec_norm, dec_query, dec_key, dec_value, dec_proj, dec_norm2, dec_up, dec_down)
    arrived, *saved = encode(tokens, lengths, enc_weights, embed_proj)
    decoded, grads = decode_and_back(
        arrived,
        grid_order,
        grid_keep,
        ground_dist,
        dec_weights,
        mask_token,
        pred_proj,
        cotangent,
        tokens,
        enc_weights,
        saved,
        embed_proj,
    )
    (
        grad_tokens,
        g_query,
        g_key,
        g_value,
        g_up,
        g_out,
        g_down,
        g_embed,
        n_enc_attn,
        n_enc_mlp,
        n_dec_attn,
        n_dec_mlp,
        n_mask,
        *dec_grads,
    ) = grads
    return (
        decoded,
        grad_tokens.reshape(tokens.shape),
        n_enc_attn[0],
        g_query,
        g_key,
        g_value,
        g_out,
        n_enc_mlp[0],
        g_up,
        g_down,
        g_embed,
        n_mask[0],
        n_dec_attn[0],
        dec_grads[0],
        dec_grads[1],
        dec_grads[2],
        dec_grads[3],
        n_dec_mlp[0],
        dec_grads[4],
        dec_grads[5],
        dec_grads[6],
    )


def solution(mesh):
    return jax.shard_map(
        per_device,
        mesh=mesh,
        in_specs=(
            P(("dp", "mp"), None, None),
            P("dp"),
            P(("dp", "mp"), None),
            P(("dp", "mp"), None),
            P(("dp", "mp")),
            P(),
            P(None, "mp"),
            P(None, "mp"),
            P(None, "mp"),
            P("mp", None),
            P(),
            P(None, "mp"),
            P("mp", None),
            P(None, "mp"),
            P(),
            P(),
            P(),
            P(),
            P(),
            P(),
            P(),
            P(),
            P(),
            P(),
            P(("dp", "mp"), None, None),
        ),
        out_specs=(
            P(("dp", "mp"), None, None),
            P(("dp", "mp"), None, None),
            P(),
            P("dp", "mp"),
            P("dp", "mp"),
            P("dp", "mp"),
            P("mp", "dp"),
            P(),
            P("dp", "mp"),
            P("mp", "dp"),
            P("dp", "mp"),
            P(),
            P(),
            P("dp", "mp"),
            P("dp", "mp"),
            P("dp", "mp"),
            P("dp", "mp"),
            P(),
            P("dp", "mp"),
            P("dp", "mp"),
            P("dp", "mp"),
        ),
        check_vma=False,
    )
```

```python
import math

import jax
import jax.numpy as jnp
from jax import lax
from jax.experimental import pallas as pl
from jax.experimental.pallas import tpu as pltpu
from jax.sharding import PartitionSpec as P

HE = 16
HD = 16
SIDE = 16
IPD = 1


eps_norm = 1e-06
masked_score = -1e30
low_type = jnp.bfloat16
full_type = jnp.float32


MESH = pl.DeviceIdType.MESH
LANES = 128


def log2_of(count):
    bits = count.bit_length() - 1
    assert 1 << bits == count
    return bits


def spot_of(data, model, stages):
    out = 0
    for axis, bit in stages:
        out = out * 2 + (((data if axis == "dp" else model) >> bit) & 1)
    return out


def partner(axis, bit):
    dp, mp = lax.axis_index("dp"), lax.axis_index("mp")
    step = 1 << bit
    if axis == "dp":
        return (dp ^ step, mp), (dp >> bit) & 1
    return (dp, mp ^ step), (mp >> bit) & 1


def enter_barrier(partners):
    barrier = pltpu.get_barrier_semaphore()
    for peer in partners:
        pl.semaphore_signal(barrier, inc=1, device_id=peer, device_id_type=MESH)
    pl.semaphore_wait(barrier, len(partners))


class HalvingSum:
    def __init__(self, stages, buffers, window, send_sems, recv_sems):
        self.stages, self.buffers, self.window = stages, buffers, window
        self.send_sems, self.recv_sems = send_sems, recv_sems

    def view(self, index, start, size):
        return self.buffers[index].at[(pl.ds(start, size),) + self.window]

    def copy(self, index):
        peer, mine = partner(*self.stages[index])
        half = self.buffers[index].shape[0] // 2
        return pltpu.make_async_remote_copy(
            src_ref=self.view(index, (1 - mine) * half, half),
            dst_ref=self.view(index + 1, 0, half),
            send_sem=self.send_sems.at[index],
            recv_sem=self.recv_sems.at[index],
            device_id=peer,
            device_id_type=MESH,
        )

    def start(self, index):
        self.copy(index).start()

    def finish(self, index):
        self.copy(index).wait()
        peer, mine = partner(*self.stages[index])
        half = self.buffers[index].shape[0] // 2

        def one(position, carry):
            there = self.buffers[index + 1].at[(position,) + self.window]
            here = self.buffers[index].at[(mine * half + position,) + self.window]
            there[...] = there[...] + here[...]
            return carry

        lax.fori_loop(0, half, one, 0)


def dec_pieces(data_count, model_count, shapes):
    offset, pieces = 0, []
    for rows, columns in shapes:
        height, width = rows // data_count, columns // model_count
        tiles = -(-width // LANES)
        pieces.append((offset, height, width, tiles))
        offset += height * tiles
    return pieces, offset


LOG2E = 1.4426950408889634


def dot_as(left, right, left_dim, right_dim):
    return lax.dot_general(
        left, right, (((left_dim,), (right_dim,)), ((), ())), preferred_element_type=full_type
    )


def norm_parts(values):
    center = values - jnp.mean(values, axis=-1, keepdims=True)
    scale = lax.rsqrt(jnp.mean(center * center, axis=-1, keepdims=True) + eps_norm)
    return center * scale, scale


def norm_back(normed, scale, grad_scaled):
    first = jnp.mean(grad_scaled, axis=-1, keepdims=True)
    second = jnp.mean(grad_scaled * normed, axis=-1, keepdims=True)
    return (grad_scaled - first - normed * second) * scale


def gelu_pair(values):
    below = 0.5 + 0.5 * lax.erf(values * (0.5**0.5))
    density = jnp.exp2(values * values * (-0.5 * LOG2E)) * ((2.0 * math.pi) ** -0.5)
    return values * below, below + values * density


def low_bit(mask):
    return (mask & -mask).bit_length() - 1


def visit_order(count):
    return sorted(range(count), key=lambda mask: (mask.bit_length(), -mask))


def visit_mask(step, count):
    mask = jnp.int32(0)
    for position, value in enumerate(visit_order(count)):
        mask = jnp.where(step == position, value, mask)
    return mask


class Gather:
    def __init__(self, own, slot_view, send_sems, recv_sems):
        self.own, self.slot_view = own, slot_view
        self.send_sems, self.recv_sems = send_sems, recv_sems
        self.count = lax.axis_size("mp")
        self.index = lax.axis_index("mp")

    def copy(self, mask):
        bit = low_bit(mask)
        carried = mask ^ (1 << bit)
        place = self.slot_view(self.index ^ carried)
        return pltpu.make_async_remote_copy(
            src_ref=self.own if carried == 0 and self.own is not None else place,
            dst_ref=place,
            send_sem=self.send_sems.at[mask],
            recv_sem=self.recv_sems.at[mask],
            device_id=partner("mp", bit)[0],
            device_id_type=MESH,
        )

    def start(self):
        for bit in reversed(range(log2_of(self.count))):
            self.copy(1 << bit).start()

    def arrive(self, mask):
        self.copy(mask).wait_recv()
        for bit in reversed(range(low_bit(mask))):
            self.copy(mask | (1 << bit)).start()

    def arrive_group(self, length):
        group = [mask for mask in range(1, self.count) if mask.bit_length() == length]
        for mask in sorted(group, key=lambda one: -low_bit(one)):
            self.arrive(mask)

    def arrive_all(self):
        for length in range(1, log2_of(self.count) + 1):
            self.arrive_group(length)

    def arrive_at(self, step):
        for length in range(1, log2_of(self.count) + 1):
            @pl.when(step == 1 << (length - 1))
            def _():
                self.arrive_group(length)

    def drain(self):
        for mask in range(1, self.count):
            self.copy(mask).wait_send()


class Scatter:
    def __init__(self, parts, total, landing, send_sems, recv_sems):
        self.parts, self.total, self.landing = parts, total, landing
        self.send_sems, self.recv_sems = send_sems, recv_sems
        self.count = lax.axis_size("mp")
        self.index = lax.axis_index("mp")

    def copy(self, mask):
        return pltpu.make_async_remote_copy(
            src_ref=self.parts.at[mask - 1],
            dst_ref=self.landing.at[mask - 1],
            send_sem=self.send_sems.at[mask],
            recv_sem=self.recv_sems.at[mask],
            device_id=partner("mp", low_bit(mask))[0],
            device_id_type=MESH,
        )

    def put(self, mask, product):
        @pl.when(mask == 0)
        def _():
            self.total[...] = self.total[...] + product

        @pl.when(mask != 0)
        def _():
            self.parts[mask - 1] = product.astype(low_type)

        for odd in range(1, self.count, 2):
            @pl.when(mask == odd)
            def _():
                self.copy(odd).start()

    def finish(self, mask):
        bit = low_bit(mask)
        self.copy(mask).wait_recv()
        rest = mask ^ (1 << bit)
        if rest:
            self.parts[rest - 1] = self.parts[rest - 1] + self.landing[mask - 1]
            if low_bit(rest) == bit + 1:
                self.copy(rest).start()
        else:
            self.total[...] = self.total[...] + self.landing[mask - 1].astype(full_type)

    def finish_bit(self, bit):
        masks = [mask for mask in range(1, self.count) if low_bit(mask) == bit]
        for mask in reversed(masks):
            self.finish(mask)

    def drain(self):
        for mask in range(1, self.count):
            self.copy(mask).wait_send()


def exchange_partners(images):
    data_count, model_count = lax.axis_size("dp"), lax.axis_size("mp")
    data, model = lax.axis_index("dp"), lax.axis_index("mp")
    out = []
    for image in range(images):
        spot = (model * images + image) * data_count + data
        device = spot // images
        out.append((device // model_count, device % model_count, spot % images))
    return out


def is_here(peer):
    return (peer[0] == lax.axis_index("dp")) & (peer[1] == lax.axis_index("mp"))


class Exchange:
    def __init__(self, images, source, target, send_sems, recv_sems):
        self.partners = exchange_partners(images)
        self.source, self.target = source, target
        self.send_sems, self.recv_sems = send_sems, recv_sems

    def copy(self, image):
        data, model, slot = self.partners[image]
        return pltpu.make_async_remote_copy(
            src_ref=self.source.at[image],
            dst_ref=self.target.at[slot],
            send_sem=self.send_sems.at[image],
            recv_sem=self.recv_sems.at[slot],
            device_id=(data, model),
            device_id_type=MESH,
        )

    def start(self):
        for image, (data, model, slot) in enumerate(self.partners):
            here = is_here((data, model))

            @pl.when(here)
            def _():
                self.target[slot] = self.source[image]

            @pl.when(jnp.logical_not(here))
            def _():
                self.copy(image).start()

    def finish(self):
        for image, (data, model, slot) in enumerate(self.partners):
            @pl.when(jnp.logical_not(is_here((data, model))))
            def _():
                pltpu.make_async_remote_copy(
                    src_ref=self.source.at[image],
                    dst_ref=self.target.at[image],
                    send_sem=self.send_sems.at[image],
                    recv_sem=self.recv_sems.at[image],
                    device_id=(data, model),
                    device_id_type=MESH,
                ).wait()


class Move:
    def __init__(self, source, target, sem):
        self.copy = pltpu.make_async_copy(source, target, sem)
        self.copy.start()

    def wait(self):
        if self.copy is not None:
            self.copy.wait()
            self.copy = None


def encoder_barrier(images, axes):
    barrier = pltpu.get_barrier_semaphore()
    count = images
    for axis in axes:
        for bit in range(log2_of(lax.axis_size(axis))):
            count += 1
            pl.semaphore_signal(
                barrier, inc=1, device_id=partner(axis, bit)[0], device_id_type=MESH
            )
    for data, model, slot in exchange_partners(images):
        pl.semaphore_signal(barrier, inc=1, device_id=(data, model), device_id_type=MESH)
    pl.semaphore_wait(barrier, count)


def encoder_kernel(images, visible, heads, *refs):
    (
        lengths,
        tokens,
        gain_attn,
        w_query_hbm,
        w_key_hbm,
        w_value_hbm,
        w_out,
        gain_mlp,
        w_up_hbm,
        w_down_hbm,
        w_embed,
        arrived,
        *saved_hbm,
    ) = refs[:24]
    (
        w_query,
        w_key,
        w_value,
        w_up,
        w_down,
        a_s,
        qkv_s,
        e_s,
        inv_s,
        o_own,
        c_s,
        g_s,
        slope_s,
        mid_s,
        low_s,
        embed_full,
        qkv_weights,
        move_sems,
        token_slots,
        out_pair,
        o_pair,
        part_own,
        part_sent,
        part_got,
        embed_slots,
        parts,
        landing,
        total,
        embedded,
        sems,
        swap_sems,
        pair_sems,
    ) = refs[24:]
    count = lax.axis_size("mp")
    index = lax.axis_index("mp")
    block_rows = images * visible
    columns = w_query.shape[1]
    size = columns // heads
    scaling = float(size) ** -0.5
    hidden = w_up.shape[1]
    chunk = 512

    loads = [
        Move(source, target, move_sems.at[position])
        for position, (source, target) in enumerate(
            (
                (w_query_hbm, w_query),
                (w_key_hbm, w_key),
                (w_value_hbm, w_value),
                (w_up_hbm, w_up),
                (w_down_hbm, w_down),
            )
        )
    ]
    saved = [a_s, qkv_s, e_s, inv_s, o_own, c_s, g_s, slope_s, mid_s, low_s, embed_full, qkv_weights]
    stores = []

    def save(*arrays):
        for array in arrays:
            position = [array is one for one in saved].index(True)
            stores.append(Move(array, saved_hbm[position], move_sems.at[len(loads) + position]))

    encoder_barrier(images, ["mp"])
    token_gather = Gather(
        tokens, lambda slot: token_slots.at[slot], sems.at[0], sems.at[1]
    )
    near, far = 0, 1

    def rows_of(slot):
        return pl.ds(pl.multiple_of(slot * block_rows, block_rows), block_rows)

    def pair_copy(which, source, target, bit):
        return pltpu.make_async_remote_copy(
            src_ref=source,
            dst_ref=target,
            send_sem=pair_sems.at[0, which],
            recv_sem=pair_sems.at[1, which],
            device_id=partner("mp", bit)[0],
            device_id_type=MESH,
        )

    out_copy = pair_copy(0, w_out, out_pair.at[columns : 2 * columns], near)

    def o_copy(mine):
        block = index ^ (1 + 2 * mine)
        target = o_pair.at[mine, columns : 2 * columns]
        return pair_copy(1 + mine, o_own.at[:, rows_of(block)], target, near)

    def part_copy(mine):
        return pair_copy(3 + mine, part_sent.at[mine], part_got.at[1 - mine], far)

    def c_copy(mine):
        place = c_s.at[rows_of(index ^ (2 * mine))]
        return pair_copy(5 + mine, place, place, near)

    embed_gather = Gather(w_embed, lambda slot: embed_slots.at[slot], sems.at[6], sems.at[7])
    scatter = Scatter(parts, total, landing, sems.at[8], sems.at[9])
    swap = Exchange(images, embedded, arrived, swap_sems.at[0], swap_sems.at[1])

    token_gather.start()
    out_copy.start()
    token_slots[index] = tokens[...]
    out_pair[:columns, :] = w_out[...]
    embed_slots[index] = w_embed[...]
    for position, weight in enumerate((w_query, w_key, w_value)):
        loads[position].wait()
        qkv_weights[position * columns : (position + 1) * columns, :] = weight[...].T
    save(qkv_weights)

    def attend(step, carry):
        token_gather.arrive_at(step)

        slot = index ^ visit_mask(step, count)
        rows = rows_of(slot)
        normed, scale = norm_parts(token_slots[slot].astype(full_type))
        a_s[rows, :] = (normed * gain_attn[...]).astype(low_type)
        for position in range(3):
            span = slice(position * columns, (position + 1) * columns)
            part = dot_as(qkv_weights[span, :], a_s[rows, :], 1, 1)
            if position == 0:
                part = part * (scaling * LOG2E)
            qkv_s[span, rows] = part.astype(low_type)
        key_row = lax.broadcasted_iota(jnp.int32, (block_rows, block_rows), 0)
        query_row = lax.broadcasted_iota(jnp.int32, (block_rows, block_rows), 1)
        valid = jnp.zeros((block_rows, block_rows), jnp.bool_)
        for image in range(images):
            first = image * visible
            keys = (key_row >= first) & (key_row < first + lengths[slot * images + image])
            valid = valid | (keys & (query_row >= first) & (query_row < first + visible))
        for head in range(heads):
            span = slice(head * size, (head + 1) * size)
            query = qkv_s[span, rows]
            key = qkv_s[columns + head * size : columns + (head + 1) * size, rows]
            value = qkv_s[2 * columns + head * size : 2 * columns + (head + 1) * size, rows]
            scores = jnp.where(valid, dot_as(key, query, 0, 0), masked_score)
            weights = jnp.exp2(scores - jnp.max(scores, axis=0, keepdims=True))
            inverse = 1.0 / jnp.sum(weights, axis=0, keepdims=True)
            weights = weights.astype(low_type)
            e_s[slot * heads + head] = weights
            inv_s[slot * heads + head] = inverse
            mixed = jnp.dot(value, weights, preferred_element_type=full_type)
            o_own[span, rows] = (mixed * inverse).astype(low_type)
        for turn, mine in ((1, 0), (2, 1)):
            @pl.when(step == turn)
            def _():
                o_copy(mine).start()

        for turn, mine in ((0, 0), (3, 1)):
            @pl.when(step == turn)
            def _():
                o_pair[mine, :columns, :] = o_own[:, rows]

        return carry

    def sum_heads(mine):
        o_copy(mine).wait_recv()
        part = dot_as(o_pair[mine], out_pair[...], 0, 0)
        part_own[mine] = part
        part_sent[mine] = part.astype(low_type)
        part_copy(mine).start()

    def middle_of(mine):
        part_copy(1 - mine).wait_recv()
        slot = index ^ (2 * mine)
        middle = token_slots[slot].astype(full_type) + part_own[mine]
        middle = middle + part_got[mine].astype(full_type)
        if mine == 0:
            mid_s[...] = middle
        normed, scale = norm_parts(middle)
        c_s[rows_of(slot), :] = (normed * gain_mlp[...]).astype(low_type)
        c_copy(mine).start()

    lax.fori_loop(0, 2, attend, 0)
    out_copy.wait_recv()
    sum_heads(0)
    lax.fori_loop(2, 4, attend, 0)
    sum_heads(1)
    embed_gather.start()
    save(a_s, qkv_s, e_s, inv_s, o_own)
    for move in loads:
        move.wait()
    total[...] = jnp.zeros_like(total)

    def expand(mask, carry):
        for odd in (1, 3):
            @pl.when(mask == odd)
            def _():
                c_copy(odd // 2).wait_recv()

        rows = rows_of(index ^ mask)
        for first in range(0, hidden, chunk):
            cols = slice(first, first + chunk)
            pre = jnp.dot(c_s[rows, :], w_up[:, cols], preferred_element_type=full_type)
            active, slope = gelu_pair(pre)
            g_s[rows, cols] = active.astype(low_type)
            slope_s[rows, cols] = slope.astype(low_type)
        scatter.put(
            mask, jnp.dot(g_s[rows, :], w_down[...], preferred_element_type=full_type)
        )
        return carry

    middle_of(1)
    lax.fori_loop(2, 4, expand, 0)
    scatter.finish(3)
    middle_of(0)
    lax.fori_loop(0, 2, expand, 0)
    scatter.finish(1)
    save(c_s, g_s, slope_s, mid_s)
    embed_gather.arrive_all()
    width = w_embed.shape[1]
    for slot in range(count):
        embed_full[:, slot * width : (slot + 1) * width] = embed_slots[slot]
    scatter.finish(2)
    low_s[...] = (mid_s[...] + total[...]).astype(low_type)
    out = jnp.dot(low_s[...], embed_full[...], preferred_element_type=full_type)
    embedded[...] = out.astype(low_type).reshape(embedded.shape)
    swap.start()
    save(embed_full, low_s)
    for one in (token_gather, embed_gather, scatter):
        one.drain()
    out_copy.wait_send()
    for mine in range(2):
        for copy in (o_copy(mine), part_copy(mine), c_copy(mine)):
            copy.wait_send()
    for move in stores:
        move.wait()
    swap.finish()


def encode(tokens, lengths, weights, embed_proj):
    gain_attn, w_query, w_key, w_value, w_out, gain_mlp, w_up, w_down = weights
    model_count = lax.axis_size("mp")
    images, visible, width = tokens.shape
    rows = images * visible
    heads = HE // model_count
    columns, hidden = w_query.shape[1], w_up.shape[1]
    out_width = embed_proj.shape[1] * model_count
    every = rows * model_count

    def kernel(*refs):
        encoder_kernel(images, visible, heads, *refs)

    vmem = pl.BlockSpec(memory_space=pltpu.VMEM)
    hbm = pl.BlockSpec(memory_space=pl.ANY)
    shapes = [
        ((images, visible, out_width), low_type),
        ((every, width), low_type),
        ((3 * columns, every), low_type),
        ((model_count * heads, rows, rows), low_type),
        ((model_count * heads, 1, rows), full_type),
        ((columns, every), low_type),
        ((every, width), low_type),
        ((every, hidden), low_type),
        ((every, hidden), low_type),
        ((rows, width), full_type),
        ((rows, width), low_type),
        ((width, out_width), low_type),
        ((3 * columns, width), low_type),
    ]
    return pl.pallas_call(
        kernel,
        out_shape=[jax.ShapeDtypeStruct(shape, kind) for shape, kind in shapes],
        in_specs=[pl.BlockSpec(memory_space=pltpu.SMEM)]
        + [vmem] * 2
        + [hbm] * 3
        + [vmem] * 2
        + [hbm] * 2
        + [vmem],
        out_specs=[vmem] + [hbm] * (len(shapes) - 1),
        scratch_shapes=[
            pltpu.VMEM((width, columns), low_type),
            pltpu.VMEM((width, columns), low_type),
            pltpu.VMEM((width, columns), low_type),
            pltpu.VMEM((width, hidden), low_type),
            pltpu.VMEM((hidden, width), low_type),
        ]
        + [pltpu.VMEM(shape, kind) for shape, kind in shapes[1:]]
        + [
            pltpu.SemaphoreType.DMA((5 + len(shapes),)),
            pltpu.VMEM((model_count, rows, width), low_type),
            pltpu.VMEM((2 * columns, width), low_type),
            pltpu.VMEM((2, 2 * columns, rows), low_type),
            pltpu.VMEM((2, rows, width), full_type),
            pltpu.VMEM((2, rows, width), low_type),
            pltpu.VMEM((2, rows, width), low_type),
            pltpu.VMEM((model_count,) + embed_proj.shape, low_type),
            pltpu.VMEM((model_count - 1, rows, width), low_type),
            pltpu.VMEM((model_count - 1, rows, width), low_type),
            pltpu.VMEM((rows, width), full_type),
            pltpu.VMEM((images, visible, out_width), low_type),
            pltpu.SemaphoreType.DMA((10, model_count)),
            pltpu.SemaphoreType.DMA((2, images)),
            pltpu.SemaphoreType.DMA((2, 7)),
        ],
        compiler_params=pltpu.CompilerParams(
            collective_id=1, has_side_effects=True, vmem_limit_bytes=60 * 2**20
        ),
    )(
        lengths,
        tokens.reshape(rows, width),
        gain_attn.reshape(1, -1),
        w_query,
        w_key,
        w_value,
        w_out,
        gain_mlp.reshape(1, -1),
        w_up,
        w_down,
        embed_proj,
    )


EARLY_DOWN, EARLY_UP, UP_FIRST = True, False, True
SUM_ORDERS = {
    "attn": ["crossed"],
    "dup": ["spread", "spreadz", "all", "spreadz"],
    "ddn": ["spread", "spread", "spread", "spread"],
    "pred": ["all"],
    "emb": ["spread", "spread"],
    "dn": ["Z", "Y", "Y", "Y"],
    "up": ["Y", "Y", "Y", "Y"],
    "oq": ["Y", "Y", "Y", "Y"],
}
PLAN = {
    "a3": [
        "pred0",
        "ddn0",
        "ddn1",
        "ddn2",
        "ddn3",
        "dup0",
        "dup1",
        "dup2",
        "dup3",
    ],
    "a4": [
        "ddn0",
        "dup1",
        "pred0",
        "ddn1",
    ],
    "a5": [
        "dup3",
        "dup2",
        "ddn2",
        "attn0",
        "ddn0",
        "ddn3",
    ],
    "f1": [
        "ddn1",
        "dup1",
        "emb0",
        "emb1",
        "dup0",
    ],
    "f2": [
        "pred0",
        "ddn2",
        "dup3",
    ],
    "f3": [
        "dup2",
        "ddn3",
    ],
    "b0": [
        "ddn0",
        "dup1",
        "ddn1",
        "dup0",
        "emb0",
        "pred0",
        "dup2",
        "ddn2",
        "emb1",
        "dup3",
        "ddn3",
    ],
    "s2": [
        "attn0",
        "ddn0",
        "dup1",
    ],
    "s3": [
        "ddn1",
        "ddn2",
        "dup3",
    ],
    "b2": [
        "ddn3",
        "dn0",
        "dn1",
    ],
    "b4": [
        "dup0",
        "emb0",
        "pred0",
    ],
    "b5": [
        "dup2",
        "emb1",
        "dn2",
        "dup0",
    ],
    "t2": [
        "attn0",
        "dn3",
        "dn1",
        "dn0",
        "up0",
    ],
    "b6": [
        "emb0",
        "emb1",
        "dn2",
    ],
    "b7": [
        "up1",
    ],
    "tail": [
        "dn3",
        "attn0",
        "up2",
        "dn1",
        "emb0",
        "up0",
        "emb1",
        "norm",
        "up3",
        "dn2",
        "up1",
        "norm",
        "dn0",
        "dn3",
        "up2",
        "o",
        "up0",
        "up3",
        "q",
        "up1",
        "up2",
        "o",
        "k",
        "up3",
        "q",
        "v",
        "o",
        "k",
        "attn0",
        "norm",
        "q",
        "v",
        "norm",
        "k",
        "v",
        "norm",
    ],
}


class Bulk:
    def __init__(self, one):
        self.one, self.stage = one, None

    def start(self):
        self.one.start(0)
        self.stage = 0

    def done(self):
        return self.stage == len(self.one.stages)

    def advance(self):
        if self.stage is None or self.done():
            return
        self.one.finish(self.stage)
        self.stage += 1
        if not self.done():
            self.one.start(self.stage)


def back_kernel(plan, *refs):
    images, visible, enc_heads, heads, side, pieces, embed_piece, scopes = plan
    refs = list(refs)

    def take(number):
        head = refs[:number]
        del refs[:number]
        return head

    (
        dist_ref,
        arrived,
        order_ref,
        keep_ref,
        dec_gain_attn,
        dec_gain_mlp,
        mask_token,
        tokens,
        gain_attn,
        gain_mlp,
    ) = take(10)
    dec_hbm = take(8)
    enc_hbm = take(15)
    decoded, grad_tokens, norm_wide, norm_thin, rows_out, cols_out, dec_out, embed_out = take(8)
    move_sems, decoded_sems = take(2)
    grad_arrived, dec_packed, small = take(3)
    demb_own, demb_slots, db_s, total = take(4)
    parts_mlp, landing_mlp, parts_attn, landing_attn = take(4)
    sems, swap_sems = take(2)
    data_count, model_count = lax.axis_size("dp"), lax.axis_size("mp")
    data_bits, model_bits = log2_of(data_count), log2_of(model_count)
    row_packed, col_packed, embed_packed = take(3)
    row_bufs = [row_packed] + take(data_bits)
    col_bufs = [col_packed] + take(data_bits)
    dec_bufs = [dec_packed] + take(data_bits + model_bits)
    embed_bufs = [embed_packed] + take(data_bits + model_bits)
    wide_acc, wide_got, thin_acc, thin_got = take(4)
    row_sems, col_sems, dec_sems, embed_sems, norm_sems = take(5)
    assert not refs

    index = lax.axis_index("mp")
    count = model_count
    enc_stages = [("dp", bit) for bit in range(data_bits)]
    late_stages = enc_stages[1:] + enc_stages[:1]
    model_stages = [("mp", bit) for bit in range(model_bits)]
    all_stages = model_stages + enc_stages
    near, far = model_stages[:1], model_stages[1:]
    orders = {
        "Y": enc_stages,
        "Z": late_stages,
        "all": all_stages,
        "crossed": model_stages + late_stages,
        "spread": near + enc_stages + far,
        "spreadz": near + late_stages + far,
    }
    sums = {}

    def pump(point):
        for name in PLAN.get(point, ()):
            if name in sums:
                sums[name].advance()

    def pump_at(step, point):
        for turn in range(count):
            if PLAN.get(point + str(turn)):
                @pl.when(step == turn)
                def _():
                    pump(point + str(turn))

    chunk = 512

    def bulk(stages, bufs, axis, first, extent, pair, cut):
        window = [slice(None), slice(None)]
        window[axis - 1] = pl.ds(first, extent)
        return Bulk(HalvingSum(stages, bufs, tuple(window), pair.at[0, cut], pair.at[1, cut]))

    limits = [pieces[0][0]] + [piece[0] for piece in pieces[4:]] + [dec_packed.shape[1]]
    dec_rows = []
    for kind, first, last in zip(("attn", "dup", "ddn", "pred"), limits, limits[1:]):
        names = SUM_ORDERS[kind]
        extent = (last - first) // len(names)
        for cut, order in enumerate(names):
            begin = first + cut * extent
            sums[kind + str(cut)] = bulk(
                orders[order], dec_bufs, 1, begin, extent, dec_sems, len(dec_rows)
            )
            dec_rows.append((begin, begin + extent, orders[order]))

    def start(kind):
        for cut in range(len(SUM_ORDERS[kind])):
            sums[kind + str(cut)].start()

    def store_dec(which, product):
        offset, height, span, tiles = pieces[which]
        for column in range(model_count):
            for tile in range(tiles):
                lanes = min(LANES, span - tile * LANES)
                first = column * span + tile * LANES
                block = product[:, first : first + lanes].astype(low_type)
                base = offset + tile * height
                for begin, end, order in dec_rows:
                    low_row, high_row = max(begin, base), min(end, base + height)
                    if low_row >= high_row:
                        continue
                    for row in range(data_count):
                        shift = row * height - base
                        dec_packed[spot_of(row, column, order), low_row:high_row, :lanes] = block[
                            low_row + shift : high_row + shift, :
                        ]

    swap = Exchange(images, grad_arrived, demb_own, swap_sems.at[0], swap_sems.at[1])

    def decoder(
        w_out,
        xs,
        qkv_weights,
        a_s,
        qkv_s,
        e_s,
        inv_s,
        o_s,
        dy_s,
        db_dec,
        do_s,
    ):
        length = side * side
        width = w_out.shape[0]
        size = width // heads
        scaling = float(size) ** -0.5
        place = lax.broadcasted_iota(jnp.int32, (length, visible), 0)
        turn = lax.broadcasted_iota(jnp.int32, (length, visible), 1)
        out_move = Move(dec_hbm[3], w_out, move_sems.at[3])

        def turned(*inputs):
            turned_moves = [
                Move(dec_hbm[position], one, move_sems.at[position])
                for position, one in enumerate(inputs)
            ]
            encoder_barrier(images, ["mp", "dp"])
            for position, one in enumerate(inputs):
                turned_moves[position].wait()
                qkv_weights[position * width : (position + 1) * width, :] = one[...].T

        pl.run_scoped(turned, *scopes[3])

        def picks(image):
            order = jnp.zeros((1, visible), jnp.int32)
            flags = jnp.zeros((1, length), jnp.int32)
            for one in range(images):
                order = jnp.where(image == one, order_ref[one : one + 1, :visible], order)
                flags = jnp.where(image == one, keep_ref[one : one + 1, :], flags)
            kept = jnp.sum(flags, axis=1, keepdims=True)
            return jnp.where((order == place) & (turn < kept), 1.0, 0.0)

        def rows_of(image):
            if isinstance(image, int):
                return slice(image * length, (image + 1) * length)
            return pl.ds(pl.multiple_of(image * length, length), length)

        def dense(w_up, w_down, w_pred, cotangent, mid_s, c_s, g_s, du_s, low_s, dm_s, staged):
            hidden = w_up.shape[1]
            second_moves = [
                Move(source, target, move_sems.at[4 + position])
                for position, (source, target) in enumerate(
                    zip(dec_hbm[4:], (w_up, w_down, w_pred, cotangent))
                )
            ]
            out_move.wait()
            for move in second_moves:
                move.wait()
            small[...] = jnp.zeros_like(small)

            def stage_copy(image):
                return pltpu.make_async_copy(staged, decoded.at[image], decoded_sems.at[image])

            def one_image(image, carry):
                rows = rows_of(image)
                pick = picks(image)
                hidden_rows = 1.0 - jnp.sum(pick, axis=1, keepdims=True)
                quarter = width // 4
                lane = lax.broadcasted_iota(jnp.int32, (side, quarter), 1).astype(full_type)
                line = lax.broadcasted_iota(jnp.int32, (side, quarter), 0).astype(full_type)
                angle = dist_ref[image] * line * jnp.exp(lane * (-math.log(10000.0) / quarter))
                table = jnp.concatenate([jnp.sin(angle), jnp.cos(angle)], axis=1)
                by_row = jnp.broadcast_to(table[:, None, :], (side, side, 2 * quarter))
                by_col = jnp.broadcast_to(table[None, :, :], (side, side, 2 * quarter))
                codes = jnp.concatenate(
                    [by_row.reshape(length, 2 * quarter), by_col.reshape(length, 2 * quarter)],
                    axis=1,
                )
                start = jnp.dot(
                    pick.astype(low_type), arrived[image], preferred_element_type=full_type
                )
                start = start + hidden_rows * mask_token[...] + codes
                xs[rows, :] = start
                normed, scale = norm_parts(start)
                a_s[rows, :] = (normed * dec_gain_attn[...]).astype(low_type)
                for position in range(3):
                    span = slice(position * width, (position + 1) * width)
                    part = dot_as(qkv_weights[span, :], a_s[rows, :], 1, 1)
                    if position == 0:
                        part = part * (scaling * LOG2E)
                    qkv_s[span, rows] = part.astype(low_type)

                def one_head(head, inner):
                    span = pl.multiple_of(head * size, size)
                    query = qkv_s[pl.ds(span, size), rows]
                    key = qkv_s[pl.ds(width + span, size), rows]
                    value = qkv_s[pl.ds(2 * width + span, size), rows]
                    scores = dot_as(key, query, 0, 0)
                    weights = jnp.exp2(scores - jnp.max(scores, axis=0, keepdims=True))
                    inverse = 1.0 / jnp.sum(weights, axis=0, keepdims=True)
                    weights = weights.astype(low_type)
                    e_s[image * heads + head] = weights
                    inv_s[image * heads + head] = inverse
                    mixed = jnp.dot(value, weights, preferred_element_type=full_type)
                    o_s[pl.ds(span, size), rows] = (mixed * inverse).astype(low_type)
                    return inner

                lax.fori_loop(0, heads, one_head, 0, unroll=heads)

                middle = start + dot_as(o_s[:, rows], w_out[...], 0, 0)
                mid_s[...] = middle
                normed, scale = norm_parts(middle)
                c_s[rows, :] = (normed * dec_gain_mlp[...]).astype(low_type)
                for first in range(0, hidden, chunk):
                    cols = slice(first, first + chunk)
                    pre = jnp.dot(c_s[rows, :], w_up[:, cols], preferred_element_type=full_type)
                    active, slope = gelu_pair(pre)
                    g_s[rows, cols] = active.astype(low_type)
                    du_s[rows, cols] = slope.astype(low_type)
                outputs = middle + jnp.dot(
                    g_s[rows, :], w_down[...], preferred_element_type=full_type
                )
                low_s[rows, :] = outputs.astype(low_type)

                @pl.when(image > 0)
                def _():
                    stage_copy(image - 1).wait()

                staged[...] = jnp.dot(
                    low_s[rows, :], w_pred[...], preferred_element_type=full_type
                )
                stage_copy(image).start()

                grad_out = dot_as(cotangent[image], w_pred[...], 1, 1)
                dm_s[rows, :] = grad_out.astype(low_type)
                for first in range(0, hidden, chunk):
                    cols = slice(first, first + chunk)
                    grad_active = dot_as(dm_s[rows, :], w_down[cols, :], 1, 1)
                    du_s[rows, cols] = (grad_active * du_s[rows, cols].astype(full_type)).astype(
                        low_type
                    )
                grad_second = dot_as(du_s[rows, :], w_up[...], 1, 1)
                normed, scale = norm_parts(mid_s[...])
                small[1:2, :] += jnp.sum(grad_second * normed, axis=0, keepdims=True)
                grad_middle = grad_out + norm_back(
                    normed, scale, grad_second * dec_gain_mlp[...]
                )
                dy_s[rows, :] = grad_middle
                db_dec[rows, :] = grad_middle.astype(low_type)
                return carry

            lax.fori_loop(0, images, one_image, 0)
            all_pixels = cotangent[...].reshape(-1, cotangent.shape[2])
            store_dec(6, dot_as(low_s[...], all_pixels, 0, 0))
            start("pred")
            store_dec(5, dot_as(g_s[...], dm_s[...], 0, 0))
            start("ddn")
            pump("a1")
            store_dec(4, dot_as(c_s[...], du_s[...], 0, 0))
            start("dup")
            pump("a2")
            stage_copy(images - 1).wait()

        pl.run_scoped(dense, *scopes[1])

        for image in range(images):
            rows = rows_of(image)
            do_s[...] = dot_as(w_out[...], db_dec[rows, :], 1, 1)

            def back_head(head, inner):
                span = pl.multiple_of(head * size, size)
                query = qkv_s[pl.ds(span, size), rows]
                key = qkv_s[pl.ds(width + span, size), rows]
                value = qkv_s[pl.ds(2 * width + span, size), rows]
                weights = e_s[image * heads + head]
                grad_full = do_s[pl.ds(span, size), :] * (inv_s[image * heads + head] * scaling)
                mixed = o_s[pl.ds(span, size), rows].astype(full_type)
                shift = jnp.sum(grad_full * mixed, axis=0, keepdims=True)
                grad_low = grad_full.astype(low_type)
                grad_probs = dot_as(value, grad_low, 0, 0)
                grad_scores = (weights.astype(full_type) * (grad_probs - shift)).astype(low_type)
                grad_value = dot_as(grad_low, weights, 1, 1) * (1.0 / scaling)
                grad_query = jnp.dot(key, grad_scores, preferred_element_type=full_type)
                grad_key = dot_as(query, grad_scores, 1, 1) * (1.0 / (scaling * LOG2E))
                qkv_s[pl.ds(span, size), rows] = grad_query.astype(low_type)
                qkv_s[pl.ds(width + span, size), rows] = grad_key.astype(low_type)
                qkv_s[pl.ds(2 * width + span, size), rows] = grad_value.astype(low_type)
                return inner

            lax.fori_loop(0, heads, back_head, 0, unroll=heads)

            grad_normed = dot_as(qkv_s[:, rows], qkv_weights[...], 0, 0)
            normed, scale = norm_parts(xs[rows, :])
            small[0:1, :] += jnp.sum(grad_normed * normed, axis=0, keepdims=True)
            grad_start = dy_s[rows, :] + norm_back(
                normed, scale, grad_normed * dec_gain_attn[...]
            )
            pick = picks(image)
            hidden_rows = 1.0 - jnp.sum(pick, axis=1, keepdims=True)
            small[2:3, :] += jnp.sum(hidden_rows * grad_start, axis=0, keepdims=True)
            grad_arrived[image] = dot_as(
                pick.astype(low_type), grad_start.astype(low_type), 0, 0
            ).astype(low_type)
            if image == 0:
                pump("a3")
        swap.start()
        for position in range(3):
            grads = qkv_s[position * width : (position + 1) * width, :]
            store_dec(position, dot_as(a_s[...], grads, 0, 1))
        store_dec(3, jnp.dot(o_s[...], db_dec[...], preferred_element_type=full_type))
        start("attn")
        pump("a4")

    pl.run_scoped(decoder, *scopes[0])
    thin_acc[0] = small[...]

    def encoder(*local):
        local = list(local)
        loaded = local[:15]
        (
            w_out,
            w_up,
            w_down,
            a_s,
            qkv_s,
            e_s,
            inv_s,
            o_own,
            c_s,
            g_s,
            slope_s,
            mid_s,
            low_s,
            embed_full,
            qkv_weights,
        ) = loaded
        dm_s, du_s, dqkv_s, dy_s, do_s = local[15:]
        block_rows = images * visible
        columns = w_out.shape[0]
        size = columns // enc_heads
        scaling = float(size) ** -0.5
        hidden, width = w_down.shape
        moves = {}
        for position in (13, 2, 10, 1, 9, 11, 8, 12, 0, 4, 5, 6, 7, 14, 3):
            moves[position] = Move(enc_hbm[position], loaded[position], move_sems.at[8 + position])

        def ready(*arrays):
            for array in arrays:
                moves[[array is one for one in loaded].index(True)].wait()

        def cut_sums(kind, bufs, axis, extent, pair, base=0):
            for cut, order in enumerate(SUM_ORDERS[kind]):
                sums[kind + str(cut)] = bulk(
                    orders[order], bufs, axis, cut * extent, extent, pair, base + cut
                )

        embed_cuts = len(SUM_ORDERS["emb"])
        embed_part = embed_packed.shape[1] // embed_cuts
        cut_sums("emb", embed_bufs, 1, embed_part, embed_sems)
        up_part = hidden // len(SUM_ORDERS["up"])
        down_part = hidden // len(SUM_ORDERS["dn"])
        cut_sums("up", row_bufs, 2, up_part, row_sems)
        cut_sums("dn", col_bufs, 1, down_part, col_sems)
        out_order, *qkv_orders = (orders[one] for one in SUM_ORDERS["oq"])
        for cut, name in enumerate("qkv"):
            sums[name] = bulk(
                qkv_orders[cut],
                row_bufs,
                2,
                hidden + cut * columns,
                columns,
                row_sems,
                len(SUM_ORDERS["up"]) + cut,
            )
        sums["o"] = bulk(
            out_order, col_bufs, 1, hidden, columns, col_sems, len(SUM_ORDERS["dn"])
        )

        swap.finish()
        demb_gather = Gather(demb_own, lambda slot: demb_slots.at[slot], sems.at[0], sems.at[1])
        demb_gather.start()
        demb_slots[index] = demb_own[...]
        ready(low_s)
        offset, high, span, tiles = embed_piece
        product = dot_as(low_s[...], demb_own[...].reshape(block_rows, -1), 0, 0)
        for column in range(model_count):
            for row in range(data_count):
                for cut, order in enumerate(SUM_ORDERS["emb"]):
                    spot = spot_of(row, column, orders[order])
                    for tile in range(tiles):
                        lanes = min(LANES, span - tile * LANES)
                        first = column * span + tile * LANES
                        base = tile * high
                        begin = max(base, cut * embed_part)
                        end = min(base + high, (cut + 1) * embed_part)
                        if begin < end:
                            shift = row * high - base
                            embed_packed[spot, begin:end, :lanes] = product[
                                begin + shift : end + shift, first : first + lanes
                            ].astype(low_type)
        start("emb")
        pump("a5")
        ready(embed_full, w_down, slope_s)

        def rows_of(slot):
            return pl.ds(pl.multiple_of(slot * block_rows, block_rows), block_rows)

        def first_back(step, carry):
            demb_gather.arrive_at(step)
            pump_at(step, "f")
            mask = visit_mask(step, count)
            slot = index ^ mask
            rows = rows_of(slot)
            grad_rows = demb_slots[slot].reshape(block_rows, -1)
            grad_out = dot_as(grad_rows, embed_full[...], 1, 1)

            @pl.when(mask == 0)
            def _():
                dy_s[...] = grad_out

            dm_s[rows, :] = grad_out.astype(low_type)
            for first in range(0, hidden, chunk):
                cols = slice(first, first + chunk)
                grad_active = dot_as(dm_s[rows, :], w_down[cols, :], 1, 1)
                du_s[rows, cols] = (grad_active * slope_s[rows, cols].astype(full_type)).astype(
                    low_type
                )
            return carry

        lax.fori_loop(0, count, first_back, 0)

        def store_rows(product, first, stages):
            high = width // data_count
            for row in range(data_count):
                row_packed[spot_of(row, 0, stages), :, first : first + product.shape[1]] = (
                    product[row * high : (row + 1) * high, :].astype(low_type)
                )

        def store_cols(product, first, stages):
            wide = width // data_count
            for col in range(data_count):
                col_packed[
                    spot_of(col, 0, stages), first : first + product.shape[0], :wide
                ] = product[:, col * wide : (col + 1) * wide].astype(low_type)

        def down_grads():
            ready(g_s)
            for cut, order in enumerate(SUM_ORDERS["dn"]):
                cols = slice(cut * down_part, (cut + 1) * down_part)
                product = dot_as(g_s[:, cols], dm_s[...], 0, 0)
                store_cols(product, cut * down_part, orders[order])
                sums["dn" + str(cut)].start()
            pump("b0" if EARLY_DOWN else "b3")

        def up_grads():
            ready(c_s)
            for cut, order in enumerate(SUM_ORDERS["up"]):
                cols = slice(cut * up_part, (cut + 1) * up_part)
                product = dot_as(c_s[...], du_s[:, cols], 0, 0)
                store_rows(product, cut * up_part, orders[order])
                sums["up" + str(cut)].start()
            pump("b1" if EARLY_UP else "b4")

        if EARLY_DOWN:
            down_grads()
        if EARLY_UP:
            up_grads()
        ready(w_up)
        scatter = Scatter(parts_mlp, total, landing_mlp, sems.at[2], sems.at[3])
        total[...] = jnp.zeros_like(total)

        def second_back(step, carry):
            pump_at(step, "s")
            mask = count - 1 - step
            rows = rows_of(index ^ mask)
            scatter.put(mask, dot_as(du_s[rows, :], w_up[...], 1, 1))
            return carry

        lax.fori_loop(0, count, second_back, 0)
        for bit in range(model_bits - 1):
            scatter.finish_bit(bit)

        pump("b2")
        if not EARLY_DOWN:
            down_grads()
        if not EARLY_UP and UP_FIRST:
            up_grads()
        ready(mid_s)
        scatter.finish_bit(model_bits - 1)

        normed, scale = norm_parts(mid_s[...])
        grad_second = total[...]
        wide_acc[0, 1:2, :] = jnp.sum(grad_second * normed, axis=0, keepdims=True)
        grad_middle = dy_s[...] + norm_back(normed, scale, grad_second * gain_mlp[...])
        dy_s[...] = grad_middle
        db_s[rows_of(index), :] = grad_middle.astype(low_type)
        db_gather = Gather(None, lambda slot: db_s.at[rows_of(slot)], sems.at[4], sems.at[5])
        db_gather.start()
        pump("b5")
        if not EARLY_UP and not UP_FIRST:
            up_grads()
        ready(w_out, qkv_s, e_s, inv_s, o_own, qkv_weights)
        second_scatter = Scatter(parts_attn, total, landing_attn, sems.at[6], sems.at[7])
        total[...] = jnp.zeros_like(total)

        def third_back(step, carry):
            db_gather.arrive_at(step)
            pump_at(step, "t")
            mask = visit_mask(step, count)
            slot = index ^ mask
            rows = rows_of(slot)
            do_s[...] = dot_as(w_out[...], db_s[rows, :], 1, 1)
            for head in range(enc_heads):
                span = slice(head * size, (head + 1) * size)
                key_span = slice(columns + head * size, columns + (head + 1) * size)
                value_span = slice(2 * columns + head * size, 2 * columns + (head + 1) * size)
                query, key, value = qkv_s[span, rows], qkv_s[key_span, rows], qkv_s[value_span, rows]
                weights = e_s[slot * enc_heads + head]
                grad_full = do_s[span, :] * (inv_s[slot * enc_heads + head] * scaling)
                shift = jnp.sum(
                    grad_full * o_own[span, rows].astype(full_type), axis=0, keepdims=True
                )
                grad_low = grad_full.astype(low_type)
                grad_probs = dot_as(value, grad_low, 0, 0)
                grad_scores = (weights.astype(full_type) * (grad_probs - shift)).astype(low_type)
                grad_value = dot_as(grad_low, weights, 1, 1) * (1.0 / scaling)
                grad_query = jnp.dot(key, grad_scores, preferred_element_type=full_type)
                grad_key = dot_as(query, grad_scores, 1, 1) * (1.0 / (scaling * LOG2E))
                dqkv_s[span, rows] = grad_query.astype(low_type)
                dqkv_s[key_span, rows] = grad_key.astype(low_type)
                dqkv_s[value_span, rows] = grad_value.astype(low_type)
            second_scatter.put(mask, dot_as(dqkv_s[:, rows], qkv_weights[...], 0, 0))
            return carry

        lax.fori_loop(0, count, third_back, 0)
        for bit in range(model_bits - 1):
            second_scatter.finish_bit(bit)
        pump("b6")
        store_cols(
            jnp.dot(o_own[...], db_s[...], preferred_element_type=full_type), hidden, out_order
        )
        sums["o"].start()
        ready(a_s)
        for cut, order in enumerate(qkv_orders):
            span = slice(cut * columns, (cut + 1) * columns)
            product = dot_as(a_s[...], dqkv_s[span, :], 0, 1)
            store_rows(product, hidden + cut * columns, order)
            sums["qkv"[cut]].start()
        pump("b7")
        second_scatter.finish_bit(model_bits - 1)
        normed, scale = norm_parts(tokens[...].astype(full_type))
        grad_normed = total[...]
        wide_acc[0, 0:1, :] = jnp.sum(grad_normed * normed, axis=0, keepdims=True)
        grad_tokens[...] = dy_s[...] + norm_back(normed, scale, grad_normed * gain_attn[...])

        def norm_copies(stage):
            peer = partner(*all_stages[stage])[0]
            return [
                pltpu.make_async_remote_copy(
                    src_ref=acc.at[stage],
                    dst_ref=got.at[stage],
                    send_sem=norm_sems.at[0, kind, stage],
                    recv_sem=norm_sems.at[1, kind, stage],
                    device_id=peer,
                    device_id_type=MESH,
                )
                for kind, (acc, got) in enumerate(((wide_acc, wide_got), (thin_acc, thin_got)))
            ]

        def norm_step(turn):
            for copy in norm_copies(turn):
                copy.wait()
            wide_acc[turn + 1] = wide_acc[turn] + wide_got[turn]
            thin_acc[turn + 1] = thin_acc[turn] + thin_got[turn]
            if turn + 1 < len(all_stages):
                for copy in norm_copies(turn + 1):
                    copy.start()

        for copy in norm_copies(0):
            copy.start()
        turn = 0
        for name in PLAN["tail"]:
            if name == "norm":
                if turn < len(all_stages):
                    norm_step(turn)
                    turn += 1
            elif name in sums:
                sums[name].advance()
        for later in range(turn, len(all_stages)):
            norm_step(later)
        for one in sums.values():
            while not one.done():
                one.advance()
        norm_wide[...] = wide_acc[len(all_stages)]
        norm_thin[...] = thin_acc[len(all_stages)]
        for one in (demb_gather, scatter, db_gather, second_scatter):
            one.drain()


    pl.run_scoped(encoder, *scopes[2])
    rows_out[...] = row_bufs[-1][0]
    cols_out[...] = col_bufs[-1][0]
    dec_out[...] = dec_bufs[-1][0]
    embed_out[...] = embed_bufs[-1][0]


def unpack_kernel(widths, dec_list, embed_list, *refs):
    hidden, columns, wide = widths
    grad_tokens, norm_wide, norm_thin, rows_in, cols_in, dec_in, embed_in = refs[:7]
    out_tokens, g_query, g_key, g_value, g_up, g_out, g_down, g_embed = refs[7:15]
    small = refs[15:20]
    dec_outs = refs[20:]
    out_tokens[...] = grad_tokens[...]
    g_up[...] = rows_in[:, :hidden].astype(full_type)
    for position, out in enumerate((g_query, g_key, g_value)):
        first = hidden + position * columns
        out[...] = rows_in[:, first : first + columns].astype(full_type)
    g_down[...] = cols_in[:hidden, :wide].astype(full_type)
    g_out[...] = cols_in[hidden : hidden + columns, :wide].astype(full_type)
    for position in range(2):
        small[position][...] = norm_wide[position : position + 1, :]
    for position in range(3):
        small[2 + position][...] = norm_thin[position : position + 1, :]
    for outs, pieces, source in (([g_embed], embed_list, embed_in), (dec_outs, dec_list, dec_in)):
        for out, (offset, rows, width, tiles) in zip(outs, pieces):
            for tile in range(tiles):
                lanes = min(LANES, width - tile * LANES)
                block = source[offset + tile * rows : offset + (tile + 1) * rows, :lanes]
                out[:, tile * LANES : tile * LANES + lanes] = block.astype(full_type)


def decode_and_back(
    arrived,
    grid_order,
    grid_keep,
    ground_dist,
    dec_weights,
    mask_token,
    pred_proj,
    cotangent,
    tokens,
    weights,
    saved,
    embed_proj,
):
    gain_attn, w_query, w_key, w_value, w_out, gain_mlp, w_up, w_down = weights
    (dec_gain_attn, dec_query, dec_key, dec_value, dec_proj, dec_gain_mlp, dec_up, dec_down) = (
        dec_weights
    )
    data_count, model_count = lax.axis_size("dp"), lax.axis_size("mp")
    data_bits, model_bits = log2_of(data_count), log2_of(model_count)
    images, visible, width = tokens.shape
    rows = images * visible
    every = rows * model_count
    enc_heads = HE // model_count
    columns, hidden = w_query.shape[1], w_up.shape[1]
    out_width = embed_proj.shape[1] * model_count
    length, pixels = cotangent.shape[1:]
    grid_rows = images * length
    dec_hidden = dec_up.shape[1]
    matrices = [dec_query, dec_key, dec_value, dec_proj, dec_up, dec_down, pred_proj]
    pieces, height = dec_pieces(data_count, model_count, [one.shape for one in matrices])
    embed_pieces, embed_height = dec_pieces(data_count, model_count, [(width, out_width)])
    high, wide = width // data_count, width // data_count
    wide_pad = -(-wide // LANES) * LANES
    devices = data_count * model_count
    stages = data_bits + model_bits
    dec_cuts = sum(len(SUM_ORDERS[kind]) for kind in ("attn", "dup", "ddn", "pred"))
    row_shape = (high, hidden + 3 * columns)
    col_shape = (hidden + columns, wide_pad)
    vmem = pl.BlockSpec(memory_space=pltpu.VMEM)
    hbm = pl.BlockSpec(memory_space=pl.ANY)
    low = lambda *shape: pltpu.VMEM(shape, low_type)
    full = lambda *shape: pltpu.VMEM(shape, full_type)
    loaded = [w_out, w_up, w_down, *saved]
    turned_scope = [low(out_width, out_width)] * 3
    attn_scope = [
        low(out_width, out_width),
        full(grid_rows, out_width),
        low(3 * out_width, out_width),
        low(grid_rows, out_width),
        low(3 * out_width, grid_rows),
        low(images * HD, length, length),
        full(images * HD, 1, length),
        low(out_width, grid_rows),
        full(grid_rows, out_width),
        low(grid_rows, out_width),
        full(out_width, length),
    ]
    dense_scope = [
        low(out_width, dec_hidden),
        low(dec_hidden, out_width),
        low(out_width, pixels),
        low(images, length, pixels),
        full(length, out_width),
        low(grid_rows, out_width),
        low(grid_rows, dec_hidden),
        low(grid_rows, dec_hidden),
        low(grid_rows, out_width),
        low(grid_rows, out_width),
        full(length, pixels),
    ]
    enc_scope = [pltpu.VMEM(one.shape, one.dtype) for one in loaded] + [
        low(every, width),
        low(every, hidden),
        low(3 * columns, every),
        full(rows, width),
        full(columns, rows),
    ]
    plan = (
        images,
        visible,
        enc_heads,
        HD,
        SIDE,
        pieces,
        embed_pieces[0],
        (attn_scope, dense_scope, enc_scope, turned_scope),
    )

    def kernel(*refs):
        back_kernel(plan, *refs)

    outs = [
        (cotangent.shape, full_type),
        ((rows, width), full_type),
        ((2, width), full_type),
        ((3, out_width), full_type),
        (row_shape, low_type),
        (col_shape, low_type),
        ((height, LANES), low_type),
        ((embed_height, LANES), low_type),
    ]
    scratch = [
        pltpu.SemaphoreType.DMA((8 + len(loaded),)),
        pltpu.SemaphoreType.DMA((images,)),
        low(images, visible, out_width),
        low(devices, height, LANES),
        full(3, out_width),
        low(images, visible, out_width),
        low(model_count, images, visible, out_width),
        low(every, width),
        full(rows, width),
        low(model_count - 1, rows, width),
        low(model_count - 1, rows, width),
        low(model_count - 1, rows, width),
        low(model_count - 1, rows, width),
        pltpu.SemaphoreType.DMA((8, model_count)),
        pltpu.SemaphoreType.DMA((2, images)),
        low(data_count, *row_shape),
        low(data_count, *col_shape),
        low(devices, embed_height, LANES),
    ]
    scratch += [low(data_count >> (bit + 1), *row_shape) for bit in range(data_bits)]
    scratch += [low(data_count >> (bit + 1), *col_shape) for bit in range(data_bits)]
    scratch += [low(devices >> (bit + 1), height, LANES) for bit in range(stages)]
    scratch += [low(devices >> (bit + 1), embed_height, LANES) for bit in range(stages)]
    for shape in ((2, width), (3, out_width)):
        scratch += [full(stages + 1, *shape), full(stages, *shape)]
    scratch += [
        pltpu.SemaphoreType.DMA((2, len(SUM_ORDERS["up"]) + 3, data_bits)),
        pltpu.SemaphoreType.DMA((2, len(SUM_ORDERS["dn"]) + 1, data_bits)),
        pltpu.SemaphoreType.DMA((2, dec_cuts, stages)),
        pltpu.SemaphoreType.DMA((2, len(SUM_ORDERS["emb"]), stages)),
        pltpu.SemaphoreType.DMA((2, 2, stages)),
    ]
    results = pl.pallas_call(
        kernel,
        out_shape=[jax.ShapeDtypeStruct(shape, kind) for shape, kind in outs],
        in_specs=[pl.BlockSpec(memory_space=pltpu.SMEM)] + [vmem] * 9 + [hbm] * (8 + len(loaded)),
        out_specs=[hbm] + [vmem] * (len(outs) - 1),
        scratch_shapes=scratch,
        compiler_params=pltpu.CompilerParams(
            collective_id=2, has_side_effects=True, vmem_limit_bytes=255 * 2**18
        ),
    )(
        ground_dist,
        arrived,
        grid_order,
        grid_keep,
        dec_gain_attn.reshape(1, -1),
        dec_gain_mlp.reshape(1, -1),
        mask_token.reshape(1, -1),
        tokens.reshape(rows, width),
        gain_attn.reshape(1, -1),
        gain_mlp.reshape(1, -1),
        dec_query,
        dec_key,
        dec_value,
        dec_proj,
        dec_up,
        dec_down,
        pred_proj,
        cotangent,
        *loaded,
    )
    final = [
        (rows, width),
        (high, columns),
        (high, columns),
        (high, columns),
        (high, hidden),
        (columns, wide),
        (hidden, wide),
        (embed_pieces[0][1], embed_pieces[0][2]),
    ]
    final += [(1, width)] * 2 + [(1, out_width)] * 3
    final += [(piece[1], piece[2]) for piece in pieces]

    def last_kernel(*refs):
        unpack_kernel((hidden, columns, wide), pieces, embed_pieces, *refs)

    return results[0], pl.pallas_call(
        last_kernel,
        out_shape=[jax.ShapeDtypeStruct(shape, full_type) for shape in final],
        in_specs=[vmem] * (len(outs) - 1),
        out_specs=[vmem] * len(final),
    )(*results[1:])


def layer_norm(values, scale_gain):
    center = values - jnp.mean(values, axis=-1, keepdims=True)
    spread = jnp.mean(center * center, axis=-1, keepdims=True)
    return center * lax.rsqrt(spread + eps_norm) * scale_gain


def exact_gelu(values):
    return jax.nn.gelu(values, approximate=False)


def matmul(left_side, right_side):
    flat_rows = left_side.reshape(-1, left_side.shape[-1])
    product = jnp.dot(flat_rows, right_side, preferred_element_type=full_type)
    return product.reshape(left_side.shape[:-1] + (right_side.shape[1],))


def matmul_t(left_side, right_side):
    flat_rows = left_side.reshape(-1, left_side.shape[-1])
    product = lax.dot_general(
        flat_rows, right_side, (((1,), (1,)), ((), ())), preferred_element_type=full_type
    )
    return product.reshape(left_side.shape[:-1] + (right_side.shape[0],))


def outer_sum(left_side, right_side):
    return lax.dot_general(
        left_side.reshape(-1, left_side.shape[-1]),
        right_side.reshape(-1, right_side.shape[-1]),
        (((0,), (0,)), ((), ())),
        preferred_element_type=full_type,
    )


def spread_rows(values, tensor_split):
    if tensor_split:
        return lax.all_gather(values, "mp", axis=0, tiled=True)
    return values


def collect_rows(values, tensor_split):
    if tensor_split:
        return lax.psum_scatter(
            values.astype(jnp.bfloat16), "mp", scatter_dimension=0, tiled=True
        ).astype(jnp.float32)
    return values


def images_per_block(images, length):
    grouped = 1
    while grouped * length < 512 and grouped < images:
        grouped = grouped * 2
    return grouped


def in_blocks(blocked_array, grouped):
    return blocked_array.reshape(
        (blocked_array.shape[0] // grouped, grouped) + blocked_array.shape[1:]
    )


def with_heads(blocked_array, head_count):
    return blocked_array.reshape(
        blocked_array.shape[:2] + (head_count, blocked_array.shape[2] // head_count)
    )


def attend_forward(queries, keys_all, values_all, key_valid, head_count):
    images, length, columns = queries.shape
    grouped = images_per_block(images, length)
    scaling = float(columns // head_count) ** (-0.5)

    def one_block(pieces):
        query_b, key_b, value_b, valid_b = pieces
        scores = (
            jnp.einsum("nqhd,nkhd->nhqk", query_b, key_b, preferred_element_type=full_type)
            * scaling
        )
        scores = jnp.where(valid_b[:, None, None, :], scores, masked_score)
        row_max = jnp.max(scores, axis=-1, keepdims=True)
        weights = jnp.exp(scores - row_max)
        totals = jnp.sum(weights, axis=-1, keepdims=True)
        prob_rows = (weights / totals).astype(low_type)
        mixed_b = jnp.einsum(
            "nhqk,nkhd->nqhd", prob_rows, value_b, preferred_element_type=full_type
        )
        return (mixed_b.astype(low_type), (row_max + jnp.log(totals))[..., 0])

    pieces_in = (
        in_blocks(with_heads(queries, head_count), grouped),
        in_blocks(with_heads(keys_all, head_count), grouped),
        in_blocks(with_heads(values_all, head_count), grouped),
        in_blocks(key_valid, grouped),
    )
    mixed_rows, log_total = lax.map(one_block, pieces_in)
    return (
        mixed_rows.reshape(images, length, columns),
        log_total.reshape(images, head_count, length),
    )


def attend_backward(queries, keys_all, values_all, key_valid, log_total, grad_mixed, head_count):
    images, length, columns = queries.shape
    grouped = images_per_block(images, length)
    scaling = float(columns // head_count) ** (-0.5)

    def one_block(pieces):
        query_b, key_b, value_b, valid_b, total_b, grad_b = pieces
        scores = (
            jnp.einsum("nqhd,nkhd->nhqk", query_b, key_b, preferred_element_type=full_type)
            * scaling
        )
        scores = jnp.where(valid_b[:, None, None, :], scores, masked_score)
        prob_rows = jnp.exp(scores - total_b[..., None])
        grad_value_b = jnp.einsum(
            "nhqk,nqhd->nkhd", prob_rows.astype(low_type), grad_b, preferred_element_type=full_type
        )
        grad_probs = jnp.einsum(
            "nqhd,nkhd->nhqk", grad_b, value_b, preferred_element_type=full_type
        )
        grad_scores = prob_rows * (
            grad_probs - jnp.sum(grad_probs * prob_rows, axis=-1, keepdims=True)
        )
        grad_scores = (grad_scores * scaling).astype(low_type)
        grad_query_b = jnp.einsum(
            "nhqk,nkhd->nqhd", grad_scores, key_b, preferred_element_type=full_type
        )
        grad_key_b = jnp.einsum(
            "nhqk,nqhd->nkhd", grad_scores, query_b, preferred_element_type=full_type
        )
        return (
            grad_query_b.astype(low_type),
            grad_key_b.astype(low_type),
            grad_value_b.astype(low_type),
        )

    pieces_in = (
        in_blocks(with_heads(queries, head_count), grouped),
        in_blocks(with_heads(keys_all, head_count), grouped),
        in_blocks(with_heads(values_all, head_count), grouped),
        in_blocks(key_valid, grouped),
        in_blocks(log_total, grouped),
        in_blocks(with_heads(grad_mixed, head_count), grouped),
    )
    grad_query, grad_key, grad_value = lax.map(one_block, pieces_in)
    return (
        grad_query.reshape(images, length, columns),
        grad_key.reshape(images, length, columns),
        grad_value.reshape(images, length, columns),
    )


def block_forward(inputs, key_valid, weights, head_count, tensor_split):
    gain_attn, w_query, w_key, w_value, w_out, gain_mlp, w_up, w_down = weights
    normed = spread_rows(layer_norm(inputs, gain_attn).astype(low_type), tensor_split)
    queries = matmul(normed, w_query).astype(low_type)
    keys_all = matmul(normed, w_key).astype(low_type)
    values_all = matmul(normed, w_value).astype(low_type)
    mixed_rows, log_total = attend_forward(queries, keys_all, values_all, key_valid, head_count)
    middle = inputs + collect_rows(matmul(mixed_rows, w_out), tensor_split)
    second = spread_rows(layer_norm(middle, gain_mlp).astype(low_type), tensor_split)
    pre_act = matmul(second, w_up)
    active = exact_gelu(pre_act).astype(low_type)
    outputs = middle + collect_rows(matmul(active, w_down), tensor_split)
    kept_state = (
        inputs,
        normed,
        queries,
        keys_all,
        values_all,
        mixed_rows,
        log_total,
        middle,
        second,
        pre_act,
        active,
    )
    return (outputs, kept_state)


def block_backward(grad_out, kept_state, key_valid, weights, head_count, tensor_split):
    gain_attn, w_query, w_key, w_value, w_out, gain_mlp, w_up, w_down = weights
    (
        inputs,
        normed,
        queries,
        keys_all,
        values_all,
        mixed_rows,
        log_total,
        middle,
        second,
        pre_act,
        active,
    ) = kept_state
    grad_branch = spread_rows(grad_out.astype(low_type), tensor_split)
    grad_down = outer_sum(active, grad_branch)
    grad_active = matmul_t(grad_branch, w_down)
    grad_pre = jax.vjp(exact_gelu, pre_act)[1](grad_active)[0].astype(low_type)
    grad_up = outer_sum(second, grad_pre)
    grad_second = collect_rows(matmul_t(grad_pre, w_up), tensor_split)
    norm_grad, grad_gain_mlp = jax.vjp(layer_norm, middle, gain_mlp)[1](grad_second)
    grad_middle = grad_out + norm_grad
    grad_attn = spread_rows(grad_middle.astype(low_type), tensor_split)
    grad_w_out = outer_sum(mixed_rows, grad_attn)
    grad_mixed = matmul_t(grad_attn, w_out).astype(low_type)
    grad_query, grad_key, grad_value = attend_backward(
        queries, keys_all, values_all, key_valid, log_total, grad_mixed, head_count
    )
    grad_w_query = outer_sum(normed, grad_query)
    grad_w_key = outer_sum(normed, grad_key)
    grad_w_value = outer_sum(normed, grad_value)
    grad_normed = (
        matmul_t(grad_query, w_query) + matmul_t(grad_key, w_key) + matmul_t(grad_value, w_value)
    )
    grad_normed = collect_rows(grad_normed, tensor_split)
    input_grad, grad_gain_attn = jax.vjp(layer_norm, inputs, gain_attn)[1](grad_normed)
    return (
        grad_middle + input_grad,
        (
            grad_gain_attn,
            grad_w_query,
            grad_w_key,
            grad_w_value,
            grad_w_out,
            grad_gain_mlp,
            grad_up,
            grad_down,
        ),
    )


def grid_codes(distance, side_count, columns):
    quarter = columns // 4
    frequency = 10000.0 ** (-jnp.arange(quarter, dtype=full_type) / quarter)
    places = jnp.arange(side_count * side_count)
    row_pos = (places // side_count).astype(full_type)
    col_pos = (places % side_count).astype(full_type)
    row_angle = distance[:, None, None] * row_pos[None, :, None] * frequency[None, None, :]
    col_angle = distance[:, None, None] * col_pos[None, :, None] * frequency[None, None, :]
    return jnp.concatenate(
        [jnp.sin(row_angle), jnp.cos(row_angle), jnp.sin(col_angle), jnp.cos(col_angle)], axis=-1
    )


def placement_table(visible_order, keep_flags, visible):
    positions = jnp.arange(visible_order.shape[1])
    matches = (visible_order[:, None, :visible] == positions[None, :, None]) & (
        keep_flags[:, :, None] == 1
    )
    return matches.astype(low_type)


def owner_blocks(full_grad, data_count, model_count):
    row_count, col_count = full_grad.shape
    reshaped = full_grad.reshape(
        data_count, row_count // data_count, model_count, col_count // model_count
    )
    return jnp.transpose(reshaped, (0, 2, 1, 3)).reshape(
        data_count * model_count, row_count // data_count, col_count // model_count
    )


def per_device_plain(
    tokens,
    lengths,
    grid_order,
    grid_keep,
    ground_dist,
    enc_norm,
    enc_query,
    enc_key,
    enc_value,
    enc_proj,
    enc_norm2,
    enc_up,
    enc_down,
    embed_proj,
    mask_token,
    dec_norm,
    dec_query,
    dec_key,
    dec_value,
    dec_proj,
    dec_norm2,
    dec_up,
    dec_down,
    pred_proj,
    cotangent,
):
    data_count = lax.axis_size("dp")
    model_count = lax.axis_size("mp")
    enc_weights = (enc_norm, enc_query, enc_key, enc_value, enc_proj, enc_norm2, enc_up, enc_down)
    dec_weights = (dec_norm, dec_query, dec_key, dec_value, dec_proj, dec_norm2, dec_up, dec_down)
    enc_heads = HE // model_count
    key_valid = jnp.arange(tokens.shape[1])[None, :] < lengths[:, None]
    enc_out, enc_saved = block_forward(
        tokens.astype(full_type), key_valid, enc_weights, enc_heads, True
    )
    enc_low = enc_out.astype(low_type)
    enc_all = spread_rows(enc_low, True)
    embedded = matmul(enc_all, embed_proj).astype(low_type)
    sectioned = embedded.reshape((data_count, -1) + embedded.shape[1:])
    arrived = lax.all_to_all(
        lax.all_to_all(sectioned, "dp", split_axis=0, concat_axis=0, tiled=True),
        "mp",
        split_axis=0,
        concat_axis=3,
        tiled=True,
    )
    arrived = arrived.reshape((-1,) + arrived.shape[2:])
    pick_table = placement_table(grid_order, grid_keep, arrived.shape[1])
    masked = (1 - grid_keep).astype(full_type)[..., None]
    dec_start = jnp.einsum("npt,ntc->npc", pick_table, arrived, preferred_element_type=full_type)
    dec_start = dec_start + masked * mask_token + grid_codes(ground_dist, SIDE, mask_token.shape[0])
    all_valid = jnp.ones(dec_start.shape[:2], jnp.bool_)
    dec_out, dec_saved = block_forward(dec_start, all_valid, dec_weights, HD, False)
    dec_low = dec_out.astype(low_type)
    decoded = matmul(dec_low, pred_proj)
    grad_pred = outer_sum(dec_low, cotangent)
    grad_dec_out = matmul_t(cotangent, pred_proj)
    grad_start, dec_grads = block_backward(
        grad_dec_out, dec_saved, all_valid, dec_weights, HD, False
    )
    grad_mask = jnp.sum(masked * grad_start, axis=(0, 1))
    grad_arrived = jnp.einsum("npt,npc->ntc", pick_table.astype(full_type), grad_start).astype(
        low_type
    )
    sent_back = grad_arrived.reshape((-1, IPD) + grad_arrived.shape[1:])
    returned = lax.all_to_all(
        lax.all_to_all(sent_back, "mp", split_axis=3, concat_axis=0, tiled=True),
        "dp",
        split_axis=0,
        concat_axis=0,
        tiled=True,
    )
    returned = returned.reshape((-1,) + returned.shape[2:])
    grad_embed = outer_sum(enc_all, returned)
    grad_enc_out = collect_rows(matmul_t(returned, embed_proj), True)
    grad_tokens, enc_grads = block_backward(
        grad_enc_out, enc_saved, key_valid, enc_weights, enc_heads, True
    )
    col_sums = (
        lax.psum_scatter(
            enc_grads[4].astype(jnp.bfloat16), "dp", scatter_dimension=1, tiled=True
        ).astype(jnp.float32),
        lax.psum_scatter(
            enc_grads[7].astype(jnp.bfloat16), "dp", scatter_dimension=1, tiled=True
        ).astype(jnp.float32),
    )
    norm_grads = lax.psum(
        (enc_grads[0], enc_grads[5], dec_grads[0], dec_grads[5], grad_mask), ("dp", "mp")
    )
    dec_list = (
        dec_grads[1],
        dec_grads[2],
        dec_grads[3],
        dec_grads[4],
        dec_grads[6],
        dec_grads[7],
        grad_pred,
    )
    row_sums = (
        lax.psum_scatter(
            enc_grads[1].astype(jnp.bfloat16), "dp", scatter_dimension=0, tiled=True
        ).astype(jnp.float32),
        lax.psum_scatter(
            enc_grads[2].astype(jnp.bfloat16), "dp", scatter_dimension=0, tiled=True
        ).astype(jnp.float32),
        lax.psum_scatter(
            enc_grads[3].astype(jnp.bfloat16), "dp", scatter_dimension=0, tiled=True
        ).astype(jnp.float32),
        lax.psum_scatter(
            enc_grads[6].astype(jnp.bfloat16), "dp", scatter_dimension=0, tiled=True
        ).astype(jnp.float32),
        lax.psum_scatter(
            grad_embed.astype(jnp.bfloat16), "dp", scatter_dimension=0, tiled=True
        ).astype(jnp.float32),
    )
    summed = (
        lax.psum_scatter(
            owner_blocks(dec_list[0], data_count, model_count),
            ("dp", "mp"),
            scatter_dimension=0,
            tiled=True,
        ),
        lax.psum_scatter(
            owner_blocks(dec_list[1], data_count, model_count),
            ("dp", "mp"),
            scatter_dimension=0,
            tiled=True,
        ),
        lax.psum_scatter(
            owner_blocks(dec_list[2], data_count, model_count),
            ("dp", "mp"),
            scatter_dimension=0,
            tiled=True,
        ),
        lax.psum_scatter(
            owner_blocks(dec_list[3], data_count, model_count),
            ("dp", "mp"),
            scatter_dimension=0,
            tiled=True,
        ),
        lax.psum_scatter(
            owner_blocks(dec_list[4], data_count, model_count),
            ("dp", "mp"),
            scatter_dimension=0,
            tiled=True,
        ),
        lax.psum_scatter(
            owner_blocks(dec_list[5], data_count, model_count),
            ("dp", "mp"),
            scatter_dimension=0,
            tiled=True,
        ),
        lax.psum_scatter(
            owner_blocks(dec_list[6], data_count, model_count),
            ("dp", "mp"),
            scatter_dimension=0,
            tiled=True,
        ),
    )
    embed_final = row_sums[4]
    dec_final = tuple((summed[index_num][0] for index_num in range(7)))
    return (
        decoded,
        grad_tokens,
        norm_grads[0],
        row_sums[0],
        row_sums[1],
        row_sums[2],
        col_sums[0],
        norm_grads[1],
        row_sums[3],
        col_sums[1],
        embed_final,
        norm_grads[4],
        norm_grads[2],
        dec_final[0],
        dec_final[1],
        dec_final[2],
        dec_final[3],
        norm_grads[3],
        dec_final[4],
        dec_final[5],
        dec_final[6],
    )


VMEM_BUDGET = 56 * 2**20


def kernel_bytes(tokens, enc_up, enc_query, dec_up, pred_proj):
    data_count, model_count = lax.axis_size("dp"), lax.axis_size("mp")
    images, visible, width = tokens.shape
    every = images * visible * model_count
    hidden, columns = enc_up.shape[1], enc_query.shape[1]
    out_width, wide = dec_up.shape[0], max(width // data_count, LANES)
    shapes = [(out_width, out_width)] * 4
    shapes += [dec_up.shape, dec_up.shape[::-1], pred_proj.shape, (width, out_width)]
    height = dec_pieces(data_count, model_count, shapes)[1]
    rows = 8 * every * width + 3 * every * hidden
    sums = width * (hidden + 3 * columns) + data_count * (hidden + columns) * wide
    sums = 2 * (sums + data_count * model_count * height * LANES)
    return 2 * (rows + sums + 2 * width * hidden + 4 * width * columns)


def per_device(
    tokens,
    lengths,
    grid_order,
    grid_keep,
    ground_dist,
    enc_norm,
    enc_query,
    enc_key,
    enc_value,
    enc_proj,
    enc_norm2,
    enc_up,
    enc_down,
    embed_proj,
    mask_token,
    dec_norm,
    dec_query,
    dec_key,
    dec_value,
    dec_proj,
    dec_norm2,
    dec_up,
    dec_down,
    pred_proj,
    cotangent,
):
    fits = kernel_bytes(tokens, enc_up, enc_query, dec_up, pred_proj) <= VMEM_BUDGET
    if not fits or lax.axis_size("mp") != 4:
        return per_device_plain(
            tokens,
            lengths,
            grid_order,
            grid_keep,
            ground_dist,
            enc_norm,
            enc_query,
            enc_key,
            enc_value,
            enc_proj,
            enc_norm2,
            enc_up,
            enc_down,
            embed_proj,
            mask_token,
            dec_norm,
            dec_query,
            dec_key,
            dec_value,
            dec_proj,
            dec_norm2,
            dec_up,
            dec_down,
            pred_proj,
            cotangent,
        )
    enc_weights = (enc_norm, enc_query, enc_key, enc_value, enc_proj, enc_norm2, enc_up, enc_down)
    dec_weights = (dec_norm, dec_query, dec_key, dec_value, dec_proj, dec_norm2, dec_up, dec_down)
    arrived, *saved = encode(tokens, lengths, enc_weights, embed_proj)
    decoded, grads = decode_and_back(
        arrived,
        grid_order,
        grid_keep,
        ground_dist,
        dec_weights,
        mask_token,
        pred_proj,
        cotangent,
        tokens,
        enc_weights,
        saved,
        embed_proj,
    )
    (
        grad_tokens,
        g_query,
        g_key,
        g_value,
        g_up,
        g_out,
        g_down,
        g_embed,
        n_enc_attn,
        n_enc_mlp,
        n_dec_attn,
        n_dec_mlp,
        n_mask,
        *dec_grads,
    ) = grads
    return (
        decoded,
        grad_tokens.reshape(tokens.shape),
        n_enc_attn[0],
        g_query,
        g_key,
        g_value,
        g_out,
        n_enc_mlp[0],
        g_up,
        g_down,
        g_embed,
        n_mask[0],
        n_dec_attn[0],
        dec_grads[0],
        dec_grads[1],
        dec_grads[2],
        dec_grads[3],
        n_dec_mlp[0],
        dec_grads[4],
        dec_grads[5],
        dec_grads[6],
    )


def solution(mesh):
    return jax.shard_map(
        per_device,
        mesh=mesh,
        in_specs=(
            P(("dp", "mp"), None, None),
            P("dp"),
            P(("dp", "mp"), None),
            P(("dp", "mp"), None),
            P(("dp", "mp")),
            P(),
            P(None, "mp"),
            P(None, "mp"),
            P(None, "mp"),
            P("mp", None),
            P(),
            P(None, "mp"),
            P("mp", None),
            P(None, "mp"),
            P(),
            P(),
            P(),
            P(),
            P(),
            P(),
            P(),
            P(),
            P(),
            P(),
            P(("dp", "mp"), None, None),
        ),
        out_specs=(
            P(("dp", "mp"), None, None),
            P(("dp", "mp"), None, None),
            P(),
            P("dp", "mp"),
            P("dp", "mp"),
            P("dp", "mp"),
            P("mp", "dp"),
            P(),
            P("dp", "mp"),
            P("mp", "dp"),
            P("dp", "mp"),
            P(),
            P(),
            P("dp", "mp"),
            P("dp", "mp"),
            P("dp", "mp"),
            P("dp", "mp"),
            P(),
            P("dp", "mp"),
            P("dp", "mp"),
            P("dp", "mp"),
        ),
        check_vma=False,
    )
```

```python
import math

import jax
import jax.numpy as jnp
from jax import lax
from jax.experimental import pallas as pl
from jax.experimental.pallas import tpu as pltpu
from jax.sharding import PartitionSpec as P

HE = 16
HD = 16
SIDE = 16
IPD = 1


eps_norm = 1e-06
masked_score = -1e30
low_type = jnp.bfloat16
full_type = jnp.float32


MESH = pl.DeviceIdType.MESH
LANES = 128


def log2_of(count):
    bits = count.bit_length() - 1
    assert 1 << bits == count
    return bits


def spot_of(data, model, stages):
    out = 0
    for axis, bit in stages:
        out = out * 2 + (((data if axis == "dp" else model) >> bit) & 1)
    return out


def partner(axis, bit):
    dp, mp = lax.axis_index("dp"), lax.axis_index("mp")
    step = 1 << bit
    if axis == "dp":
        return (dp ^ step, mp), (dp >> bit) & 1
    return (dp, mp ^ step), (mp >> bit) & 1


def enter_barrier(partners):
    barrier = pltpu.get_barrier_semaphore()
    for peer in partners:
        pl.semaphore_signal(barrier, inc=1, device_id=peer, device_id_type=MESH)
    pl.semaphore_wait(barrier, len(partners))


class HalvingSum:
    def __init__(self, stages, buffers, window, send_sems, recv_sems):
        self.stages, self.buffers, self.window = stages, buffers, window
        self.send_sems, self.recv_sems = send_sems, recv_sems

    def view(self, index, start, size):
        return self.buffers[index].at[(pl.ds(start, size),) + self.window]

    def copy(self, index):
        peer, mine = partner(*self.stages[index])
        half = self.buffers[index].shape[0] // 2
        return pltpu.make_async_remote_copy(
            src_ref=self.view(index, (1 - mine) * half, half),
            dst_ref=self.view(index + 1, 0, half),
            send_sem=self.send_sems.at[index],
            recv_sem=self.recv_sems.at[index],
            device_id=peer,
            device_id_type=MESH,
        )

    def start(self, index):
        self.copy(index).start()

    def finish(self, index):
        self.copy(index).wait()
        peer, mine = partner(*self.stages[index])
        half = self.buffers[index].shape[0] // 2

        def one(position, carry):
            there = self.buffers[index + 1].at[(position,) + self.window]
            here = self.buffers[index].at[(mine * half + position,) + self.window]
            there[...] = there[...] + here[...]
            return carry

        lax.fori_loop(0, half, one, 0)


def dec_pieces(data_count, model_count, shapes):
    offset, pieces = 0, []
    for rows, columns in shapes:
        height, width = rows // data_count, columns // model_count
        tiles = -(-width // LANES)
        pieces.append((offset, height, width, tiles))
        offset += height * tiles
    return pieces, offset


LOG2E = 1.4426950408889634


def dot_as(left, right, left_dim, right_dim):
    return lax.dot_general(
        left, right, (((left_dim,), (right_dim,)), ((), ())), preferred_element_type=full_type
    )


def norm_parts(values):
    center = values - jnp.mean(values, axis=-1, keepdims=True)
    scale = lax.rsqrt(jnp.mean(center * center, axis=-1, keepdims=True) + eps_norm)
    return center * scale, scale


def norm_back(normed, scale, grad_scaled):
    first = jnp.mean(grad_scaled, axis=-1, keepdims=True)
    second = jnp.mean(grad_scaled * normed, axis=-1, keepdims=True)
    return (grad_scaled - first - normed * second) * scale


def gelu_pair(values):
    below = 0.5 + 0.5 * lax.erf(values * (0.5**0.5))
    density = jnp.exp2(values * values * (-0.5 * LOG2E)) * ((2.0 * math.pi) ** -0.5)
    return values * below, below + values * density


def low_bit(mask):
    return (mask & -mask).bit_length() - 1


def visit_order(count):
    return sorted(range(count), key=lambda mask: (mask.bit_length(), -mask))


def visit_mask(step, count):
    mask = jnp.int32(0)
    for position, value in enumerate(visit_order(count)):
        mask = jnp.where(step == position, value, mask)
    return mask


class Gather:
    def __init__(self, own, slot_view, send_sems, recv_sems):
        self.own, self.slot_view = own, slot_view
        self.send_sems, self.recv_sems = send_sems, recv_sems
        self.count = lax.axis_size("mp")
        self.index = lax.axis_index("mp")

    def copy(self, mask):
        bit = low_bit(mask)
        carried = mask ^ (1 << bit)
        place = self.slot_view(self.index ^ carried)
        return pltpu.make_async_remote_copy(
            src_ref=self.own if carried == 0 and self.own is not None else place,
            dst_ref=place,
            send_sem=self.send_sems.at[mask],
            recv_sem=self.recv_sems.at[mask],
            device_id=partner("mp", bit)[0],
            device_id_type=MESH,
        )

    def start(self):
        for bit in reversed(range(log2_of(self.count))):
            self.copy(1 << bit).start()

    def arrive(self, mask):
        self.copy(mask).wait_recv()
        for bit in reversed(range(low_bit(mask))):
            self.copy(mask | (1 << bit)).start()

    def arrive_group(self, length):
        group = [mask for mask in range(1, self.count) if mask.bit_length() == length]
        for mask in sorted(group, key=lambda one: -low_bit(one)):
            self.arrive(mask)

    def arrive_all(self):
        for length in range(1, log2_of(self.count) + 1):
            self.arrive_group(length)

    def arrive_at(self, step):
        for length in range(1, log2_of(self.count) + 1):
            @pl.when(step == 1 << (length - 1))
            def _():
                self.arrive_group(length)

    def drain(self):
        for mask in range(1, self.count):
            self.copy(mask).wait_send()


class Scatter:
    def __init__(self, parts, total, landing, send_sems, recv_sems):
        self.parts, self.total, self.landing = parts, total, landing
        self.send_sems, self.recv_sems = send_sems, recv_sems
        self.count = lax.axis_size("mp")
        self.index = lax.axis_index("mp")

    def copy(self, mask):
        return pltpu.make_async_remote_copy(
            src_ref=self.parts.at[mask - 1],
            dst_ref=self.landing.at[mask - 1],
            send_sem=self.send_sems.at[mask],
            recv_sem=self.recv_sems.at[mask],
            device_id=partner("mp", low_bit(mask))[0],
            device_id_type=MESH,
        )

    def put(self, mask, product):
        @pl.when(mask == 0)
        def _():
            self.total[...] = self.total[...] + product

        @pl.when(mask != 0)
        def _():
            self.parts[mask - 1] = product.astype(low_type)

        for odd in range(1, self.count, 2):
            @pl.when(mask == odd)
            def _():
                self.copy(odd).start()

    def finish(self, mask):
        bit = low_bit(mask)
        self.copy(mask).wait_recv()
        rest = mask ^ (1 << bit)
        if rest:
            self.parts[rest - 1] = self.parts[rest - 1] + self.landing[mask - 1]
            if low_bit(rest) == bit + 1:
                self.copy(rest).start()
        else:
            self.total[...] = self.total[...] + self.landing[mask - 1].astype(full_type)

    def finish_bit(self, bit):
        masks = [mask for mask in range(1, self.count) if low_bit(mask) == bit]
        for mask in reversed(masks):
            self.finish(mask)

    def drain(self):
        for mask in range(1, self.count):
            self.copy(mask).wait_send()


def exchange_partners(images):
    data_count, model_count = lax.axis_size("dp"), lax.axis_size("mp")
    data, model = lax.axis_index("dp"), lax.axis_index("mp")
    out = []
    for image in range(images):
        spot = (model * images + image) * data_count + data
        device = spot // images
        out.append((device // model_count, device % model_count, spot % images))
    return out


def is_here(peer):
    return (peer[0] == lax.axis_index("dp")) & (peer[1] == lax.axis_index("mp"))


class Exchange:
    def __init__(self, images, source, target, send_sems, recv_sems):
        self.partners = exchange_partners(images)
        self.source, self.target = source, target
        self.send_sems, self.recv_sems = send_sems, recv_sems

    def copy(self, image):
        data, model, slot = self.partners[image]
        return pltpu.make_async_remote_copy(
            src_ref=self.source.at[image],
            dst_ref=self.target.at[slot],
            send_sem=self.send_sems.at[image],
            recv_sem=self.recv_sems.at[slot],
            device_id=(data, model),
            device_id_type=MESH,
        )

    def start_one(self, image):
        data, model, slot = self.partners[image]
        here = is_here((data, model))

        @pl.when(here)
        def _():
            self.target[slot] = self.source[image]

        @pl.when(jnp.logical_not(here))
        def _():
            self.copy(image).start()

    def start(self):
        for image in range(len(self.partners)):
            self.start_one(image)

    def finish(self):
        for image, (data, model, slot) in enumerate(self.partners):
            @pl.when(jnp.logical_not(is_here((data, model))))
            def _():
                pltpu.make_async_remote_copy(
                    src_ref=self.source.at[image],
                    dst_ref=self.target.at[image],
                    send_sem=self.send_sems.at[image],
                    recv_sem=self.recv_sems.at[image],
                    device_id=(data, model),
                    device_id_type=MESH,
                ).wait()


class Move:
    def __init__(self, source, target, sem):
        self.copy = pltpu.make_async_copy(source, target, sem)
        self.copy.start()

    def wait(self):
        if self.copy is not None:
            self.copy.wait()
            self.copy = None


def signal_partners(images, axes):
    barrier = pltpu.get_barrier_semaphore()
    count = images
    for axis in axes:
        for bit in range(log2_of(lax.axis_size(axis))):
            count += 1
            pl.semaphore_signal(
                barrier, inc=1, device_id=partner(axis, bit)[0], device_id_type=MESH
            )
    for data, model, slot in exchange_partners(images):
        pl.semaphore_signal(barrier, inc=1, device_id=(data, model), device_id_type=MESH)
    return count


def encoder_barrier(images, axes):
    count = signal_partners(images, axes)
    pl.semaphore_wait(pltpu.get_barrier_semaphore(), count)


def encoder_kernel(images, visible, heads, *refs):
    (
        lengths,
        tokens,
        gain_attn,
        w_query_hbm,
        w_key_hbm,
        w_value_hbm,
        w_out,
        gain_mlp,
        w_up_hbm,
        w_down_hbm,
        w_embed,
        *dec_hbm,
        arrived,
    ) = refs[:15]
    saved_hbm = refs[15:28]
    (
        w_query,
        w_key,
        w_value,
        w_up,
        w_down,
        a_s,
        qkv_s,
        e_s,
        inv_s,
        o_own,
        c_s,
        g_s,
        slope_s,
        mid_s,
        low_s,
        embed_full,
        qkv_weights,
        dec_turned,
        dec_query,
        dec_key,
        dec_value,
        move_sems,
        token_slots,
        out_pair,
        o_pair,
        part_own,
        part_sent,
        part_got,
        embed_slots,
        parts,
        landing,
        total,
        embedded,
        sems,
        swap_sems,
        pair_sems,
    ) = refs[28:]
    count = lax.axis_size("mp")
    index = lax.axis_index("mp")
    block_rows = images * visible
    columns = w_query.shape[1]
    size = columns // heads
    scaling = float(size) ** -0.5
    hidden = w_up.shape[1]
    chunk = 512

    loads = [
        Move(source, target, move_sems.at[position])
        for position, (source, target) in enumerate(
            (
                (w_query_hbm, w_query),
                (w_key_hbm, w_key),
                (w_value_hbm, w_value),
                (w_up_hbm, w_up),
                (w_down_hbm, w_down),
                (dec_hbm[0], dec_query),
                (dec_hbm[1], dec_key),
                (dec_hbm[2], dec_value),
            )
        )
    ]
    saved = [a_s, qkv_s, e_s, inv_s, o_own, c_s, g_s, slope_s, mid_s, low_s, embed_full]
    saved += [qkv_weights, dec_turned]
    stores = []

    def save(*arrays):
        for array in arrays:
            position = [array is one for one in saved].index(True)
            stores.append(Move(array, saved_hbm[position], move_sems.at[len(loads) + position]))

    encoder_barrier(images, ["mp"])
    token_gather = Gather(
        tokens, lambda slot: token_slots.at[slot], sems.at[0], sems.at[1]
    )
    near, far = 0, 1

    def rows_of(slot):
        return pl.ds(pl.multiple_of(slot * block_rows, block_rows), block_rows)

    def pair_copy(which, source, target, bit):
        return pltpu.make_async_remote_copy(
            src_ref=source,
            dst_ref=target,
            send_sem=pair_sems.at[0, which],
            recv_sem=pair_sems.at[1, which],
            device_id=partner("mp", bit)[0],
            device_id_type=MESH,
        )

    out_copy = pair_copy(0, w_out, out_pair.at[columns : 2 * columns], near)

    def o_copy(mine):
        block = index ^ (1 + 2 * mine)
        target = o_pair.at[mine, columns : 2 * columns]
        return pair_copy(1 + mine, o_own.at[:, rows_of(block)], target, near)

    def part_copy(mine):
        return pair_copy(3 + mine, part_sent.at[mine], part_got.at[1 - mine], far)

    def c_copy(mine):
        place = c_s.at[rows_of(index ^ (2 * mine))]
        return pair_copy(5 + mine, place, place, near)

    embed_gather = Gather(w_embed, lambda slot: embed_slots.at[slot], sems.at[6], sems.at[7])
    scatter = Scatter(parts, total, landing, sems.at[8], sems.at[9])
    swap = Exchange(images, embedded, arrived, swap_sems.at[0], swap_sems.at[1])

    token_gather.start()
    out_copy.start()
    token_slots[index] = tokens[...]
    out_pair[:columns, :] = w_out[...]
    embed_slots[index] = w_embed[...]
    for position, weight in enumerate((w_query, w_key, w_value)):
        loads[position].wait()
        qkv_weights[position * columns : (position + 1) * columns, :] = weight[...].T
    dec_width = dec_query.shape[0]
    for position, weight in enumerate((dec_query, dec_key, dec_value)):
        loads[5 + position].wait()
        dec_turned[position * dec_width : (position + 1) * dec_width, :] = weight[...].T
    save(qkv_weights, dec_turned)

    def attend(step, carry):
        token_gather.arrive_at(step)

        slot = index ^ visit_mask(step, count)
        rows = rows_of(slot)
        normed, scale = norm_parts(token_slots[slot].astype(full_type))
        a_s[rows, :] = (normed * gain_attn[...]).astype(low_type)
        for position in range(3):
            span = slice(position * columns, (position + 1) * columns)
            part = dot_as(qkv_weights[span, :], a_s[rows, :], 1, 1)
            if position == 0:
                part = part * (scaling * LOG2E)
            qkv_s[span, rows] = part.astype(low_type)
        key_row = lax.broadcasted_iota(jnp.int32, (block_rows, block_rows), 0)
        query_row = lax.broadcasted_iota(jnp.int32, (block_rows, block_rows), 1)
        valid = jnp.zeros((block_rows, block_rows), jnp.bool_)
        for image in range(images):
            first = image * visible
            keys = (key_row >= first) & (key_row < first + lengths[slot * images + image])
            valid = valid | (keys & (query_row >= first) & (query_row < first + visible))
        for head in range(heads):
            span = slice(head * size, (head + 1) * size)
            query = qkv_s[span, rows]
            key = qkv_s[columns + head * size : columns + (head + 1) * size, rows]
            value = qkv_s[2 * columns + head * size : 2 * columns + (head + 1) * size, rows]
            scores = jnp.where(valid, dot_as(key, query, 0, 0), masked_score)
            weights = jnp.exp2(scores - jnp.max(scores, axis=0, keepdims=True))
            inverse = 1.0 / jnp.sum(weights, axis=0, keepdims=True)
            weights = weights.astype(low_type)
            e_s[slot * heads + head] = weights
            inv_s[slot * heads + head] = inverse
            mixed = jnp.dot(value, weights, preferred_element_type=full_type)
            o_own[span, rows] = (mixed * inverse).astype(low_type)
        for turn, mine in ((1, 0), (2, 1)):
            @pl.when(step == turn)
            def _():
                o_copy(mine).start()

        for turn, mine in ((0, 0), (3, 1)):
            @pl.when(step == turn)
            def _():
                o_pair[mine, :columns, :] = o_own[:, rows]

        return carry

    def sum_heads(mine):
        o_copy(mine).wait_recv()
        part = dot_as(o_pair[mine], out_pair[...], 0, 0)
        part_own[mine] = part
        part_sent[mine] = part.astype(low_type)
        part_copy(mine).start()

    def middle_of(mine):
        part_copy(1 - mine).wait_recv()
        slot = index ^ (2 * mine)
        middle = token_slots[slot].astype(full_type) + part_own[mine]
        middle = middle + part_got[mine].astype(full_type)
        if mine == 0:
            mid_s[...] = middle
        normed, scale = norm_parts(middle)
        c_s[rows_of(slot), :] = (normed * gain_mlp[...]).astype(low_type)
        c_copy(mine).start()

    lax.fori_loop(0, 2, attend, 0)
    out_copy.wait_recv()
    sum_heads(0)
    lax.fori_loop(2, 4, attend, 0)
    sum_heads(1)
    embed_gather.start()
    save(a_s, qkv_s, e_s, inv_s, o_own)
    for move in loads:
        move.wait()
    total[...] = jnp.zeros_like(total)

    def expand(mask, carry):
        for odd in (1, 3):
            @pl.when(mask == odd)
            def _():
                c_copy(odd // 2).wait_recv()

        rows = rows_of(index ^ mask)
        for first in range(0, hidden, chunk):
            cols = slice(first, first + chunk)
            pre = jnp.dot(c_s[rows, :], w_up[:, cols], preferred_element_type=full_type)
            active, slope = gelu_pair(pre)
            g_s[rows, cols] = active.astype(low_type)
            slope_s[rows, cols] = slope.astype(low_type)
        scatter.put(
            mask, jnp.dot(g_s[rows, :], w_down[...], preferred_element_type=full_type)
        )
        return carry

    middle_of(1)
    lax.fori_loop(2, 4, expand, 0)
    scatter.finish(3)
    middle_of(0)
    lax.fori_loop(0, 2, expand, 0)
    scatter.finish(1)
    save(c_s, g_s, slope_s, mid_s)
    embed_gather.arrive_all()
    width = w_embed.shape[1]
    for slot in range(count):
        embed_full[:, slot * width : (slot + 1) * width] = embed_slots[slot]
    scatter.finish(2)
    low_s[...] = (mid_s[...] + total[...]).astype(low_type)
    out = jnp.dot(low_s[...], embed_full[...], preferred_element_type=full_type)
    embedded[...] = out.astype(low_type).reshape(embedded.shape)
    swap.start()
    save(embed_full, low_s)
    for one in (token_gather, embed_gather, scatter):
        one.drain()
    out_copy.wait_send()
    for mine in range(2):
        for copy in (o_copy(mine), part_copy(mine), c_copy(mine)):
            copy.wait_send()
    for move in stores:
        move.wait()
    swap.finish()


def encode(tokens, lengths, weights, embed_proj, dec_inputs):
    gain_attn, w_query, w_key, w_value, w_out, gain_mlp, w_up, w_down = weights
    model_count = lax.axis_size("mp")
    images, visible, width = tokens.shape
    rows = images * visible
    heads = HE // model_count
    columns, hidden = w_query.shape[1], w_up.shape[1]
    out_width = embed_proj.shape[1] * model_count
    every = rows * model_count

    def kernel(*refs):
        encoder_kernel(images, visible, heads, *refs)

    vmem = pl.BlockSpec(memory_space=pltpu.VMEM)
    hbm = pl.BlockSpec(memory_space=pl.ANY)
    shapes = [
        ((images, visible, out_width), low_type),
        ((every, width), low_type),
        ((3 * columns, every), low_type),
        ((model_count * heads, rows, rows), low_type),
        ((model_count * heads, 1, rows), full_type),
        ((columns, every), low_type),
        ((every, width), low_type),
        ((every, hidden), low_type),
        ((every, hidden), low_type),
        ((rows, width), full_type),
        ((rows, width), low_type),
        ((width, out_width), low_type),
        ((3 * columns, width), low_type),
        ((3 * out_width, out_width), low_type),
    ]
    return pl.pallas_call(
        kernel,
        out_shape=[jax.ShapeDtypeStruct(shape, kind) for shape, kind in shapes],
        in_specs=[pl.BlockSpec(memory_space=pltpu.SMEM)]
        + [vmem] * 2
        + [hbm] * 3
        + [vmem] * 2
        + [hbm] * 2
        + [vmem]
        + [hbm] * 3,
        out_specs=[vmem] + [hbm] * (len(shapes) - 1),
        scratch_shapes=[
            pltpu.VMEM((width, columns), low_type),
            pltpu.VMEM((width, columns), low_type),
            pltpu.VMEM((width, columns), low_type),
            pltpu.VMEM((width, hidden), low_type),
            pltpu.VMEM((hidden, width), low_type),
        ]
        + [pltpu.VMEM(shape, kind) for shape, kind in shapes[1:]]
        + [pltpu.VMEM((out_width, out_width), low_type)] * 3
        + [
            pltpu.SemaphoreType.DMA((8 + len(shapes),)),
            pltpu.VMEM((model_count, rows, width), low_type),
            pltpu.VMEM((2 * columns, width), low_type),
            pltpu.VMEM((2, 2 * columns, rows), low_type),
            pltpu.VMEM((2, rows, width), full_type),
            pltpu.VMEM((2, rows, width), low_type),
            pltpu.VMEM((2, rows, width), low_type),
            pltpu.VMEM((model_count,) + embed_proj.shape, low_type),
            pltpu.VMEM((model_count - 1, rows, width), low_type),
            pltpu.VMEM((model_count - 1, rows, width), low_type),
            pltpu.VMEM((rows, width), full_type),
            pltpu.VMEM((images, visible, out_width), low_type),
            pltpu.SemaphoreType.DMA((10, model_count)),
            pltpu.SemaphoreType.DMA((2, images)),
            pltpu.SemaphoreType.DMA((2, 7)),
        ],
        compiler_params=pltpu.CompilerParams(
            collective_id=1, has_side_effects=True, vmem_limit_bytes=60 * 2**20
        ),
    )(
        lengths,
        tokens.reshape(rows, width),
        gain_attn.reshape(1, -1),
        w_query,
        w_key,
        w_value,
        w_out,
        gain_mlp.reshape(1, -1),
        w_up,
        w_down,
        embed_proj,
        *dec_inputs,
    )


EARLY_DOWN, EARLY_UP, UP_FIRST = True, False, True
SUM_ORDERS = {
    "attn": ["all"],
    "dup": ["spread", "all"],
    "ddn": ["spreadz", "spread", "spread", "spreadz"],
    "pred": ["spread", "spread"],
    "emb": ["all"],
    "dn": ["Y", "Z", "Y", "Y"],
    "up": ["Y", "Y", "Z", "Y"],
    "oq": ["Y", "Y", "Y", "Y"],
}
PLAN = {
    "a3": [
        "pred0",
        "pred1",
        "ddn0",
        "ddn1",
        "ddn2",
        "ddn3",
        "dup0",
        "dup1",
    ],
    "a4": [
        "pred0",
        "ddn0",
        "pred1",
    ],
    "a5": [
        "ddn3",
        "dup1",
        "ddn1",
        "attn0",
        "pred0",
        "ddn2",
    ],
    "f1": [
        "pred1",
        "ddn0",
    ],
    "f2": [
        "emb0",
    ],
    "f3": [
        "dup0",
        "ddn1",
        "ddn3",
    ],
    "b0": [
        "pred0",
        "ddn2",
        "dup1",
        "ddn0",
        "pred1",
        "ddn3",
    ],
    "d2": [
        "dup0",
    ],
    "d3": [
        "ddn1",
    ],
    "s2": [
        "attn0",
        "dn0",
    ],
    "b2": [
        "dn1",
    ],
    "b4": [
        "ddn2",
        "dup1",
        "emb0",
        "dn2",
        "pred0",
        "ddn0",
        "pred1",
        "ddn3",
        "ddn1",
        "dup0",
    ],
    "b5": [
        "dn0",
        "dn3",
    ],
    "t1": [
        "ddn2",
        "dup0",
        "dn1",
    ],
    "t2": [
        "up2",
        "attn0",
        "dup1",
        "dn2",
        "up0",
    ],
    "t3": [
        "dn0",
        "dn3",
    ],
    "b7": [
        "up1",
    ],
    "tail": [
        "attn0",
        "up2",
        "up3",
        "dn2",
        "up0",
        "emb0",
        "norm",
        "dn1",
        "dn3",
        "up1",
        "norm",
        "attn0",
        "up3",
        "o",
        "emb0",
        "up0",
        "q",
        "up1",
        "up3",
        "o",
        "k",
        "emb0",
        "q",
        "o",
        "v",
        "k",
        "up2",
        "norm",
        "q",
        "v",
        "norm",
        "k",
        "v",
        "norm",
    ],
}


class Bulk:
    def __init__(self, one):
        self.one, self.stage = one, None

    def start(self):
        self.one.start(0)
        self.stage = 0

    def done(self):
        return self.stage == len(self.one.stages)

    def advance(self):
        if self.stage is None or self.done():
            return
        self.one.finish(self.stage)
        self.stage += 1
        if not self.done():
            self.one.start(self.stage)


def back_kernel(plan, *refs):
    images, visible, enc_heads, heads, side, pieces, embed_piece, scopes = plan
    refs = list(refs)

    def take(number):
        head = refs[:number]
        del refs[:number]
        return head

    (
        dist_ref,
        arrived,
        order_ref,
        keep_ref,
        dec_gain_attn,
        dec_gain_mlp,
        mask_token,
        tokens,
        gain_attn,
        gain_mlp,
    ) = take(10)
    dec_hbm = take(6)
    enc_hbm = take(15)
    decoded, grad_tokens, norm_wide, norm_thin, rows_out, cols_out, dec_out, embed_out = take(8)
    move_sems, decoded_sems = take(2)
    grad_arrived, dec_packed, small = take(3)
    demb_own, demb_slots, db_s, total = take(4)
    parts_mlp, landing_mlp, parts_attn, landing_attn = take(4)
    sems, swap_sems = take(2)
    data_count, model_count = lax.axis_size("dp"), lax.axis_size("mp")
    data_bits, model_bits = log2_of(data_count), log2_of(model_count)
    row_packed, col_packed, embed_packed = take(3)
    row_bufs = [row_packed] + take(data_bits)
    col_bufs = [col_packed] + take(data_bits)
    dec_bufs = [dec_packed] + take(data_bits + model_bits)
    embed_bufs = [embed_packed] + take(data_bits + model_bits)
    wide_acc, wide_got, thin_acc, thin_got = take(4)
    row_sems, col_sems, dec_sems, embed_sems, norm_sems = take(5)
    assert not refs

    index = lax.axis_index("mp")
    count = model_count
    enc_stages = [("dp", bit) for bit in range(data_bits)]
    late_stages = enc_stages[1:] + enc_stages[:1]
    model_stages = [("mp", bit) for bit in range(model_bits)]
    all_stages = model_stages + enc_stages
    near, far = model_stages[:1], model_stages[1:]
    orders = {
        "Y": enc_stages,
        "Z": late_stages,
        "all": all_stages,
        "crossed": model_stages + late_stages,
        "spread": near + enc_stages + far,
        "spreadz": near + late_stages + far,
    }
    sums = {}

    def pump(point):
        for name in PLAN.get(point, ()):
            if name in sums:
                sums[name].advance()

    def pump_at(step, point):
        for turn in range(count):
            if PLAN.get(point + str(turn)):
                @pl.when(step == turn)
                def _():
                    pump(point + str(turn))

    chunk = 512

    def bulk(stages, bufs, axis, first, extent, pair, cut):
        window = [slice(None), slice(None)]
        window[axis - 1] = pl.ds(first, extent)
        return Bulk(HalvingSum(stages, bufs, tuple(window), pair.at[0, cut], pair.at[1, cut]))

    limits = [pieces[0][0]] + [piece[0] for piece in pieces[4:]] + [dec_packed.shape[1]]
    dec_rows = []
    for kind, first, last in zip(("attn", "dup", "ddn", "pred"), limits, limits[1:]):
        names = SUM_ORDERS[kind]
        extent = (last - first) // len(names)
        for cut, order in enumerate(names):
            begin = first + cut * extent
            sums[kind + str(cut)] = bulk(
                orders[order], dec_bufs, 1, begin, extent, dec_sems, len(dec_rows)
            )
            dec_rows.append((begin, begin + extent, orders[order]))

    def start(kind):
        for cut in range(len(SUM_ORDERS[kind])):
            sums[kind + str(cut)].start()

    def store_dec(which, product):
        offset, height, span, tiles = pieces[which]
        for column in range(model_count):
            for tile in range(tiles):
                lanes = min(LANES, span - tile * LANES)
                first = column * span + tile * LANES
                block = product[:, first : first + lanes].astype(low_type)
                base = offset + tile * height
                for begin, end, order in dec_rows:
                    low_row, high_row = max(begin, base), min(end, base + height)
                    if low_row >= high_row:
                        continue
                    for row in range(data_count):
                        shift = row * height - base
                        dec_packed[spot_of(row, column, order), low_row:high_row, :lanes] = block[
                            low_row + shift : high_row + shift, :
                        ]

    swap = Exchange(images, grad_arrived, demb_own, swap_sems.at[0], swap_sems.at[1])

    def decoder(
        w_out,
        xs,
        qkv_weights,
        a_s,
        qkv_s,
        e_s,
        inv_s,
        o_s,
        dy_s,
        db_dec,
        do_s,
    ):
        length = side * side
        width = w_out.shape[0]
        size = width // heads
        scaling = float(size) ** -0.5
        place = lax.broadcasted_iota(jnp.int32, (length, visible), 0)
        turn = lax.broadcasted_iota(jnp.int32, (length, visible), 1)
        arrivals = signal_partners(images, ["mp", "dp"])
        turned_move = Move(dec_hbm[0], qkv_weights, move_sems.at[0])
        out_move = Move(dec_hbm[1], w_out, move_sems.at[1])

        def picks(image):
            order = jnp.zeros((1, visible), jnp.int32)
            flags = jnp.zeros((1, length), jnp.int32)
            for one in range(images):
                order = jnp.where(image == one, order_ref[one : one + 1, :visible], order)
                flags = jnp.where(image == one, keep_ref[one : one + 1, :], flags)
            kept = jnp.sum(flags, axis=1, keepdims=True)
            return jnp.where((order == place) & (turn < kept), 1.0, 0.0)

        def rows_of(image):
            if isinstance(image, int):
                return slice(image * length, (image + 1) * length)
            return pl.ds(pl.multiple_of(image * length, length), length)

        def dense(w_up, w_down, w_pred, cotangent, mid_s, c_s, g_s, du_s, low_s, dm_s, staged):
            hidden = w_up.shape[1]
            second_moves = [
                Move(source, target, move_sems.at[2 + position])
                for position, (source, target) in enumerate(
                    zip(dec_hbm[2:], (w_up, w_down, w_pred, cotangent))
                )
            ]
            turned_move.wait()
            out_move.wait()
            small[...] = jnp.zeros_like(small)

            def stage_copy(image):
                return pltpu.make_async_copy(staged, decoded.at[image], decoded_sems.at[image])

            def one_image(image, carry):
                rows = rows_of(image)
                pick = picks(image)
                hidden_rows = 1.0 - jnp.sum(pick, axis=1, keepdims=True)
                quarter = width // 4
                lane = lax.broadcasted_iota(jnp.int32, (side, quarter), 1).astype(full_type)
                line = lax.broadcasted_iota(jnp.int32, (side, quarter), 0).astype(full_type)
                angle = dist_ref[image] * line * jnp.exp(lane * (-math.log(10000.0) / quarter))
                table = jnp.concatenate([jnp.sin(angle), jnp.cos(angle)], axis=1)
                by_row = jnp.broadcast_to(table[:, None, :], (side, side, 2 * quarter))
                by_col = jnp.broadcast_to(table[None, :, :], (side, side, 2 * quarter))
                codes = jnp.concatenate(
                    [by_row.reshape(length, 2 * quarter), by_col.reshape(length, 2 * quarter)],
                    axis=1,
                )
                start = jnp.dot(
                    pick.astype(low_type), arrived[image], preferred_element_type=full_type
                )
                start = start + hidden_rows * mask_token[...] + codes
                xs[rows, :] = start
                normed, scale = norm_parts(start)
                a_s[rows, :] = (normed * dec_gain_attn[...]).astype(low_type)
                for position in range(3):
                    span = slice(position * width, (position + 1) * width)
                    part = dot_as(qkv_weights[span, :], a_s[rows, :], 1, 1)
                    if position == 0:
                        part = part * (scaling * LOG2E)
                    qkv_s[span, rows] = part.astype(low_type)

                def one_head(head, inner):
                    span = pl.multiple_of(head * size, size)
                    query = qkv_s[pl.ds(span, size), rows]
                    key = qkv_s[pl.ds(width + span, size), rows]
                    value = qkv_s[pl.ds(2 * width + span, size), rows]
                    scores = dot_as(key, query, 0, 0)
                    weights = jnp.exp2(scores - jnp.max(scores, axis=0, keepdims=True))
                    inverse = 1.0 / jnp.sum(weights, axis=0, keepdims=True)
                    weights = weights.astype(low_type)
                    e_s[image * heads + head] = weights
                    inv_s[image * heads + head] = inverse
                    mixed = jnp.dot(value, weights, preferred_element_type=full_type)
                    o_s[pl.ds(span, size), rows] = (mixed * inverse).astype(low_type)
                    return inner

                lax.fori_loop(0, heads, one_head, 0, unroll=heads)

                middle = start + dot_as(o_s[:, rows], w_out[...], 0, 0)
                mid_s[...] = middle
                normed, scale = norm_parts(middle)
                c_s[rows, :] = (normed * dec_gain_mlp[...]).astype(low_type)

                @pl.when(image == 0)
                def _():
                    for move in second_moves:
                        move.wait()

                for first in range(0, hidden, chunk):
                    cols = slice(first, first + chunk)
                    pre = jnp.dot(c_s[rows, :], w_up[:, cols], preferred_element_type=full_type)
                    active, slope = gelu_pair(pre)
                    g_s[rows, cols] = active.astype(low_type)
                    du_s[rows, cols] = slope.astype(low_type)
                outputs = middle + jnp.dot(
                    g_s[rows, :], w_down[...], preferred_element_type=full_type
                )
                low_s[rows, :] = outputs.astype(low_type)

                @pl.when(image > 0)
                def _():
                    stage_copy(image - 1).wait()

                staged[...] = jnp.dot(
                    low_s[rows, :], w_pred[...], preferred_element_type=full_type
                )
                stage_copy(image).start()

                grad_out = dot_as(cotangent[image], w_pred[...], 1, 1)
                dm_s[rows, :] = grad_out.astype(low_type)
                for first in range(0, hidden, chunk):
                    cols = slice(first, first + chunk)
                    grad_active = dot_as(dm_s[rows, :], w_down[cols, :], 1, 1)
                    du_s[rows, cols] = (grad_active * du_s[rows, cols].astype(full_type)).astype(
                        low_type
                    )
                grad_second = dot_as(du_s[rows, :], w_up[...], 1, 1)
                normed, scale = norm_parts(mid_s[...])
                small[1:2, :] += jnp.sum(grad_second * normed, axis=0, keepdims=True)
                grad_middle = grad_out + norm_back(
                    normed, scale, grad_second * dec_gain_mlp[...]
                )
                dy_s[rows, :] = grad_middle
                db_dec[rows, :] = grad_middle.astype(low_type)
                return carry

            lax.fori_loop(0, images, one_image, 0)
            all_pixels = cotangent[...].reshape(-1, cotangent.shape[2])
            store_dec(6, dot_as(low_s[...], all_pixels, 0, 0))
            pl.semaphore_wait(pltpu.get_barrier_semaphore(), arrivals)
            start("pred")
            store_dec(5, dot_as(g_s[...], dm_s[...], 0, 0))
            start("ddn")
            pump("a1")
            store_dec(4, dot_as(c_s[...], du_s[...], 0, 0))
            start("dup")
            pump("a2")
            stage_copy(images - 1).wait()

        pl.run_scoped(dense, *scopes[1])

        for image in range(images):
            rows = rows_of(image)
            do_s[...] = dot_as(w_out[...], db_dec[rows, :], 1, 1)

            def back_head(head, inner):
                span = pl.multiple_of(head * size, size)
                query = qkv_s[pl.ds(span, size), rows]
                key = qkv_s[pl.ds(width + span, size), rows]
                value = qkv_s[pl.ds(2 * width + span, size), rows]
                weights = e_s[image * heads + head]
                grad_full = do_s[pl.ds(span, size), :] * (inv_s[image * heads + head] * scaling)
                mixed = o_s[pl.ds(span, size), rows].astype(full_type)
                shift = jnp.sum(grad_full * mixed, axis=0, keepdims=True)
                grad_low = grad_full.astype(low_type)
                grad_probs = dot_as(value, grad_low, 0, 0)
                grad_scores = (weights.astype(full_type) * (grad_probs - shift)).astype(low_type)
                grad_value = dot_as(grad_low, weights, 1, 1) * (1.0 / scaling)
                grad_query = jnp.dot(key, grad_scores, preferred_element_type=full_type)
                grad_key = dot_as(query, grad_scores, 1, 1) * (1.0 / (scaling * LOG2E))
                qkv_s[pl.ds(span, size), rows] = grad_query.astype(low_type)
                qkv_s[pl.ds(width + span, size), rows] = grad_key.astype(low_type)
                qkv_s[pl.ds(2 * width + span, size), rows] = grad_value.astype(low_type)
                return inner

            lax.fori_loop(0, heads, back_head, 0, unroll=heads)

            grad_normed = dot_as(qkv_s[:, rows], qkv_weights[...], 0, 0)
            normed, scale = norm_parts(xs[rows, :])
            small[0:1, :] += jnp.sum(grad_normed * normed, axis=0, keepdims=True)
            grad_start = dy_s[rows, :] + norm_back(
                normed, scale, grad_normed * dec_gain_attn[...]
            )
            pick = picks(image)
            hidden_rows = 1.0 - jnp.sum(pick, axis=1, keepdims=True)
            small[2:3, :] += jnp.sum(hidden_rows * grad_start, axis=0, keepdims=True)
            grad_arrived[image] = dot_as(
                pick.astype(low_type), grad_start.astype(low_type), 0, 0
            ).astype(low_type)
            swap.start_one(image)
            if image == 0:
                pump("a3")
        for position in range(3):
            grads = qkv_s[position * width : (position + 1) * width, :]
            store_dec(position, dot_as(a_s[...], grads, 0, 1))
        store_dec(3, jnp.dot(o_s[...], db_dec[...], preferred_element_type=full_type))
        start("attn")
        pump("a4")

    pl.run_scoped(decoder, *scopes[0])
    thin_acc[0] = small[...]

    def encoder(*local):
        local = list(local)
        loaded = local[:15]
        (
            w_out,
            w_up,
            w_down,
            a_s,
            qkv_s,
            e_s,
            inv_s,
            o_own,
            c_s,
            g_s,
            slope_s,
            mid_s,
            low_s,
            embed_full,
            qkv_weights,
        ) = loaded
        dm_s, du_s, dqkv_s, dy_s, do_s = local[15:]
        block_rows = images * visible
        columns = w_out.shape[0]
        size = columns // enc_heads
        scaling = float(size) ** -0.5
        hidden, width = w_down.shape
        moves = {}
        for position in (12, 13, 9, 2, 10, 1, 11, 8, 0, 4, 5, 6, 7, 14, 3):
            moves[position] = Move(enc_hbm[position], loaded[position], move_sems.at[8 + position])

        def ready(*arrays):
            for array in arrays:
                moves[[array is one for one in loaded].index(True)].wait()

        def cut_sums(kind, bufs, axis, extent, pair, base=0):
            for cut, order in enumerate(SUM_ORDERS[kind]):
                sums[kind + str(cut)] = bulk(
                    orders[order], bufs, axis, cut * extent, extent, pair, base + cut
                )

        embed_cuts = len(SUM_ORDERS["emb"])
        embed_part = embed_packed.shape[1] // embed_cuts
        cut_sums("emb", embed_bufs, 1, embed_part, embed_sems)
        up_part = hidden // len(SUM_ORDERS["up"])
        down_part = hidden // len(SUM_ORDERS["dn"])
        cut_sums("up", row_bufs, 2, up_part, row_sems)
        cut_sums("dn", col_bufs, 1, down_part, col_sems)
        out_order, *qkv_orders = (orders[one] for one in SUM_ORDERS["oq"])
        for cut, name in enumerate("qkv"):
            sums[name] = bulk(
                qkv_orders[cut],
                row_bufs,
                2,
                hidden + cut * columns,
                columns,
                row_sems,
                len(SUM_ORDERS["up"]) + cut,
            )
        sums["o"] = bulk(
            out_order, col_bufs, 1, hidden, columns, col_sems, len(SUM_ORDERS["dn"])
        )

        swap.finish()
        demb_gather = Gather(demb_own, lambda slot: demb_slots.at[slot], sems.at[0], sems.at[1])
        demb_gather.start()
        demb_slots[index] = demb_own[...]
        ready(low_s)
        offset, high, span, tiles = embed_piece
        product = dot_as(low_s[...], demb_own[...].reshape(block_rows, -1), 0, 0)
        for column in range(model_count):
            for row in range(data_count):
                for cut, order in enumerate(SUM_ORDERS["emb"]):
                    spot = spot_of(row, column, orders[order])
                    for tile in range(tiles):
                        lanes = min(LANES, span - tile * LANES)
                        first = column * span + tile * LANES
                        base = tile * high
                        begin = max(base, cut * embed_part)
                        end = min(base + high, (cut + 1) * embed_part)
                        if begin < end:
                            shift = row * high - base
                            embed_packed[spot, begin:end, :lanes] = product[
                                begin + shift : end + shift, first : first + lanes
                            ].astype(low_type)
        start("emb")
        pump("a5")
        ready(embed_full)

        def rows_of(slot):
            return pl.ds(pl.multiple_of(slot * block_rows, block_rows), block_rows)

        def first_back(step, carry):
            demb_gather.arrive_at(step)
            pump_at(step, "f")
            mask = visit_mask(step, count)
            slot = index ^ mask
            rows = rows_of(slot)
            grad_rows = demb_slots[slot].reshape(block_rows, -1)
            grad_out = dot_as(grad_rows, embed_full[...], 1, 1)

            @pl.when(mask == 0)
            def _():
                dy_s[...] = grad_out

            dm_s[rows, :] = grad_out.astype(low_type)
            return carry

        def active_back(step, carry):
            pump_at(step, "d")
            rows = rows_of(index ^ visit_mask(step, count))
            for first in range(0, hidden, chunk):
                cols = slice(first, first + chunk)
                grad_active = dot_as(dm_s[rows, :], w_down[cols, :], 1, 1)
                du_s[rows, cols] = (grad_active * slope_s[rows, cols].astype(full_type)).astype(
                    low_type
                )
            return carry

        lax.fori_loop(0, count, first_back, 0)

        def store_rows(product, first, stages):
            high = width // data_count
            for row in range(data_count):
                row_packed[spot_of(row, 0, stages), :, first : first + product.shape[1]] = (
                    product[row * high : (row + 1) * high, :].astype(low_type)
                )

        def store_cols(product, first, stages):
            wide = width // data_count
            for col in range(data_count):
                col_packed[
                    spot_of(col, 0, stages), first : first + product.shape[0], :wide
                ] = product[:, col * wide : (col + 1) * wide].astype(low_type)

        def down_grads():
            ready(g_s)
            for cut, order in enumerate(SUM_ORDERS["dn"]):
                cols = slice(cut * down_part, (cut + 1) * down_part)
                product = dot_as(g_s[:, cols], dm_s[...], 0, 0)
                store_cols(product, cut * down_part, orders[order])
                sums["dn" + str(cut)].start()
            pump("b0" if EARLY_DOWN else "b3")

        def up_grads():
            ready(c_s)
            for cut, order in enumerate(SUM_ORDERS["up"]):
                cols = slice(cut * up_part, (cut + 1) * up_part)
                product = dot_as(c_s[...], du_s[:, cols], 0, 0)
                store_rows(product, cut * up_part, orders[order])
                sums["up" + str(cut)].start()
            pump("b1" if EARLY_UP else "b4")

        if EARLY_DOWN:
            down_grads()
        ready(w_down, slope_s)
        lax.fori_loop(0, count, active_back, 0)
        if EARLY_UP:
            up_grads()
        ready(w_up)
        scatter = Scatter(parts_mlp, total, landing_mlp, sems.at[2], sems.at[3])
        total[...] = jnp.zeros_like(total)

        def second_back(step, carry):
            pump_at(step, "s")
            mask = count - 1 - step
            rows = rows_of(index ^ mask)
            scatter.put(mask, dot_as(du_s[rows, :], w_up[...], 1, 1))
            return carry

        lax.fori_loop(0, count, second_back, 0)
        for bit in range(model_bits - 1):
            scatter.finish_bit(bit)

        pump("b2")
        if not EARLY_DOWN:
            down_grads()
        if not EARLY_UP and UP_FIRST:
            up_grads()
        ready(mid_s)
        scatter.finish_bit(model_bits - 1)

        normed, scale = norm_parts(mid_s[...])
        grad_second = total[...]
        wide_acc[0, 1:2, :] = jnp.sum(grad_second * normed, axis=0, keepdims=True)
        grad_middle = dy_s[...] + norm_back(normed, scale, grad_second * gain_mlp[...])
        dy_s[...] = grad_middle
        db_s[rows_of(index), :] = grad_middle.astype(low_type)
        db_gather = Gather(None, lambda slot: db_s.at[rows_of(slot)], sems.at[4], sems.at[5])
        db_gather.start()
        pump("b5")
        if not EARLY_UP and not UP_FIRST:
            up_grads()
        ready(w_out, qkv_s, e_s, inv_s, o_own, qkv_weights)
        second_scatter = Scatter(parts_attn, total, landing_attn, sems.at[6], sems.at[7])
        total[...] = jnp.zeros_like(total)

        def third_back(step, carry):
            db_gather.arrive_at(step)
            pump_at(step, "t")
            mask = visit_mask(step, count)
            slot = index ^ mask
            rows = rows_of(slot)
            do_s[...] = dot_as(w_out[...], db_s[rows, :], 1, 1)
            for head in range(enc_heads):
                span = slice(head * size, (head + 1) * size)
                key_span = slice(columns + head * size, columns + (head + 1) * size)
                value_span = slice(2 * columns + head * size, 2 * columns + (head + 1) * size)
                query, key, value = qkv_s[span, rows], qkv_s[key_span, rows], qkv_s[value_span, rows]
                weights = e_s[slot * enc_heads + head]
                grad_full = do_s[span, :] * (inv_s[slot * enc_heads + head] * scaling)
                shift = jnp.sum(
                    grad_full * o_own[span, rows].astype(full_type), axis=0, keepdims=True
                )
                grad_low = grad_full.astype(low_type)
                grad_probs = dot_as(value, grad_low, 0, 0)
                grad_scores = (weights.astype(full_type) * (grad_probs - shift)).astype(low_type)
                grad_value = dot_as(grad_low, weights, 1, 1) * (1.0 / scaling)
                grad_query = jnp.dot(key, grad_scores, preferred_element_type=full_type)
                grad_key = dot_as(query, grad_scores, 1, 1) * (1.0 / (scaling * LOG2E))
                dqkv_s[span, rows] = grad_query.astype(low_type)
                dqkv_s[key_span, rows] = grad_key.astype(low_type)
                dqkv_s[value_span, rows] = grad_value.astype(low_type)
            second_scatter.put(mask, dot_as(dqkv_s[:, rows], qkv_weights[...], 0, 0))
            return carry

        lax.fori_loop(0, count, third_back, 0)
        for bit in range(model_bits - 1):
            second_scatter.finish_bit(bit)
        pump("b6")
        store_cols(
            jnp.dot(o_own[...], db_s[...], preferred_element_type=full_type), hidden, out_order
        )
        sums["o"].start()
        ready(a_s)
        for cut, order in enumerate(qkv_orders):
            span = slice(cut * columns, (cut + 1) * columns)
            product = dot_as(a_s[...], dqkv_s[span, :], 0, 1)
            store_rows(product, hidden + cut * columns, order)
            sums["qkv"[cut]].start()
        pump("b7")
        second_scatter.finish_bit(model_bits - 1)
        normed, scale = norm_parts(tokens[...].astype(full_type))
        grad_normed = total[...]
        wide_acc[0, 0:1, :] = jnp.sum(grad_normed * normed, axis=0, keepdims=True)
        grad_tokens[...] = dy_s[...] + norm_back(normed, scale, grad_normed * gain_attn[...])

        def norm_copies(stage):
            peer = partner(*all_stages[stage])[0]
            return [
                pltpu.make_async_remote_copy(
                    src_ref=acc.at[stage],
                    dst_ref=got.at[stage],
                    send_sem=norm_sems.at[0, kind, stage],
                    recv_sem=norm_sems.at[1, kind, stage],
                    device_id=peer,
                    device_id_type=MESH,
                )
                for kind, (acc, got) in enumerate(((wide_acc, wide_got), (thin_acc, thin_got)))
            ]

        def norm_step(turn):
            for copy in norm_copies(turn):
                copy.wait()
            wide_acc[turn + 1] = wide_acc[turn] + wide_got[turn]
            thin_acc[turn + 1] = thin_acc[turn] + thin_got[turn]
            if turn + 1 < len(all_stages):
                for copy in norm_copies(turn + 1):
                    copy.start()

        for copy in norm_copies(0):
            copy.start()
        turn = 0
        for name in PLAN["tail"]:
            if name == "norm":
                if turn < len(all_stages):
                    norm_step(turn)
                    turn += 1
            elif name in sums:
                sums[name].advance()
        for later in range(turn, len(all_stages)):
            norm_step(later)
        for one in sums.values():
            while not one.done():
                one.advance()
        norm_wide[...] = wide_acc[len(all_stages)]
        norm_thin[...] = thin_acc[len(all_stages)]
        for one in (demb_gather, scatter, db_gather, second_scatter):
            one.drain()


    pl.run_scoped(encoder, *scopes[2])
    rows_out[...] = row_bufs[-1][0]
    cols_out[...] = col_bufs[-1][0]
    dec_out[...] = dec_bufs[-1][0]
    embed_out[...] = embed_bufs[-1][0]


def unpack_kernel(widths, dec_list, embed_list, *refs):
    hidden, columns, wide = widths
    grad_tokens, norm_wide, norm_thin, rows_in, cols_in, dec_in, embed_in = refs[:7]
    out_tokens, g_query, g_key, g_value, g_up, g_out, g_down, g_embed = refs[7:15]
    small = refs[15:20]
    dec_outs = refs[20:]
    out_tokens[...] = grad_tokens[...]
    g_up[...] = rows_in[:, :hidden].astype(full_type)
    for position, out in enumerate((g_query, g_key, g_value)):
        first = hidden + position * columns
        out[...] = rows_in[:, first : first + columns].astype(full_type)
    g_down[...] = cols_in[:hidden, :wide].astype(full_type)
    g_out[...] = cols_in[hidden : hidden + columns, :wide].astype(full_type)
    for position in range(2):
        small[position][...] = norm_wide[position : position + 1, :]
    for position in range(3):
        small[2 + position][...] = norm_thin[position : position + 1, :]
    for outs, pieces, source in (([g_embed], embed_list, embed_in), (dec_outs, dec_list, dec_in)):
        for out, (offset, rows, width, tiles) in zip(outs, pieces):
            for tile in range(tiles):
                lanes = min(LANES, width - tile * LANES)
                block = source[offset + tile * rows : offset + (tile + 1) * rows, :lanes]
                out[:, tile * LANES : tile * LANES + lanes] = block.astype(full_type)


def decode_and_back(
    arrived,
    grid_order,
    grid_keep,
    ground_dist,
    dec_weights,
    mask_token,
    pred_proj,
    cotangent,
    tokens,
    weights,
    saved,
    dec_turned,
    embed_proj,
):
    gain_attn, w_query, w_key, w_value, w_out, gain_mlp, w_up, w_down = weights
    (dec_gain_attn, dec_query, dec_key, dec_value, dec_proj, dec_gain_mlp, dec_up, dec_down) = (
        dec_weights
    )
    data_count, model_count = lax.axis_size("dp"), lax.axis_size("mp")
    data_bits, model_bits = log2_of(data_count), log2_of(model_count)
    images, visible, width = tokens.shape
    rows = images * visible
    every = rows * model_count
    enc_heads = HE // model_count
    columns, hidden = w_query.shape[1], w_up.shape[1]
    out_width = embed_proj.shape[1] * model_count
    length, pixels = cotangent.shape[1:]
    grid_rows = images * length
    dec_hidden = dec_up.shape[1]
    matrices = [dec_query, dec_key, dec_value, dec_proj, dec_up, dec_down, pred_proj]
    pieces, height = dec_pieces(data_count, model_count, [one.shape for one in matrices])
    embed_pieces, embed_height = dec_pieces(data_count, model_count, [(width, out_width)])
    high, wide = width // data_count, width // data_count
    wide_pad = -(-wide // LANES) * LANES
    devices = data_count * model_count
    stages = data_bits + model_bits
    dec_cuts = sum(len(SUM_ORDERS[kind]) for kind in ("attn", "dup", "ddn", "pred"))
    row_shape = (high, hidden + 3 * columns)
    col_shape = (hidden + columns, wide_pad)
    vmem = pl.BlockSpec(memory_space=pltpu.VMEM)
    hbm = pl.BlockSpec(memory_space=pl.ANY)
    low = lambda *shape: pltpu.VMEM(shape, low_type)
    full = lambda *shape: pltpu.VMEM(shape, full_type)
    loaded = [w_out, w_up, w_down, *saved]
    attn_scope = [
        low(out_width, out_width),
        full(grid_rows, out_width),
        low(3 * out_width, out_width),
        low(grid_rows, out_width),
        low(3 * out_width, grid_rows),
        low(images * HD, length, length),
        full(images * HD, 1, length),
        low(out_width, grid_rows),
        full(grid_rows, out_width),
        low(grid_rows, out_width),
        full(out_width, length),
    ]
    dense_scope = [
        low(out_width, dec_hidden),
        low(dec_hidden, out_width),
        low(out_width, pixels),
        low(images, length, pixels),
        full(length, out_width),
        low(grid_rows, out_width),
        low(grid_rows, dec_hidden),
        low(grid_rows, dec_hidden),
        low(grid_rows, out_width),
        low(grid_rows, out_width),
        full(length, pixels),
    ]
    enc_scope = [pltpu.VMEM(one.shape, one.dtype) for one in loaded] + [
        low(every, width),
        low(every, hidden),
        low(3 * columns, every),
        full(rows, width),
        full(columns, rows),
    ]
    plan = (
        images,
        visible,
        enc_heads,
        HD,
        SIDE,
        pieces,
        embed_pieces[0],
        (attn_scope, dense_scope, enc_scope),
    )

    def kernel(*refs):
        back_kernel(plan, *refs)

    outs = [
        (cotangent.shape, full_type),
        ((rows, width), full_type),
        ((2, width), full_type),
        ((3, out_width), full_type),
        (row_shape, low_type),
        (col_shape, low_type),
        ((height, LANES), low_type),
        ((embed_height, LANES), low_type),
    ]
    scratch = [
        pltpu.SemaphoreType.DMA((8 + len(loaded),)),
        pltpu.SemaphoreType.DMA((images,)),
        low(images, visible, out_width),
        low(devices, height, LANES),
        full(3, out_width),
        low(images, visible, out_width),
        low(model_count, images, visible, out_width),
        low(every, width),
        full(rows, width),
        low(model_count - 1, rows, width),
        low(model_count - 1, rows, width),
        low(model_count - 1, rows, width),
        low(model_count - 1, rows, width),
        pltpu.SemaphoreType.DMA((8, model_count)),
        pltpu.SemaphoreType.DMA((2, images)),
        low(data_count, *row_shape),
        low(data_count, *col_shape),
        low(devices, embed_height, LANES),
    ]
    scratch += [low(data_count >> (bit + 1), *row_shape) for bit in range(data_bits)]
    scratch += [low(data_count >> (bit + 1), *col_shape) for bit in range(data_bits)]
    scratch += [low(devices >> (bit + 1), height, LANES) for bit in range(stages)]
    scratch += [low(devices >> (bit + 1), embed_height, LANES) for bit in range(stages)]
    for shape in ((2, width), (3, out_width)):
        scratch += [full(stages + 1, *shape), full(stages, *shape)]
    scratch += [
        pltpu.SemaphoreType.DMA((2, len(SUM_ORDERS["up"]) + 3, data_bits)),
        pltpu.SemaphoreType.DMA((2, len(SUM_ORDERS["dn"]) + 1, data_bits)),
        pltpu.SemaphoreType.DMA((2, dec_cuts, stages)),
        pltpu.SemaphoreType.DMA((2, len(SUM_ORDERS["emb"]), stages)),
        pltpu.SemaphoreType.DMA((2, 2, stages)),
    ]
    results = pl.pallas_call(
        kernel,
        out_shape=[jax.ShapeDtypeStruct(shape, kind) for shape, kind in outs],
        in_specs=[pl.BlockSpec(memory_space=pltpu.SMEM)] + [vmem] * 9 + [hbm] * (6 + len(loaded)),
        out_specs=[hbm] + [vmem] * (len(outs) - 1),
        scratch_shapes=scratch,
        compiler_params=pltpu.CompilerParams(
            collective_id=2, has_side_effects=True, vmem_limit_bytes=255 * 2**18
        ),
    )(
        ground_dist,
        arrived,
        grid_order,
        grid_keep,
        dec_gain_attn.reshape(1, -1),
        dec_gain_mlp.reshape(1, -1),
        mask_token.reshape(1, -1),
        tokens.reshape(rows, width),
        gain_attn.reshape(1, -1),
        gain_mlp.reshape(1, -1),
        dec_turned,
        dec_proj,
        dec_up,
        dec_down,
        pred_proj,
        cotangent,
        *loaded,
    )
    final = [
        (rows, width),
        (high, columns),
        (high, columns),
        (high, columns),
        (high, hidden),
        (columns, wide),
        (hidden, wide),
        (embed_pieces[0][1], embed_pieces[0][2]),
    ]
    final += [(1, width)] * 2 + [(1, out_width)] * 3
    final += [(piece[1], piece[2]) for piece in pieces]

    def last_kernel(*refs):
        unpack_kernel((hidden, columns, wide), pieces, embed_pieces, *refs)

    return results[0], pl.pallas_call(
        last_kernel,
        out_shape=[jax.ShapeDtypeStruct(shape, full_type) for shape in final],
        in_specs=[vmem] * (len(outs) - 1),
        out_specs=[vmem] * len(final),
    )(*results[1:])


def layer_norm(values, scale_gain):
    center = values - jnp.mean(values, axis=-1, keepdims=True)
    spread = jnp.mean(center * center, axis=-1, keepdims=True)
    return center * lax.rsqrt(spread + eps_norm) * scale_gain


def exact_gelu(values):
    return jax.nn.gelu(values, approximate=False)


def matmul(left_side, right_side):
    flat_rows = left_side.reshape(-1, left_side.shape[-1])
    product = jnp.dot(flat_rows, right_side, preferred_element_type=full_type)
    return product.reshape(left_side.shape[:-1] + (right_side.shape[1],))


def matmul_t(left_side, right_side):
    flat_rows = left_side.reshape(-1, left_side.shape[-1])
    product = lax.dot_general(
        flat_rows, right_side, (((1,), (1,)), ((), ())), preferred_element_type=full_type
    )
    return product.reshape(left_side.shape[:-1] + (right_side.shape[0],))


def outer_sum(left_side, right_side):
    return lax.dot_general(
        left_side.reshape(-1, left_side.shape[-1]),
        right_side.reshape(-1, right_side.shape[-1]),
        (((0,), (0,)), ((), ())),
        preferred_element_type=full_type,
    )


def spread_rows(values, tensor_split):
    if tensor_split:
        return lax.all_gather(values, "mp", axis=0, tiled=True)
    return values


def collect_rows(values, tensor_split):
    if tensor_split:
        return lax.psum_scatter(
            values.astype(jnp.bfloat16), "mp", scatter_dimension=0, tiled=True
        ).astype(jnp.float32)
    return values


def images_per_block(images, length):
    grouped = 1
    while grouped * length < 512 and grouped < images:
        grouped = grouped * 2
    return grouped


def in_blocks(blocked_array, grouped):
    return blocked_array.reshape(
        (blocked_array.shape[0] // grouped, grouped) + blocked_array.shape[1:]
    )


def with_heads(blocked_array, head_count):
    return blocked_array.reshape(
        blocked_array.shape[:2] + (head_count, blocked_array.shape[2] // head_count)
    )


def attend_forward(queries, keys_all, values_all, key_valid, head_count):
    images, length, columns = queries.shape
    grouped = images_per_block(images, length)
    scaling = float(columns // head_count) ** (-0.5)

    def one_block(pieces):
        query_b, key_b, value_b, valid_b = pieces
        scores = (
            jnp.einsum("nqhd,nkhd->nhqk", query_b, key_b, preferred_element_type=full_type)
            * scaling
        )
        scores = jnp.where(valid_b[:, None, None, :], scores, masked_score)
        row_max = jnp.max(scores, axis=-1, keepdims=True)
        weights = jnp.exp(scores - row_max)
        totals = jnp.sum(weights, axis=-1, keepdims=True)
        prob_rows = (weights / totals).astype(low_type)
        mixed_b = jnp.einsum(
            "nhqk,nkhd->nqhd", prob_rows, value_b, preferred_element_type=full_type
        )
        return (mixed_b.astype(low_type), (row_max + jnp.log(totals))[..., 0])

    pieces_in = (
        in_blocks(with_heads(queries, head_count), grouped),
        in_blocks(with_heads(keys_all, head_count), grouped),
        in_blocks(with_heads(values_all, head_count), grouped),
        in_blocks(key_valid, grouped),
    )
    mixed_rows, log_total = lax.map(one_block, pieces_in)
    return (
        mixed_rows.reshape(images, length, columns),
        log_total.reshape(images, head_count, length),
    )


def attend_backward(queries, keys_all, values_all, key_valid, log_total, grad_mixed, head_count):
    images, length, columns = queries.shape
    grouped = images_per_block(images, length)
    scaling = float(columns // head_count) ** (-0.5)

    def one_block(pieces):
        query_b, key_b, value_b, valid_b, total_b, grad_b = pieces
        scores = (
            jnp.einsum("nqhd,nkhd->nhqk", query_b, key_b, preferred_element_type=full_type)
            * scaling
        )
        scores = jnp.where(valid_b[:, None, None, :], scores, masked_score)
        prob_rows = jnp.exp(scores - total_b[..., None])
        grad_value_b = jnp.einsum(
            "nhqk,nqhd->nkhd", prob_rows.astype(low_type), grad_b, preferred_element_type=full_type
        )
        grad_probs = jnp.einsum(
            "nqhd,nkhd->nhqk", grad_b, value_b, preferred_element_type=full_type
        )
        grad_scores = prob_rows * (
            grad_probs - jnp.sum(grad_probs * prob_rows, axis=-1, keepdims=True)
        )
        grad_scores = (grad_scores * scaling).astype(low_type)
        grad_query_b = jnp.einsum(
            "nhqk,nkhd->nqhd", grad_scores, key_b, preferred_element_type=full_type
        )
        grad_key_b = jnp.einsum(
            "nhqk,nqhd->nkhd", grad_scores, query_b, preferred_element_type=full_type
        )
        return (
            grad_query_b.astype(low_type),
            grad_key_b.astype(low_type),
            grad_value_b.astype(low_type),
        )

    pieces_in = (
        in_blocks(with_heads(queries, head_count), grouped),
        in_blocks(with_heads(keys_all, head_count), grouped),
        in_blocks(with_heads(values_all, head_count), grouped),
        in_blocks(key_valid, grouped),
        in_blocks(log_total, grouped),
        in_blocks(with_heads(grad_mixed, head_count), grouped),
    )
    grad_query, grad_key, grad_value = lax.map(one_block, pieces_in)
    return (
        grad_query.reshape(images, length, columns),
        grad_key.reshape(images, length, columns),
        grad_value.reshape(images, length, columns),
    )


def block_forward(inputs, key_valid, weights, head_count, tensor_split):
    gain_attn, w_query, w_key, w_value, w_out, gain_mlp, w_up, w_down = weights
    normed = spread_rows(layer_norm(inputs, gain_attn).astype(low_type), tensor_split)
    queries = matmul(normed, w_query).astype(low_type)
    keys_all = matmul(normed, w_key).astype(low_type)
    values_all = matmul(normed, w_value).astype(low_type)
    mixed_rows, log_total = attend_forward(queries, keys_all, values_all, key_valid, head_count)
    middle = inputs + collect_rows(matmul(mixed_rows, w_out), tensor_split)
    second = spread_rows(layer_norm(middle, gain_mlp).astype(low_type), tensor_split)
    pre_act = matmul(second, w_up)
    active = exact_gelu(pre_act).astype(low_type)
    outputs = middle + collect_rows(matmul(active, w_down), tensor_split)
    kept_state = (
        inputs,
        normed,
        queries,
        keys_all,
        values_all,
        mixed_rows,
        log_total,
        middle,
        second,
        pre_act,
        active,
    )
    return (outputs, kept_state)


def block_backward(grad_out, kept_state, key_valid, weights, head_count, tensor_split):
    gain_attn, w_query, w_key, w_value, w_out, gain_mlp, w_up, w_down = weights
    (
        inputs,
        normed,
        queries,
        keys_all,
        values_all,
        mixed_rows,
        log_total,
        middle,
        second,
        pre_act,
        active,
    ) = kept_state
    grad_branch = spread_rows(grad_out.astype(low_type), tensor_split)
    grad_down = outer_sum(active, grad_branch)
    grad_active = matmul_t(grad_branch, w_down)
    grad_pre = jax.vjp(exact_gelu, pre_act)[1](grad_active)[0].astype(low_type)
    grad_up = outer_sum(second, grad_pre)
    grad_second = collect_rows(matmul_t(grad_pre, w_up), tensor_split)
    norm_grad, grad_gain_mlp = jax.vjp(layer_norm, middle, gain_mlp)[1](grad_second)
    grad_middle = grad_out + norm_grad
    grad_attn = spread_rows(grad_middle.astype(low_type), tensor_split)
    grad_w_out = outer_sum(mixed_rows, grad_attn)
    grad_mixed = matmul_t(grad_attn, w_out).astype(low_type)
    grad_query, grad_key, grad_value = attend_backward(
        queries, keys_all, values_all, key_valid, log_total, grad_mixed, head_count
    )
    grad_w_query = outer_sum(normed, grad_query)
    grad_w_key = outer_sum(normed, grad_key)
    grad_w_value = outer_sum(normed, grad_value)
    grad_normed = (
        matmul_t(grad_query, w_query) + matmul_t(grad_key, w_key) + matmul_t(grad_value, w_value)
    )
    grad_normed = collect_rows(grad_normed, tensor_split)
    input_grad, grad_gain_attn = jax.vjp(layer_norm, inputs, gain_attn)[1](grad_normed)
    return (
        grad_middle + input_grad,
        (
            grad_gain_attn,
            grad_w_query,
            grad_w_key,
            grad_w_value,
            grad_w_out,
            grad_gain_mlp,
            grad_up,
            grad_down,
        ),
    )


def grid_codes(distance, side_count, columns):
    quarter = columns // 4
    frequency = 10000.0 ** (-jnp.arange(quarter, dtype=full_type) / quarter)
    places = jnp.arange(side_count * side_count)
    row_pos = (places // side_count).astype(full_type)
    col_pos = (places % side_count).astype(full_type)
    row_angle = distance[:, None, None] * row_pos[None, :, None] * frequency[None, None, :]
    col_angle = distance[:, None, None] * col_pos[None, :, None] * frequency[None, None, :]
    return jnp.concatenate(
        [jnp.sin(row_angle), jnp.cos(row_angle), jnp.sin(col_angle), jnp.cos(col_angle)], axis=-1
    )


def placement_table(visible_order, keep_flags, visible):
    positions = jnp.arange(visible_order.shape[1])
    matches = (visible_order[:, None, :visible] == positions[None, :, None]) & (
        keep_flags[:, :, None] == 1
    )
    return matches.astype(low_type)


def owner_blocks(full_grad, data_count, model_count):
    row_count, col_count = full_grad.shape
    reshaped = full_grad.reshape(
        data_count, row_count // data_count, model_count, col_count // model_count
    )
    return jnp.transpose(reshaped, (0, 2, 1, 3)).reshape(
        data_count * model_count, row_count // data_count, col_count // model_count
    )


def per_device_plain(
    tokens,
    lengths,
    grid_order,
    grid_keep,
    ground_dist,
    enc_norm,
    enc_query,
    enc_key,
    enc_value,
    enc_proj,
    enc_norm2,
    enc_up,
    enc_down,
    embed_proj,
    mask_token,
    dec_norm,
    dec_query,
    dec_key,
    dec_value,
    dec_proj,
    dec_norm2,
    dec_up,
    dec_down,
    pred_proj,
    cotangent,
):
    data_count = lax.axis_size("dp")
    model_count = lax.axis_size("mp")
    enc_weights = (enc_norm, enc_query, enc_key, enc_value, enc_proj, enc_norm2, enc_up, enc_down)
    dec_weights = (dec_norm, dec_query, dec_key, dec_value, dec_proj, dec_norm2, dec_up, dec_down)
    enc_heads = HE // model_count
    key_valid = jnp.arange(tokens.shape[1])[None, :] < lengths[:, None]
    enc_out, enc_saved = block_forward(
        tokens.astype(full_type), key_valid, enc_weights, enc_heads, True
    )
    enc_low = enc_out.astype(low_type)
    enc_all = spread_rows(enc_low, True)
    embedded = matmul(enc_all, embed_proj).astype(low_type)
    sectioned = embedded.reshape((data_count, -1) + embedded.shape[1:])
    arrived = lax.all_to_all(
        lax.all_to_all(sectioned, "dp", split_axis=0, concat_axis=0, tiled=True),
        "mp",
        split_axis=0,
        concat_axis=3,
        tiled=True,
    )
    arrived = arrived.reshape((-1,) + arrived.shape[2:])
    pick_table = placement_table(grid_order, grid_keep, arrived.shape[1])
    masked = (1 - grid_keep).astype(full_type)[..., None]
    dec_start = jnp.einsum("npt,ntc->npc", pick_table, arrived, preferred_element_type=full_type)
    dec_start = dec_start + masked * mask_token + grid_codes(ground_dist, SIDE, mask_token.shape[0])
    all_valid = jnp.ones(dec_start.shape[:2], jnp.bool_)
    dec_out, dec_saved = block_forward(dec_start, all_valid, dec_weights, HD, False)
    dec_low = dec_out.astype(low_type)
    decoded = matmul(dec_low, pred_proj)
    grad_pred = outer_sum(dec_low, cotangent)
    grad_dec_out = matmul_t(cotangent, pred_proj)
    grad_start, dec_grads = block_backward(
        grad_dec_out, dec_saved, all_valid, dec_weights, HD, False
    )
    grad_mask = jnp.sum(masked * grad_start, axis=(0, 1))
    grad_arrived = jnp.einsum("npt,npc->ntc", pick_table.astype(full_type), grad_start).astype(
        low_type
    )
    sent_back = grad_arrived.reshape((-1, IPD) + grad_arrived.shape[1:])
    returned = lax.all_to_all(
        lax.all_to_all(sent_back, "mp", split_axis=3, concat_axis=0, tiled=True),
        "dp",
        split_axis=0,
        concat_axis=0,
        tiled=True,
    )
    returned = returned.reshape((-1,) + returned.shape[2:])
    grad_embed = outer_sum(enc_all, returned)
    grad_enc_out = collect_rows(matmul_t(returned, embed_proj), True)
    grad_tokens, enc_grads = block_backward(
        grad_enc_out, enc_saved, key_valid, enc_weights, enc_heads, True
    )
    col_sums = (
        lax.psum_scatter(
            enc_grads[4].astype(jnp.bfloat16), "dp", scatter_dimension=1, tiled=True
        ).astype(jnp.float32),
        lax.psum_scatter(
            enc_grads[7].astype(jnp.bfloat16), "dp", scatter_dimension=1, tiled=True
        ).astype(jnp.float32),
    )
    norm_grads = lax.psum(
        (enc_grads[0], enc_grads[5], dec_grads[0], dec_grads[5], grad_mask), ("dp", "mp")
    )
    dec_list = (
        dec_grads[1],
        dec_grads[2],
        dec_grads[3],
        dec_grads[4],
        dec_grads[6],
        dec_grads[7],
        grad_pred,
    )
    row_sums = (
        lax.psum_scatter(
            enc_grads[1].astype(jnp.bfloat16), "dp", scatter_dimension=0, tiled=True
        ).astype(jnp.float32),
        lax.psum_scatter(
            enc_grads[2].astype(jnp.bfloat16), "dp", scatter_dimension=0, tiled=True
        ).astype(jnp.float32),
        lax.psum_scatter(
            enc_grads[3].astype(jnp.bfloat16), "dp", scatter_dimension=0, tiled=True
        ).astype(jnp.float32),
        lax.psum_scatter(
            enc_grads[6].astype(jnp.bfloat16), "dp", scatter_dimension=0, tiled=True
        ).astype(jnp.float32),
        lax.psum_scatter(
            grad_embed.astype(jnp.bfloat16), "dp", scatter_dimension=0, tiled=True
        ).astype(jnp.float32),
    )
    summed = (
        lax.psum_scatter(
            owner_blocks(dec_list[0], data_count, model_count),
            ("dp", "mp"),
            scatter_dimension=0,
            tiled=True,
        ),
        lax.psum_scatter(
            owner_blocks(dec_list[1], data_count, model_count),
            ("dp", "mp"),
            scatter_dimension=0,
            tiled=True,
        ),
        lax.psum_scatter(
            owner_blocks(dec_list[2], data_count, model_count),
            ("dp", "mp"),
            scatter_dimension=0,
            tiled=True,
        ),
        lax.psum_scatter(
            owner_blocks(dec_list[3], data_count, model_count),
            ("dp", "mp"),
            scatter_dimension=0,
            tiled=True,
        ),
        lax.psum_scatter(
            owner_blocks(dec_list[4], data_count, model_count),
            ("dp", "mp"),
            scatter_dimension=0,
            tiled=True,
        ),
        lax.psum_scatter(
            owner_blocks(dec_list[5], data_count, model_count),
            ("dp", "mp"),
            scatter_dimension=0,
            tiled=True,
        ),
        lax.psum_scatter(
            owner_blocks(dec_list[6], data_count, model_count),
            ("dp", "mp"),
            scatter_dimension=0,
            tiled=True,
        ),
    )
    embed_final = row_sums[4]
    dec_final = tuple((summed[index_num][0] for index_num in range(7)))
    return (
        decoded,
        grad_tokens,
        norm_grads[0],
        row_sums[0],
        row_sums[1],
        row_sums[2],
        col_sums[0],
        norm_grads[1],
        row_sums[3],
        col_sums[1],
        embed_final,
        norm_grads[4],
        norm_grads[2],
        dec_final[0],
        dec_final[1],
        dec_final[2],
        dec_final[3],
        norm_grads[3],
        dec_final[4],
        dec_final[5],
        dec_final[6],
    )


VMEM_BUDGET = 56 * 2**20


def kernel_bytes(tokens, enc_up, enc_query, dec_up, pred_proj):
    data_count, model_count = lax.axis_size("dp"), lax.axis_size("mp")
    images, visible, width = tokens.shape
    every = images * visible * model_count
    hidden, columns = enc_up.shape[1], enc_query.shape[1]
    out_width, wide = dec_up.shape[0], max(width // data_count, LANES)
    shapes = [(out_width, out_width)] * 4
    shapes += [dec_up.shape, dec_up.shape[::-1], pred_proj.shape, (width, out_width)]
    height = dec_pieces(data_count, model_count, shapes)[1]
    rows = 8 * every * width + 3 * every * hidden
    sums = width * (hidden + 3 * columns) + data_count * (hidden + columns) * wide
    sums = 2 * (sums + data_count * model_count * height * LANES)
    return 2 * (rows + sums + 2 * width * hidden + 4 * width * columns)


def per_device(
    tokens,
    lengths,
    grid_order,
    grid_keep,
    ground_dist,
    enc_norm,
    enc_query,
    enc_key,
    enc_value,
    enc_proj,
    enc_norm2,
    enc_up,
    enc_down,
    embed_proj,
    mask_token,
    dec_norm,
    dec_query,
    dec_key,
    dec_value,
    dec_proj,
    dec_norm2,
    dec_up,
    dec_down,
    pred_proj,
    cotangent,
):
    fits = kernel_bytes(tokens, enc_up, enc_query, dec_up, pred_proj) <= VMEM_BUDGET
    if not fits or lax.axis_size("mp") != 4:
        return per_device_plain(
            tokens,
            lengths,
            grid_order,
            grid_keep,
            ground_dist,
            enc_norm,
            enc_query,
            enc_key,
            enc_value,
            enc_proj,
            enc_norm2,
            enc_up,
            enc_down,
            embed_proj,
            mask_token,
            dec_norm,
            dec_query,
            dec_key,
            dec_value,
            dec_proj,
            dec_norm2,
            dec_up,
            dec_down,
            pred_proj,
            cotangent,
        )
    enc_weights = (enc_norm, enc_query, enc_key, enc_value, enc_proj, enc_norm2, enc_up, enc_down)
    dec_weights = (dec_norm, dec_query, dec_key, dec_value, dec_proj, dec_norm2, dec_up, dec_down)
    dec_inputs = (dec_query, dec_key, dec_value)
    arrived, *saved, dec_turned = encode(tokens, lengths, enc_weights, embed_proj, dec_inputs)
    decoded, grads = decode_and_back(
        arrived,
        grid_order,
        grid_keep,
        ground_dist,
        dec_weights,
        mask_token,
        pred_proj,
        cotangent,
        tokens,
        enc_weights,
        saved,
        dec_turned,
        embed_proj,
    )
    (
        grad_tokens,
        g_query,
        g_key,
        g_value,
        g_up,
        g_out,
        g_down,
        g_embed,
        n_enc_attn,
        n_enc_mlp,
        n_dec_attn,
        n_dec_mlp,
        n_mask,
        *dec_grads,
    ) = grads
    return (
        decoded,
        grad_tokens.reshape(tokens.shape),
        n_enc_attn[0],
        g_query,
        g_key,
        g_value,
        g_out,
        n_enc_mlp[0],
        g_up,
        g_down,
        g_embed,
        n_mask[0],
        n_dec_attn[0],
        dec_grads[0],
        dec_grads[1],
        dec_grads[2],
        dec_grads[3],
        n_dec_mlp[0],
        dec_grads[4],
        dec_grads[5],
        dec_grads[6],
    )


def solution(mesh):
    return jax.shard_map(
        per_device,
        mesh=mesh,
        in_specs=(
            P(("dp", "mp"), None, None),
            P("dp"),
            P(("dp", "mp"), None),
            P(("dp", "mp"), None),
            P(("dp", "mp")),
            P(),
            P(None, "mp"),
            P(None, "mp"),
            P(None, "mp"),
            P("mp", None),
            P(),
            P(None, "mp"),
            P("mp", None),
            P(None, "mp"),
            P(),
            P(),
            P(),
            P(),
            P(),
            P(),
            P(),
            P(),
            P(),
            P(),
            P(("dp", "mp"), None, None),
        ),
        out_specs=(
            P(("dp", "mp"), None, None),
            P(("dp", "mp"), None, None),
            P(),
            P("dp", "mp"),
            P("dp", "mp"),
            P("dp", "mp"),
            P("mp", "dp"),
            P(),
            P("dp", "mp"),
            P("mp", "dp"),
            P("dp", "mp"),
            P(),
            P(),
            P("dp", "mp"),
            P("dp", "mp"),
            P("dp", "mp"),
            P("dp", "mp"),
            P(),
            P("dp", "mp"),
            P("dp", "mp"),
            P("dp", "mp"),
        ),
        check_vma=False,
    )
```

```python
import math

import jax
import jax.numpy as jnp
from jax import lax
from jax.experimental import pallas as pl
from jax.experimental.pallas import tpu as pltpu
from jax.sharding import PartitionSpec as P

HE = 16
HD = 16
SIDE = 16
IPD = 1


eps_norm = 1e-06
masked_score = -1e30
low_type = jnp.bfloat16
full_type = jnp.float32


MESH = pl.DeviceIdType.MESH
LANES = 128


def log2_of(count):
    bits = count.bit_length() - 1
    assert 1 << bits == count
    return bits


def spot_of(data, model, stages):
    out = 0
    for axis, bit in stages:
        out = out * 2 + (((data if axis == "dp" else model) >> bit) & 1)
    return out


def partner(axis, bit):
    dp, mp = lax.axis_index("dp"), lax.axis_index("mp")
    step = 1 << bit
    if axis == "dp":
        return (dp ^ step, mp), (dp >> bit) & 1
    return (dp, mp ^ step), (mp >> bit) & 1


def enter_barrier(partners):
    barrier = pltpu.get_barrier_semaphore()
    for peer in partners:
        pl.semaphore_signal(barrier, inc=1, device_id=peer, device_id_type=MESH)
    pl.semaphore_wait(barrier, len(partners))


class HalvingSum:
    def __init__(self, stages, buffers, window, send_sems, recv_sems):
        self.stages, self.buffers, self.window = stages, buffers, window
        self.send_sems, self.recv_sems = send_sems, recv_sems

    def view(self, index, start, size):
        return self.buffers[index].at[(pl.ds(start, size),) + self.window]

    def copy(self, index):
        peer, mine = partner(*self.stages[index])
        half = self.buffers[index].shape[0] // 2
        return pltpu.make_async_remote_copy(
            src_ref=self.view(index, (1 - mine) * half, half),
            dst_ref=self.view(index + 1, 0, half),
            send_sem=self.send_sems.at[index],
            recv_sem=self.recv_sems.at[index],
            device_id=peer,
            device_id_type=MESH,
        )

    def start(self, index):
        self.copy(index).start()

    def finish(self, index):
        self.copy(index).wait()
        peer, mine = partner(*self.stages[index])
        half = self.buffers[index].shape[0] // 2

        def one(position, carry):
            there = self.buffers[index + 1].at[(position,) + self.window]
            here = self.buffers[index].at[(mine * half + position,) + self.window]
            there[...] = there[...] + here[...]
            return carry

        lax.fori_loop(0, half, one, 0)


def dec_pieces(data_count, model_count, shapes):
    offset, pieces = 0, []
    for rows, columns in shapes:
        height, width = rows // data_count, columns // model_count
        tiles = -(-width // LANES)
        pieces.append((offset, height, width, tiles))
        offset += height * tiles
    return pieces, offset


LOG2E = 1.4426950408889634


def dot_as(left, right, left_dim, right_dim):
    return lax.dot_general(
        left, right, (((left_dim,), (right_dim,)), ((), ())), preferred_element_type=full_type
    )


def norm_parts(values):
    center = values - jnp.mean(values, axis=-1, keepdims=True)
    scale = lax.rsqrt(jnp.mean(center * center, axis=-1, keepdims=True) + eps_norm)
    return center * scale, scale


def norm_back(normed, scale, grad_scaled):
    first = jnp.mean(grad_scaled, axis=-1, keepdims=True)
    second = jnp.mean(grad_scaled * normed, axis=-1, keepdims=True)
    return (grad_scaled - first - normed * second) * scale


def gelu_pair(values):
    below = 0.5 + 0.5 * lax.erf(values * (0.5**0.5))
    density = jnp.exp2(values * values * (-0.5 * LOG2E)) * ((2.0 * math.pi) ** -0.5)
    return values * below, below + values * density


def low_bit(mask):
    return (mask & -mask).bit_length() - 1


def visit_order(count):
    return sorted(range(count), key=lambda mask: (mask.bit_length(), -mask))


def visit_mask(step, count):
    mask = jnp.int32(0)
    for position, value in enumerate(visit_order(count)):
        mask = jnp.where(step == position, value, mask)
    return mask


class Gather:
    def __init__(self, own, slot_view, send_sems, recv_sems):
        self.own, self.slot_view = own, slot_view
        self.send_sems, self.recv_sems = send_sems, recv_sems
        self.count = lax.axis_size("mp")
        self.index = lax.axis_index("mp")

    def copy(self, mask):
        bit = low_bit(mask)
        carried = mask ^ (1 << bit)
        place = self.slot_view(self.index ^ carried)
        return pltpu.make_async_remote_copy(
            src_ref=self.own if carried == 0 and self.own is not None else place,
            dst_ref=place,
            send_sem=self.send_sems.at[mask],
            recv_sem=self.recv_sems.at[mask],
            device_id=partner("mp", bit)[0],
            device_id_type=MESH,
        )

    def start(self):
        for bit in reversed(range(log2_of(self.count))):
            self.copy(1 << bit).start()

    def arrive(self, mask):
        self.copy(mask).wait_recv()
        for bit in reversed(range(low_bit(mask))):
            self.copy(mask | (1 << bit)).start()

    def arrive_group(self, length):
        group = [mask for mask in range(1, self.count) if mask.bit_length() == length]
        for mask in sorted(group, key=lambda one: -low_bit(one)):
            self.arrive(mask)

    def arrive_all(self):
        for length in range(1, log2_of(self.count) + 1):
            self.arrive_group(length)

    def arrive_at(self, step):
        for length in range(1, log2_of(self.count) + 1):
            @pl.when(step == 1 << (length - 1))
            def _():
                self.arrive_group(length)

    def drain(self):
        for mask in range(1, self.count):
            self.copy(mask).wait_send()


class Scatter:
    def __init__(self, parts, total, landing, send_sems, recv_sems):
        self.parts, self.total, self.landing = parts, total, landing
        self.send_sems, self.recv_sems = send_sems, recv_sems
        self.count = lax.axis_size("mp")
        self.index = lax.axis_index("mp")

    def copy(self, mask):
        return pltpu.make_async_remote_copy(
            src_ref=self.parts.at[mask - 1],
            dst_ref=self.landing.at[mask - 1],
            send_sem=self.send_sems.at[mask],
            recv_sem=self.recv_sems.at[mask],
            device_id=partner("mp", low_bit(mask))[0],
            device_id_type=MESH,
        )

    def put(self, mask, product):
        @pl.when(mask == 0)
        def _():
            self.total[...] = self.total[...] + product

        @pl.when(mask != 0)
        def _():
            self.parts[mask - 1] = product.astype(low_type)

        for odd in range(1, self.count, 2):
            @pl.when(mask == odd)
            def _():
                self.copy(odd).start()

    def finish(self, mask):
        bit = low_bit(mask)
        self.copy(mask).wait_recv()
        rest = mask ^ (1 << bit)
        if rest:
            self.parts[rest - 1] = self.parts[rest - 1] + self.landing[mask - 1]
            if low_bit(rest) == bit + 1:
                self.copy(rest).start()
        else:
            self.total[...] = self.total[...] + self.landing[mask - 1].astype(full_type)

    def finish_bit(self, bit):
        masks = [mask for mask in range(1, self.count) if low_bit(mask) == bit]
        for mask in reversed(masks):
            self.finish(mask)

    def drain(self):
        for mask in range(1, self.count):
            self.copy(mask).wait_send()


def exchange_partners(images):
    data_count, model_count = lax.axis_size("dp"), lax.axis_size("mp")
    data, model = lax.axis_index("dp"), lax.axis_index("mp")
    out = []
    for image in range(images):
        spot = (model * images + image) * data_count + data
        device = spot // images
        out.append((device // model_count, device % model_count, spot % images))
    return out


def is_here(peer):
    return (peer[0] == lax.axis_index("dp")) & (peer[1] == lax.axis_index("mp"))


class Exchange:
    def __init__(self, images, source, target, send_sems, recv_sems):
        self.partners = exchange_partners(images)
        self.source, self.target = source, target
        self.send_sems, self.recv_sems = send_sems, recv_sems

    def copy(self, image):
        data, model, slot = self.partners[image]
        return pltpu.make_async_remote_copy(
            src_ref=self.source.at[image],
            dst_ref=self.target.at[slot],
            send_sem=self.send_sems.at[image],
            recv_sem=self.recv_sems.at[slot],
            device_id=(data, model),
            device_id_type=MESH,
        )

    def start_one(self, image):
        data, model, slot = self.partners[image]
        here = is_here((data, model))

        @pl.when(here)
        def _():
            self.target[slot] = self.source[image]

        @pl.when(jnp.logical_not(here))
        def _():
            self.copy(image).start()

    def start(self):
        for image in range(len(self.partners)):
            self.start_one(image)

    def finish(self):
        for image, (data, model, slot) in enumerate(self.partners):
            @pl.when(jnp.logical_not(is_here((data, model))))
            def _():
                pltpu.make_async_remote_copy(
                    src_ref=self.source.at[image],
                    dst_ref=self.target.at[image],
                    send_sem=self.send_sems.at[image],
                    recv_sem=self.recv_sems.at[image],
                    device_id=(data, model),
                    device_id_type=MESH,
                ).wait()


class Move:
    def __init__(self, source, target, sem):
        self.copy = pltpu.make_async_copy(source, target, sem)
        self.copy.start()

    def wait(self):
        if self.copy is not None:
            self.copy.wait()
            self.copy = None


def signal_partners(images, axes):
    barrier = pltpu.get_barrier_semaphore()
    count = images
    for axis in axes:
        for bit in range(log2_of(lax.axis_size(axis))):
            count += 1
            pl.semaphore_signal(
                barrier, inc=1, device_id=partner(axis, bit)[0], device_id_type=MESH
            )
    for data, model, slot in exchange_partners(images):
        pl.semaphore_signal(barrier, inc=1, device_id=(data, model), device_id_type=MESH)
    return count


def encoder_barrier(images, axes):
    count = signal_partners(images, axes)
    pl.semaphore_wait(pltpu.get_barrier_semaphore(), count)


def encoder_kernel(images, visible, heads, *refs):
    (
        lengths,
        tokens,
        gain_attn,
        w_query_hbm,
        w_key_hbm,
        w_value_hbm,
        w_out,
        gain_mlp,
        w_up_hbm,
        w_down_hbm,
        w_embed,
        *dec_hbm,
        arrived,
    ) = refs[:15]
    saved_hbm = refs[15:28]
    (
        w_query,
        w_key,
        w_value,
        w_up,
        w_down,
        a_s,
        qkv_s,
        e_s,
        inv_s,
        o_own,
        c_s,
        g_s,
        slope_s,
        mid_s,
        low_s,
        embed_full,
        qkv_weights,
        dec_turned,
        dec_query,
        dec_key,
        dec_value,
        move_sems,
        token_slots,
        out_pair,
        o_pair,
        part_own,
        part_sent,
        part_got,
        embed_slots,
        parts,
        landing,
        total,
        embedded,
        sems,
        swap_sems,
        pair_sems,
    ) = refs[28:]
    count = lax.axis_size("mp")
    index = lax.axis_index("mp")
    block_rows = images * visible
    columns = w_query.shape[1]
    size = columns // heads
    scaling = float(size) ** -0.5
    hidden = w_up.shape[1]
    chunk = 512

    loads = [
        Move(source, target, move_sems.at[position])
        for position, (source, target) in enumerate(
            (
                (w_query_hbm, w_query),
                (w_key_hbm, w_key),
                (w_value_hbm, w_value),
                (w_up_hbm, w_up),
                (w_down_hbm, w_down),
                (dec_hbm[0], dec_query),
                (dec_hbm[1], dec_key),
                (dec_hbm[2], dec_value),
            )
        )
    ]
    saved = [a_s, qkv_s, e_s, inv_s, o_own, c_s, g_s, slope_s, mid_s, low_s, embed_full]
    saved += [qkv_weights, dec_turned]
    stores = []

    def save(*arrays):
        for array in arrays:
            position = [array is one for one in saved].index(True)
            stores.append(Move(array, saved_hbm[position], move_sems.at[len(loads) + position]))

    encoder_barrier(images, ["mp"])
    token_gather = Gather(
        tokens, lambda slot: token_slots.at[slot], sems.at[0], sems.at[1]
    )
    near, far = 0, 1

    def rows_of(slot):
        return pl.ds(pl.multiple_of(slot * block_rows, block_rows), block_rows)

    def pair_copy(which, source, target, bit):
        return pltpu.make_async_remote_copy(
            src_ref=source,
            dst_ref=target,
            send_sem=pair_sems.at[0, which],
            recv_sem=pair_sems.at[1, which],
            device_id=partner("mp", bit)[0],
            device_id_type=MESH,
        )

    out_copy = pair_copy(0, w_out, out_pair.at[columns : 2 * columns], near)

    def o_copy(mine):
        block = index ^ (1 + 2 * mine)
        target = o_pair.at[mine, columns : 2 * columns]
        return pair_copy(1 + mine, o_own.at[:, rows_of(block)], target, near)

    def part_copy(mine):
        return pair_copy(3 + mine, part_sent.at[mine], part_got.at[1 - mine], far)

    def c_copy(mine):
        place = c_s.at[rows_of(index ^ (2 * mine))]
        return pair_copy(5 + mine, place, place, near)

    embed_gather = Gather(w_embed, lambda slot: embed_slots.at[slot], sems.at[6], sems.at[7])
    scatter = Scatter(parts, total, landing, sems.at[8], sems.at[9])
    swap = Exchange(images, embedded, arrived, swap_sems.at[0], swap_sems.at[1])

    token_gather.start()
    out_copy.start()
    token_slots[index] = tokens[...]
    out_pair[:columns, :] = w_out[...]
    embed_slots[index] = w_embed[...]
    for position, weight in enumerate((w_query, w_key, w_value)):
        loads[position].wait()
        qkv_weights[position * columns : (position + 1) * columns, :] = weight[...].T
    dec_width = dec_query.shape[0]
    for position, weight in enumerate((dec_query, dec_key, dec_value)):
        loads[5 + position].wait()
        dec_turned[position * dec_width : (position + 1) * dec_width, :] = weight[...].T
    save(qkv_weights, dec_turned)

    def attend(step, carry):
        token_gather.arrive_at(step)

        slot = index ^ visit_mask(step, count)
        rows = rows_of(slot)
        normed, scale = norm_parts(token_slots[slot].astype(full_type))
        a_s[rows, :] = (normed * gain_attn[...]).astype(low_type)
        for position in range(3):
            span = slice(position * columns, (position + 1) * columns)
            part = dot_as(qkv_weights[span, :], a_s[rows, :], 1, 1)
            if position == 0:
                part = part * (scaling * LOG2E)
            qkv_s[span, rows] = part.astype(low_type)
        key_row = lax.broadcasted_iota(jnp.int32, (block_rows, block_rows), 0)
        query_row = lax.broadcasted_iota(jnp.int32, (block_rows, block_rows), 1)
        valid = jnp.zeros((block_rows, block_rows), jnp.bool_)
        for image in range(images):
            first = image * visible
            keys = (key_row >= first) & (key_row < first + lengths[slot * images + image])
            valid = valid | (keys & (query_row >= first) & (query_row < first + visible))
        for head in range(heads):
            span = slice(head * size, (head + 1) * size)
            query = qkv_s[span, rows]
            key = qkv_s[columns + head * size : columns + (head + 1) * size, rows]
            value = qkv_s[2 * columns + head * size : 2 * columns + (head + 1) * size, rows]
            scores = jnp.where(valid, dot_as(key, query, 0, 0), masked_score)
            weights = jnp.exp2(scores - jnp.max(scores, axis=0, keepdims=True))
            inverse = 1.0 / jnp.sum(weights, axis=0, keepdims=True)
            weights = weights.astype(low_type)
            e_s[slot * heads + head] = weights
            inv_s[slot * heads + head] = inverse
            mixed = jnp.dot(value, weights, preferred_element_type=full_type)
            o_own[span, rows] = (mixed * inverse).astype(low_type)
        for turn, mine in ((1, 0), (2, 1)):
            @pl.when(step == turn)
            def _():
                o_copy(mine).start()

        for turn, mine in ((0, 0), (3, 1)):
            @pl.when(step == turn)
            def _():
                o_pair[mine, :columns, :] = o_own[:, rows]

        return carry

    def sum_heads(mine):
        o_copy(mine).wait_recv()
        part = dot_as(o_pair[mine], out_pair[...], 0, 0)
        part_own[mine] = part
        part_sent[mine] = part.astype(low_type)
        part_copy(mine).start()

    def middle_of(mine):
        part_copy(1 - mine).wait_recv()
        slot = index ^ (2 * mine)
        middle = token_slots[slot].astype(full_type) + part_own[mine]
        middle = middle + part_got[mine].astype(full_type)
        if mine == 0:
            mid_s[...] = middle
        normed, scale = norm_parts(middle)
        c_s[rows_of(slot), :] = (normed * gain_mlp[...]).astype(low_type)
        c_copy(mine).start()

    lax.fori_loop(0, 2, attend, 0)
    out_copy.wait_recv()
    sum_heads(0)
    lax.fori_loop(2, 4, attend, 0)
    sum_heads(1)
    embed_gather.start()
    save(a_s, qkv_s, e_s, inv_s, o_own)
    for move in loads:
        move.wait()
    total[...] = jnp.zeros_like(total)

    def expand(mask, carry):
        for odd in (1, 3):
            @pl.when(mask == odd)
            def _():
                c_copy(odd // 2).wait_recv()

        rows = rows_of(index ^ mask)
        for first in range(0, hidden, chunk):
            cols = slice(first, first + chunk)
            pre = jnp.dot(c_s[rows, :], w_up[:, cols], preferred_element_type=full_type)
            active, slope = gelu_pair(pre)
            g_s[rows, cols] = active.astype(low_type)
            slope_s[rows, cols] = slope.astype(low_type)
        scatter.put(
            mask, jnp.dot(g_s[rows, :], w_down[...], preferred_element_type=full_type)
        )
        return carry

    middle_of(1)
    lax.fori_loop(2, 4, expand, 0)
    scatter.finish(3)
    middle_of(0)
    lax.fori_loop(0, 2, expand, 0)
    scatter.finish(1)
    save(c_s, g_s, slope_s, mid_s)
    embed_gather.arrive_all()
    width = w_embed.shape[1]
    for slot in range(count):
        embed_full[:, slot * width : (slot + 1) * width] = embed_slots[slot]
    scatter.finish(2)
    low_s[...] = (mid_s[...] + total[...]).astype(low_type)
    for image in range(images):
        own = low_s[image * visible : (image + 1) * visible, :]
        out = jnp.dot(own, embed_full[...], preferred_element_type=full_type)
        embedded[image] = out.astype(low_type)
        swap.start_one(image)
    save(embed_full, low_s)
    for one in (token_gather, embed_gather, scatter):
        one.drain()
    out_copy.wait_send()
    for mine in range(2):
        for copy in (o_copy(mine), part_copy(mine), c_copy(mine)):
            copy.wait_send()
    for move in stores:
        move.wait()
    swap.finish()


def encode(tokens, lengths, weights, embed_proj, dec_inputs):
    gain_attn, w_query, w_key, w_value, w_out, gain_mlp, w_up, w_down = weights
    model_count = lax.axis_size("mp")
    images, visible, width = tokens.shape
    rows = images * visible
    heads = HE // model_count
    columns, hidden = w_query.shape[1], w_up.shape[1]
    out_width = embed_proj.shape[1] * model_count
    every = rows * model_count

    def kernel(*refs):
        encoder_kernel(images, visible, heads, *refs)

    vmem = pl.BlockSpec(memory_space=pltpu.VMEM)
    hbm = pl.BlockSpec(memory_space=pl.ANY)
    shapes = [
        ((images, visible, out_width), low_type),
        ((every, width), low_type),
        ((3 * columns, every), low_type),
        ((model_count * heads, rows, rows), low_type),
        ((model_count * heads, 1, rows), full_type),
        ((columns, every), low_type),
        ((every, width), low_type),
        ((every, hidden), low_type),
        ((every, hidden), low_type),
        ((rows, width), full_type),
        ((rows, width), low_type),
        ((width, out_width), low_type),
        ((3 * columns, width), low_type),
        ((3 * out_width, out_width), low_type),
    ]
    return pl.pallas_call(
        kernel,
        out_shape=[jax.ShapeDtypeStruct(shape, kind) for shape, kind in shapes],
        in_specs=[pl.BlockSpec(memory_space=pltpu.SMEM)]
        + [vmem] * 2
        + [hbm] * 3
        + [vmem] * 2
        + [hbm] * 2
        + [vmem]
        + [hbm] * 3,
        out_specs=[vmem] + [hbm] * (len(shapes) - 1),
        scratch_shapes=[
            pltpu.VMEM((width, columns), low_type),
            pltpu.VMEM((width, columns), low_type),
            pltpu.VMEM((width, columns), low_type),
            pltpu.VMEM((width, hidden), low_type),
            pltpu.VMEM((hidden, width), low_type),
        ]
        + [pltpu.VMEM(shape, kind) for shape, kind in shapes[1:]]
        + [pltpu.VMEM((out_width, out_width), low_type)] * 3
        + [
            pltpu.SemaphoreType.DMA((8 + len(shapes),)),
            pltpu.VMEM((model_count, rows, width), low_type),
            pltpu.VMEM((2 * columns, width), low_type),
            pltpu.VMEM((2, 2 * columns, rows), low_type),
            pltpu.VMEM((2, rows, width), full_type),
            pltpu.VMEM((2, rows, width), low_type),
            pltpu.VMEM((2, rows, width), low_type),
            pltpu.VMEM((model_count,) + embed_proj.shape, low_type),
            pltpu.VMEM((model_count - 1, rows, width), low_type),
            pltpu.VMEM((model_count - 1, rows, width), low_type),
            pltpu.VMEM((rows, width), full_type),
            pltpu.VMEM((images, visible, out_width), low_type),
            pltpu.SemaphoreType.DMA((10, model_count)),
            pltpu.SemaphoreType.DMA((2, images)),
            pltpu.SemaphoreType.DMA((2, 7)),
        ],
        compiler_params=pltpu.CompilerParams(
            collective_id=1, has_side_effects=True, vmem_limit_bytes=60 * 2**20
        ),
    )(
        lengths,
        tokens.reshape(rows, width),
        gain_attn.reshape(1, -1),
        w_query,
        w_key,
        w_value,
        w_out,
        gain_mlp.reshape(1, -1),
        w_up,
        w_down,
        embed_proj,
        *dec_inputs,
    )


EARLY_DOWN, EARLY_UP, UP_FIRST = True, False, True
SUM_ORDERS = {
    "attn": ["all"],
    "dup": ["spread", "all"],
    "ddn": ["spreadz", "spread", "spread", "spreadz"],
    "pred": ["spread", "spread"],
    "emb": ["all"],
    "dn": ["Y", "Z", "Y", "Y"],
    "up": ["Y", "Y", "Z", "Y"],
    "oq": ["Y", "Y", "Y", "Y"],
}
PLAN = {
    "a3": [
        "pred0",
        "pred1",
        "ddn0",
        "ddn1",
        "ddn2",
        "ddn3",
        "dup0",
        "dup1",
    ],
    "a4": [
        "pred0",
        "ddn0",
        "pred1",
    ],
    "a5": [
        "ddn3",
        "dup1",
        "ddn1",
        "attn0",
        "pred0",
        "ddn2",
    ],
    "f1": [
        "pred1",
        "ddn0",
    ],
    "f2": [
        "emb0",
    ],
    "f3": [
        "dup0",
        "ddn1",
        "ddn3",
    ],
    "b0": [
        "pred0",
        "ddn2",
        "dup1",
        "ddn0",
        "pred1",
        "ddn3",
    ],
    "d2": [
        "dup0",
    ],
    "d3": [
        "ddn1",
    ],
    "s2": [
        "attn0",
        "dn0",
    ],
    "b2": [
        "dn1",
    ],
    "b4": [
        "ddn2",
        "dup1",
        "emb0",
        "dn2",
        "pred0",
        "ddn0",
        "pred1",
        "ddn3",
        "ddn1",
        "dup0",
    ],
    "b5": [
        "dn0",
        "dn3",
    ],
    "t1": [
        "ddn2",
        "dup0",
        "dn1",
    ],
    "t2": [
        "up2",
        "attn0",
        "dup1",
        "dn2",
        "up0",
    ],
    "t3": [
        "dn0",
        "dn3",
    ],
    "b7": [
        "up1",
    ],
    "tail": [
        "attn0",
        "up2",
        "up3",
        "dn2",
        "up0",
        "emb0",
        "norm",
        "dn1",
        "dn3",
        "up1",
        "norm",
        "attn0",
        "up3",
        "o",
        "emb0",
        "up0",
        "q",
        "up1",
        "up3",
        "o",
        "k",
        "emb0",
        "q",
        "o",
        "v",
        "k",
        "up2",
        "norm",
        "q",
        "v",
        "norm",
        "k",
        "v",
        "norm",
    ],
}


class Bulk:
    def __init__(self, one):
        self.one, self.stage = one, None

    def start(self):
        self.one.start(0)
        self.stage = 0

    def done(self):
        return self.stage == len(self.one.stages)

    def advance(self):
        if self.stage is None or self.done():
            return
        self.one.finish(self.stage)
        self.stage += 1
        if not self.done():
            self.one.start(self.stage)


def back_kernel(plan, *refs):
    images, visible, enc_heads, heads, side, pieces, embed_piece, scopes = plan
    refs = list(refs)

    def take(number):
        head = refs[:number]
        del refs[:number]
        return head

    (
        dist_ref,
        arrived,
        order_ref,
        keep_ref,
        dec_gain_attn,
        dec_gain_mlp,
        mask_token,
        tokens,
        gain_attn,
        gain_mlp,
    ) = take(10)
    dec_hbm = take(6)
    enc_hbm = take(15)
    decoded, tokens_out, norm_wide, norm_thin, rows_out, cols_out, dec_out, embed_out = take(8)
    move_sems, decoded_sems = take(2)
    grad_arrived, dec_packed, small = take(3)
    demb_own, demb_slots, db_s, total = take(4)
    parts_mlp, landing_mlp, parts_attn, landing_attn = take(4)
    sems, swap_sems = take(2)
    data_count, model_count = lax.axis_size("dp"), lax.axis_size("mp")
    data_bits, model_bits = log2_of(data_count), log2_of(model_count)
    row_packed, col_packed, embed_packed = take(3)
    row_bufs = [row_packed] + take(data_bits)
    col_bufs = [col_packed] + take(data_bits)
    dec_bufs = [dec_packed] + take(data_bits + model_bits)
    embed_bufs = [embed_packed] + take(data_bits + model_bits)
    wide_acc, wide_got, thin_acc, thin_got = take(4)
    row_sems, col_sems, dec_sems, embed_sems, norm_sems = take(5)
    assert not refs

    index = lax.axis_index("mp")
    count = model_count
    enc_stages = [("dp", bit) for bit in range(data_bits)]
    late_stages = enc_stages[1:] + enc_stages[:1]
    model_stages = [("mp", bit) for bit in range(model_bits)]
    all_stages = model_stages + enc_stages
    near, far = model_stages[:1], model_stages[1:]
    orders = {
        "Y": enc_stages,
        "Z": late_stages,
        "all": all_stages,
        "crossed": model_stages + late_stages,
        "spread": near + enc_stages + far,
        "spreadz": near + late_stages + far,
    }
    sums = {}

    def pump(point):
        for name in PLAN.get(point, ()):
            if name in sums:
                sums[name].advance()

    def pump_at(step, point):
        for turn in range(count):
            if PLAN.get(point + str(turn)):
                @pl.when(step == turn)
                def _():
                    pump(point + str(turn))

    chunk = 512

    def bulk(stages, bufs, axis, first, extent, pair, cut):
        window = [slice(None), slice(None)]
        window[axis - 1] = pl.ds(first, extent)
        return Bulk(HalvingSum(stages, bufs, tuple(window), pair.at[0, cut], pair.at[1, cut]))

    limits = [pieces[0][0]] + [piece[0] for piece in pieces[4:]] + [dec_packed.shape[1]]
    dec_rows = []
    for kind, first, last in zip(("attn", "dup", "ddn", "pred"), limits, limits[1:]):
        names = SUM_ORDERS[kind]
        extent = (last - first) // len(names)
        for cut, order in enumerate(names):
            begin = first + cut * extent
            sums[kind + str(cut)] = bulk(
                orders[order], dec_bufs, 1, begin, extent, dec_sems, len(dec_rows)
            )
            dec_rows.append((begin, begin + extent, orders[order]))

    def start(kind):
        for cut in range(len(SUM_ORDERS[kind])):
            sums[kind + str(cut)].start()

    def store_dec(which, product):
        offset, height, span, tiles = pieces[which]
        for column in range(model_count):
            for tile in range(tiles):
                lanes = min(LANES, span - tile * LANES)
                first = column * span + tile * LANES
                block = product[:, first : first + lanes].astype(low_type)
                base = offset + tile * height
                for begin, end, order in dec_rows:
                    low_row, high_row = max(begin, base), min(end, base + height)
                    if low_row >= high_row:
                        continue
                    for row in range(data_count):
                        shift = row * height - base
                        dec_packed[spot_of(row, column, order), low_row:high_row, :lanes] = block[
                            low_row + shift : high_row + shift, :
                        ]

    swap = Exchange(images, grad_arrived, demb_own, swap_sems.at[0], swap_sems.at[1])

    def decoder(
        w_out,
        xs,
        qkv_weights,
        a_s,
        qkv_s,
        e_s,
        inv_s,
        o_s,
        dy_s,
        db_dec,
        do_s,
    ):
        length = side * side
        width = w_out.shape[0]
        size = width // heads
        scaling = float(size) ** -0.5
        place = lax.broadcasted_iota(jnp.int32, (length, visible), 0)
        turn = lax.broadcasted_iota(jnp.int32, (length, visible), 1)
        arrivals = signal_partners(images, ["mp", "dp"])
        turned_move = Move(dec_hbm[0], qkv_weights, move_sems.at[0])
        out_move = Move(dec_hbm[1], w_out, move_sems.at[1])

        def picks(image):
            order = jnp.zeros((1, visible), jnp.int32)
            flags = jnp.zeros((1, length), jnp.int32)
            for one in range(images):
                order = jnp.where(image == one, order_ref[one : one + 1, :visible], order)
                flags = jnp.where(image == one, keep_ref[one : one + 1, :], flags)
            kept = jnp.sum(flags, axis=1, keepdims=True)
            return jnp.where((order == place) & (turn < kept), 1.0, 0.0)

        def rows_of(image):
            if isinstance(image, int):
                return slice(image * length, (image + 1) * length)
            return pl.ds(pl.multiple_of(image * length, length), length)

        def dense(w_up, w_down, w_pred, cotangent, mid_s, c_s, g_s, du_s, low_s, dm_s, staged):
            hidden = w_up.shape[1]
            second_moves = [
                Move(source, target, move_sems.at[2 + position])
                for position, (source, target) in enumerate(
                    zip(dec_hbm[2:], (w_up, w_down, w_pred, cotangent))
                )
            ]
            turned_move.wait()
            out_move.wait()
            small[...] = jnp.zeros_like(small)

            def stage_copy(image):
                return pltpu.make_async_copy(staged, decoded.at[image], decoded_sems.at[image])

            def one_image(image, carry):
                rows = rows_of(image)
                pick = picks(image)
                hidden_rows = 1.0 - jnp.sum(pick, axis=1, keepdims=True)
                quarter = width // 4
                lane = lax.broadcasted_iota(jnp.int32, (side, quarter), 1).astype(full_type)
                line = lax.broadcasted_iota(jnp.int32, (side, quarter), 0).astype(full_type)
                angle = dist_ref[image] * line * jnp.exp(lane * (-math.log(10000.0) / quarter))
                table = jnp.concatenate([jnp.sin(angle), jnp.cos(angle)], axis=1)
                by_row = jnp.broadcast_to(table[:, None, :], (side, side, 2 * quarter))
                by_col = jnp.broadcast_to(table[None, :, :], (side, side, 2 * quarter))
                codes = jnp.concatenate(
                    [by_row.reshape(length, 2 * quarter), by_col.reshape(length, 2 * quarter)],
                    axis=1,
                )
                start = jnp.dot(
                    pick.astype(low_type), arrived[image], preferred_element_type=full_type
                )
                start = start + hidden_rows * mask_token[...] + codes
                xs[rows, :] = start
                normed, scale = norm_parts(start)
                a_s[rows, :] = (normed * dec_gain_attn[...]).astype(low_type)
                for position in range(3):
                    span = slice(position * width, (position + 1) * width)
                    part = dot_as(qkv_weights[span, :], a_s[rows, :], 1, 1)
                    if position == 0:
                        part = part * (scaling * LOG2E)
                    qkv_s[span, rows] = part.astype(low_type)

                def one_head(head, inner):
                    span = pl.multiple_of(head * size, size)
                    query = qkv_s[pl.ds(span, size), rows]
                    key = qkv_s[pl.ds(width + span, size), rows]
                    value = qkv_s[pl.ds(2 * width + span, size), rows]
                    scores = dot_as(key, query, 0, 0)
                    weights = jnp.exp2(scores - jnp.max(scores, axis=0, keepdims=True))
                    inverse = 1.0 / jnp.sum(weights, axis=0, keepdims=True)
                    weights = weights.astype(low_type)
                    e_s[image * heads + head] = weights
                    inv_s[image * heads + head] = inverse
                    mixed = jnp.dot(value, weights, preferred_element_type=full_type)
                    o_s[pl.ds(span, size), rows] = (mixed * inverse).astype(low_type)
                    return inner

                lax.fori_loop(0, heads, one_head, 0, unroll=heads)

                middle = start + dot_as(o_s[:, rows], w_out[...], 0, 0)
                mid_s[...] = middle
                normed, scale = norm_parts(middle)
                c_s[rows, :] = (normed * dec_gain_mlp[...]).astype(low_type)

                @pl.when(image == 0)
                def _():
                    for move in second_moves:
                        move.wait()

                for first in range(0, hidden, chunk):
                    cols = slice(first, first + chunk)
                    pre = jnp.dot(c_s[rows, :], w_up[:, cols], preferred_element_type=full_type)
                    active, slope = gelu_pair(pre)
                    g_s[rows, cols] = active.astype(low_type)
                    du_s[rows, cols] = slope.astype(low_type)
                outputs = middle + jnp.dot(
                    g_s[rows, :], w_down[...], preferred_element_type=full_type
                )
                low_s[rows, :] = outputs.astype(low_type)

                @pl.when(image > 0)
                def _():
                    stage_copy(image - 1).wait()

                staged[...] = jnp.dot(
                    low_s[rows, :], w_pred[...], preferred_element_type=full_type
                )
                stage_copy(image).start()

                grad_out = dot_as(cotangent[image], w_pred[...], 1, 1)
                dm_s[rows, :] = grad_out.astype(low_type)
                for first in range(0, hidden, chunk):
                    cols = slice(first, first + chunk)
                    grad_active = dot_as(dm_s[rows, :], w_down[cols, :], 1, 1)
                    du_s[rows, cols] = (grad_active * du_s[rows, cols].astype(full_type)).astype(
                        low_type
                    )
                grad_second = dot_as(du_s[rows, :], w_up[...], 1, 1)
                normed, scale = norm_parts(mid_s[...])
                small[1:2, :] += jnp.sum(grad_second * normed, axis=0, keepdims=True)
                grad_middle = grad_out + norm_back(
                    normed, scale, grad_second * dec_gain_mlp[...]
                )
                dy_s[rows, :] = grad_middle
                db_dec[rows, :] = grad_middle.astype(low_type)
                return carry

            lax.fori_loop(0, images, one_image, 0)
            all_pixels = cotangent[...].reshape(-1, cotangent.shape[2])
            store_dec(6, dot_as(low_s[...], all_pixels, 0, 0))
            pl.semaphore_wait(pltpu.get_barrier_semaphore(), arrivals)
            start("pred")
            store_dec(5, dot_as(g_s[...], dm_s[...], 0, 0))
            start("ddn")
            pump("a1")
            store_dec(4, dot_as(c_s[...], du_s[...], 0, 0))
            start("dup")
            pump("a2")
            stage_copy(images - 1).wait()

        pl.run_scoped(dense, *scopes[1])

        for image in range(images):
            rows = rows_of(image)
            do_s[...] = dot_as(w_out[...], db_dec[rows, :], 1, 1)

            def back_head(head, inner):
                span = pl.multiple_of(head * size, size)
                query = qkv_s[pl.ds(span, size), rows]
                key = qkv_s[pl.ds(width + span, size), rows]
                value = qkv_s[pl.ds(2 * width + span, size), rows]
                weights = e_s[image * heads + head]
                grad_full = do_s[pl.ds(span, size), :] * (inv_s[image * heads + head] * scaling)
                mixed = o_s[pl.ds(span, size), rows].astype(full_type)
                shift = jnp.sum(grad_full * mixed, axis=0, keepdims=True)
                grad_low = grad_full.astype(low_type)
                grad_probs = dot_as(value, grad_low, 0, 0)
                grad_scores = (weights.astype(full_type) * (grad_probs - shift)).astype(low_type)
                grad_value = dot_as(grad_low, weights, 1, 1) * (1.0 / scaling)
                grad_query = jnp.dot(key, grad_scores, preferred_element_type=full_type)
                grad_key = dot_as(query, grad_scores, 1, 1) * (1.0 / (scaling * LOG2E))
                qkv_s[pl.ds(span, size), rows] = grad_query.astype(low_type)
                qkv_s[pl.ds(width + span, size), rows] = grad_key.astype(low_type)
                qkv_s[pl.ds(2 * width + span, size), rows] = grad_value.astype(low_type)
                return inner

            lax.fori_loop(0, heads, back_head, 0, unroll=heads)

            grad_normed = dot_as(qkv_s[:, rows], qkv_weights[...], 0, 0)
            normed, scale = norm_parts(xs[rows, :])
            small[0:1, :] += jnp.sum(grad_normed * normed, axis=0, keepdims=True)
            grad_start = dy_s[rows, :] + norm_back(
                normed, scale, grad_normed * dec_gain_attn[...]
            )
            pick = picks(image)
            hidden_rows = 1.0 - jnp.sum(pick, axis=1, keepdims=True)
            small[2:3, :] += jnp.sum(hidden_rows * grad_start, axis=0, keepdims=True)
            grad_arrived[image] = dot_as(
                pick.astype(low_type), grad_start.astype(low_type), 0, 0
            ).astype(low_type)
            swap.start_one(image)
            if image == 0:
                pump("a3")
        for position in range(3):
            grads = qkv_s[position * width : (position + 1) * width, :]
            store_dec(position, dot_as(a_s[...], grads, 0, 1))
        store_dec(3, jnp.dot(o_s[...], db_dec[...], preferred_element_type=full_type))
        start("attn")
        pump("a4")

    pl.run_scoped(decoder, *scopes[0])
    thin_acc[0] = small[...]

    def encoder(*local):
        local = list(local)
        loaded = local[:15]
        (
            w_out,
            w_up,
            w_down,
            a_s,
            qkv_s,
            e_s,
            inv_s,
            o_own,
            c_s,
            g_s,
            slope_s,
            mid_s,
            low_s,
            embed_full,
            qkv_weights,
        ) = loaded
        dm_s, du_s, dqkv_s, dy_s, do_s = local[15:]
        block_rows = images * visible
        columns = w_out.shape[0]
        size = columns // enc_heads
        scaling = float(size) ** -0.5
        hidden, width = w_down.shape
        moves = {}
        for position in (12, 13, 9, 2, 10, 1, 11, 8, 0, 4, 5, 6, 7, 14, 3):
            moves[position] = Move(enc_hbm[position], loaded[position], move_sems.at[8 + position])

        def ready(*arrays):
            for array in arrays:
                moves[[array is one for one in loaded].index(True)].wait()

        def cut_sums(kind, bufs, axis, extent, pair, base=0):
            for cut, order in enumerate(SUM_ORDERS[kind]):
                sums[kind + str(cut)] = bulk(
                    orders[order], bufs, axis, cut * extent, extent, pair, base + cut
                )

        embed_cuts = len(SUM_ORDERS["emb"])
        embed_part = embed_packed.shape[1] // embed_cuts
        cut_sums("emb", embed_bufs, 1, embed_part, embed_sems)
        up_part = hidden // len(SUM_ORDERS["up"])
        down_part = hidden // len(SUM_ORDERS["dn"])
        cut_sums("up", row_bufs, 2, up_part, row_sems)
        cut_sums("dn", col_bufs, 1, down_part, col_sems)
        out_order, *qkv_orders = (orders[one] for one in SUM_ORDERS["oq"])
        for cut, name in enumerate("qkv"):
            sums[name] = bulk(
                qkv_orders[cut],
                row_bufs,
                2,
                hidden + cut * columns,
                columns,
                row_sems,
                len(SUM_ORDERS["up"]) + cut,
            )
        sums["o"] = bulk(
            out_order, col_bufs, 1, hidden, columns, col_sems, len(SUM_ORDERS["dn"])
        )

        swap.finish()
        demb_gather = Gather(demb_own, lambda slot: demb_slots.at[slot], sems.at[0], sems.at[1])
        demb_gather.start()
        demb_slots[index] = demb_own[...]
        ready(low_s)
        offset, high, span, tiles = embed_piece
        product = dot_as(low_s[...], demb_own[...].reshape(block_rows, -1), 0, 0)
        for column in range(model_count):
            for row in range(data_count):
                for cut, order in enumerate(SUM_ORDERS["emb"]):
                    spot = spot_of(row, column, orders[order])
                    for tile in range(tiles):
                        lanes = min(LANES, span - tile * LANES)
                        first = column * span + tile * LANES
                        base = tile * high
                        begin = max(base, cut * embed_part)
                        end = min(base + high, (cut + 1) * embed_part)
                        if begin < end:
                            shift = row * high - base
                            embed_packed[spot, begin:end, :lanes] = product[
                                begin + shift : end + shift, first : first + lanes
                            ].astype(low_type)
        start("emb")
        pump("a5")
        ready(embed_full)

        def rows_of(slot):
            return pl.ds(pl.multiple_of(slot * block_rows, block_rows), block_rows)

        def first_back(step, carry):
            demb_gather.arrive_at(step)
            pump_at(step, "f")
            mask = visit_mask(step, count)
            slot = index ^ mask
            rows = rows_of(slot)
            grad_rows = demb_slots[slot].reshape(block_rows, -1)
            grad_out = dot_as(grad_rows, embed_full[...], 1, 1)

            @pl.when(mask == 0)
            def _():
                dy_s[...] = grad_out

            dm_s[rows, :] = grad_out.astype(low_type)
            return carry

        def active_back(step, carry):
            pump_at(step, "d")
            rows = rows_of(index ^ visit_mask(step, count))
            for first in range(0, hidden, chunk):
                cols = slice(first, first + chunk)
                grad_active = dot_as(dm_s[rows, :], w_down[cols, :], 1, 1)
                du_s[rows, cols] = (grad_active * slope_s[rows, cols].astype(full_type)).astype(
                    low_type
                )
            return carry

        lax.fori_loop(0, count, first_back, 0)

        def store_rows(product, first, stages):
            high = width // data_count
            for row in range(data_count):
                row_packed[spot_of(row, 0, stages), :, first : first + product.shape[1]] = (
                    product[row * high : (row + 1) * high, :].astype(low_type)
                )

        def store_cols(product, first, stages):
            wide = width // data_count
            for col in range(data_count):
                col_packed[
                    spot_of(col, 0, stages), first : first + product.shape[0], :wide
                ] = product[:, col * wide : (col + 1) * wide].astype(low_type)

        def down_grads():
            ready(g_s)
            for cut, order in enumerate(SUM_ORDERS["dn"]):
                cols = slice(cut * down_part, (cut + 1) * down_part)
                product = dot_as(g_s[:, cols], dm_s[...], 0, 0)
                store_cols(product, cut * down_part, orders[order])
                sums["dn" + str(cut)].start()
            pump("b0" if EARLY_DOWN else "b3")

        def up_grads():
            ready(c_s)
            for cut, order in enumerate(SUM_ORDERS["up"]):
                cols = slice(cut * up_part, (cut + 1) * up_part)
                product = dot_as(c_s[...], du_s[:, cols], 0, 0)
                store_rows(product, cut * up_part, orders[order])
                sums["up" + str(cut)].start()
            pump("b1" if EARLY_UP else "b4")

        if EARLY_DOWN:
            down_grads()
        ready(w_down, slope_s)
        lax.fori_loop(0, count, active_back, 0)
        if EARLY_UP:
            up_grads()
        ready(w_up)
        scatter = Scatter(parts_mlp, total, landing_mlp, sems.at[2], sems.at[3])
        total[...] = jnp.zeros_like(total)

        def second_back(step, carry):
            pump_at(step, "s")
            mask = count - 1 - step
            rows = rows_of(index ^ mask)
            scatter.put(mask, dot_as(du_s[rows, :], w_up[...], 1, 1))
            return carry

        lax.fori_loop(0, count, second_back, 0)
        for bit in range(model_bits - 1):
            scatter.finish_bit(bit)

        pump("b2")
        if not EARLY_DOWN:
            down_grads()
        if not EARLY_UP and UP_FIRST:
            up_grads()
        ready(mid_s)
        scatter.finish_bit(model_bits - 1)

        normed, scale = norm_parts(mid_s[...])
        grad_second = total[...]
        wide_acc[0, 1:2, :] = jnp.sum(grad_second * normed, axis=0, keepdims=True)
        grad_middle = dy_s[...] + norm_back(normed, scale, grad_second * gain_mlp[...])
        dy_s[...] = grad_middle
        db_s[rows_of(index), :] = grad_middle.astype(low_type)
        db_gather = Gather(None, lambda slot: db_s.at[rows_of(slot)], sems.at[4], sems.at[5])
        db_gather.start()
        pump("b5")
        if not EARLY_UP and not UP_FIRST:
            up_grads()
        ready(w_out, qkv_s, e_s, inv_s, o_own, qkv_weights)
        second_scatter = Scatter(parts_attn, total, landing_attn, sems.at[6], sems.at[7])
        total[...] = jnp.zeros_like(total)

        def third_back(step, carry):
            db_gather.arrive_at(step)
            pump_at(step, "t")
            mask = visit_mask(step, count)
            slot = index ^ mask
            rows = rows_of(slot)
            do_s[...] = dot_as(w_out[...], db_s[rows, :], 1, 1)
            for head in range(enc_heads):
                span = slice(head * size, (head + 1) * size)
                key_span = slice(columns + head * size, columns + (head + 1) * size)
                value_span = slice(2 * columns + head * size, 2 * columns + (head + 1) * size)
                query, key, value = qkv_s[span, rows], qkv_s[key_span, rows], qkv_s[value_span, rows]
                weights = e_s[slot * enc_heads + head]
                grad_full = do_s[span, :] * (inv_s[slot * enc_heads + head] * scaling)
                shift = jnp.sum(
                    grad_full * o_own[span, rows].astype(full_type), axis=0, keepdims=True
                )
                grad_low = grad_full.astype(low_type)
                grad_probs = dot_as(value, grad_low, 0, 0)
                grad_scores = (weights.astype(full_type) * (grad_probs - shift)).astype(low_type)
                grad_value = dot_as(grad_low, weights, 1, 1) * (1.0 / scaling)
                grad_query = jnp.dot(key, grad_scores, preferred_element_type=full_type)
                grad_key = dot_as(query, grad_scores, 1, 1) * (1.0 / (scaling * LOG2E))
                dqkv_s[span, rows] = grad_query.astype(low_type)
                dqkv_s[key_span, rows] = grad_key.astype(low_type)
                dqkv_s[value_span, rows] = grad_value.astype(low_type)
            second_scatter.put(mask, dot_as(dqkv_s[:, rows], qkv_weights[...], 0, 0))
            return carry

        lax.fori_loop(0, count, third_back, 0)
        for bit in range(model_bits - 1):
            second_scatter.finish_bit(bit)
        pump("b6")
        store_cols(
            jnp.dot(o_own[...], db_s[...], preferred_element_type=full_type), hidden, out_order
        )
        sums["o"].start()
        ready(a_s)
        for cut, order in enumerate(qkv_orders):
            span = slice(cut * columns, (cut + 1) * columns)
            product = dot_as(a_s[...], dqkv_s[span, :], 0, 1)
            store_rows(product, hidden + cut * columns, order)
            sums["qkv"[cut]].start()
        pump("b7")
        second_scatter.finish_bit(model_bits - 1)
        normed, scale = norm_parts(tokens[...].astype(full_type))
        grad_normed = total[...]
        wide_acc[0, 0:1, :] = jnp.sum(grad_normed * normed, axis=0, keepdims=True)
        dy_s[...] = dy_s[...] + norm_back(normed, scale, grad_normed * gain_attn[...])
        tokens_move = Move(dy_s, tokens_out, move_sems.at[0])

        def norm_copies(stage):
            peer = partner(*all_stages[stage])[0]
            return [
                pltpu.make_async_remote_copy(
                    src_ref=acc.at[stage],
                    dst_ref=got.at[stage],
                    send_sem=norm_sems.at[0, kind, stage],
                    recv_sem=norm_sems.at[1, kind, stage],
                    device_id=peer,
                    device_id_type=MESH,
                )
                for kind, (acc, got) in enumerate(((wide_acc, wide_got), (thin_acc, thin_got)))
            ]

        def norm_step(turn):
            for copy in norm_copies(turn):
                copy.wait()
            wide_acc[turn + 1] = wide_acc[turn] + wide_got[turn]
            thin_acc[turn + 1] = thin_acc[turn] + thin_got[turn]
            if turn + 1 < len(all_stages):
                for copy in norm_copies(turn + 1):
                    copy.start()

        for copy in norm_copies(0):
            copy.start()
        turn = 0
        for name in PLAN["tail"]:
            if name == "norm":
                if turn < len(all_stages):
                    norm_step(turn)
                    turn += 1
            elif name in sums:
                sums[name].advance()
        for later in range(turn, len(all_stages)):
            norm_step(later)
        for one in sums.values():
            while not one.done():
                one.advance()
        norm_wide[...] = wide_acc[len(all_stages)]
        norm_thin[...] = thin_acc[len(all_stages)]
        for one in (demb_gather, scatter, db_gather, second_scatter):
            one.drain()
        tokens_move.wait()


    pl.run_scoped(encoder, *scopes[2])
    rows_out[...] = row_bufs[-1][0]
    cols_out[...] = col_bufs[-1][0]
    dec_out[...] = dec_bufs[-1][0]
    embed_out[...] = embed_bufs[-1][0]


def unpack_kernel(widths, dec_list, embed_list, *refs):
    hidden, columns, wide = widths
    grad_tokens, norm_wide, norm_thin, rows_in, cols_in, dec_in, embed_in = refs[:7]
    out_tokens, g_query, g_key, g_value, g_up, g_out, g_down, g_embed = refs[7:15]
    small = refs[15:20]
    dec_outs = refs[20:]
    out_tokens[...] = grad_tokens[...]
    g_up[...] = rows_in[:, :hidden].astype(full_type)
    for position, out in enumerate((g_query, g_key, g_value)):
        first = hidden + position * columns
        out[...] = rows_in[:, first : first + columns].astype(full_type)
    g_down[...] = cols_in[:hidden, :wide].astype(full_type)
    g_out[...] = cols_in[hidden : hidden + columns, :wide].astype(full_type)
    for position in range(2):
        small[position][...] = norm_wide[position : position + 1, :]
    for position in range(3):
        small[2 + position][...] = norm_thin[position : position + 1, :]
    for outs, pieces, source in (([g_embed], embed_list, embed_in), (dec_outs, dec_list, dec_in)):
        for out, (offset, rows, width, tiles) in zip(outs, pieces):
            for tile in range(tiles):
                lanes = min(LANES, width - tile * LANES)
                block = source[offset + tile * rows : offset + (tile + 1) * rows, :lanes]
                out[:, tile * LANES : tile * LANES + lanes] = block.astype(full_type)


def decode_and_back(
    arrived,
    grid_order,
    grid_keep,
    ground_dist,
    dec_weights,
    mask_token,
    pred_proj,
    cotangent,
    tokens,
    weights,
    saved,
    dec_turned,
    embed_proj,
):
    gain_attn, w_query, w_key, w_value, w_out, gain_mlp, w_up, w_down = weights
    (dec_gain_attn, dec_query, dec_key, dec_value, dec_proj, dec_gain_mlp, dec_up, dec_down) = (
        dec_weights
    )
    data_count, model_count = lax.axis_size("dp"), lax.axis_size("mp")
    data_bits, model_bits = log2_of(data_count), log2_of(model_count)
    images, visible, width = tokens.shape
    rows = images * visible
    every = rows * model_count
    enc_heads = HE // model_count
    columns, hidden = w_query.shape[1], w_up.shape[1]
    out_width = embed_proj.shape[1] * model_count
    length, pixels = cotangent.shape[1:]
    grid_rows = images * length
    dec_hidden = dec_up.shape[1]
    matrices = [dec_query, dec_key, dec_value, dec_proj, dec_up, dec_down, pred_proj]
    pieces, height = dec_pieces(data_count, model_count, [one.shape for one in matrices])
    embed_pieces, embed_height = dec_pieces(data_count, model_count, [(width, out_width)])
    high, wide = width // data_count, width // data_count
    wide_pad = -(-wide // LANES) * LANES
    devices = data_count * model_count
    stages = data_bits + model_bits
    dec_cuts = sum(len(SUM_ORDERS[kind]) for kind in ("attn", "dup", "ddn", "pred"))
    row_shape = (high, hidden + 3 * columns)
    col_shape = (hidden + columns, wide_pad)
    vmem = pl.BlockSpec(memory_space=pltpu.VMEM)
    hbm = pl.BlockSpec(memory_space=pl.ANY)
    low = lambda *shape: pltpu.VMEM(shape, low_type)
    full = lambda *shape: pltpu.VMEM(shape, full_type)
    loaded = [w_out, w_up, w_down, *saved]
    attn_scope = [
        low(out_width, out_width),
        full(grid_rows, out_width),
        low(3 * out_width, out_width),
        low(grid_rows, out_width),
        low(3 * out_width, grid_rows),
        low(images * HD, length, length),
        full(images * HD, 1, length),
        low(out_width, grid_rows),
        full(grid_rows, out_width),
        low(grid_rows, out_width),
        full(out_width, length),
    ]
    dense_scope = [
        low(out_width, dec_hidden),
        low(dec_hidden, out_width),
        low(out_width, pixels),
        low(images, length, pixels),
        full(length, out_width),
        low(grid_rows, out_width),
        low(grid_rows, dec_hidden),
        low(grid_rows, dec_hidden),
        low(grid_rows, out_width),
        low(grid_rows, out_width),
        full(length, pixels),
    ]
    enc_scope = [pltpu.VMEM(one.shape, one.dtype) for one in loaded] + [
        low(every, width),
        low(every, hidden),
        low(3 * columns, every),
        full(rows, width),
        full(columns, rows),
    ]
    plan = (
        images,
        visible,
        enc_heads,
        HD,
        SIDE,
        pieces,
        embed_pieces[0],
        (attn_scope, dense_scope, enc_scope),
    )

    def kernel(*refs):
        back_kernel(plan, *refs)

    outs = [
        (cotangent.shape, full_type),
        ((rows, width), full_type),
        ((2, width), full_type),
        ((3, out_width), full_type),
        (row_shape, low_type),
        (col_shape, low_type),
        ((height, LANES), low_type),
        ((embed_height, LANES), low_type),
    ]
    scratch = [
        pltpu.SemaphoreType.DMA((8 + len(loaded),)),
        pltpu.SemaphoreType.DMA((images,)),
        low(images, visible, out_width),
        low(devices, height, LANES),
        full(3, out_width),
        low(images, visible, out_width),
        low(model_count, images, visible, out_width),
        low(every, width),
        full(rows, width),
        low(model_count - 1, rows, width),
        low(model_count - 1, rows, width),
        low(model_count - 1, rows, width),
        low(model_count - 1, rows, width),
        pltpu.SemaphoreType.DMA((8, model_count)),
        pltpu.SemaphoreType.DMA((2, images)),
        low(data_count, *row_shape),
        low(data_count, *col_shape),
        low(devices, embed_height, LANES),
    ]
    scratch += [low(data_count >> (bit + 1), *row_shape) for bit in range(data_bits)]
    scratch += [low(data_count >> (bit + 1), *col_shape) for bit in range(data_bits)]
    scratch += [low(devices >> (bit + 1), height, LANES) for bit in range(stages)]
    scratch += [low(devices >> (bit + 1), embed_height, LANES) for bit in range(stages)]
    for shape in ((2, width), (3, out_width)):
        scratch += [full(stages + 1, *shape), full(stages, *shape)]
    scratch += [
        pltpu.SemaphoreType.DMA((2, len(SUM_ORDERS["up"]) + 3, data_bits)),
        pltpu.SemaphoreType.DMA((2, len(SUM_ORDERS["dn"]) + 1, data_bits)),
        pltpu.SemaphoreType.DMA((2, dec_cuts, stages)),
        pltpu.SemaphoreType.DMA((2, len(SUM_ORDERS["emb"]), stages)),
        pltpu.SemaphoreType.DMA((2, 2, stages)),
    ]
    results = pl.pallas_call(
        kernel,
        out_shape=[jax.ShapeDtypeStruct(shape, kind) for shape, kind in outs],
        in_specs=[pl.BlockSpec(memory_space=pltpu.SMEM)] + [vmem] * 9 + [hbm] * (6 + len(loaded)),
        out_specs=[hbm] * 2 + [vmem] * (len(outs) - 2),
        scratch_shapes=scratch,
        compiler_params=pltpu.CompilerParams(
            collective_id=2, has_side_effects=True, vmem_limit_bytes=255 * 2**18
        ),
    )(
        ground_dist,
        arrived,
        grid_order,
        grid_keep,
        dec_gain_attn.reshape(1, -1),
        dec_gain_mlp.reshape(1, -1),
        mask_token.reshape(1, -1),
        tokens.reshape(rows, width),
        gain_attn.reshape(1, -1),
        gain_mlp.reshape(1, -1),
        dec_turned,
        dec_proj,
        dec_up,
        dec_down,
        pred_proj,
        cotangent,
        *loaded,
    )
    final = [
        (rows, width),
        (high, columns),
        (high, columns),
        (high, columns),
        (high, hidden),
        (columns, wide),
        (hidden, wide),
        (embed_pieces[0][1], embed_pieces[0][2]),
    ]
    final += [(1, width)] * 2 + [(1, out_width)] * 3
    final += [(piece[1], piece[2]) for piece in pieces]

    def last_kernel(*refs):
        unpack_kernel((hidden, columns, wide), pieces, embed_pieces, *refs)

    return results[0], pl.pallas_call(
        last_kernel,
        out_shape=[jax.ShapeDtypeStruct(shape, full_type) for shape in final],
        in_specs=[vmem] * (len(outs) - 1),
        out_specs=[vmem] * len(final),
    )(*results[1:])


def layer_norm(values, scale_gain):
    center = values - jnp.mean(values, axis=-1, keepdims=True)
    spread = jnp.mean(center * center, axis=-1, keepdims=True)
    return center * lax.rsqrt(spread + eps_norm) * scale_gain


def exact_gelu(values):
    return jax.nn.gelu(values, approximate=False)


def matmul(left_side, right_side):
    flat_rows = left_side.reshape(-1, left_side.shape[-1])
    product = jnp.dot(flat_rows, right_side, preferred_element_type=full_type)
    return product.reshape(left_side.shape[:-1] + (right_side.shape[1],))


def matmul_t(left_side, right_side):
    flat_rows = left_side.reshape(-1, left_side.shape[-1])
    product = lax.dot_general(
        flat_rows, right_side, (((1,), (1,)), ((), ())), preferred_element_type=full_type
    )
    return product.reshape(left_side.shape[:-1] + (right_side.shape[0],))


def outer_sum(left_side, right_side):
    return lax.dot_general(
        left_side.reshape(-1, left_side.shape[-1]),
        right_side.reshape(-1, right_side.shape[-1]),
        (((0,), (0,)), ((), ())),
        preferred_element_type=full_type,
    )


def spread_rows(values, tensor_split):
    if tensor_split:
        return lax.all_gather(values, "mp", axis=0, tiled=True)
    return values


def collect_rows(values, tensor_split):
    if tensor_split:
        return lax.psum_scatter(
            values.astype(jnp.bfloat16), "mp", scatter_dimension=0, tiled=True
        ).astype(jnp.float32)
    return values


def images_per_block(images, length):
    grouped = 1
    while grouped * length < 512 and grouped < images:
        grouped = grouped * 2
    return grouped


def in_blocks(blocked_array, grouped):
    return blocked_array.reshape(
        (blocked_array.shape[0] // grouped, grouped) + blocked_array.shape[1:]
    )


def with_heads(blocked_array, head_count):
    return blocked_array.reshape(
        blocked_array.shape[:2] + (head_count, blocked_array.shape[2] // head_count)
    )


def attend_forward(queries, keys_all, values_all, key_valid, head_count):
    images, length, columns = queries.shape
    grouped = images_per_block(images, length)
    scaling = float(columns // head_count) ** (-0.5)

    def one_block(pieces):
        query_b, key_b, value_b, valid_b = pieces
        scores = (
            jnp.einsum("nqhd,nkhd->nhqk", query_b, key_b, preferred_element_type=full_type)
            * scaling
        )
        scores = jnp.where(valid_b[:, None, None, :], scores, masked_score)
        row_max = jnp.max(scores, axis=-1, keepdims=True)
        weights = jnp.exp(scores - row_max)
        totals = jnp.sum(weights, axis=-1, keepdims=True)
        prob_rows = (weights / totals).astype(low_type)
        mixed_b = jnp.einsum(
            "nhqk,nkhd->nqhd", prob_rows, value_b, preferred_element_type=full_type
        )
        return (mixed_b.astype(low_type), (row_max + jnp.log(totals))[..., 0])

    pieces_in = (
        in_blocks(with_heads(queries, head_count), grouped),
        in_blocks(with_heads(keys_all, head_count), grouped),
        in_blocks(with_heads(values_all, head_count), grouped),
        in_blocks(key_valid, grouped),
    )
    mixed_rows, log_total = lax.map(one_block, pieces_in)
    return (
        mixed_rows.reshape(images, length, columns),
        log_total.reshape(images, head_count, length),
    )


def attend_backward(queries, keys_all, values_all, key_valid, log_total, grad_mixed, head_count):
    images, length, columns = queries.shape
    grouped = images_per_block(images, length)
    scaling = float(columns // head_count) ** (-0.5)

    def one_block(pieces):
        query_b, key_b, value_b, valid_b, total_b, grad_b = pieces
        scores = (
            jnp.einsum("nqhd,nkhd->nhqk", query_b, key_b, preferred_element_type=full_type)
            * scaling
        )
        scores = jnp.where(valid_b[:, None, None, :], scores, masked_score)
        prob_rows = jnp.exp(scores - total_b[..., None])
        grad_value_b = jnp.einsum(
            "nhqk,nqhd->nkhd", prob_rows.astype(low_type), grad_b, preferred_element_type=full_type
        )
        grad_probs = jnp.einsum(
            "nqhd,nkhd->nhqk", grad_b, value_b, preferred_element_type=full_type
        )
        grad_scores = prob_rows * (
            grad_probs - jnp.sum(grad_probs * prob_rows, axis=-1, keepdims=True)
        )
        grad_scores = (grad_scores * scaling).astype(low_type)
        grad_query_b = jnp.einsum(
            "nhqk,nkhd->nqhd", grad_scores, key_b, preferred_element_type=full_type
        )
        grad_key_b = jnp.einsum(
            "nhqk,nqhd->nkhd", grad_scores, query_b, preferred_element_type=full_type
        )
        return (
            grad_query_b.astype(low_type),
            grad_key_b.astype(low_type),
            grad_value_b.astype(low_type),
        )

    pieces_in = (
        in_blocks(with_heads(queries, head_count), grouped),
        in_blocks(with_heads(keys_all, head_count), grouped),
        in_blocks(with_heads(values_all, head_count), grouped),
        in_blocks(key_valid, grouped),
        in_blocks(log_total, grouped),
        in_blocks(with_heads(grad_mixed, head_count), grouped),
    )
    grad_query, grad_key, grad_value = lax.map(one_block, pieces_in)
    return (
        grad_query.reshape(images, length, columns),
        grad_key.reshape(images, length, columns),
        grad_value.reshape(images, length, columns),
    )


def block_forward(inputs, key_valid, weights, head_count, tensor_split):
    gain_attn, w_query, w_key, w_value, w_out, gain_mlp, w_up, w_down = weights
    normed = spread_rows(layer_norm(inputs, gain_attn).astype(low_type), tensor_split)
    queries = matmul(normed, w_query).astype(low_type)
    keys_all = matmul(normed, w_key).astype(low_type)
    values_all = matmul(normed, w_value).astype(low_type)
    mixed_rows, log_total = attend_forward(queries, keys_all, values_all, key_valid, head_count)
    middle = inputs + collect_rows(matmul(mixed_rows, w_out), tensor_split)
    second = spread_rows(layer_norm(middle, gain_mlp).astype(low_type), tensor_split)
    pre_act = matmul(second, w_up)
    active = exact_gelu(pre_act).astype(low_type)
    outputs = middle + collect_rows(matmul(active, w_down), tensor_split)
    kept_state = (
        inputs,
        normed,
        queries,
        keys_all,
        values_all,
        mixed_rows,
        log_total,
        middle,
        second,
        pre_act,
        active,
    )
    return (outputs, kept_state)


def block_backward(grad_out, kept_state, key_valid, weights, head_count, tensor_split):
    gain_attn, w_query, w_key, w_value, w_out, gain_mlp, w_up, w_down = weights
    (
        inputs,
        normed,
        queries,
        keys_all,
        values_all,
        mixed_rows,
        log_total,
        middle,
        second,
        pre_act,
        active,
    ) = kept_state
    grad_branch = spread_rows(grad_out.astype(low_type), tensor_split)
    grad_down = outer_sum(active, grad_branch)
    grad_active = matmul_t(grad_branch, w_down)
    grad_pre = jax.vjp(exact_gelu, pre_act)[1](grad_active)[0].astype(low_type)
    grad_up = outer_sum(second, grad_pre)
    grad_second = collect_rows(matmul_t(grad_pre, w_up), tensor_split)
    norm_grad, grad_gain_mlp = jax.vjp(layer_norm, middle, gain_mlp)[1](grad_second)
    grad_middle = grad_out + norm_grad
    grad_attn = spread_rows(grad_middle.astype(low_type), tensor_split)
    grad_w_out = outer_sum(mixed_rows, grad_attn)
    grad_mixed = matmul_t(grad_attn, w_out).astype(low_type)
    grad_query, grad_key, grad_value = attend_backward(
        queries, keys_all, values_all, key_valid, log_total, grad_mixed, head_count
    )
    grad_w_query = outer_sum(normed, grad_query)
    grad_w_key = outer_sum(normed, grad_key)
    grad_w_value = outer_sum(normed, grad_value)
    grad_normed = (
        matmul_t(grad_query, w_query) + matmul_t(grad_key, w_key) + matmul_t(grad_value, w_value)
    )
    grad_normed = collect_rows(grad_normed, tensor_split)
    input_grad, grad_gain_attn = jax.vjp(layer_norm, inputs, gain_attn)[1](grad_normed)
    return (
        grad_middle + input_grad,
        (
            grad_gain_attn,
            grad_w_query,
            grad_w_key,
            grad_w_value,
            grad_w_out,
            grad_gain_mlp,
            grad_up,
            grad_down,
        ),
    )


def grid_codes(distance, side_count, columns):
    quarter = columns // 4
    frequency = 10000.0 ** (-jnp.arange(quarter, dtype=full_type) / quarter)
    places = jnp.arange(side_count * side_count)
    row_pos = (places // side_count).astype(full_type)
    col_pos = (places % side_count).astype(full_type)
    row_angle = distance[:, None, None] * row_pos[None, :, None] * frequency[None, None, :]
    col_angle = distance[:, None, None] * col_pos[None, :, None] * frequency[None, None, :]
    return jnp.concatenate(
        [jnp.sin(row_angle), jnp.cos(row_angle), jnp.sin(col_angle), jnp.cos(col_angle)], axis=-1
    )


def placement_table(visible_order, keep_flags, visible):
    positions = jnp.arange(visible_order.shape[1])
    matches = (visible_order[:, None, :visible] == positions[None, :, None]) & (
        keep_flags[:, :, None] == 1
    )
    return matches.astype(low_type)


def owner_blocks(full_grad, data_count, model_count):
    row_count, col_count = full_grad.shape
    reshaped = full_grad.reshape(
        data_count, row_count // data_count, model_count, col_count // model_count
    )
    return jnp.transpose(reshaped, (0, 2, 1, 3)).reshape(
        data_count * model_count, row_count // data_count, col_count // model_count
    )


def per_device_plain(
    tokens,
    lengths,
    grid_order,
    grid_keep,
    ground_dist,
    enc_norm,
    enc_query,
    enc_key,
    enc_value,
    enc_proj,
    enc_norm2,
    enc_up,
    enc_down,
    embed_proj,
    mask_token,
    dec_norm,
    dec_query,
    dec_key,
    dec_value,
    dec_proj,
    dec_norm2,
    dec_up,
    dec_down,
    pred_proj,
    cotangent,
):
    data_count = lax.axis_size("dp")
    model_count = lax.axis_size("mp")
    enc_weights = (enc_norm, enc_query, enc_key, enc_value, enc_proj, enc_norm2, enc_up, enc_down)
    dec_weights = (dec_norm, dec_query, dec_key, dec_value, dec_proj, dec_norm2, dec_up, dec_down)
    enc_heads = HE // model_count
    key_valid = jnp.arange(tokens.shape[1])[None, :] < lengths[:, None]
    enc_out, enc_saved = block_forward(
        tokens.astype(full_type), key_valid, enc_weights, enc_heads, True
    )
    enc_low = enc_out.astype(low_type)
    enc_all = spread_rows(enc_low, True)
    embedded = matmul(enc_all, embed_proj).astype(low_type)
    sectioned = embedded.reshape((data_count, -1) + embedded.shape[1:])
    arrived = lax.all_to_all(
        lax.all_to_all(sectioned, "dp", split_axis=0, concat_axis=0, tiled=True),
        "mp",
        split_axis=0,
        concat_axis=3,
        tiled=True,
    )
    arrived = arrived.reshape((-1,) + arrived.shape[2:])
    pick_table = placement_table(grid_order, grid_keep, arrived.shape[1])
    masked = (1 - grid_keep).astype(full_type)[..., None]
    dec_start = jnp.einsum("npt,ntc->npc", pick_table, arrived, preferred_element_type=full_type)
    dec_start = dec_start + masked * mask_token + grid_codes(ground_dist, SIDE, mask_token.shape[0])
    all_valid = jnp.ones(dec_start.shape[:2], jnp.bool_)
    dec_out, dec_saved = block_forward(dec_start, all_valid, dec_weights, HD, False)
    dec_low = dec_out.astype(low_type)
    decoded = matmul(dec_low, pred_proj)
    grad_pred = outer_sum(dec_low, cotangent)
    grad_dec_out = matmul_t(cotangent, pred_proj)
    grad_start, dec_grads = block_backward(
        grad_dec_out, dec_saved, all_valid, dec_weights, HD, False
    )
    grad_mask = jnp.sum(masked * grad_start, axis=(0, 1))
    grad_arrived = jnp.einsum("npt,npc->ntc", pick_table.astype(full_type), grad_start).astype(
        low_type
    )
    sent_back = grad_arrived.reshape((-1, IPD) + grad_arrived.shape[1:])
    returned = lax.all_to_all(
        lax.all_to_all(sent_back, "mp", split_axis=3, concat_axis=0, tiled=True),
        "dp",
        split_axis=0,
        concat_axis=0,
        tiled=True,
    )
    returned = returned.reshape((-1,) + returned.shape[2:])
    grad_embed = outer_sum(enc_all, returned)
    grad_enc_out = collect_rows(matmul_t(returned, embed_proj), True)
    grad_tokens, enc_grads = block_backward(
        grad_enc_out, enc_saved, key_valid, enc_weights, enc_heads, True
    )
    col_sums = (
        lax.psum_scatter(
            enc_grads[4].astype(jnp.bfloat16), "dp", scatter_dimension=1, tiled=True
        ).astype(jnp.float32),
        lax.psum_scatter(
            enc_grads[7].astype(jnp.bfloat16), "dp", scatter_dimension=1, tiled=True
        ).astype(jnp.float32),
    )
    norm_grads = lax.psum(
        (enc_grads[0], enc_grads[5], dec_grads[0], dec_grads[5], grad_mask), ("dp", "mp")
    )
    dec_list = (
        dec_grads[1],
        dec_grads[2],
        dec_grads[3],
        dec_grads[4],
        dec_grads[6],
        dec_grads[7],
        grad_pred,
    )
    row_sums = (
        lax.psum_scatter(
            enc_grads[1].astype(jnp.bfloat16), "dp", scatter_dimension=0, tiled=True
        ).astype(jnp.float32),
        lax.psum_scatter(
            enc_grads[2].astype(jnp.bfloat16), "dp", scatter_dimension=0, tiled=True
        ).astype(jnp.float32),
        lax.psum_scatter(
            enc_grads[3].astype(jnp.bfloat16), "dp", scatter_dimension=0, tiled=True
        ).astype(jnp.float32),
        lax.psum_scatter(
            enc_grads[6].astype(jnp.bfloat16), "dp", scatter_dimension=0, tiled=True
        ).astype(jnp.float32),
        lax.psum_scatter(
            grad_embed.astype(jnp.bfloat16), "dp", scatter_dimension=0, tiled=True
        ).astype(jnp.float32),
    )
    summed = (
        lax.psum_scatter(
            owner_blocks(dec_list[0], data_count, model_count),
            ("dp", "mp"),
            scatter_dimension=0,
            tiled=True,
        ),
        lax.psum_scatter(
            owner_blocks(dec_list[1], data_count, model_count),
            ("dp", "mp"),
            scatter_dimension=0,
            tiled=True,
        ),
        lax.psum_scatter(
            owner_blocks(dec_list[2], data_count, model_count),
            ("dp", "mp"),
            scatter_dimension=0,
            tiled=True,
        ),
        lax.psum_scatter(
            owner_blocks(dec_list[3], data_count, model_count),
            ("dp", "mp"),
            scatter_dimension=0,
            tiled=True,
        ),
        lax.psum_scatter(
            owner_blocks(dec_list[4], data_count, model_count),
            ("dp", "mp"),
            scatter_dimension=0,
            tiled=True,
        ),
        lax.psum_scatter(
            owner_blocks(dec_list[5], data_count, model_count),
            ("dp", "mp"),
            scatter_dimension=0,
            tiled=True,
        ),
        lax.psum_scatter(
            owner_blocks(dec_list[6], data_count, model_count),
            ("dp", "mp"),
            scatter_dimension=0,
            tiled=True,
        ),
    )
    embed_final = row_sums[4]
    dec_final = tuple((summed[index_num][0] for index_num in range(7)))
    return (
        decoded,
        grad_tokens,
        norm_grads[0],
        row_sums[0],
        row_sums[1],
        row_sums[2],
        col_sums[0],
        norm_grads[1],
        row_sums[3],
        col_sums[1],
        embed_final,
        norm_grads[4],
        norm_grads[2],
        dec_final[0],
        dec_final[1],
        dec_final[2],
        dec_final[3],
        norm_grads[3],
        dec_final[4],
        dec_final[5],
        dec_final[6],
    )


VMEM_BUDGET = 56 * 2**20


def kernel_bytes(tokens, enc_up, enc_query, dec_up, pred_proj):
    data_count, model_count = lax.axis_size("dp"), lax.axis_size("mp")
    images, visible, width = tokens.shape
    every = images * visible * model_count
    hidden, columns = enc_up.shape[1], enc_query.shape[1]
    out_width, wide = dec_up.shape[0], max(width // data_count, LANES)
    shapes = [(out_width, out_width)] * 4
    shapes += [dec_up.shape, dec_up.shape[::-1], pred_proj.shape, (width, out_width)]
    height = dec_pieces(data_count, model_count, shapes)[1]
    rows = 8 * every * width + 3 * every * hidden
    sums = width * (hidden + 3 * columns) + data_count * (hidden + columns) * wide
    sums = 2 * (sums + data_count * model_count * height * LANES)
    return 2 * (rows + sums + 2 * width * hidden + 4 * width * columns)


def per_device(
    tokens,
    lengths,
    grid_order,
    grid_keep,
    ground_dist,
    enc_norm,
    enc_query,
    enc_key,
    enc_value,
    enc_proj,
    enc_norm2,
    enc_up,
    enc_down,
    embed_proj,
    mask_token,
    dec_norm,
    dec_query,
    dec_key,
    dec_value,
    dec_proj,
    dec_norm2,
    dec_up,
    dec_down,
    pred_proj,
    cotangent,
):
    fits = kernel_bytes(tokens, enc_up, enc_query, dec_up, pred_proj) <= VMEM_BUDGET
    if not fits or lax.axis_size("mp") != 4:
        return per_device_plain(
            tokens,
            lengths,
            grid_order,
            grid_keep,
            ground_dist,
            enc_norm,
            enc_query,
            enc_key,
            enc_value,
            enc_proj,
            enc_norm2,
            enc_up,
            enc_down,
            embed_proj,
            mask_token,
            dec_norm,
            dec_query,
            dec_key,
            dec_value,
            dec_proj,
            dec_norm2,
            dec_up,
            dec_down,
            pred_proj,
            cotangent,
        )
    enc_weights = (enc_norm, enc_query, enc_key, enc_value, enc_proj, enc_norm2, enc_up, enc_down)
    dec_weights = (dec_norm, dec_query, dec_key, dec_value, dec_proj, dec_norm2, dec_up, dec_down)
    dec_inputs = (dec_query, dec_key, dec_value)
    arrived, *saved, dec_turned = encode(tokens, lengths, enc_weights, embed_proj, dec_inputs)
    decoded, grads = decode_and_back(
        arrived,
        grid_order,
        grid_keep,
        ground_dist,
        dec_weights,
        mask_token,
        pred_proj,
        cotangent,
        tokens,
        enc_weights,
        saved,
        dec_turned,
        embed_proj,
    )
    (
        grad_tokens,
        g_query,
        g_key,
        g_value,
        g_up,
        g_out,
        g_down,
        g_embed,
        n_enc_attn,
        n_enc_mlp,
        n_dec_attn,
        n_dec_mlp,
        n_mask,
        *dec_grads,
    ) = grads
    return (
        decoded,
        grad_tokens.reshape(tokens.shape),
        n_enc_attn[0],
        g_query,
        g_key,
        g_value,
        g_out,
        n_enc_mlp[0],
        g_up,
        g_down,
        g_embed,
        n_mask[0],
        n_dec_attn[0],
        dec_grads[0],
        dec_grads[1],
        dec_grads[2],
        dec_grads[3],
        n_dec_mlp[0],
        dec_grads[4],
        dec_grads[5],
        dec_grads[6],
    )


def solution(mesh):
    return jax.shard_map(
        per_device,
        mesh=mesh,
        in_specs=(
            P(("dp", "mp"), None, None),
            P("dp"),
            P(("dp", "mp"), None),
            P(("dp", "mp"), None),
            P(("dp", "mp")),
            P(),
            P(None, "mp"),
            P(None, "mp"),
            P(None, "mp"),
            P("mp", None),
            P(),
            P(None, "mp"),
            P("mp", None),
            P(None, "mp"),
            P(),
            P(),
            P(),
            P(),
            P(),
            P(),
            P(),
            P(),
            P(),
            P(),
            P(("dp", "mp"), None, None),
        ),
        out_specs=(
            P(("dp", "mp"), None, None),
            P(("dp", "mp"), None, None),
            P(),
            P("dp", "mp"),
            P("dp", "mp"),
            P("dp", "mp"),
            P("mp", "dp"),
            P(),
            P("dp", "mp"),
            P("mp", "dp"),
            P("dp", "mp"),
            P(),
            P(),
            P("dp", "mp"),
            P("dp", "mp"),
            P("dp", "mp"),
            P("dp", "mp"),
            P(),
            P("dp", "mp"),
            P("dp", "mp"),
            P("dp", "mp"),
        ),
        check_vma=False,
    )
```
